32 devices in a mesh: group: 4 (over y, x), wide: 8 (over z, core).
Axes of the slice: x: 2, y: 2, z: 4, core: 2. Of those that a mesh axis runs over, the one named last changes fastest.
Arguments:
- tokens: bfloat16 [2, 8, 1024, 1024], P(None, 'wide', 'group'), may hold values from -6 to 6
- segment_ids: int32 [2, 8, 1024], P(None, 'wide'), may hold values from 0 to 7, never falling along the last dimension, each value on 1 to 512 neighbouring positions
- project_weight: bfloat16 [1024, 3072], P(('group', 'wide')), may hold values from -0.1875 to 0.1875
- project_bias: bfloat16 [3072], P(('group', 'wide')), may hold values from -1.5 to 1.5
- output_weight: bfloat16 [1024, 1024], P(('group', 'wide')), may hold values from -1 to 1
- output_bias: bfloat16 [1024], P(('group', 'wide')), may hold values from -1.5 to 1.5
- first_gain: bfloat16 [1024], P(('group', 'wide')), may hold values from 0.5 to 1.5
- first_shift: bfloat16 [1024], P(('group', 'wide')), may hold values from -1.5 to 1.5
- up_weight: bfloat16 [1024, 4096], P(('group', 'wide')), may hold values from -0.1875 to 0.1875
- up_bias: bfloat16 [4096], P(('group', 'wide')), may hold values from -1.5 to 1.5
- down_weight: bfloat16 [4096, 1024], P(('group', 'wide')), may hold values from -0.09375 to 0.09375
- down_bias: bfloat16 [1024], P(('group', 'wide')), may hold values from -1.5 to 1.5
- second_gain: bfloat16 [1024], P(('group', 'wide')), may hold values from 0.5 to 1.5
- second_shift: bfloat16 [1024], P(('group', 'wide')), may hold values from -1.5 to 1.5
- embed_weight: bfloat16 [1024, 128], P(('group', 'wide')), may hold values from -0.1875 to 0.1875
- out_cotangent: bfloat16 [2, 8, 1024, 1024], P(None, 'wide', 'group'), may hold values from -6 to 6
- embed_cotangent: bfloat16 [2, 8, 1024, 128], P(None, 'wide', 'group'), may hold values from -6 to 6
Outputs:
- layer_out: bfloat16 [2, 8, 1024, 1024], P(None, 'wide', 'group')
- embed_out: bfloat16 [2, 8, 1024, 128], P(None, 'wide', 'group')
- token_grad: float32 [2, 8, 1024, 1024], P(None, 'wide', 'group')
- project_weight_grad: float32 [1024, 3072], P(('group', 'wide'))
- project_bias_grad: float32 [3072], P(('group', 'wide'))
- output_weight_grad: float32 [1024, 1024], P(('group', 'wide'))
- output_bias_grad: float32 [1024], P(('group', 'wide'))
- first_gain_grad: float32 [1024], P(('group', 'wide'))
- first_shift_grad: float32 [1024], P(('group', 'wide'))
- up_weight_grad: float32 [1024, 4096], P(('group', 'wide'))
- up_bias_grad: float32 [4096], P(('group', 'wide'))
- down_weight_grad: float32 [4096, 1024], P(('group', 'wide'))
- down_bias_grad: float32 [1024], P(('group', 'wide'))
- second_gain_grad: float32 [1024], P(('group', 'wide'))
- second_shift_grad: float32 [1024], P(('group', 'wide'))
- embed_weight_grad: float32 [1024, 128], P(('group', 'wide'))
The draws below stay inside these ranges and needn't reach their ends.
Inputs may be any that keep to these rules, and one draw needn't show every extreme that they name: `segment_ids`: in each packed sequence the document numbers never fall, each document has 1 to 512 tokens, and one has exactly 512.
All inputs are finite; a program needn't handle non-finite values.
Results may differ from the reference program's by a relative error of at most 0.015.
Values may be sent and summed in bfloat16 or wider, within the bound.
A program may use at most 192 MiB of HBM per device.

```python
import math
import jax
import jax.numpy as jnp
import numpy as np
from jax import lax

D = 1024
HEADS = 16
HEAD_DIM = 64
FF = 4096
PROJ = 128
MB = 2
DOCS = 8
SEQ = 1024
NSEQ = 8


def shard_levels(rng, dims, split, least, high):
    def one(axis_at, shards_of):
        heights = jax.random.uniform(jax.random.fold_in(jax.random.fold_in(rng, 6), axis_at), (shards_of,), jnp.float32, least / len(split), high / len(split))
        return jnp.repeat(jnp.exp(heights), dims[axis_at] // shards_of).reshape((-1,) + (1,) * (len(dims) - axis_at - 1))

    level = one(*split[0])
    for cut in split[1:]:
        level = level * one(*cut)
    return level


def profile(count, total, limit, lean):
    portions = [(1 << 20) // math.isqrt(standing ** lean) + 1 for standing in range(2, count + 1)]
    rest, given = total - limit - (count - 1), [1] * (count - 1)
    while rest > 0:
        free = [i for i in range(count - 1) if given[i] < limit]
        whole, budget = sum([portions[i] for i in free]), rest
        for i in free:
            more = min(limit - given[i], max(1, budget * portions[i] // whole), rest)
            given[i] = given[i] + more
            rest = rest - more
    return np.array([limit] + given)


def uneven(stream_key, count, total, most, lean):
    if count == 2:
        one = jax.random.randint(stream_key, (), max(1, total - most), min(most, total - 1) + 1)
        return jnp.stack([one, total - one])
    tallies = jnp.asarray(profile(count, total, most, lean), jnp.int32)
    twos = (count - 1) // 2
    donor, taker = tallies[1:1 + 2 * twos:2], tallies[2:2 + 2 * twos:2]
    slack = jnp.minimum(donor - 1, most - taker)
    shifted = jax.random.randint(jax.random.fold_in(stream_key, 1), (twos,), 0, 1 << 20) % (slack + 1)
    tallies = tallies.at[1:1 + 2 * twos:2].set(donor - shifted).at[2:2 + 2 * twos:2].set(taker + shifted)
    return tallies[jax.random.permutation(jax.random.fold_in(stream_key, 2), count)]


def noise(own_key, extent, scale, limit, split=(), kind=jnp.bfloat16):
    entries = jax.random.normal(own_key, extent, jnp.float32) * scale
    if len(split) > 0:
        entries = shard_levels(own_key, extent, split, -0.22, 0.18) * entries
    return jnp.clip(entries, min=-limit, max=limit).astype(kind)


def setup_inputs(seed: int = 0) -> dict:
    streams_of = jax.random.split(jax.random.key(seed), 18)
    return {
        "tokens": noise(streams_of[0], (MB, NSEQ, SEQ, D), 1.0, 6.0, ((1, 8), (2, 4))),
        "segment_ids": jax.vmap(lambda own: jnp.searchsorted(jnp.cumsum(uneven(own, DOCS, SEQ, SEQ // 2, 2)), jnp.arange(SEQ), side="right"))(jax.random.split(streams_of[1], MB * NSEQ)).reshape((MB, NSEQ, SEQ)).astype(jnp.int32),
        "project_weight": noise(streams_of[2], (D, 3 * D), D ** -0.5, 0.1875, ((0, 32),)),
        "project_bias": noise(streams_of[3], (3 * D,), 0.3, 1.5, ((0, 32),)),
        "output_weight": noise(streams_of[4], (D, D), (D // 32) ** -0.5, 1.0, ((0, 32),)),
        "output_bias": noise(streams_of[5], (D,), 0.3, 1.5, ((0, 32),)),
        "first_gain": jnp.clip(1.0 + 0.1 * jax.random.normal(streams_of[6], (D,), jnp.float32), 0.5, 1.5).astype(jnp.bfloat16),
        "first_shift": noise(streams_of[7], (D,), 0.3, 1.5, ((0, 32),)),
        "up_weight": noise(streams_of[8], (D, FF), D ** -0.5, 0.1875, ((0, 32),)),
        "up_bias": noise(streams_of[9], (FF,), 0.3, 1.5, ((0, 32),)),
        "down_weight": noise(streams_of[10], (FF, D), FF ** -0.5, 0.09375, ((0, 32),)),
        "down_bias": noise(streams_of[11], (D,), 0.3, 1.5, ((0, 32),)),
        "second_gain": jnp.clip(1.0 + 0.1 * jax.random.normal(streams_of[12], (D,), jnp.float32), 0.5, 1.5).astype(jnp.bfloat16),
        "second_shift": noise(streams_of[13], (D,), 0.3, 1.5, ((0, 32),)),
        "embed_weight": noise(streams_of[14], (D, PROJ), D ** -0.5, 0.1875, ((0, 32),)),
        "out_cotangent": noise(streams_of[15], (MB, NSEQ, SEQ, D), 1.0, 6.0, ((1, 8), (2, 4))),
        "embed_cotangent": noise(streams_of[16], (MB, NSEQ, SEQ, PROJ), 1.0, 6.0, ((1, 8), (2, 4))),
    }


eps_norm = 1e-05
neg_large = -1e+30

@jax.custom_vjp
def low(v):
    return lax.optimization_barrier(v.astype(jnp.bfloat16)).astype(jnp.float32)

@jax.custom_vjp
def low_back(v):
    return v

def low_keep(v):
    return (low(v), None)

def low_pass(kept, grad):
    return (grad,)

def back_keep(v):
    return (v, None)

def back_low(kept, grad):
    return (low(grad),)
low.defvjp(low_keep, low_pass)
low_back.defvjp(back_keep, back_low)

def highest_dot(left, right):
    return jnp.dot(left, right, precision=lax.Precision.HIGHEST)

def rotary_tables(length):
    half_dim = HEAD_DIM // 2
    frequency = 10000.0 ** (-jnp.arange(half_dim, dtype=jnp.float32) * (2.0 / HEAD_DIM))
    angles = jnp.arange(length, dtype=jnp.float32)[:, None] * frequency[None, :]
    angles = jnp.concatenate([angles, angles], axis=1)
    return (jnp.cos(angles), jnp.sin(angles))

def rotate(values, cosine_table, sine_table):
    half_dim = HEAD_DIM // 2
    swapped = jnp.concatenate([-values[..., half_dim:], values[..., :half_dim]], axis=-1)
    return values * cosine_table[:, None, :] + swapped * sine_table[:, None, :]

def layer_norm(resid, gain, shift):
    center = resid - lax.optimization_barrier(jnp.mean(resid, axis=-1, keepdims=True))
    spread = lax.optimization_barrier(jnp.mean(center * center, axis=-1, keepdims=True))
    return center * lax.rsqrt(spread + eps_norm) * gain + shift

def attend(queries, key_rows, value_rows, segments):
    total_rows = queries.shape[0]
    block_rows = min(512, total_rows)
    count = total_rows // block_rows
    query_blocks = queries.reshape(count, block_rows, HEADS, HEAD_DIM)
    seg_blocks = segments.reshape(count, block_rows)
    scale = HEAD_DIM ** (-0.5)

    def one_block(pieces):
        query_block, seg_block = pieces
        scores = jnp.einsum('qhd,khd->hqk', query_block, key_rows, precision=lax.Precision.HIGHEST) * scale
        scores = low_back(scores)
        same = seg_block[:, None] == segments[None, :]
        scores = jnp.where(same[None], scores, neg_large)
        row_max = lax.optimization_barrier(jnp.max(scores, axis=-1, keepdims=True))
        expon = jnp.exp(scores - row_max)
        probs = low(expon / lax.optimization_barrier(jnp.sum(expon, axis=-1, keepdims=True)))
        return jnp.einsum('hqk,khd->qhd', probs, value_rows, precision=lax.Precision.HIGHEST)
    result = lax.map(jax.checkpoint(one_block), (query_blocks, seg_blocks))
    return result.reshape(total_rows, HEADS, HEAD_DIM)

def forward(tokens, segments, params):
    project_weight, project_bias, output_weight, output_bias, first_gain, first_shift, up_weight, up_bias, down_weight, down_bias, second_gain, second_shift, embed_weight = params
    length = tokens.shape[0]
    projected = low_back(highest_dot(tokens, project_weight) + project_bias)
    cosine_table, sine_table = rotary_tables(length)
    head_shape = (length, HEADS, HEAD_DIM)
    queries = low(rotate(projected[:, :D].reshape(head_shape), cosine_table, sine_table))
    key_rows = low(rotate(projected[:, D:2 * D].reshape(head_shape), cosine_table, sine_table))
    value_rows = low(projected[:, 2 * D:].reshape(head_shape))
    context = attend(queries, key_rows, value_rows, segments)
    context = low(low_back(context.reshape(length, D)))
    branch = low_back(highest_dot(context, output_weight) + output_bias)
    hidden = layer_norm(tokens + branch, first_gain, first_shift)
    up_value = low_back(highest_dot(low(hidden), up_weight) + up_bias)
    down_value = low_back(highest_dot(low(jax.nn.gelu(up_value, approximate=False)), down_weight) + down_bias)
    result = low(layer_norm(hidden + down_value, second_gain, second_shift))
    return (result, highest_dot(result, embed_weight))

def reference(tokens, segment_ids, project_weight, project_bias, output_weight, output_bias, first_gain, first_shift, up_weight, up_bias, down_weight, down_bias, second_gain, second_shift, embed_weight, out_cotangent, embed_cotangent):
    params = tuple((item.astype(jnp.float32) for item in (project_weight, project_bias, output_weight, output_bias, first_gain, first_shift, up_weight, up_bias, down_weight, down_bias, second_gain, second_shift, embed_weight)))
    count = MB * NSEQ
    token_seqs = tokens.reshape(count, SEQ, D).astype(jnp.float32)
    seg_seqs = segment_ids.reshape(count, SEQ)
    out_seqs = out_cotangent.reshape(count, SEQ, D).astype(jnp.float32)
    embed_seqs = embed_cotangent.reshape(count, SEQ, PROJ).astype(jnp.float32)

    def one_sequence(carry, pieces):
        token_rows, seg_rows, out_rows, embed_rows = pieces

        def apply(inputs, weights):
            return forward(inputs, seg_rows, weights)
        (result, embedded), pull = jax.vjp(apply, token_rows, params)
        input_grad, param_grads = pull((out_rows, embed_rows))
        carry = tuple((total + part for total, part in zip(carry, param_grads)))
        return (carry, (result, embedded, input_grad))
    zeros = tuple((jnp.zeros(item.shape, jnp.float32) for item in params))
    grads, (results, embeddings, input_grads) = lax.scan(one_sequence, zeros, (token_seqs, seg_seqs, out_seqs, embed_seqs))
    layer_out = results.reshape(MB, NSEQ, SEQ, D).astype(jnp.bfloat16)
    embed_out = embeddings.reshape(MB, NSEQ, SEQ, PROJ).astype(jnp.bfloat16)
    token_grad = input_grads.reshape(MB, NSEQ, SEQ, D)
    return (layer_out, embed_out, token_grad, grads[0], grads[1], grads[2], grads[3], grads[4], grads[5], grads[6], grads[7], grads[8], grads[9], grads[10], grads[11], grads[12])
```

```python
import functools

import jax
import jax.numpy as jnp
from jax import lax
from jax.experimental import pallas as pl
from jax.experimental.pallas import tpu as pltpu
from jax.sharding import PartitionSpec as P

HEADS = 16
HEAD_DIM = 64


eps_norm = 1e-05
neg_large = -1e30


def rotary_tables(positions):
    half_dim = HEAD_DIM // 2
    frequency = 10000.0 ** (-jnp.arange(half_dim, dtype=jnp.float32) * (2.0 / HEAD_DIM))
    angles = positions[:, None] * frequency[None, :]
    angles = jnp.concatenate([angles, angles], axis=1)
    return (jnp.cos(angles), jnp.sin(angles))


def rotate(values, cosine_table, sine_table):
    half_dim = HEAD_DIM // 2
    swapped = jnp.concatenate([-values[..., half_dim:], values[..., :half_dim]], axis=-1)
    return values * cosine_table[:, None, :] + swapped * sine_table[:, None, :]


def unrotate(grads, cosine_table, sine_table):
    half_dim = HEAD_DIM // 2
    scaled = grads * sine_table[:, None, :]
    swapped = jnp.concatenate([scaled[..., half_dim:], -scaled[..., :half_dim]], axis=-1)
    return grads * cosine_table[:, None, :] + swapped


def norm_forward(resid, gain, shift):
    center = resid - jnp.mean(resid, axis=-1, keepdims=True)
    spread = jnp.mean(center * center, axis=-1, keepdims=True)
    rstd_rows = lax.rsqrt(spread + eps_norm)
    normed = center * rstd_rows
    return (normed * gain + shift, normed, rstd_rows)


def norm_backward(grads, normed, rstd_rows, gain):
    scaled = grads * gain
    resid_grad = rstd_rows * (
        scaled
        - jnp.mean(scaled, axis=-1, keepdims=True)
        - normed * jnp.mean(scaled * normed, axis=-1, keepdims=True)
    )
    return (resid_grad, jnp.sum(grads * normed, axis=0), jnp.sum(grads, axis=0))


def contract_rows(left, right):
    return lax.dot_general(
        left, right, (((0,), (0,)), ((), ())), preferred_element_type=jnp.float32
    )


def times_transpose(left, right):
    return lax.dot_general(
        left, right, (((1,), (1,)), ((), ())), preferred_element_type=jnp.float32
    )


def gelu_slope(value):
    normal_cdf = 0.5 * (1.0 + lax.erf(value * 0.7071067811865476))
    density = jnp.exp(-0.5 * value * value) * 0.3989422804014327
    return normal_cdf + value * density


def key_blocks(kv_rows, seg_all):
    seq_len = kv_rows.shape[0]
    block_rows = min(512, seq_len)
    count = seq_len // block_rows
    return (
        kv_rows.reshape(count, block_rows, 2, HEADS, HEAD_DIM),
        seg_all.reshape(count, block_rows),
    )


def block_scores(queries, key_block, same):
    scores = jnp.einsum("qhd,khd->hqk", queries, key_block, preferred_element_type=jnp.float32)
    scores = scores * HEAD_DIM ** (-0.5)
    return jnp.where(same[None], scores, neg_large)


def attention_forward(queries, blocks, seg_blocks, seg_local):
    length = queries.shape[0]

    def norm_step(carry, pieces):
        kv_block, seg_block = pieces
        same = seg_local[:, None] == seg_block[None, :]

        def norm_update(running):
            run_max, run_sum = running
            scores = block_scores(queries, kv_block[:, 0], same)
            new_max = jnp.maximum(run_max, jnp.max(scores, axis=-1))
            new_sum = run_sum * jnp.exp(run_max - new_max) + jnp.sum(
                jnp.exp(scores - new_max[..., None]), axis=-1
            )
            return (new_max, new_sum)

        def norm_unchanged(running):
            return running

        return (lax.cond(jnp.any(same), norm_update, norm_unchanged, carry), None)

    start = (
        jnp.full((HEADS, length), neg_large, jnp.float32),
        jnp.zeros((HEADS, length), jnp.float32),
    )
    (run_max, run_sum), unused = lax.scan(norm_step, start, (blocks, seg_blocks))
    log_norm = run_max + jnp.log(run_sum)

    def value_step(total, pieces):
        kv_block, seg_block = pieces
        same = seg_local[:, None] == seg_block[None, :]

        def value_update(running):
            scores = block_scores(queries, kv_block[:, 0], same)
            weights = jnp.exp(scores - log_norm[..., None]).astype(jnp.bfloat16)
            return running + jnp.einsum(
                "hqk,khd->qhd", weights, kv_block[:, 1], preferred_element_type=jnp.float32
            )

        def value_unchanged(running):
            return running

        return (lax.cond(jnp.any(same), value_update, value_unchanged, total), None)

    context, unused = lax.scan(
        value_step, jnp.zeros(queries.shape, jnp.float32), (blocks, seg_blocks)
    )
    return (context, log_norm)


def attention_backward(queries, blocks, seg_blocks, seg_local, log_norm, context_grad, delta):

    def grad_step(query_grad, pieces):
        kv_block, seg_block = pieces
        same = seg_local[:, None] == seg_block[None, :]

        def work(running):
            scores = block_scores(queries, kv_block[:, 0], same)
            probs = jnp.exp(scores - log_norm[..., None])
            prob_grad = jnp.einsum(
                "qhd,khd->hqk", context_grad, kv_block[:, 1], preferred_element_type=jnp.float32
            )
            score_grad = (probs * (prob_grad - delta[..., None])).astype(jnp.bfloat16)
            running = running + jnp.einsum(
                "hqk,khd->qhd", score_grad, kv_block[:, 0], preferred_element_type=jnp.float32
            ) * HEAD_DIM ** (-0.5)
            prob_low = probs.astype(jnp.bfloat16)
            key_grad = jnp.einsum(
                "hqk,qhd->khd", score_grad, queries, preferred_element_type=jnp.float32
            ) * HEAD_DIM ** (-0.5)
            value_grad = jnp.einsum(
                "hqk,qhd->khd", prob_low, context_grad, preferred_element_type=jnp.float32
            )
            return (running, jnp.stack([key_grad, value_grad], axis=1))

        def skipped(running):
            return (running, jnp.zeros(kv_block.shape, jnp.float32))

        return lax.cond(jnp.any(same), work, skipped, query_grad)

    query_grad, kv_grad = lax.scan(
        grad_step, jnp.zeros(queries.shape, jnp.float32), (blocks, seg_blocks)
    )
    return (query_grad, kv_grad.reshape(-1, 2 * HEADS * HEAD_DIM))


def general_device(
    tokens,
    segment_ids,
    project_weight,
    project_bias,
    output_weight,
    output_bias,
    first_gain,
    first_shift,
    up_weight,
    up_bias,
    down_weight,
    down_bias,
    second_gain,
    second_shift,
    embed_weight,
    out_cotangent,
    embed_cotangent,
):
    shards = (
        project_weight,
        project_bias,
        output_weight,
        output_bias,
        first_gain,
        first_shift,
        up_weight,
        up_bias,
        down_weight,
        down_bias,
        second_gain,
        second_shift,
        embed_weight,
    )
    length = tokens.shape[2]
    width = HEADS * HEAD_DIM
    head_shape = (length, HEADS, HEAD_DIM)
    place = lax.axis_index("group")
    positions = (place * length + jnp.arange(length)).astype(jnp.float32)
    cosine_table, sine_table = rotary_tables(positions)
    grad_total = None
    results = []
    embeddings = []
    input_grads = []
    for micro_index in range(tokens.shape[0]):
        params = (
            lax.all_gather(shards[0], ("group", "wide"), axis=0, tiled=True),
            lax.all_gather(shards[1], ("group", "wide"), axis=0, tiled=True),
            lax.all_gather(shards[2], ("group", "wide"), axis=0, tiled=True),
            lax.all_gather(shards[3], ("group", "wide"), axis=0, tiled=True),
            lax.all_gather(shards[4], ("group", "wide"), axis=0, tiled=True),
            lax.all_gather(shards[5], ("group", "wide"), axis=0, tiled=True),
            lax.all_gather(shards[6], ("group", "wide"), axis=0, tiled=True),
            lax.all_gather(shards[7], ("group", "wide"), axis=0, tiled=True),
            lax.all_gather(shards[8], ("group", "wide"), axis=0, tiled=True),
            lax.all_gather(shards[9], ("group", "wide"), axis=0, tiled=True),
            lax.all_gather(shards[10], ("group", "wide"), axis=0, tiled=True),
            lax.all_gather(shards[11], ("group", "wide"), axis=0, tiled=True),
            lax.all_gather(shards[12], ("group", "wide"), axis=0, tiled=True),
        )
        seg_all = segment_ids[micro_index, 0]
        seg_local = lax.dynamic_slice_in_dim(seg_all, place * length, length)
        token_low = tokens[micro_index, 0]
        token_wide = token_low.astype(jnp.float32)
        projected = jnp.dot(token_low, params[0], preferred_element_type=jnp.float32) + params[
            1
        ].astype(jnp.float32)
        queries = rotate(projected[:, :width].reshape(head_shape), cosine_table, sine_table).astype(
            jnp.bfloat16
        )
        key_rows = rotate(
            projected[:, width : 2 * width].reshape(head_shape), cosine_table, sine_table
        ).astype(jnp.bfloat16)
        value_rows = projected[:, 2 * width :].astype(jnp.bfloat16)
        local_kv = jnp.concatenate([key_rows.reshape(length, width), value_rows], axis=1)
        kv_all = lax.all_gather(local_kv, "group", axis=0, tiled=True)
        blocks, seg_blocks = key_blocks(kv_all, seg_all)
        context, log_norm = attention_forward(queries, blocks, seg_blocks, seg_local)
        context_low = context.reshape(length, width).astype(jnp.bfloat16)
        branch = jnp.dot(context_low, params[2], preferred_element_type=jnp.float32) + params[
            3
        ].astype(jnp.float32)
        first_gain_wide = params[4].astype(jnp.float32)
        hidden, first_normed, first_rstd = norm_forward(
            token_wide + branch, first_gain_wide, params[5].astype(jnp.float32)
        )
        hidden_low = hidden.astype(jnp.bfloat16)
        up_value = jnp.dot(hidden_low, params[6], preferred_element_type=jnp.float32) + params[
            7
        ].astype(jnp.float32)
        act_low = jax.nn.gelu(up_value, approximate=False).astype(jnp.bfloat16)
        down_value = jnp.dot(act_low, params[8], preferred_element_type=jnp.float32) + params[
            9
        ].astype(jnp.float32)
        second_gain_wide = params[10].astype(jnp.float32)
        result, second_normed, second_rstd = norm_forward(
            hidden + down_value, second_gain_wide, params[11].astype(jnp.float32)
        )
        result_low = result.astype(jnp.bfloat16)
        embedded = jnp.dot(result_low, params[12], preferred_element_type=jnp.float32)
        results.append(result_low)
        embeddings.append(embedded.astype(jnp.bfloat16))
        params = (
            lax.all_gather(shards[0], ("group", "wide"), axis=0, tiled=True),
            lax.all_gather(shards[1], ("group", "wide"), axis=0, tiled=True),
            lax.all_gather(shards[2], ("group", "wide"), axis=0, tiled=True),
            lax.all_gather(shards[3], ("group", "wide"), axis=0, tiled=True),
            lax.all_gather(shards[4], ("group", "wide"), axis=0, tiled=True),
            lax.all_gather(shards[5], ("group", "wide"), axis=0, tiled=True),
            lax.all_gather(shards[6], ("group", "wide"), axis=0, tiled=True),
            lax.all_gather(shards[7], ("group", "wide"), axis=0, tiled=True),
            lax.all_gather(shards[8], ("group", "wide"), axis=0, tiled=True),
            lax.all_gather(shards[9], ("group", "wide"), axis=0, tiled=True),
            lax.all_gather(shards[10], ("group", "wide"), axis=0, tiled=True),
            lax.all_gather(shards[11], ("group", "wide"), axis=0, tiled=True),
            lax.all_gather(shards[12], ("group", "wide"), axis=0, tiled=True),
        )
        embed_cot = embed_cotangent[micro_index, 0]
        result_grad = out_cotangent[micro_index, 0].astype(jnp.float32) + times_transpose(
            embed_cot, params[12]
        )
        embed_weight_grad = contract_rows(result_low, embed_cot)
        sum_grad, second_gain_grad, second_shift_grad = norm_backward(
            result_grad, second_normed, second_rstd, second_gain_wide
        )
        down_grad = sum_grad.astype(jnp.bfloat16)
        down_bias_grad = jnp.sum(down_grad.astype(jnp.float32), axis=0)
        down_weight_grad = contract_rows(act_low, down_grad)
        up_grad = (times_transpose(down_grad, params[8]) * gelu_slope(up_value)).astype(
            jnp.bfloat16
        )
        up_bias_grad = jnp.sum(up_grad.astype(jnp.float32), axis=0)
        up_weight_grad = contract_rows(hidden_low, up_grad)
        hidden_grad = sum_grad + times_transpose(up_grad, params[6])
        first_grad, first_gain_grad, first_shift_grad = norm_backward(
            hidden_grad, first_normed, first_rstd, first_gain_wide
        )
        branch_grad = first_grad.astype(jnp.bfloat16)
        output_bias_grad = jnp.sum(branch_grad.astype(jnp.float32), axis=0)
        output_weight_grad = contract_rows(context_low, branch_grad)
        context_grad = (
            times_transpose(branch_grad, params[2]).astype(jnp.bfloat16).reshape(head_shape)
        )
        delta = jnp.transpose(jnp.sum(context_grad.astype(jnp.float32) * context, axis=-1))
        kv_again = lax.all_gather(local_kv, "group", axis=0, tiled=True)
        blocks, seg_blocks = key_blocks(kv_again, seg_all)
        query_grad, kv_partial = attention_backward(
            queries, blocks, seg_blocks, seg_local, log_norm, context_grad, delta
        )
        kv_grad = lax.psum_scatter(
            kv_partial.astype(jnp.bfloat16), "group", scatter_dimension=0, tiled=True
        ).astype(jnp.float32)
        key_part = kv_grad[:, :width].reshape(head_shape)
        value_part = kv_grad[:, width:]
        query_back = unrotate(query_grad, cosine_table, sine_table).reshape(length, width)
        key_back = unrotate(key_part, cosine_table, sine_table).reshape(length, width)
        projected_grad = jnp.concatenate([query_back, key_back, value_part], axis=1).astype(
            jnp.bfloat16
        )
        project_bias_grad = jnp.sum(projected_grad.astype(jnp.float32), axis=0)
        project_weight_grad = contract_rows(token_low, projected_grad)
        input_grads.append(first_grad + times_transpose(projected_grad, params[0]))
        local_grads = (
            project_weight_grad,
            project_bias_grad,
            output_weight_grad,
            output_bias_grad,
            first_gain_grad,
            first_shift_grad,
            up_weight_grad,
            up_bias_grad,
            down_weight_grad,
            down_bias_grad,
            second_gain_grad,
            second_shift_grad,
            embed_weight_grad,
        )
        summed = (
            lax.psum_scatter(local_grads[0], ("group", "wide"), scatter_dimension=0, tiled=True),
            lax.psum_scatter(local_grads[1], ("group", "wide"), scatter_dimension=0, tiled=True),
            lax.psum_scatter(local_grads[2], ("group", "wide"), scatter_dimension=0, tiled=True),
            lax.psum_scatter(local_grads[3], ("group", "wide"), scatter_dimension=0, tiled=True),
            lax.psum_scatter(local_grads[4], ("group", "wide"), scatter_dimension=0, tiled=True),
            lax.psum_scatter(local_grads[5], ("group", "wide"), scatter_dimension=0, tiled=True),
            lax.psum_scatter(local_grads[6], ("group", "wide"), scatter_dimension=0, tiled=True),
            lax.psum_scatter(local_grads[7], ("group", "wide"), scatter_dimension=0, tiled=True),
            lax.psum_scatter(local_grads[8], ("group", "wide"), scatter_dimension=0, tiled=True),
            lax.psum_scatter(local_grads[9], ("group", "wide"), scatter_dimension=0, tiled=True),
            lax.psum_scatter(local_grads[10], ("group", "wide"), scatter_dimension=0, tiled=True),
            lax.psum_scatter(local_grads[11], ("group", "wide"), scatter_dimension=0, tiled=True),
            lax.psum_scatter(local_grads[12], ("group", "wide"), scatter_dimension=0, tiled=True),
        )
        grad_total = (
            summed
            if grad_total is None
            else tuple((total + part for total, part in zip(grad_total, summed)))
        )
    layer_out = jnp.stack(results)[:, None]
    embed_out = jnp.stack(embeddings)[:, None]
    token_grad = jnp.stack(input_grads)[:, None]
    return (
        layer_out,
        embed_out,
        token_grad,
        grad_total[0],
        grad_total[1],
        grad_total[2],
        grad_total[3],
        grad_total[4],
        grad_total[5],
        grad_total[6],
        grad_total[7],
        grad_total[8],
        grad_total[9],
        grad_total[10],
        grad_total[11],
        grad_total[12],
    )


MESH = pl.DeviceIdType.MESH
F32 = jnp.float32
BF16 = jnp.bfloat16
PLANE = 4
LINE = 4
GATHER_SEMS = 42
REDUCE_SEMS = 56
GATHER_AHEAD = (3, 6)
REDUCE_AHEAD = (3, 5, 7)
SMALL_ROWS = 16


def place():
    group = lax.axis_index("group")
    wide = lax.axis_index("wide")
    return (group, lax.rem(group, 2), group // 2, wide // 2, lax.rem(wide, 2))


def when(cond, act):
    if cond is True:
        act()
    else:
        pl.when(cond)(act)


def both(left, right):
    return right if left is True else jnp.logical_and(left, right)


def remote(src, dst, send_sem, recv_sem, device):
    return pltpu.make_async_remote_copy(
        src_ref=src,
        dst_ref=dst,
        send_sem=send_sem,
        recv_sem=recv_sem,
        device_id=device,
        device_id_type=MESH,
    )


def entry_barrier():
    g, x, y, z, c = place()
    devices = []
    for step in range(1, 8):
        other = lax.rem(g * 2 + c + step, 8)
        devices.append((other // 2, z * 2 + lax.rem(other, 2)))
    devices.append((g, lax.rem(z + 1, LINE) * 2 + c))
    devices.append((g, lax.rem(z + LINE - 1, LINE) * 2 + c))
    barrier = pltpu.get_barrier_semaphore()
    for device in devices:
        pl.semaphore_signal(barrier, inc=1, device_id=device, device_id_type=MESH)
    pl.semaphore_wait(barrier, len(devices))


class Sender:
    def __init__(self, send_sems, recv_sems):
        self.send_sems, self.recv_sems, self.pending = send_sems, recv_sems, []

    def copy(self, src, dst, index, device):
        return remote(src, dst, self.send_sems.at[index], self.recv_sems.at[index], device)

    def send(self, cond, src, dst, index, device):
        when(cond, lambda: self.copy(src, dst, index, device).start())
        self.pending.append((cond, lambda: self.copy(src, dst, index, device).wait_send()))

    def land(self, ref, index, device):
        self.copy(ref, ref, index, device).wait_recv()

    def drain(self):
        for cond, done in self.pending:
            when(cond, done)


def near_items(z, distance):
    if distance == 0:
        return [(0, z, True)]
    return [
        (distance, jnp.maximum(z - distance, 0), z >= distance),
        (3 + distance, jnp.minimum(z + distance, LINE - 1), z + distance < LINE),
    ]


def gather_ticks(shards, fulls, splits, sender, local_sems):
    g, x, y, z, c = place()
    gx, gy, gd = g + 1 - 2 * x, g + 2 - 4 * y, 3 - g
    to_x, to_y, to_core = (gx, z * 2 + c), (gy, z * 2 + c), (g, z * 2 + 1 - c)
    above = (g, jnp.minimum(z + 1, LINE - 1) * 2 + c)
    below = (g, jnp.maximum(z - 1, 0) * 2 + c)

    def first(a, k):
        base = a * GATHER_SEMS
        for slot, zi, cond in near_items(z, k):
            region = fulls[a].at[g, zi, c]
            if k == 0:
                pltpu.make_async_copy(shards[a], region, local_sems.at[a]).start()
                source = shards[a]
                sender.send(z < LINE - 1, source, region, base + 1, above)
                sender.send(z > 0, source, region, base + 4, below)
            else:
                source = region
                when(cond, lambda: sender.land(region, base + slot, to_x))
                if k < LINE - 1:
                    if slot < 4:
                        sender.send(both(cond, z < LINE - 1), source, region, base + slot + 1, above)
                    else:
                        sender.send(both(cond, z > 0), source, region, base + slot + 1, below)
            sender.send(cond, source, region, base + 7 + slot, to_x)
            sender.send(cond, source, region, base + 14 + slot, to_y)

    def second(a, k):
        base, cut, rows = a * GATHER_SEMS, splits[a], fulls[a].shape[3]
        for slot, zi, cond in near_items(z, k):
            when(cond, lambda: sender.land(fulls[a].at[gx, zi, c], base + 7 + slot, to_x))
            upper = fulls[a].at[gx, zi, c, 0:cut]
            sender.send(cond, upper, upper, base + 21 + slot, to_y)
            when(cond, lambda: sender.land(fulls[a].at[gy, zi, c], base + 14 + slot, to_x))
            lower = fulls[a].at[gy, zi, c, cut:rows]
            sender.send(cond, lower, lower, base + 28 + slot, to_x)

    def third(a, k):
        base, cut, rows = a * GATHER_SEMS, splits[a], fulls[a].shape[3]
        if k == 0:
            pltpu.make_async_copy(shards[a], fulls[a].at[g, z, c], local_sems.at[a]).wait()
        for slot, zi, cond in near_items(z, k):
            when(cond, lambda: sender.land(fulls[a].at[gd, zi, c, 0:cut], base + 21 + slot, to_x))
            when(cond, lambda: sender.land(fulls[a].at[gd, zi, c, cut:rows], base + 28 + slot, to_x))
            ring = fulls[a].at[:, zi, c]
            sender.send(cond, ring, ring, base + 35 + slot, to_core)

    def finish():
        for a in range(len(shards)):
            for k in range(LINE):
                for slot, zi, cond in near_items(z, k):
                    when(
                        cond,
                        lambda: sender.land(
                            fulls[a].at[:, zi, 1 - c], a * GATHER_SEMS + 35 + slot, to_x
                        ),
                    )

    order = [(a, k) for a in range(len(shards)) for k in range(LINE)]
    return (staged(order, (first, second, third), (0,) + GATHER_AHEAD), finish)


def staged(order, stages, delays):
    ticks = []
    for t in range(len(order) + delays[-1]):

        def tick(t=t):
            for stage, delay in zip(stages, delays):
                if 0 <= t - delay < len(order):
                    stage(*order[t - delay])

        ticks.append(tick)
    return ticks


def add_into(target, terms):
    rows, columns = target.shape
    step = min(columns, 512)

    def body(i, carry):
        cut = pl.ds(pl.multiple_of(i * step, step), step)
        value = terms[0][:, cut].astype(F32)
        for term in terms[1:]:
            value = value + term[:, cut].astype(F32)
        target[:, cut] = value.astype(target.dtype)
        return carry

    lax.fori_loop(0, columns // step, body, 0)


def reduce_ticks(grads, outs, splits, held, core_in, half_in, whole_in, rise_in, fall_in, sender, local_sems):
    g, x, y, z, c = place()
    gx, gy, gd = g + 1 - 2 * x, g + 2 - 4 * y, 3 - g
    to_x, to_y, to_core = (gx, z * 2 + c), (gy, z * 2 + c), (g, z * 2 + 1 - c)
    above = (g, jnp.minimum(z + 1, LINE - 1) * 2 + c)
    below = (g, jnp.maximum(z - 1, 0) * 2 + c)

    def far_items(k):
        items = near_items(z, k)
        if k == 0:
            return items
        return [(k,) + items[1][1:], (3 + k,) + items[0][1:]]

    def load(a, zi, slot):
        return pltpu.make_async_copy(
            grads[a].at[:, zi, c], held[a].at[zi], local_sems.at[a * 7 + slot]
        )

    def zeroth(a, k):
        base = a * REDUCE_SEMS
        for slot, zi, cond in far_items(k):
            sender.send(cond, grads[a].at[:, zi, 1 - c], core_in[a].at[zi], base + slot, to_core)
            when(cond, lambda: load(a, zi, slot).start())

    def first(a, k):
        base, cut, rows = a * REDUCE_SEMS, splits[a], held[a].shape[2]
        for slot, zi, cond in far_items(k):

            def work():
                load(a, zi, slot).wait()
                sender.land(core_in[a].at[zi], base + slot, to_x)
                for j in range(PLANE):
                    add_into(held[a].at[zi, j], [held[a].at[zi, j], core_in[a].at[zi, j]])

            when(cond, work)
            sender.send(
                cond, held[a].at[zi, gd, 0:cut], half_in[a].at[zi, 0:cut], base + 7 + slot, to_y
            )
            sender.send(
                cond, held[a].at[zi, gd, cut:rows], half_in[a].at[zi, cut:rows], base + 14 + slot, to_x
            )

    def second(a, k):
        base, cut, rows = a * REDUCE_SEMS, splits[a], held[a].shape[2]
        for slot, zi, cond in far_items(k):

            def upper():
                sender.land(half_in[a].at[zi, 0:cut], base + 7 + slot, to_x)
                mine = held[a].at[zi, gx, 0:cut]
                add_into(mine, [mine, half_in[a].at[zi, 0:cut]])

            when(cond, upper)
            sender.send(cond, held[a].at[zi, gx], whole_in[a].at[zi, 0], base + 21 + slot, to_x)

            def lower():
                sender.land(half_in[a].at[zi, cut:rows], base + 14 + slot, to_x)
                mine = held[a].at[zi, gy, cut:rows]
                add_into(mine, [mine, half_in[a].at[zi, cut:rows]])

            when(cond, lower)
            sender.send(cond, held[a].at[zi, gy], whole_in[a].at[zi, 1], base + 28 + slot, to_y)

    def third(a, k):
        base = a * REDUCE_SEMS
        for slot, zi, cond in far_items(k):
            mine = held[a].at[zi, g]
            terms = [mine, whole_in[a].at[zi, 0], whole_in[a].at[zi, 1]]
            rise, fall = rise_in[a].at[zi], fall_in[a].at[zi]

            def arrive():
                sender.land(whole_in[a].at[zi, 0], base + 21 + slot, to_x)
                sender.land(whole_in[a].at[zi, 1], base + 28 + slot, to_x)

            when(cond, arrive)
            if k == 0:
                when(z > 0, lambda: sender.land(rise, base + 36, to_x))
                when(z < LINE - 1, lambda: sender.land(fall, base + 43, to_x))
                when(z == 0, lambda: add_into(outs[a], terms + [fall]))
                when(z == LINE - 1, lambda: add_into(outs[a], terms + [rise]))
                when(
                    jnp.logical_and(z > 0, z < LINE - 1),
                    lambda: add_into(outs[a], terms + [rise, fall]),
                )
            else:
                going_up = slot < 4
                moved = rise if going_up else fall
                offset = base + (35 if going_up else 42)
                inner = (z > 0) if going_up else (z < LINE - 1)

                def join():
                    sender.land(moved, offset + k + 1, to_x)
                    add_into(mine, terms + [moved])

                if k < LINE - 1:
                    when(both(cond, inner), join)
                when(both(cond, jnp.logical_not(inner)), lambda: add_into(mine, terms))
                sender.send(cond, mine, moved, offset + k, above if going_up else below)

    order = [(a, k) for a in range(len(grads)) for k in (3, 2, 1, 0)]
    return staged(order, (zeroth, first, second, third), (0,) + REDUCE_AHEAD)


def exchange(sources, targets, outward, sender, base, local_sems, local_base):
    g, x, y, z, c = place()

    def partner(index):
        if outward:
            return (index * 2 + c, z * 2 + g // 2)
        return (2 * c + index, z * 2 + lax.rem(g, 2))

    def origin(index):
        if outward:
            return (2 * c + index, z * 2 + lax.rem(g, 2))
        return (index * 2 + c, z * 2 + g // 2)

    slot = lax.rem(g, 2) if outward else g // 2

    def post(i, index):
        chip, wide = partner(index)
        same = jnp.logical_and(chip == g, wide == z * 2 + c)
        other = jnp.logical_not(same)
        source, target = sources[i].at[index], targets[i].at[slot]
        at = base + i * 4

        def copy():
            return remote(
                source,
                target,
                sender.send_sems.at[at + 2 + index],
                sender.recv_sems.at[at + slot],
                (chip, wide),
            )

        when(
            same,
            lambda: pltpu.make_async_copy(source, target, local_sems.at[local_base + i]).start(),
        )
        when(other, lambda: copy().start())
        sender.pending.append((other, lambda: copy().wait_send()))

    for i in range(len(sources)):
        for index in range(2):
            post(i, index)

    def arrive():
        for i in range(len(sources)):
            for index in range(2):
                chip, wide = origin(index)
                same = jnp.logical_and(chip == g, wide == z * 2 + c)
                target = targets[i].at[index]
                when(
                    same,
                    lambda: pltpu.make_async_copy(
                        sources[i].at[index], target, local_sems.at[local_base + i]
                    ).wait(),
                )
                when(
                    jnp.logical_not(same),
                    lambda: sender.land(target, base + i * 4 + index, (g, z * 2 + 1 - c)),
                )

    return arrive


def hbm():
    return pl.BlockSpec(memory_space=pltpu.HBM)


def vmem():
    return pl.BlockSpec(memory_space=pltpu.VMEM)


def gather_kernel(count, moved, splits, *refs):
    shards, sources = refs[:count], refs[count : count + moved]
    refs = refs[count + moved :]
    fulls, targets = refs[:count], refs[count : count + moved]
    send_sems, recv_sems, local_sems = refs[count + moved :]
    sender = Sender(send_sems, recv_sems)
    entry_barrier()
    arrive = exchange(
        sources, targets, True, sender, count * GATHER_SEMS, local_sems, count
    )
    ticks, finish = gather_ticks(shards, fulls, splits, sender, local_sems)
    for tick in ticks:
        tick()
    arrive()
    finish()
    sender.drain()


def gather(shards, splits, sources, collective_id):
    count, moved = len(shards), len(sources)
    semaphores = count * GATHER_SEMS + moved * 4
    results = pl.pallas_call(
        functools.partial(gather_kernel, count, moved, splits),
        out_shape=[jax.ShapeDtypeStruct((PLANE, LINE, 2) + s.shape, s.dtype) for s in shards]
        + [jax.ShapeDtypeStruct(s.shape, s.dtype) for s in sources],
        in_specs=[hbm()] * count + [vmem()] * moved,
        out_specs=[hbm()] * (count + moved),
        scratch_shapes=[
            pltpu.SemaphoreType.DMA((semaphores,)),
            pltpu.SemaphoreType.DMA((semaphores,)),
            pltpu.SemaphoreType.DMA((count + moved,)),
        ],
        compiler_params=pltpu.CompilerParams(
            collective_id=collective_id, has_side_effects=True
        ),
        name="gather_weights",
    )(*shards, *sources)
    return (results[:count], results[count:])


def reduce_kernel(count, moved, splits, *refs):
    grads, sources = refs[:count], refs[count : count + moved]
    refs = refs[count + moved :]
    outs, targets = refs[:count], refs[count : count + moved]
    refs = refs[count + moved :]
    scratch = [refs[i * count : (i + 1) * count] for i in range(6)]
    send_sems, recv_sems, local_sems = refs[6 * count :]
    sender = Sender(send_sems, recv_sems)
    entry_barrier()
    arrive = exchange(
        sources, targets, False, sender, count * REDUCE_SEMS, local_sems, count * 7
    )
    for tick in reduce_ticks(grads, outs, splits, *scratch, sender, local_sems):
        tick()
    arrive()
    sender.drain()


def reduce_grads(grads, splits, sources, collective_id):
    count, moved = len(grads), len(sources)
    semaphores = count * REDUCE_SEMS + moved * 4
    shapes = [g.shape[3:] for g in grads]
    scratch = []
    for lead in ((LINE, PLANE), (LINE, PLANE), (LINE,), (LINE, 2), (LINE,), (LINE,)):
        scratch += [pltpu.VMEM(lead + s, BF16) for s in shapes]
    results = pl.pallas_call(
        functools.partial(reduce_kernel, count, moved, splits),
        out_shape=[jax.ShapeDtypeStruct(s, F32) for s in shapes]
        + [jax.ShapeDtypeStruct(s.shape, s.dtype) for s in sources],
        in_specs=[hbm()] * count + [vmem()] * moved,
        out_specs=[vmem()] * count + [hbm()] * moved,
        scratch_shapes=scratch
        + [
            pltpu.SemaphoreType.DMA((semaphores,)),
            pltpu.SemaphoreType.DMA((semaphores,)),
            pltpu.SemaphoreType.DMA((count * 7 + moved,)),
        ],
        compiler_params=pltpu.CompilerParams(
            collective_id=collective_id, has_side_effects=True, vmem_limit_bytes=60 * 1024 * 1024
        ),
        name="reduce_grads",
    )(*grads, *sources)
    return (results[:count], results[count:])


def lane_half(shape, period, half):
    lanes = lax.broadcasted_iota(jnp.int32, shape, 1)
    return lax.rem(lanes, period) < half


def turn(values):
    first = lane_half(values.shape, HEAD_DIM, HEAD_DIM // 2)
    return jnp.where(
        first,
        -pltpu.roll(values, values.shape[1] - HEAD_DIM // 2, 1),
        pltpu.roll(values, HEAD_DIM // 2, 1),
    )


def dot_rows(left, right):
    return lax.dot_general(left, right, (((1,), (0,)), ((), ())), preferred_element_type=F32)


def dot_columns(left, right):
    return lax.dot_general(left, right, (((1,), (1,)), ((), ())), preferred_element_type=F32)


def project_kernel(turned, token_ref, weight_ref, bias_ref, cosine_ref, sine_ref, out_ref):
    step = pl.program_id(0)
    value = dot_rows(token_ref[...], weight_ref[...]) + bias_ref[...].astype(F32)

    @pl.when(step < turned)
    def _():
        factor = jnp.where(step < turned // 2, HEAD_DIM ** (-0.5), 1.0)
        pairs = value.shape[1] // 128
        for j in range(pairs):
            part = value[:, j * 128 : (j + 1) * 128]
            part = part * cosine_ref[...] + turn(part) * sine_ref[...]
            out_ref[:, j * 128 : (j + 1) * 128] = (part * factor).astype(BF16)

    @pl.when(step >= turned)
    def _():
        out_ref[...] = value.astype(BF16)


def project(token_rows, weight, bias, cosine, sine):
    rows, width = token_rows.shape
    columns = weight.shape[1]
    tile = 512
    return pl.pallas_call(
        functools.partial(project_kernel, 2 * width // tile),
        out_shape=jax.ShapeDtypeStruct((rows, columns), BF16),
        grid=(columns // tile,),
        in_specs=[
            pl.BlockSpec((rows, width), lambda j: (0, 0)),
            pl.BlockSpec((width, tile), lambda j: (0, j)),
            pl.BlockSpec((1, tile), lambda j: (0, j)),
            pl.BlockSpec((rows, 128), lambda j: (0, 0)),
            pl.BlockSpec((rows, 128), lambda j: (0, 0)),
        ],
        out_specs=pl.BlockSpec((rows, tile), lambda j: (0, j)),
        compiler_params=pltpu.CompilerParams(vmem_limit_bytes=32 * 1024 * 1024),
        name="project",
    )(token_rows, weight, bias, cosine, sine)


def attend_kernel(
    query_ref, key_ref, value_ref, far_key_ref, far_value_ref, seg_ref, seg_near_ref, seg_far_ref, out_ref, norm_ref
):
    rows = query_ref.shape[0]
    first = lane_half((rows, 128), 128, HEAD_DIM)
    tile = 256
    for r in range(rows // tile):
        rs = pl.ds(r * tile, tile)
        query = query_ref[rs, :]
        low_half = first[:tile]
        seg = seg_ref[rs, :]
        near, far = seg == seg_near_ref[...], seg == seg_far_ref[...]
        outs, norms = [], []
        for h in range(2):
            keep = low_half if h == 0 else jnp.logical_not(low_half)
            one = jnp.where(keep, query, jnp.zeros_like(query))
            near_scores = jnp.where(near, dot_columns(one, key_ref[...]), neg_large)
            far_scores = jnp.where(far, dot_columns(one, far_key_ref[...]), neg_large)
            top = jnp.maximum(
                jnp.max(near_scores, axis=1, keepdims=True), jnp.max(far_scores, axis=1, keepdims=True)
            )
            near_expon, far_expon = jnp.exp(near_scores - top), jnp.exp(far_scores - top)
            total = jnp.sum(near_expon, axis=1, keepdims=True) + jnp.sum(
                far_expon, axis=1, keepdims=True
            )
            mixed = dot_rows(near_expon.astype(BF16), value_ref[...]) + dot_rows(
                far_expon.astype(BF16), far_value_ref[...]
            )
            outs.append(mixed / total)
            norms.append(jnp.broadcast_to(top + jnp.log(total), (tile, 128)))
        out_ref[rs, :] = jnp.where(low_half, outs[0], outs[1]).astype(BF16)
        flipped = jnp.transpose(jnp.where(low_half, norms[0], norms[1]))
        norm_ref[0, 0:1, rs] = flipped[0:1]
        norm_ref[0, 1:2, rs] = flipped[HEAD_DIM : HEAD_DIM + 1]


def attend(qkv, far_kv, seg_column, seg_near, seg_far):
    rows = qkv.shape[0]
    width = HEADS * HEAD_DIM
    pairs = width // 128
    block = lambda at: pl.BlockSpec((rows, 128), lambda h: (0, at + h))
    whole = lambda a: pl.BlockSpec(a.shape, lambda h: (0, 0))
    return pl.pallas_call(
        attend_kernel,
        out_shape=[
            jax.ShapeDtypeStruct((rows, width), BF16),
            jax.ShapeDtypeStruct((pairs, 8, rows), F32),
        ],
        grid=(pairs,),
        in_specs=[
            block(0),
            block(pairs),
            block(2 * pairs),
            block(0),
            block(pairs),
            whole(seg_column),
            whole(seg_near),
            whole(seg_far),
        ],
        out_specs=[block(0), pl.BlockSpec((1, 8, rows), lambda h: (h, 0, 0))],
        compiler_params=pltpu.CompilerParams(vmem_limit_bytes=48 * 1024 * 1024),
        name="attend",
    )(qkv, qkv, qkv, far_kv, far_kv, seg_column, seg_near, seg_far)


def attend_back_kernel(
    query_ref, key_ref, value_ref, far_key_ref, far_value_ref, grad_ref, norm_ref,
    seg_ref, seg_near_ref, seg_far_ref, cosine_ref, sine_ref, far_cosine_ref, far_sine_ref,
    query_out, key_out, value_out, far_key_out, far_value_out,
):
    rows = query_ref.shape[0]
    low_half = lane_half((rows, 128), 128, HEAD_DIM)
    query, grad = query_ref[...], grad_ref[...]
    seg = seg_ref[...]
    sides = (
        (key_ref[...], value_ref[...], seg_near_ref[...]),
        (far_key_ref[...], far_value_ref[...], seg_far_ref[...]),
    )
    query_grads, key_grads, value_grads = [], [[], []], [[], []]
    for h in range(2):
        keep = low_half if h == 0 else jnp.logical_not(low_half)
        one = jnp.where(keep, query, jnp.zeros_like(query))
        one_grad = jnp.where(keep, grad, jnp.zeros_like(grad))
        norm = norm_ref[0, h : h + 1, :]
        kept = []
        delta = jnp.zeros((1, rows), F32)
        for key, value, seg_key in sides:
            scores = jnp.where(seg_key == seg, dot_columns(key, one), neg_large)
            probs = jnp.exp(scores - norm)
            product = probs * dot_columns(value, one_grad)
            delta = delta + jnp.sum(product, axis=0, keepdims=True)
            kept.append((probs, product))
        total = None
        for i, (key, value, seg_key) in enumerate(sides):
            probs, product = kept[i]
            score_grad = (product - probs * delta).astype(BF16)
            key_grads[i].append(dot_rows(score_grad, query))
            value_grads[i].append(dot_rows(probs.astype(BF16), grad))
            part = lax.dot_general(
                score_grad, key, (((0,), (0,)), ((), ())), preferred_element_type=F32
            )
            total = part if total is None else total + part
        query_grads.append(total)

    def join(pair):
        return jnp.where(low_half, pair[0], pair[1])

    def unturn(value, cosine, sine):
        return value * cosine - turn(value) * sine

    query_grad = join(query_grads) * HEAD_DIM ** (-0.5)
    query_out[...] = unturn(query_grad, cosine_ref[...], sine_ref[...]).astype(BF16)
    key_out[...] = unturn(join(key_grads[0]), cosine_ref[...], sine_ref[...])
    value_out[...] = join(value_grads[0])
    far_key_out[...] = unturn(join(key_grads[1]), far_cosine_ref[...], far_sine_ref[...]).astype(BF16)
    far_value_out[...] = join(value_grads[1]).astype(BF16)


def attend_back(qkv, far_kv, context_grad, norms, seg_row, seg_near, seg_far, tables):
    rows = qkv.shape[0]
    width = HEADS * HEAD_DIM
    pairs = width // 128
    block = lambda at: pl.BlockSpec((rows, 128), lambda h: (0, at + h))
    whole = lambda a: pl.BlockSpec(a.shape, lambda h: (0, 0))
    return pl.pallas_call(
        attend_back_kernel,
        out_shape=[
            jax.ShapeDtypeStruct((rows, width), BF16),
            jax.ShapeDtypeStruct((rows, width), F32),
            jax.ShapeDtypeStruct((rows, width), F32),
            jax.ShapeDtypeStruct((rows, width), BF16),
            jax.ShapeDtypeStruct((rows, width), BF16),
        ],
        grid=(pairs,),
        in_specs=[
            block(0),
            block(pairs),
            block(2 * pairs),
            block(0),
            block(pairs),
            block(0),
            pl.BlockSpec((1, 8, rows), lambda h: (h, 0, 0)),
            whole(seg_row),
            whole(seg_near),
            whole(seg_far),
        ]
        + [whole(t) for t in tables],
        out_specs=[block(0)] * 5,
        compiler_params=pltpu.CompilerParams(vmem_limit_bytes=60 * 1024 * 1024),
        name="attend_back",
    )(qkv, qkv, qkv, far_kv, far_kv, context_grad, norms, seg_row, seg_near, seg_far, *tables)


def pair_tables(positions):
    cosine, sine = rotary_tables(positions)
    return (jnp.concatenate([cosine, cosine], axis=1), jnp.concatenate([sine, sine], axis=1))


def swap_cores(value, wide_size):
    pairs = [(w, w + 1 - 2 * (w % 2)) for w in range(wide_size)]
    return lax.ppermute(value, "wide", pairs)


def plane_device(
    tokens,
    segment_ids,
    project_weight,
    project_bias,
    output_weight,
    output_bias,
    first_gain,
    first_shift,
    up_weight,
    up_bias,
    down_weight,
    down_bias,
    second_gain,
    second_shift,
    embed_weight,
    out_cotangent,
    embed_cotangent,
):
    width = HEADS * HEAD_DIM
    piece = tokens.shape[2]
    rows = 2 * piece
    wide_size = 2 * LINE
    group = lax.axis_index("group")
    core = lax.rem(lax.axis_index("wide"), 2)
    devices = PLANE * LINE * 2
    vectors = (
        project_bias,
        output_bias,
        first_gain,
        first_shift,
        up_bias,
        down_bias,
        second_gain,
        second_shift,
    )
    sizes = [v.shape[0] for v in vectors]
    lanes = embed_weight.shape[1]
    pad = SMALL_ROWS * lanes - sum(sizes)
    small = jnp.pad(jnp.concatenate(vectors), (0, pad)).reshape(SMALL_ROWS, lanes)
    embed_small = jnp.concatenate([embed_weight, small])
    embed_rows = embed_weight.shape[0]

    other_ids = swap_cores(segment_ids, wide_size)
    micro_mine = group // 2
    from_core = lax.rem(group, 2)
    ids = jnp.where(from_core == core, segment_ids[:, 0], other_ids[:, 0])
    ids = lax.dynamic_index_in_dim(ids, micro_mine, 0, keepdims=False)
    near_ids = lax.dynamic_slice_in_dim(ids, core * rows, rows)
    far_ids = lax.dynamic_slice_in_dim(ids, (1 - core) * rows, rows)

    (project_full, small_full), (token_pieces,) = gather(
        [project_weight, embed_small], [project_weight.shape[0] // 2, embed_rows], [tokens[:, 0]], 1
    )
    token_rows = token_pieces.reshape(rows, width)
    small_full = small_full.reshape(devices, embed_rows + SMALL_ROWS, lanes)
    embed_full = small_full[:, :embed_rows].reshape(devices * embed_rows, lanes)
    small_full = small_full[:, embed_rows:].reshape(devices, SMALL_ROWS * lanes)
    gathered, start = [], 0
    for size in sizes:
        gathered.append(small_full[:, start : start + size].reshape(1, devices * size).astype(F32))
        start += size
    bias_p, bias_o, gain1, shift1, bias_u, bias_d, gain2, shift2 = gathered

    place_of = jnp.arange(rows)
    cosine, sine = pair_tables((core * rows + place_of).astype(F32))
    far_cosine, far_sine = pair_tables(((1 - core) * rows + place_of).astype(F32))
    project_full = project_full.reshape(width, 3 * width)
    qkv = project(token_rows, project_full, bias_p, cosine, sine)
    far_kv = swap_cores(qkv[:, width:], wide_size)
    context_low, norms = attend(
        qkv, far_kv, near_ids[:, None], near_ids[None, :], far_ids[None, :]
    )

    (output_full, up_full, down_full), (cot_pieces, embed_cot_pieces) = gather(
        [output_weight, up_weight, down_weight],
        [output_weight.shape[0] // 2, up_weight.shape[0] // 2, down_weight.shape[0] // 2],
        [out_cotangent[:, 0], embed_cotangent[:, 0]],
        2,
    )
    output_full = output_full.reshape(width, width)
    up_full = up_full.reshape(width, -1)
    down_full = down_full.reshape(-1, width)

    branch = jnp.dot(context_low, output_full, preferred_element_type=F32) + bias_o
    hidden, first_normed, first_rstd = norm_forward(
        token_rows.astype(F32) + branch, gain1, shift1
    )
    hidden_low = hidden.astype(BF16)
    up_value = jnp.dot(hidden_low, up_full, preferred_element_type=F32) + bias_u
    act_low = jax.nn.gelu(up_value, approximate=False).astype(BF16)
    down_value = jnp.dot(act_low, down_full, preferred_element_type=F32) + bias_d
    result, second_normed, second_rstd = norm_forward(hidden + down_value, gain2, shift2)
    result_low = result.astype(BF16)
    embedded = jnp.dot(result_low, embed_full, preferred_element_type=F32).astype(BF16)

    embed_cot = embed_cot_pieces.reshape(rows, lanes)
    result_grad = cot_pieces.reshape(rows, width).astype(F32) + times_transpose(
        embed_cot, embed_full
    )
    embed_weight_grad = contract_rows(result_low, embed_cot)
    sum_grad, second_gain_grad, second_shift_grad = norm_backward(
        result_grad, second_normed, second_rstd, gain2
    )
    down_grad = sum_grad.astype(BF16)
    down_bias_grad = jnp.sum(down_grad.astype(F32), axis=0)
    down_weight_grad = contract_rows(act_low, down_grad)
    up_grad = (times_transpose(down_grad, down_full) * gelu_slope(up_value)).astype(BF16)
    up_bias_grad = jnp.sum(up_grad.astype(F32), axis=0)
    up_weight_grad = contract_rows(hidden_low, up_grad)
    hidden_grad = sum_grad + times_transpose(up_grad, up_full)
    first_grad, first_gain_grad, first_shift_grad = norm_backward(
        hidden_grad, first_normed, first_rstd, gain1
    )
    branch_grad = first_grad.astype(BF16)
    output_bias_grad = jnp.sum(branch_grad.astype(F32), axis=0)
    output_weight_grad = contract_rows(context_low, branch_grad)
    context_grad = times_transpose(branch_grad, output_full).astype(BF16)

    query_back, key_near, value_near, key_far, value_far = attend_back(
        qkv,
        far_kv,
        context_grad,
        norms,
        near_ids[None, :],
        near_ids[:, None],
        far_ids[:, None],
        (cosine, sine, far_cosine, far_sine),
    )
    key_back = (key_near + swap_cores(key_far, wide_size).astype(F32)).astype(BF16)
    value_back = (value_near + swap_cores(value_far, wide_size).astype(F32)).astype(BF16)
    projected_grad = jnp.concatenate([query_back, key_back, value_back], axis=1)
    project_bias_grad = jnp.sum(projected_grad.astype(F32), axis=0)
    project_weight_grad = contract_rows(token_rows, projected_grad)
    token_grad = (first_grad + times_transpose(projected_grad, project_full)).astype(BF16)

    small_grads = jnp.concatenate(
        [
            v.reshape(devices, -1)
            for v in (
                project_bias_grad,
                output_bias_grad,
                first_gain_grad,
                first_shift_grad,
                up_bias_grad,
                down_bias_grad,
                second_gain_grad,
                second_shift_grad,
            )
        ],
        axis=1,
    )
    small_grads = jnp.pad(small_grads, ((0, 0), (0, pad))).reshape(devices, SMALL_ROWS, lanes)
    embed_grads = jnp.concatenate(
        [embed_weight_grad.reshape(devices, embed_rows, lanes), small_grads], axis=1
    )

    def spread(full):
        return full.astype(BF16).reshape(PLANE, LINE, 2, -1, full.shape[-1])

    grads = [
        spread(g)
        for g in (
            down_weight_grad,
            up_weight_grad,
            output_weight_grad,
            project_weight_grad,
            embed_grads,
        )
    ]
    splits = [g.shape[3] // 2 for g in grads[:4]] + [embed_rows]
    outs, moved = reduce_grads(
        grads,
        splits,
        [
            result_low.reshape(2, piece, width),
            embedded.reshape(2, piece, lanes),
            token_grad.reshape(2, piece, width),
        ],
        3,
    )
    down_out, up_out, output_out, project_out, small_out = outs
    vector_out = small_out[embed_rows:].reshape(-1)
    parts, start = [], 0
    for size in sizes:
        parts.append(vector_out[start : start + size])
        start += size
    layer_out, embed_out, token_back = [m[:, None] for m in moved]
    return (
        layer_out,
        embed_out,
        token_back.astype(F32),
        project_out,
        parts[0],
        output_out,
        parts[1],
        parts[2],
        parts[3],
        up_out,
        parts[4],
        down_out,
        parts[5],
        parts[6],
        parts[7],
        small_out[:embed_rows],
    )


def choose_device(mesh):
    if mesh.shape["group"] == PLANE and mesh.shape["wide"] == 2 * LINE:
        return plane_device
    return general_device


def solution(mesh):
    in_specs = (
        P(None, "wide", "group", None),
        P(None, "wide", None),
        P(("group", "wide"), None),
        P(("group", "wide")),
        P(("group", "wide"), None),
        P(("group", "wide")),
        P(("group", "wide")),
        P(("group", "wide")),
        P(("group", "wide"), None),
        P(("group", "wide")),
        P(("group", "wide"), None),
        P(("group", "wide")),
        P(("group", "wide")),
        P(("group", "wide")),
        P(("group", "wide"), None),
        P(None, "wide", "group", None),
        P(None, "wide", "group", None),
    )
    out_specs = (
        P(None, "wide", "group", None),
        P(None, "wide", "group", None),
        P(None, "wide", "group", None),
        P(("group", "wide"), None),
        P(("group", "wide")),
        P(("group", "wide"), None),
        P(("group", "wide")),
        P(("group", "wide")),
        P(("group", "wide")),
        P(("group", "wide"), None),
        P(("group", "wide")),
        P(("group", "wide"), None),
        P(("group", "wide")),
        P(("group", "wide")),
        P(("group", "wide")),
        P(("group", "wide"), None),
    )
    return jax.shard_map(
        choose_device(mesh), mesh=mesh, in_specs=in_specs, out_specs=out_specs, check_vma=False
    )
```

```python
import functools

import jax
import jax.numpy as jnp
from jax import lax
from jax.experimental import pallas as pl
from jax.experimental.pallas import tpu as pltpu
from jax.sharding import PartitionSpec as P

HEADS = 16
HEAD_DIM = 64


eps_norm = 1e-05
neg_large = -1e30


def rotary_tables(positions):
    half_dim = HEAD_DIM // 2
    frequency = 10000.0 ** (-jnp.arange(half_dim, dtype=jnp.float32) * (2.0 / HEAD_DIM))
    angles = positions[:, None] * frequency[None, :]
    angles = jnp.concatenate([angles, angles], axis=1)
    return (jnp.cos(angles), jnp.sin(angles))


def rotate(values, cosine_table, sine_table):
    half_dim = HEAD_DIM // 2
    swapped = jnp.concatenate([-values[..., half_dim:], values[..., :half_dim]], axis=-1)
    return values * cosine_table[:, None, :] + swapped * sine_table[:, None, :]


def unrotate(grads, cosine_table, sine_table):
    half_dim = HEAD_DIM // 2
    scaled = grads * sine_table[:, None, :]
    swapped = jnp.concatenate([scaled[..., half_dim:], -scaled[..., :half_dim]], axis=-1)
    return grads * cosine_table[:, None, :] + swapped


def norm_forward(resid, gain, shift):
    center = resid - jnp.mean(resid, axis=-1, keepdims=True)
    spread = jnp.mean(center * center, axis=-1, keepdims=True)
    rstd_rows = lax.rsqrt(spread + eps_norm)
    normed = center * rstd_rows
    return (normed * gain + shift, normed, rstd_rows)


def norm_backward(grads, normed, rstd_rows, gain):
    scaled = grads * gain
    resid_grad = rstd_rows * (
        scaled
        - jnp.mean(scaled, axis=-1, keepdims=True)
        - normed * jnp.mean(scaled * normed, axis=-1, keepdims=True)
    )
    return (resid_grad, jnp.sum(grads * normed, axis=0), jnp.sum(grads, axis=0))


def contract_rows(left, right):
    return lax.dot_general(
        left, right, (((0,), (0,)), ((), ())), preferred_element_type=jnp.float32
    )


def times_transpose(left, right):
    return lax.dot_general(
        left, right, (((1,), (1,)), ((), ())), preferred_element_type=jnp.float32
    )


def gelu_slope(value):
    normal_cdf = 0.5 * (1.0 + lax.erf(value * 0.7071067811865476))
    density = jnp.exp(-0.5 * value * value) * 0.3989422804014327
    return normal_cdf + value * density


def key_blocks(kv_rows, seg_all):
    seq_len = kv_rows.shape[0]
    block_rows = min(512, seq_len)
    count = seq_len // block_rows
    return (
        kv_rows.reshape(count, block_rows, 2, HEADS, HEAD_DIM),
        seg_all.reshape(count, block_rows),
    )


def block_scores(queries, key_block, same):
    scores = jnp.einsum("qhd,khd->hqk", queries, key_block, preferred_element_type=jnp.float32)
    scores = scores * HEAD_DIM ** (-0.5)
    return jnp.where(same[None], scores, neg_large)


def attention_forward(queries, blocks, seg_blocks, seg_local):
    length = queries.shape[0]

    def norm_step(carry, pieces):
        kv_block, seg_block = pieces
        same = seg_local[:, None] == seg_block[None, :]

        def norm_update(running):
            run_max, run_sum = running
            scores = block_scores(queries, kv_block[:, 0], same)
            new_max = jnp.maximum(run_max, jnp.max(scores, axis=-1))
            new_sum = run_sum * jnp.exp(run_max - new_max) + jnp.sum(
                jnp.exp(scores - new_max[..., None]), axis=-1
            )
            return (new_max, new_sum)

        def norm_unchanged(running):
            return running

        return (lax.cond(jnp.any(same), norm_update, norm_unchanged, carry), None)

    start = (
        jnp.full((HEADS, length), neg_large, jnp.float32),
        jnp.zeros((HEADS, length), jnp.float32),
    )
    (run_max, run_sum), unused = lax.scan(norm_step, start, (blocks, seg_blocks))
    log_norm = run_max + jnp.log(run_sum)

    def value_step(total, pieces):
        kv_block, seg_block = pieces
        same = seg_local[:, None] == seg_block[None, :]

        def value_update(running):
            scores = block_scores(queries, kv_block[:, 0], same)
            weights = jnp.exp(scores - log_norm[..., None]).astype(jnp.bfloat16)
            return running + jnp.einsum(
                "hqk,khd->qhd", weights, kv_block[:, 1], preferred_element_type=jnp.float32
            )

        def value_unchanged(running):
            return running

        return (lax.cond(jnp.any(same), value_update, value_unchanged, total), None)

    context, unused = lax.scan(
        value_step, jnp.zeros(queries.shape, jnp.float32), (blocks, seg_blocks)
    )
    return (context, log_norm)


def attention_backward(queries, blocks, seg_blocks, seg_local, log_norm, context_grad, delta):

    def grad_step(query_grad, pieces):
        kv_block, seg_block = pieces
        same = seg_local[:, None] == seg_block[None, :]

        def work(running):
            scores = block_scores(queries, kv_block[:, 0], same)
            probs = jnp.exp(scores - log_norm[..., None])
            prob_grad = jnp.einsum(
                "qhd,khd->hqk", context_grad, kv_block[:, 1], preferred_element_type=jnp.float32
            )
            score_grad = (probs * (prob_grad - delta[..., None])).astype(jnp.bfloat16)
            running = running + jnp.einsum(
                "hqk,khd->qhd", score_grad, kv_block[:, 0], preferred_element_type=jnp.float32
            ) * HEAD_DIM ** (-0.5)
            prob_low = probs.astype(jnp.bfloat16)
            key_grad = jnp.einsum(
                "hqk,qhd->khd", score_grad, queries, preferred_element_type=jnp.float32
            ) * HEAD_DIM ** (-0.5)
            value_grad = jnp.einsum(
                "hqk,qhd->khd", prob_low, context_grad, preferred_element_type=jnp.float32
            )
            return (running, jnp.stack([key_grad, value_grad], axis=1))

        def skipped(running):
            return (running, jnp.zeros(kv_block.shape, jnp.float32))

        return lax.cond(jnp.any(same), work, skipped, query_grad)

    query_grad, kv_grad = lax.scan(
        grad_step, jnp.zeros(queries.shape, jnp.float32), (blocks, seg_blocks)
    )
    return (query_grad, kv_grad.reshape(-1, 2 * HEADS * HEAD_DIM))


def general_device(
    tokens,
    segment_ids,
    project_weight,
    project_bias,
    output_weight,
    output_bias,
    first_gain,
    first_shift,
    up_weight,
    up_bias,
    down_weight,
    down_bias,
    second_gain,
    second_shift,
    embed_weight,
    out_cotangent,
    embed_cotangent,
):
    shards = (
        project_weight,
        project_bias,
        output_weight,
        output_bias,
        first_gain,
        first_shift,
        up_weight,
        up_bias,
        down_weight,
        down_bias,
        second_gain,
        second_shift,
        embed_weight,
    )
    length = tokens.shape[2]
    width = HEADS * HEAD_DIM
    head_shape = (length, HEADS, HEAD_DIM)
    place = lax.axis_index("group")
    positions = (place * length + jnp.arange(length)).astype(jnp.float32)
    cosine_table, sine_table = rotary_tables(positions)
    grad_total = None
    results = []
    embeddings = []
    input_grads = []
    for micro_index in range(tokens.shape[0]):
        params = (
            lax.all_gather(shards[0], ("group", "wide"), axis=0, tiled=True),
            lax.all_gather(shards[1], ("group", "wide"), axis=0, tiled=True),
            lax.all_gather(shards[2], ("group", "wide"), axis=0, tiled=True),
            lax.all_gather(shards[3], ("group", "wide"), axis=0, tiled=True),
            lax.all_gather(shards[4], ("group", "wide"), axis=0, tiled=True),
            lax.all_gather(shards[5], ("group", "wide"), axis=0, tiled=True),
            lax.all_gather(shards[6], ("group", "wide"), axis=0, tiled=True),
            lax.all_gather(shards[7], ("group", "wide"), axis=0, tiled=True),
            lax.all_gather(shards[8], ("group", "wide"), axis=0, tiled=True),
            lax.all_gather(shards[9], ("group", "wide"), axis=0, tiled=True),
            lax.all_gather(shards[10], ("group", "wide"), axis=0, tiled=True),
            lax.all_gather(shards[11], ("group", "wide"), axis=0, tiled=True),
            lax.all_gather(shards[12], ("group", "wide"), axis=0, tiled=True),
        )
        seg_all = segment_ids[micro_index, 0]
        seg_local = lax.dynamic_slice_in_dim(seg_all, place * length, length)
        token_low = tokens[micro_index, 0]
        token_wide = token_low.astype(jnp.float32)
        projected = jnp.dot(token_low, params[0], preferred_element_type=jnp.float32) + params[
            1
        ].astype(jnp.float32)
        queries = rotate(projected[:, :width].reshape(head_shape), cosine_table, sine_table).astype(
            jnp.bfloat16
        )
        key_rows = rotate(
            projected[:, width : 2 * width].reshape(head_shape), cosine_table, sine_table
        ).astype(jnp.bfloat16)
        value_rows = projected[:, 2 * width :].astype(jnp.bfloat16)
        local_kv = jnp.concatenate([key_rows.reshape(length, width), value_rows], axis=1)
        kv_all = lax.all_gather(local_kv, "group", axis=0, tiled=True)
        blocks, seg_blocks = key_blocks(kv_all, seg_all)
        context, log_norm = attention_forward(queries, blocks, seg_blocks, seg_local)
        context_low = context.reshape(length, width).astype(jnp.bfloat16)
        branch = jnp.dot(context_low, params[2], preferred_element_type=jnp.float32) + params[
            3
        ].astype(jnp.float32)
        first_gain_wide = params[4].astype(jnp.float32)
        hidden, first_normed, first_rstd = norm_forward(
            token_wide + branch, first_gain_wide, params[5].astype(jnp.float32)
        )
        hidden_low = hidden.astype(jnp.bfloat16)
        up_value = jnp.dot(hidden_low, params[6], preferred_element_type=jnp.float32) + params[
            7
        ].astype(jnp.float32)
        act_low = jax.nn.gelu(up_value, approximate=False).astype(jnp.bfloat16)
        down_value = jnp.dot(act_low, params[8], preferred_element_type=jnp.float32) + params[
            9
        ].astype(jnp.float32)
        second_gain_wide = params[10].astype(jnp.float32)
        result, second_normed, second_rstd = norm_forward(
            hidden + down_value, second_gain_wide, params[11].astype(jnp.float32)
        )
        result_low = result.astype(jnp.bfloat16)
        embedded = jnp.dot(result_low, params[12], preferred_element_type=jnp.float32)
        results.append(result_low)
        embeddings.append(embedded.astype(jnp.bfloat16))
        params = (
            lax.all_gather(shards[0], ("group", "wide"), axis=0, tiled=True),
            lax.all_gather(shards[1], ("group", "wide"), axis=0, tiled=True),
            lax.all_gather(shards[2], ("group", "wide"), axis=0, tiled=True),
            lax.all_gather(shards[3], ("group", "wide"), axis=0, tiled=True),
            lax.all_gather(shards[4], ("group", "wide"), axis=0, tiled=True),
            lax.all_gather(shards[5], ("group", "wide"), axis=0, tiled=True),
            lax.all_gather(shards[6], ("group", "wide"), axis=0, tiled=True),
            lax.all_gather(shards[7], ("group", "wide"), axis=0, tiled=True),
            lax.all_gather(shards[8], ("group", "wide"), axis=0, tiled=True),
            lax.all_gather(shards[9], ("group", "wide"), axis=0, tiled=True),
            lax.all_gather(shards[10], ("group", "wide"), axis=0, tiled=True),
            lax.all_gather(shards[11], ("group", "wide"), axis=0, tiled=True),
            lax.all_gather(shards[12], ("group", "wide"), axis=0, tiled=True),
        )
        embed_cot = embed_cotangent[micro_index, 0]
        result_grad = out_cotangent[micro_index, 0].astype(jnp.float32) + times_transpose(
            embed_cot, params[12]
        )
        embed_weight_grad = contract_rows(result_low, embed_cot)
        sum_grad, second_gain_grad, second_shift_grad = norm_backward(
            result_grad, second_normed, second_rstd, second_gain_wide
        )
        down_grad = sum_grad.astype(jnp.bfloat16)
        down_bias_grad = jnp.sum(down_grad.astype(jnp.float32), axis=0)
        down_weight_grad = contract_rows(act_low, down_grad)
        up_grad = (times_transpose(down_grad, params[8]) * gelu_slope(up_value)).astype(
            jnp.bfloat16
        )
        up_bias_grad = jnp.sum(up_grad.astype(jnp.float32), axis=0)
        up_weight_grad = contract_rows(hidden_low, up_grad)
        hidden_grad = sum_grad + times_transpose(up_grad, params[6])
        first_grad, first_gain_grad, first_shift_grad = norm_backward(
            hidden_grad, first_normed, first_rstd, first_gain_wide
        )
        branch_grad = first_grad.astype(jnp.bfloat16)
        output_bias_grad = jnp.sum(branch_grad.astype(jnp.float32), axis=0)
        output_weight_grad = contract_rows(context_low, branch_grad)
        context_grad = (
            times_transpose(branch_grad, params[2]).astype(jnp.bfloat16).reshape(head_shape)
        )
        delta = jnp.transpose(jnp.sum(context_grad.astype(jnp.float32) * context, axis=-1))
        kv_again = lax.all_gather(local_kv, "group", axis=0, tiled=True)
        blocks, seg_blocks = key_blocks(kv_again, seg_all)
        query_grad, kv_partial = attention_backward(
            queries, blocks, seg_blocks, seg_local, log_norm, context_grad, delta
        )
        kv_grad = lax.psum_scatter(
            kv_partial.astype(jnp.bfloat16), "group", scatter_dimension=0, tiled=True
        ).astype(jnp.float32)
        key_part = kv_grad[:, :width].reshape(head_shape)
        value_part = kv_grad[:, width:]
        query_back = unrotate(query_grad, cosine_table, sine_table).reshape(length, width)
        key_back = unrotate(key_part, cosine_table, sine_table).reshape(length, width)
        projected_grad = jnp.concatenate([query_back, key_back, value_part], axis=1).astype(
            jnp.bfloat16
        )
        project_bias_grad = jnp.sum(projected_grad.astype(jnp.float32), axis=0)
        project_weight_grad = contract_rows(token_low, projected_grad)
        input_grads.append(first_grad + times_transpose(projected_grad, params[0]))
        local_grads = (
            project_weight_grad,
            project_bias_grad,
            output_weight_grad,
            output_bias_grad,
            first_gain_grad,
            first_shift_grad,
            up_weight_grad,
            up_bias_grad,
            down_weight_grad,
            down_bias_grad,
            second_gain_grad,
            second_shift_grad,
            embed_weight_grad,
        )
        summed = (
            lax.psum_scatter(local_grads[0], ("group", "wide"), scatter_dimension=0, tiled=True),
            lax.psum_scatter(local_grads[1], ("group", "wide"), scatter_dimension=0, tiled=True),
            lax.psum_scatter(local_grads[2], ("group", "wide"), scatter_dimension=0, tiled=True),
            lax.psum_scatter(local_grads[3], ("group", "wide"), scatter_dimension=0, tiled=True),
            lax.psum_scatter(local_grads[4], ("group", "wide"), scatter_dimension=0, tiled=True),
            lax.psum_scatter(local_grads[5], ("group", "wide"), scatter_dimension=0, tiled=True),
            lax.psum_scatter(local_grads[6], ("group", "wide"), scatter_dimension=0, tiled=True),
            lax.psum_scatter(local_grads[7], ("group", "wide"), scatter_dimension=0, tiled=True),
            lax.psum_scatter(local_grads[8], ("group", "wide"), scatter_dimension=0, tiled=True),
            lax.psum_scatter(local_grads[9], ("group", "wide"), scatter_dimension=0, tiled=True),
            lax.psum_scatter(local_grads[10], ("group", "wide"), scatter_dimension=0, tiled=True),
            lax.psum_scatter(local_grads[11], ("group", "wide"), scatter_dimension=0, tiled=True),
            lax.psum_scatter(local_grads[12], ("group", "wide"), scatter_dimension=0, tiled=True),
        )
        grad_total = (
            summed
            if grad_total is None
            else tuple((total + part for total, part in zip(grad_total, summed)))
        )
    layer_out = jnp.stack(results)[:, None]
    embed_out = jnp.stack(embeddings)[:, None]
    token_grad = jnp.stack(input_grads)[:, None]
    return (
        layer_out,
        embed_out,
        token_grad,
        grad_total[0],
        grad_total[1],
        grad_total[2],
        grad_total[3],
        grad_total[4],
        grad_total[5],
        grad_total[6],
        grad_total[7],
        grad_total[8],
        grad_total[9],
        grad_total[10],
        grad_total[11],
        grad_total[12],
    )


MESH = pl.DeviceIdType.MESH
F32 = jnp.float32
BF16 = jnp.bfloat16
PLANE = 4
LINE = 4
GATHER_SEMS = 42
REDUCE_SEMS = 56
REDUCE_AHEAD = (3, 5, 7)
SMALL_ROWS = 16


def place():
    group = lax.axis_index("group")
    wide = lax.axis_index("wide")
    return (group, lax.rem(group, 2), group // 2, wide // 2, lax.rem(wide, 2))


def when(cond, act):
    if cond is True:
        act()
    else:
        pl.when(cond)(act)


def both(left, right):
    return right if left is True else jnp.logical_and(left, right)


def remote(src, dst, send_sem, recv_sem, device):
    return pltpu.make_async_remote_copy(
        src_ref=src,
        dst_ref=dst,
        send_sem=send_sem,
        recv_sem=recv_sem,
        device_id=device,
        device_id_type=MESH,
    )


def entry_barrier():
    g, x, y, z, c = place()
    devices = []
    for step in range(1, 8):
        other = lax.rem(g * 2 + c + step, 8)
        devices.append((other // 2, z * 2 + lax.rem(other, 2)))
    devices.append((g, lax.rem(z + 1, LINE) * 2 + c))
    devices.append((g, lax.rem(z + LINE - 1, LINE) * 2 + c))
    barrier = pltpu.get_barrier_semaphore()
    for device in devices:
        pl.semaphore_signal(barrier, inc=1, device_id=device, device_id_type=MESH)
    pl.semaphore_wait(barrier, len(devices))


class Sender:
    def __init__(self, send_sems, recv_sems):
        self.send_sems, self.recv_sems = send_sems, recv_sems
        self.pending, self.draining = [], False

    def copy(self, src, dst, index, device):
        return remote(src, dst, self.send_sems.at[index], self.recv_sems.at[index], device)

    def send(self, cond, src, dst, index, device):
        copy = self.copy(src, dst, index, device)
        when(cond, copy.wait_send if self.draining else copy.start)

    def post(self, cond, src, dst, index, device):
        self.send(cond, src, dst, index, device)
        self.pending.append((cond, src, dst, index, device))

    def land(self, ref, index, device):
        self.copy(ref, ref, index, device).wait_recv()

    def do(self, cond, act):
        if not self.draining:
            when(cond, act)

    def drain(self, ticks):
        self.draining = True
        for tick in ticks:
            tick()
        for call in self.pending:
            self.send(*call)


def near_items(z, distance):
    if distance == 0:
        return [(0, z, True)]
    return [
        (distance, jnp.maximum(z - distance, 0), z >= distance),
        (3 + distance, jnp.minimum(z + distance, LINE - 1), z + distance < LINE),
    ]


def gather_ticks(shards, fulls, splits, chunks, ahead, sender, local_sems):
    g, x, y, z, c = place()
    gx, gy, gd = g + 1 - 2 * x, g + 2 - 4 * y, 3 - g
    to_x, to_y, to_core = (gx, z * 2 + c), (gy, z * 2 + c), (g, z * 2 + 1 - c)
    above = (g, jnp.minimum(z + 1, LINE - 1) * 2 + c)
    below = (g, jnp.maximum(z - 1, 0) * 2 + c)

    def first(a, k):
        base = a * GATHER_SEMS
        for slot, zi, cond in near_items(z, k):
            region = fulls[a].at[g, zi, c]
            if k == 0:
                sender.do(
                    True, lambda: pltpu.make_async_copy(shards[a], region, local_sems.at[a]).start()
                )
                source = shards[a]
                sender.send(z < LINE - 1, source, region, base + 1, above)
                sender.send(z > 0, source, region, base + 4, below)
            else:
                source = region
                sender.do(cond, lambda: sender.land(region, base + slot, to_x))
                if k < LINE - 1:
                    if slot < 4:
                        sender.send(both(cond, z < LINE - 1), source, region, base + slot + 1, above)
                    else:
                        sender.send(both(cond, z > 0), source, region, base + slot + 1, below)
            sender.send(cond, source, region, base + 7 + slot, to_x)
            sender.send(cond, source, region, base + 14 + slot, to_y)

    def second(a, k):
        base, cut, rows = a * GATHER_SEMS, splits[a], fulls[a].shape[3]
        for slot, zi, cond in near_items(z, k):
            sender.do(cond, lambda: sender.land(fulls[a].at[gx, zi, c], base + 7 + slot, to_x))
            upper = fulls[a].at[gx, zi, c, 0:cut]
            sender.send(cond, upper, upper, base + 21 + slot, to_y)
            sender.do(cond, lambda: sender.land(fulls[a].at[gy, zi, c], base + 14 + slot, to_x))
            lower = fulls[a].at[gy, zi, c, cut:rows]
            sender.send(cond, lower, lower, base + 28 + slot, to_x)

    def third(a, k):
        base, cut, rows = a * GATHER_SEMS, splits[a], fulls[a].shape[3]
        if k == 0:
            sender.do(
                True,
                lambda: pltpu.make_async_copy(
                    shards[a], fulls[a].at[g, z, c], local_sems.at[a]
                ).wait(),
            )
        for slot, zi, cond in near_items(z, k):
            sender.do(cond, lambda: sender.land(fulls[a].at[gd, zi, c, 0:cut], base + 21 + slot, to_x))
            sender.do(cond, lambda: sender.land(fulls[a].at[gd, zi, c, cut:rows], base + 28 + slot, to_x))
            ring = fulls[a].at[:, zi, c]
            sender.send(cond, ring, ring, base + 35 + slot, to_core)

    def finish():
        for a in range(len(shards)):
            for k in range(LINE):
                for slot, zi, cond in near_items(z, k):
                    when(
                        cond,
                        lambda: sender.land(
                            fulls[a].at[:, zi, 1 - c], a * GATHER_SEMS + 35 + slot, to_x
                        ),
                    )

    def grouped(stage):
        def act(chunk, k):
            for a in chunk:
                stage(a, k)

        return act

    order = [(chunk, k) for chunk in chunks for k in range(LINE)]
    stages = [grouped(stage) for stage in (first, second, third)]
    return (staged(order, stages, (0,) + ahead), finish)


def staged(order, stages, delays):
    ticks = []
    for t in range(len(order) + delays[-1]):

        def tick(t=t):
            for stage, delay in zip(stages, delays):
                if 0 <= t - delay < len(order):
                    stage(*order[t - delay])

        ticks.append(tick)
    return ticks


def add_into(target, terms):
    rows, columns = target.shape
    step = min(columns, 512)

    def body(i, carry):
        cut = pl.ds(pl.multiple_of(i * step, step), step)
        value = terms[0][:, cut].astype(F32)
        for term in terms[1:]:
            value = value + term[:, cut].astype(F32)
        target[:, cut] = value.astype(target.dtype)
        return carry

    lax.fori_loop(0, columns // step, body, 0)


def reduce_ticks(grads, outs, splits, held, core_in, half_in, whole_in, rise_in, fall_in, sender, local_sems):
    g, x, y, z, c = place()
    gx, gy, gd = g + 1 - 2 * x, g + 2 - 4 * y, 3 - g
    to_x, to_y, to_core = (gx, z * 2 + c), (gy, z * 2 + c), (g, z * 2 + 1 - c)
    above = (g, jnp.minimum(z + 1, LINE - 1) * 2 + c)
    below = (g, jnp.maximum(z - 1, 0) * 2 + c)

    def far_items(k):
        items = near_items(z, k)
        if k == 0:
            return items
        return [(k,) + items[1][1:], (3 + k,) + items[0][1:]]

    def load(a, zi, slot):
        return pltpu.make_async_copy(
            grads[a].at[:, zi, c], held[a].at[zi], local_sems.at[a * 7 + slot]
        )

    def zeroth(a, k):
        base = a * REDUCE_SEMS
        for slot, zi, cond in far_items(k):
            sender.send(cond, grads[a].at[:, zi, 1 - c], core_in[a].at[zi], base + slot, to_core)
            sender.do(cond, lambda: load(a, zi, slot).start())

    def first(a, k):
        base, cut, rows = a * REDUCE_SEMS, splits[a], held[a].shape[2]
        for slot, zi, cond in far_items(k):

            def work():
                load(a, zi, slot).wait()
                sender.land(core_in[a].at[zi], base + slot, to_x)
                for j in range(PLANE):
                    add_into(held[a].at[zi, j], [held[a].at[zi, j], core_in[a].at[zi, j]])

            sender.do(cond, work)
            sender.send(
                cond, held[a].at[zi, gd, 0:cut], half_in[a].at[zi, 0:cut], base + 7 + slot, to_y
            )
            sender.send(
                cond, held[a].at[zi, gd, cut:rows], half_in[a].at[zi, cut:rows], base + 14 + slot, to_x
            )

    def second(a, k):
        base, cut, rows = a * REDUCE_SEMS, splits[a], held[a].shape[2]
        for slot, zi, cond in far_items(k):

            def upper():
                sender.land(half_in[a].at[zi, 0:cut], base + 7 + slot, to_x)
                mine = held[a].at[zi, gx, 0:cut]
                add_into(mine, [mine, half_in[a].at[zi, 0:cut]])

            sender.do(cond, upper)
            sender.send(cond, held[a].at[zi, gx], whole_in[a].at[zi, 0], base + 21 + slot, to_x)

            def lower():
                sender.land(half_in[a].at[zi, cut:rows], base + 14 + slot, to_x)
                mine = held[a].at[zi, gy, cut:rows]
                add_into(mine, [mine, half_in[a].at[zi, cut:rows]])

            sender.do(cond, lower)
            sender.send(cond, held[a].at[zi, gy], whole_in[a].at[zi, 1], base + 28 + slot, to_y)

    def third(a, k):
        base = a * REDUCE_SEMS
        for slot, zi, cond in far_items(k):
            mine = held[a].at[zi, g]
            terms = [mine, whole_in[a].at[zi, 0], whole_in[a].at[zi, 1]]
            rise, fall = rise_in[a].at[zi], fall_in[a].at[zi]

            def arrive():
                sender.land(whole_in[a].at[zi, 0], base + 21 + slot, to_x)
                sender.land(whole_in[a].at[zi, 1], base + 28 + slot, to_x)

            sender.do(cond, arrive)
            if k == 0:
                sender.do(z > 0, lambda: sender.land(rise, base + 36, to_x))
                sender.do(z < LINE - 1, lambda: sender.land(fall, base + 43, to_x))
                sender.do(z == 0, lambda: add_into(outs[a], terms + [fall]))
                sender.do(z == LINE - 1, lambda: add_into(outs[a], terms + [rise]))
                sender.do(
                    jnp.logical_and(z > 0, z < LINE - 1),
                    lambda: add_into(outs[a], terms + [rise, fall]),
                )
            else:
                going_up = slot < 4
                moved = rise if going_up else fall
                offset = base + (35 if going_up else 42)
                inner = (z > 0) if going_up else (z < LINE - 1)

                def join():
                    sender.land(moved, offset + k + 1, to_x)
                    add_into(mine, terms + [moved])

                if k < LINE - 1:
                    sender.do(both(cond, inner), join)
                sender.do(both(cond, jnp.logical_not(inner)), lambda: add_into(mine, terms))
                sender.send(cond, mine, moved, offset + k, above if going_up else below)

    order = [(a, k) for a in range(len(grads)) for k in (3, 2, 1, 0)]
    return staged(order, (zeroth, first, second, third), (0,) + REDUCE_AHEAD)


def exchange(sources, targets, outward, sender, base, local_sems, local_base):
    g, x, y, z, c = place()

    def partner(index):
        if outward:
            return (index * 2 + c, z * 2 + g // 2)
        return (2 * c + index, z * 2 + lax.rem(g, 2))

    def origin(index):
        if outward:
            return (2 * c + index, z * 2 + lax.rem(g, 2))
        return (index * 2 + c, z * 2 + g // 2)

    slot = lax.rem(g, 2) if outward else g // 2
    finals = []

    def post(i, index):
        chip, wide = partner(index)
        same = jnp.logical_and(chip == g, wide == z * 2 + c)
        other = jnp.logical_not(same)
        source, target = sources[i].at[index], targets[i].at[slot]
        at = base + i * 4

        def copy():
            return remote(
                source,
                target,
                sender.send_sems.at[at + 2 + index],
                sender.recv_sems.at[at + slot],
                (chip, wide),
            )

        when(
            same,
            lambda: pltpu.make_async_copy(source, target, local_sems.at[local_base + i]).start(),
        )
        when(other, lambda: copy().start())
        finals.append((other, lambda: copy().wait_send()))

    for i in range(len(sources)):
        for index in range(2):
            post(i, index)

    def arrive():
        for i in range(len(sources)):
            for index in range(2):
                chip, wide = origin(index)
                same = jnp.logical_and(chip == g, wide == z * 2 + c)
                target = targets[i].at[index]
                when(
                    same,
                    lambda: pltpu.make_async_copy(
                        sources[i].at[index], target, local_sems.at[local_base + i]
                    ).wait(),
                )
                when(
                    jnp.logical_not(same),
                    lambda: sender.land(target, base + i * 4 + index, (g, z * 2 + 1 - c)),
                )
        for other, final in finals:
            when(other, final)

    return arrive


def hbm():
    return pl.BlockSpec(memory_space=pltpu.HBM)


def vmem():
    return pl.BlockSpec(memory_space=pltpu.VMEM)


def gather_kernel(count, moved, splits, *refs):
    shards, sources = refs[:count], refs[count : count + moved]
    refs = refs[count + moved :]
    fulls, targets = refs[:count], refs[count : count + moved]
    send_sems, recv_sems, local_sems = refs[count + moved :]
    sender = Sender(send_sems, recv_sems)
    entry_barrier()
    arrive = exchange(
        sources, targets, True, sender, count * GATHER_SEMS, local_sems, count
    )
    ticks, finish = gather_ticks(
        shards, fulls, splits, [range(count)], (1, 2), sender, local_sems
    )
    for tick in ticks:
        tick()
    arrive()
    finish()
    sender.drain(ticks)


def gather(shards, splits, sources, collective_id):
    count, moved = len(shards), len(sources)
    semaphores = count * GATHER_SEMS + moved * 4
    results = pl.pallas_call(
        functools.partial(gather_kernel, count, moved, splits),
        out_shape=[jax.ShapeDtypeStruct((PLANE, LINE, 2) + s.shape, s.dtype) for s in shards]
        + [jax.ShapeDtypeStruct(s.shape, s.dtype) for s in sources],
        in_specs=[hbm()] * count + [vmem()] * moved,
        out_specs=[hbm()] * (count + moved),
        scratch_shapes=[
            pltpu.SemaphoreType.DMA((semaphores,)),
            pltpu.SemaphoreType.DMA((semaphores,)),
            pltpu.SemaphoreType.DMA((count + moved,)),
        ],
        compiler_params=pltpu.CompilerParams(
            collective_id=collective_id, has_side_effects=True
        ),
        name="gather_weights",
    )(*shards, *sources)
    return (results[:count], results[count:])


def run_with(ticks, steps, body):
    def act(i, carry):
        body(i)
        for j, tick in enumerate(ticks[:steps]):
            pl.when(i == j)(tick)
        return carry

    lax.fori_loop(0, steps, act, 0)
    for tick in ticks[steps:]:
        tick()


def gather_attend_kernel(count, moved, splits, *refs):
    shards, sources = refs[:count], refs[count : count + moved]
    qkv, seg, seg_near, seg_far = refs[count + moved : count + moved + 4]
    refs = refs[count + moved + 4 :]
    fulls, targets = refs[:count], refs[count : count + moved]
    far, context, norm = refs[count + moved : count + moved + 3]
    send_sems, recv_sems, local_sems = refs[count + moved + 3 :]
    g, x, y, z, c = place()
    partner = (g, z * 2 + 1 - c)
    sender = Sender(send_sems, recv_sems)
    entry_barrier()
    width = far.shape[1] // 2
    far_index = count * GATHER_SEMS + moved * 4
    sender.post(True, qkv.at[:, width:], far, far_index, partner)
    ticks, finish = gather_ticks(
        shards, fulls, splits, [[a] for a in range(count)], (3, 6), sender, local_sems
    )
    for tick in ticks[:2]:
        tick()
    arrive = exchange(
        sources, targets, True, sender, count * GATHER_SEMS, local_sems, count
    )
    sender.land(far, far_index, partner)

    def pair(i):
        at = pl.multiple_of(i * 128, 128)
        cut = lambda ref, base: ref.at[:, pl.ds(base + at, 128)]
        attend_pair(
            cut(qkv, 0),
            cut(qkv, width),
            cut(qkv, 2 * width),
            cut(far, 0),
            cut(far, width),
            seg,
            seg_near,
            seg_far,
            cut(context, 0),
            norm.at[i],
        )

    run_with(ticks[2:], width // 128, pair)
    arrive()
    finish()
    sender.drain(ticks)


def gather_attend(shards, splits, sources, qkv, segs, collective_id):
    count, moved = len(shards), len(sources)
    rows, width = qkv.shape[0], qkv.shape[1] // 3
    semaphores = count * GATHER_SEMS + moved * 4 + 1
    results = pl.pallas_call(
        functools.partial(gather_attend_kernel, count, moved, splits),
        out_shape=[jax.ShapeDtypeStruct((PLANE, LINE, 2) + s.shape, s.dtype) for s in shards]
        + [jax.ShapeDtypeStruct(s.shape, s.dtype) for s in sources]
        + [
            jax.ShapeDtypeStruct((rows, 2 * width), BF16),
            jax.ShapeDtypeStruct((rows, width), BF16),
            jax.ShapeDtypeStruct((width // 128, 8, rows), F32),
        ],
        in_specs=[hbm()] * count + [vmem()] * (moved + 4),
        out_specs=[hbm()] * (count + moved) + [vmem()] * 3,
        scratch_shapes=[
            pltpu.SemaphoreType.DMA((semaphores,)),
            pltpu.SemaphoreType.DMA((semaphores,)),
            pltpu.SemaphoreType.DMA((count + moved,)),
        ],
        compiler_params=pltpu.CompilerParams(
            collective_id=collective_id, has_side_effects=True, vmem_limit_bytes=48 * 1024 * 1024
        ),
        name="gather_attend",
    )(*shards, *sources, qkv, *segs)
    return (results[:count], results[count : count + moved], results[count + moved :])


def reduce_kernel(count, moved, splits, *refs):
    grads, sources = refs[:count], refs[count : count + moved]
    refs = refs[count + moved :]
    outs, targets = refs[:count], refs[count : count + moved]
    refs = refs[count + moved :]
    scratch = [refs[i * count : (i + 1) * count] for i in range(6)]
    send_sems, recv_sems, local_sems = refs[6 * count :]
    sender = Sender(send_sems, recv_sems)
    entry_barrier()
    arrive = exchange(
        sources, targets, False, sender, count * REDUCE_SEMS, local_sems, count * 7
    )
    ticks = reduce_ticks(grads, outs, splits, *scratch, sender, local_sems)
    for tick in ticks:
        tick()
    arrive()
    sender.drain(ticks)


def reduce_grads(grads, splits, sources, collective_id):
    count, moved = len(grads), len(sources)
    semaphores = count * REDUCE_SEMS + moved * 4
    shapes = [g.shape[3:] for g in grads]
    scratch = []
    for lead in ((LINE, PLANE), (LINE, PLANE), (LINE,), (LINE, 2), (LINE,), (LINE,)):
        scratch += [pltpu.VMEM(lead + s, BF16) for s in shapes]
    results = pl.pallas_call(
        functools.partial(reduce_kernel, count, moved, splits),
        out_shape=[jax.ShapeDtypeStruct(s, F32) for s in shapes]
        + [jax.ShapeDtypeStruct(s.shape, s.dtype) for s in sources],
        in_specs=[hbm()] * count + [vmem()] * moved,
        out_specs=[vmem()] * count + [hbm()] * moved,
        scratch_shapes=scratch
        + [
            pltpu.SemaphoreType.DMA((semaphores,)),
            pltpu.SemaphoreType.DMA((semaphores,)),
            pltpu.SemaphoreType.DMA((count * 7 + moved,)),
        ],
        compiler_params=pltpu.CompilerParams(
            collective_id=collective_id, has_side_effects=True, vmem_limit_bytes=60 * 1024 * 1024
        ),
        name="reduce_grads",
    )(*grads, *sources)
    return (results[:count], results[count:])


def lane_half(shape, period, half):
    lanes = lax.broadcasted_iota(jnp.int32, shape, 1)
    return lax.rem(lanes, period) < half


def turn(values):
    first = lane_half(values.shape, HEAD_DIM, HEAD_DIM // 2)
    return jnp.where(
        first,
        -pltpu.roll(values, values.shape[1] - HEAD_DIM // 2, 1),
        pltpu.roll(values, HEAD_DIM // 2, 1),
    )


def dot_rows(left, right):
    return lax.dot_general(left, right, (((1,), (0,)), ((), ())), preferred_element_type=F32)


def dot_columns(left, right):
    return lax.dot_general(left, right, (((1,), (1,)), ((), ())), preferred_element_type=F32)


def project_kernel(turned, token_ref, weight_ref, bias_ref, cosine_ref, sine_ref, out_ref):
    step = pl.program_id(0)
    value = dot_rows(token_ref[...], weight_ref[...]) + bias_ref[...].astype(F32)

    @pl.when(step < turned)
    def _():
        factor = jnp.where(step < turned // 2, HEAD_DIM ** (-0.5), 1.0)
        pairs = value.shape[1] // 128
        for j in range(pairs):
            part = value[:, j * 128 : (j + 1) * 128]
            part = part * cosine_ref[...] + turn(part) * sine_ref[...]
            out_ref[:, j * 128 : (j + 1) * 128] = (part * factor).astype(BF16)

    @pl.when(step >= turned)
    def _():
        out_ref[...] = value.astype(BF16)


def project(token_rows, weight, bias, cosine, sine):
    rows, width = token_rows.shape
    columns = weight.shape[1]
    tile = 512
    return pl.pallas_call(
        functools.partial(project_kernel, 2 * width // tile),
        out_shape=jax.ShapeDtypeStruct((rows, columns), BF16),
        grid=(columns // tile,),
        in_specs=[
            pl.BlockSpec((rows, width), lambda j: (0, 0)),
            pl.BlockSpec((width, tile), lambda j: (0, j)),
            pl.BlockSpec((1, tile), lambda j: (0, j)),
            pl.BlockSpec((rows, 128), lambda j: (0, 0)),
            pl.BlockSpec((rows, 128), lambda j: (0, 0)),
        ],
        out_specs=pl.BlockSpec((rows, tile), lambda j: (0, j)),
        compiler_params=pltpu.CompilerParams(vmem_limit_bytes=32 * 1024 * 1024),
        name="project",
    )(token_rows, weight, bias, cosine, sine)


def attend_pair(
    query_ref, key_ref, value_ref, far_key_ref, far_value_ref, seg_ref, seg_near_ref, seg_far_ref, out_ref, norm_ref
):
    rows = query_ref.shape[0]
    first = lane_half((rows, 128), 128, HEAD_DIM)
    tile = 256
    for r in range(rows // tile):
        rs = pl.ds(r * tile, tile)
        query = query_ref[rs, :]
        low_half = first[:tile]
        seg = seg_ref[rs, :]
        near, far = seg == seg_near_ref[...], seg == seg_far_ref[...]
        outs, norms = [], []
        for h in range(2):
            keep = low_half if h == 0 else jnp.logical_not(low_half)
            one = jnp.where(keep, query, jnp.zeros_like(query))
            near_scores = jnp.where(near, dot_columns(one, key_ref[...]), neg_large)
            far_scores = jnp.where(far, dot_columns(one, far_key_ref[...]), neg_large)
            top = jnp.maximum(
                jnp.max(near_scores, axis=1, keepdims=True), jnp.max(far_scores, axis=1, keepdims=True)
            )
            near_expon, far_expon = jnp.exp(near_scores - top), jnp.exp(far_scores - top)
            total = jnp.sum(near_expon, axis=1, keepdims=True) + jnp.sum(
                far_expon, axis=1, keepdims=True
            )
            mixed = dot_rows(near_expon.astype(BF16), value_ref[...]) + dot_rows(
                far_expon.astype(BF16), far_value_ref[...]
            )
            outs.append(mixed / total)
            norms.append(jnp.broadcast_to(top + jnp.log(total), (tile, 128)))
        out_ref[rs, :] = jnp.where(low_half, outs[0], outs[1]).astype(BF16)
        flipped = jnp.transpose(jnp.where(low_half, norms[0], norms[1]))
        norm_ref[0:1, rs] = flipped[0:1]
        norm_ref[1:2, rs] = flipped[HEAD_DIM : HEAD_DIM + 1]


def attend_back_kernel(
    query_ref, key_ref, value_ref, far_key_ref, far_value_ref, grad_ref, norm_ref,
    seg_ref, seg_near_ref, seg_far_ref, cosine_ref, sine_ref, far_cosine_ref, far_sine_ref,
    query_out, key_out, value_out, far_key_out, far_value_out,
):
    rows = query_ref.shape[0]
    low_half = lane_half((rows, 128), 128, HEAD_DIM)
    query, grad = query_ref[...], grad_ref[...]
    seg = seg_ref[...]
    sides = (
        (key_ref[...], value_ref[...], seg_near_ref[...]),
        (far_key_ref[...], far_value_ref[...], seg_far_ref[...]),
    )
    query_grads, key_grads, value_grads = [], [[], []], [[], []]
    for h in range(2):
        keep = low_half if h == 0 else jnp.logical_not(low_half)
        one = jnp.where(keep, query, jnp.zeros_like(query))
        one_grad = jnp.where(keep, grad, jnp.zeros_like(grad))
        norm = norm_ref[0, h : h + 1, :]
        kept = []
        delta = jnp.zeros((1, rows), F32)
        for key, value, seg_key in sides:
            scores = jnp.where(seg_key == seg, dot_columns(key, one), neg_large)
            probs = jnp.exp(scores - norm)
            product = probs * dot_columns(value, one_grad)
            delta = delta + jnp.sum(product, axis=0, keepdims=True)
            kept.append((probs, product))
        total = None
        for i, (key, value, seg_key) in enumerate(sides):
            probs, product = kept[i]
            score_grad = (product - probs * delta).astype(BF16)
            key_grads[i].append(dot_rows(score_grad, query))
            value_grads[i].append(dot_rows(probs.astype(BF16), grad))
            part = lax.dot_general(
                score_grad, key, (((0,), (0,)), ((), ())), preferred_element_type=F32
            )
            total = part if total is None else total + part
        query_grads.append(total)

    def join(pair):
        return jnp.where(low_half, pair[0], pair[1])

    def unturn(value, cosine, sine):
        return value * cosine - turn(value) * sine

    query_grad = join(query_grads) * HEAD_DIM ** (-0.5)
    query_out[...] = unturn(query_grad, cosine_ref[...], sine_ref[...]).astype(BF16)
    key_out[...] = unturn(join(key_grads[0]), cosine_ref[...], sine_ref[...])
    value_out[...] = join(value_grads[0])
    far_key_out[...] = unturn(join(key_grads[1]), far_cosine_ref[...], far_sine_ref[...]).astype(BF16)
    far_value_out[...] = join(value_grads[1]).astype(BF16)


def attend_back(qkv, far_kv, context_grad, norms, seg_row, seg_near, seg_far, tables):
    rows = qkv.shape[0]
    width = HEADS * HEAD_DIM
    pairs = width // 128
    block = lambda at: pl.BlockSpec((rows, 128), lambda h: (0, at + h))
    whole = lambda a: pl.BlockSpec(a.shape, lambda h: (0, 0))
    return pl.pallas_call(
        attend_back_kernel,
        out_shape=[
            jax.ShapeDtypeStruct((rows, width), BF16),
            jax.ShapeDtypeStruct((rows, width), F32),
            jax.ShapeDtypeStruct((rows, width), F32),
            jax.ShapeDtypeStruct((rows, width), BF16),
            jax.ShapeDtypeStruct((rows, width), BF16),
        ],
        grid=(pairs,),
        in_specs=[
            block(0),
            block(pairs),
            block(2 * pairs),
            block(0),
            block(pairs),
            block(0),
            pl.BlockSpec((1, 8, rows), lambda h: (h, 0, 0)),
            whole(seg_row),
            whole(seg_near),
            whole(seg_far),
        ]
        + [whole(t) for t in tables],
        out_specs=[block(0)] * 5,
        compiler_params=pltpu.CompilerParams(vmem_limit_bytes=60 * 1024 * 1024),
        name="attend_back",
    )(qkv, qkv, qkv, far_kv, far_kv, context_grad, norms, seg_row, seg_near, seg_far, *tables)


def pair_tables(positions):
    cosine, sine = rotary_tables(positions)
    return (jnp.concatenate([cosine, cosine], axis=1), jnp.concatenate([sine, sine], axis=1))


def swap_cores(value, wide_size):
    pairs = [(w, w + 1 - 2 * (w % 2)) for w in range(wide_size)]
    return lax.ppermute(value, "wide", pairs)


def plane_device(
    tokens,
    segment_ids,
    project_weight,
    project_bias,
    output_weight,
    output_bias,
    first_gain,
    first_shift,
    up_weight,
    up_bias,
    down_weight,
    down_bias,
    second_gain,
    second_shift,
    embed_weight,
    out_cotangent,
    embed_cotangent,
):
    width = HEADS * HEAD_DIM
    piece = tokens.shape[2]
    rows = 2 * piece
    wide_size = 2 * LINE
    group = lax.axis_index("group")
    core = lax.rem(lax.axis_index("wide"), 2)
    devices = PLANE * LINE * 2
    vectors = (
        project_bias,
        output_bias,
        first_gain,
        first_shift,
        up_bias,
        down_bias,
        second_gain,
        second_shift,
    )
    sizes = [v.shape[0] for v in vectors]
    lanes = embed_weight.shape[1]
    pad = SMALL_ROWS * lanes - sum(sizes)
    small = jnp.pad(jnp.concatenate(vectors), (0, pad)).reshape(SMALL_ROWS, lanes)
    embed_small = jnp.concatenate([embed_weight, small])
    embed_rows = embed_weight.shape[0]

    other_ids = swap_cores(segment_ids, wide_size)
    micro_mine = group // 2
    from_core = lax.rem(group, 2)
    ids = jnp.where(from_core == core, segment_ids[:, 0], other_ids[:, 0])
    ids = lax.dynamic_index_in_dim(ids, micro_mine, 0, keepdims=False)
    near_ids = lax.dynamic_slice_in_dim(ids, core * rows, rows)
    far_ids = lax.dynamic_slice_in_dim(ids, (1 - core) * rows, rows)

    (project_full, small_full), (token_pieces,) = gather(
        [project_weight, embed_small], [project_weight.shape[0] // 2, embed_rows], [tokens[:, 0]], 1
    )
    token_rows = token_pieces.reshape(rows, width)
    small_full = small_full.reshape(devices, embed_rows + SMALL_ROWS, lanes)
    embed_full = small_full[:, :embed_rows].reshape(devices * embed_rows, lanes)
    small_full = small_full[:, embed_rows:].reshape(devices, SMALL_ROWS * lanes)
    gathered, start = [], 0
    for size in sizes:
        gathered.append(small_full[:, start : start + size].reshape(1, devices * size).astype(F32))
        start += size
    bias_p, bias_o, gain1, shift1, bias_u, bias_d, gain2, shift2 = gathered

    place_of = jnp.arange(rows)
    cosine, sine = pair_tables((core * rows + place_of).astype(F32))
    far_cosine, far_sine = pair_tables(((1 - core) * rows + place_of).astype(F32))
    project_full = project_full.reshape(width, 3 * width)
    qkv = project(token_rows, project_full, bias_p, cosine, sine)
    fulls, pieces, (far_kv, context_low, norms) = gather_attend(
        [output_weight, up_weight, down_weight],
        [output_weight.shape[0] // 2, up_weight.shape[0] // 2, down_weight.shape[0] // 2],
        [out_cotangent[:, 0], embed_cotangent[:, 0]],
        qkv,
        (near_ids[:, None], near_ids[None, :], far_ids[None, :]),
        2,
    )
    output_full, up_full, down_full = fulls
    cot_pieces, embed_cot_pieces = pieces
    output_full = output_full.reshape(width, width)
    up_full = up_full.reshape(width, -1)
    down_full = down_full.reshape(-1, width)

    branch = jnp.dot(context_low, output_full, preferred_element_type=F32) + bias_o
    hidden, first_normed, first_rstd = norm_forward(
        token_rows.astype(F32) + branch, gain1, shift1
    )
    hidden_low = hidden.astype(BF16)
    up_value = jnp.dot(hidden_low, up_full, preferred_element_type=F32) + bias_u
    act_low = jax.nn.gelu(up_value, approximate=False).astype(BF16)
    down_value = jnp.dot(act_low, down_full, preferred_element_type=F32) + bias_d
    result, second_normed, second_rstd = norm_forward(hidden + down_value, gain2, shift2)
    result_low = result.astype(BF16)
    embedded = jnp.dot(result_low, embed_full, preferred_element_type=F32).astype(BF16)

    embed_cot = embed_cot_pieces.reshape(rows, lanes)
    result_grad = cot_pieces.reshape(rows, width).astype(F32) + times_transpose(
        embed_cot, embed_full
    )
    embed_weight_grad = contract_rows(result_low, embed_cot)
    sum_grad, second_gain_grad, second_shift_grad = norm_backward(
        result_grad, second_normed, second_rstd, gain2
    )
    down_grad = sum_grad.astype(BF16)
    down_bias_grad = jnp.sum(down_grad.astype(F32), axis=0)
    down_weight_grad = contract_rows(act_low, down_grad)
    up_grad = (times_transpose(down_grad, down_full) * gelu_slope(up_value)).astype(BF16)
    up_bias_grad = jnp.sum(up_grad.astype(F32), axis=0)
    up_weight_grad = contract_rows(hidden_low, up_grad)
    hidden_grad = sum_grad + times_transpose(up_grad, up_full)
    first_grad, first_gain_grad, first_shift_grad = norm_backward(
        hidden_grad, first_normed, first_rstd, gain1
    )
    branch_grad = first_grad.astype(BF16)
    output_bias_grad = jnp.sum(branch_grad.astype(F32), axis=0)
    output_weight_grad = contract_rows(context_low, branch_grad)
    context_grad = times_transpose(branch_grad, output_full).astype(BF16)

    query_back, key_near, value_near, key_far, value_far = attend_back(
        qkv,
        far_kv,
        context_grad,
        norms,
        near_ids[None, :],
        near_ids[:, None],
        far_ids[:, None],
        (cosine, sine, far_cosine, far_sine),
    )
    key_back = (key_near + swap_cores(key_far, wide_size).astype(F32)).astype(BF16)
    value_back = (value_near + swap_cores(value_far, wide_size).astype(F32)).astype(BF16)
    projected_grad = jnp.concatenate([query_back, key_back, value_back], axis=1)
    project_bias_grad = jnp.sum(projected_grad.astype(F32), axis=0)
    project_weight_grad = contract_rows(token_rows, projected_grad)
    token_grad = (first_grad + times_transpose(projected_grad, project_full)).astype(BF16)

    small_grads = jnp.concatenate(
        [
            v.reshape(devices, -1)
            for v in (
                project_bias_grad,
                output_bias_grad,
                first_gain_grad,
                first_shift_grad,
                up_bias_grad,
                down_bias_grad,
                second_gain_grad,
                second_shift_grad,
            )
        ],
        axis=1,
    )
    small_grads = jnp.pad(small_grads, ((0, 0), (0, pad))).reshape(devices, SMALL_ROWS, lanes)
    embed_grads = jnp.concatenate(
        [embed_weight_grad.reshape(devices, embed_rows, lanes), small_grads], axis=1
    )

    def spread(full):
        return full.astype(BF16).reshape(PLANE, LINE, 2, -1, full.shape[-1])

    grads = [
        spread(g)
        for g in (
            down_weight_grad,
            up_weight_grad,
            output_weight_grad,
            project_weight_grad,
            embed_grads,
        )
    ]
    splits = [g.shape[3] // 2 for g in grads[:4]] + [embed_rows]
    outs, moved = reduce_grads(
        grads,
        splits,
        [
            result_low.reshape(2, piece, width),
            embedded.reshape(2, piece, lanes),
            token_grad.reshape(2, piece, width),
        ],
        3,
    )
    down_out, up_out, output_out, project_out, small_out = outs
    vector_out = small_out[embed_rows:].reshape(-1)
    parts, start = [], 0
    for size in sizes:
        parts.append(vector_out[start : start + size])
        start += size
    layer_out, embed_out, token_back = [m[:, None] for m in moved]
    return (
        layer_out,
        embed_out,
        token_back.astype(F32),
        project_out,
        parts[0],
        output_out,
        parts[1],
        parts[2],
        parts[3],
        up_out,
        parts[4],
        down_out,
        parts[5],
        parts[6],
        parts[7],
        small_out[:embed_rows],
    )


def choose_device(mesh):
    if mesh.shape["group"] == PLANE and mesh.shape["wide"] == 2 * LINE:
        return plane_device
    return general_device


def solution(mesh):
    in_specs = (
        P(None, "wide", "group", None),
        P(None, "wide", None),
        P(("group", "wide"), None),
        P(("group", "wide")),
        P(("group", "wide"), None),
        P(("group", "wide")),
        P(("group", "wide")),
        P(("group", "wide")),
        P(("group", "wide"), None),
        P(("group", "wide")),
        P(("group", "wide"), None),
        P(("group", "wide")),
        P(("group", "wide")),
        P(("group", "wide")),
        P(("group", "wide"), None),
        P(None, "wide", "group", None),
        P(None, "wide", "group", None),
    )
    out_specs = (
        P(None, "wide", "group", None),
        P(None, "wide", "group", None),
        P(None, "wide", "group", None),
        P(("group", "wide"), None),
        P(("group", "wide")),
        P(("group", "wide"), None),
        P(("group", "wide")),
        P(("group", "wide")),
        P(("group", "wide")),
        P(("group", "wide"), None),
        P(("group", "wide")),
        P(("group", "wide"), None),
        P(("group", "wide")),
        P(("group", "wide")),
        P(("group", "wide")),
        P(("group", "wide"), None),
    )
    return jax.shard_map(
        choose_device(mesh), mesh=mesh, in_specs=in_specs, out_specs=out_specs, check_vma=False
    )
```

```python
import functools

import jax
import jax.numpy as jnp
from jax import lax
from jax.experimental import pallas as pl
from jax.experimental.pallas import tpu as pltpu
from jax.sharding import PartitionSpec as P

HEADS = 16
HEAD_DIM = 64


eps_norm = 1e-05
neg_large = -1e30


def rotary_tables(positions):
    half_dim = HEAD_DIM // 2
    frequency = 10000.0 ** (-jnp.arange(half_dim, dtype=jnp.float32) * (2.0 / HEAD_DIM))
    angles = positions[:, None] * frequency[None, :]
    angles = jnp.concatenate([angles, angles], axis=1)
    return (jnp.cos(angles), jnp.sin(angles))


def rotate(values, cosine_table, sine_table):
    half_dim = HEAD_DIM // 2
    swapped = jnp.concatenate([-values[..., half_dim:], values[..., :half_dim]], axis=-1)
    return values * cosine_table[:, None, :] + swapped * sine_table[:, None, :]


def unrotate(grads, cosine_table, sine_table):
    half_dim = HEAD_DIM // 2
    scaled = grads * sine_table[:, None, :]
    swapped = jnp.concatenate([scaled[..., half_dim:], -scaled[..., :half_dim]], axis=-1)
    return grads * cosine_table[:, None, :] + swapped


def norm_forward(resid, gain, shift):
    center = resid - jnp.mean(resid, axis=-1, keepdims=True)
    spread = jnp.mean(center * center, axis=-1, keepdims=True)
    rstd_rows = lax.rsqrt(spread + eps_norm)
    normed = center * rstd_rows
    return (normed * gain + shift, normed, rstd_rows)


def norm_backward(grads, normed, rstd_rows, gain):
    scaled = grads * gain
    resid_grad = rstd_rows * (
        scaled
        - jnp.mean(scaled, axis=-1, keepdims=True)
        - normed * jnp.mean(scaled * normed, axis=-1, keepdims=True)
    )
    return (resid_grad, jnp.sum(grads * normed, axis=0), jnp.sum(grads, axis=0))


def contract_rows(left, right):
    return lax.dot_general(
        left, right, (((0,), (0,)), ((), ())), preferred_element_type=jnp.float32
    )


def times_transpose(left, right):
    return lax.dot_general(
        left, right, (((1,), (1,)), ((), ())), preferred_element_type=jnp.float32
    )


def gelu_slope(value):
    normal_cdf = 0.5 * (1.0 + lax.erf(value * 0.7071067811865476))
    density = jnp.exp(-0.5 * value * value) * 0.3989422804014327
    return normal_cdf + value * density


def key_blocks(kv_rows, seg_all):
    seq_len = kv_rows.shape[0]
    block_rows = min(512, seq_len)
    count = seq_len // block_rows
    return (
        kv_rows.reshape(count, block_rows, 2, HEADS, HEAD_DIM),
        seg_all.reshape(count, block_rows),
    )


def block_scores(queries, key_block, same):
    scores = jnp.einsum("qhd,khd->hqk", queries, key_block, preferred_element_type=jnp.float32)
    scores = scores * HEAD_DIM ** (-0.5)
    return jnp.where(same[None], scores, neg_large)


def attention_forward(queries, blocks, seg_blocks, seg_local):
    length = queries.shape[0]

    def norm_step(carry, pieces):
        kv_block, seg_block = pieces
        same = seg_local[:, None] == seg_block[None, :]

        def norm_update(running):
            run_max, run_sum = running
            scores = block_scores(queries, kv_block[:, 0], same)
            new_max = jnp.maximum(run_max, jnp.max(scores, axis=-1))
            new_sum = run_sum * jnp.exp(run_max - new_max) + jnp.sum(
                jnp.exp(scores - new_max[..., None]), axis=-1
            )
            return (new_max, new_sum)

        def norm_unchanged(running):
            return running

        return (lax.cond(jnp.any(same), norm_update, norm_unchanged, carry), None)

    start = (
        jnp.full((HEADS, length), neg_large, jnp.float32),
        jnp.zeros((HEADS, length), jnp.float32),
    )
    (run_max, run_sum), unused = lax.scan(norm_step, start, (blocks, seg_blocks))
    log_norm = run_max + jnp.log(run_sum)

    def value_step(total, pieces):
        kv_block, seg_block = pieces
        same = seg_local[:, None] == seg_block[None, :]

        def value_update(running):
            scores = block_scores(queries, kv_block[:, 0], same)
            weights = jnp.exp(scores - log_norm[..., None]).astype(jnp.bfloat16)
            return running + jnp.einsum(
                "hqk,khd->qhd", weights, kv_block[:, 1], preferred_element_type=jnp.float32
            )

        def value_unchanged(running):
            return running

        return (lax.cond(jnp.any(same), value_update, value_unchanged, total), None)

    context, unused = lax.scan(
        value_step, jnp.zeros(queries.shape, jnp.float32), (blocks, seg_blocks)
    )
    return (context, log_norm)


def attention_backward(queries, blocks, seg_blocks, seg_local, log_norm, context_grad, delta):

    def grad_step(query_grad, pieces):
        kv_block, seg_block = pieces
        same = seg_local[:, None] == seg_block[None, :]

        def work(running):
            scores = block_scores(queries, kv_block[:, 0], same)
            probs = jnp.exp(scores - log_norm[..., None])
            prob_grad = jnp.einsum(
                "qhd,khd->hqk", context_grad, kv_block[:, 1], preferred_element_type=jnp.float32
            )
            score_grad = (probs * (prob_grad - delta[..., None])).astype(jnp.bfloat16)
            running = running + jnp.einsum(
                "hqk,khd->qhd", score_grad, kv_block[:, 0], preferred_element_type=jnp.float32
            ) * HEAD_DIM ** (-0.5)
            prob_low = probs.astype(jnp.bfloat16)
            key_grad = jnp.einsum(
                "hqk,qhd->khd", score_grad, queries, preferred_element_type=jnp.float32
            ) * HEAD_DIM ** (-0.5)
            value_grad = jnp.einsum(
                "hqk,qhd->khd", prob_low, context_grad, preferred_element_type=jnp.float32
            )
            return (running, jnp.stack([key_grad, value_grad], axis=1))

        def skipped(running):
            return (running, jnp.zeros(kv_block.shape, jnp.float32))

        return lax.cond(jnp.any(same), work, skipped, query_grad)

    query_grad, kv_grad = lax.scan(
        grad_step, jnp.zeros(queries.shape, jnp.float32), (blocks, seg_blocks)
    )
    return (query_grad, kv_grad.reshape(-1, 2 * HEADS * HEAD_DIM))


def general_device(
    tokens,
    segment_ids,
    project_weight,
    project_bias,
    output_weight,
    output_bias,
    first_gain,
    first_shift,
    up_weight,
    up_bias,
    down_weight,
    down_bias,
    second_gain,
    second_shift,
    embed_weight,
    out_cotangent,
    embed_cotangent,
):
    shards = (
        project_weight,
        project_bias,
        output_weight,
        output_bias,
        first_gain,
        first_shift,
        up_weight,
        up_bias,
        down_weight,
        down_bias,
        second_gain,
        second_shift,
        embed_weight,
    )
    length = tokens.shape[2]
    width = HEADS * HEAD_DIM
    head_shape = (length, HEADS, HEAD_DIM)
    place = lax.axis_index("group")
    positions = (place * length + jnp.arange(length)).astype(jnp.float32)
    cosine_table, sine_table = rotary_tables(positions)
    grad_total = None
    results = []
    embeddings = []
    input_grads = []
    for micro_index in range(tokens.shape[0]):
        params = (
            lax.all_gather(shards[0], ("group", "wide"), axis=0, tiled=True),
            lax.all_gather(shards[1], ("group", "wide"), axis=0, tiled=True),
            lax.all_gather(shards[2], ("group", "wide"), axis=0, tiled=True),
            lax.all_gather(shards[3], ("group", "wide"), axis=0, tiled=True),
            lax.all_gather(shards[4], ("group", "wide"), axis=0, tiled=True),
            lax.all_gather(shards[5], ("group", "wide"), axis=0, tiled=True),
            lax.all_gather(shards[6], ("group", "wide"), axis=0, tiled=True),
            lax.all_gather(shards[7], ("group", "wide"), axis=0, tiled=True),
            lax.all_gather(shards[8], ("group", "wide"), axis=0, tiled=True),
            lax.all_gather(shards[9], ("group", "wide"), axis=0, tiled=True),
            lax.all_gather(shards[10], ("group", "wide"), axis=0, tiled=True),
            lax.all_gather(shards[11], ("group", "wide"), axis=0, tiled=True),
            lax.all_gather(shards[12], ("group", "wide"), axis=0, tiled=True),
        )
        seg_all = segment_ids[micro_index, 0]
        seg_local = lax.dynamic_slice_in_dim(seg_all, place * length, length)
        token_low = tokens[micro_index, 0]
        token_wide = token_low.astype(jnp.float32)
        projected = jnp.dot(token_low, params[0], preferred_element_type=jnp.float32) + params[
            1
        ].astype(jnp.float32)
        queries = rotate(projected[:, :width].reshape(head_shape), cosine_table, sine_table).astype(
            jnp.bfloat16
        )
        key_rows = rotate(
            projected[:, width : 2 * width].reshape(head_shape), cosine_table, sine_table
        ).astype(jnp.bfloat16)
        value_rows = projected[:, 2 * width :].astype(jnp.bfloat16)
        local_kv = jnp.concatenate([key_rows.reshape(length, width), value_rows], axis=1)
        kv_all = lax.all_gather(local_kv, "group", axis=0, tiled=True)
        blocks, seg_blocks = key_blocks(kv_all, seg_all)
        context, log_norm = attention_forward(queries, blocks, seg_blocks, seg_local)
        context_low = context.reshape(length, width).astype(jnp.bfloat16)
        branch = jnp.dot(context_low, params[2], preferred_element_type=jnp.float32) + params[
            3
        ].astype(jnp.float32)
        first_gain_wide = params[4].astype(jnp.float32)
        hidden, first_normed, first_rstd = norm_forward(
            token_wide + branch, first_gain_wide, params[5].astype(jnp.float32)
        )
        hidden_low = hidden.astype(jnp.bfloat16)
        up_value = jnp.dot(hidden_low, params[6], preferred_element_type=jnp.float32) + params[
            7
        ].astype(jnp.float32)
        act_low = jax.nn.gelu(up_value, approximate=False).astype(jnp.bfloat16)
        down_value = jnp.dot(act_low, params[8], preferred_element_type=jnp.float32) + params[
            9
        ].astype(jnp.float32)
        second_gain_wide = params[10].astype(jnp.float32)
        result, second_normed, second_rstd = norm_forward(
            hidden + down_value, second_gain_wide, params[11].astype(jnp.float32)
        )
        result_low = result.astype(jnp.bfloat16)
        embedded = jnp.dot(result_low, params[12], preferred_element_type=jnp.float32)
        results.append(result_low)
        embeddings.append(embedded.astype(jnp.bfloat16))
        params = (
            lax.all_gather(shards[0], ("group", "wide"), axis=0, tiled=True),
            lax.all_gather(shards[1], ("group", "wide"), axis=0, tiled=True),
            lax.all_gather(shards[2], ("group", "wide"), axis=0, tiled=True),
            lax.all_gather(shards[3], ("group", "wide"), axis=0, tiled=True),
            lax.all_gather(shards[4], ("group", "wide"), axis=0, tiled=True),
            lax.all_gather(shards[5], ("group", "wide"), axis=0, tiled=True),
            lax.all_gather(shards[6], ("group", "wide"), axis=0, tiled=True),
            lax.all_gather(shards[7], ("group", "wide"), axis=0, tiled=True),
            lax.all_gather(shards[8], ("group", "wide"), axis=0, tiled=True),
            lax.all_gather(shards[9], ("group", "wide"), axis=0, tiled=True),
            lax.all_gather(shards[10], ("group", "wide"), axis=0, tiled=True),
            lax.all_gather(shards[11], ("group", "wide"), axis=0, tiled=True),
            lax.all_gather(shards[12], ("group", "wide"), axis=0, tiled=True),
        )
        embed_cot = embed_cotangent[micro_index, 0]
        result_grad = out_cotangent[micro_index, 0].astype(jnp.float32) + times_transpose(
            embed_cot, params[12]
        )
        embed_weight_grad = contract_rows(result_low, embed_cot)
        sum_grad, second_gain_grad, second_shift_grad = norm_backward(
            result_grad, second_normed, second_rstd, second_gain_wide
        )
        down_grad = sum_grad.astype(jnp.bfloat16)
        down_bias_grad = jnp.sum(down_grad.astype(jnp.float32), axis=0)
        down_weight_grad = contract_rows(act_low, down_grad)
        up_grad = (times_transpose(down_grad, params[8]) * gelu_slope(up_value)).astype(
            jnp.bfloat16
        )
        up_bias_grad = jnp.sum(up_grad.astype(jnp.float32), axis=0)
        up_weight_grad = contract_rows(hidden_low, up_grad)
        hidden_grad = sum_grad + times_transpose(up_grad, params[6])
        first_grad, first_gain_grad, first_shift_grad = norm_backward(
            hidden_grad, first_normed, first_rstd, first_gain_wide
        )
        branch_grad = first_grad.astype(jnp.bfloat16)
        output_bias_grad = jnp.sum(branch_grad.astype(jnp.float32), axis=0)
        output_weight_grad = contract_rows(context_low, branch_grad)
        context_grad = (
            times_transpose(branch_grad, params[2]).astype(jnp.bfloat16).reshape(head_shape)
        )
        delta = jnp.transpose(jnp.sum(context_grad.astype(jnp.float32) * context, axis=-1))
        kv_again = lax.all_gather(local_kv, "group", axis=0, tiled=True)
        blocks, seg_blocks = key_blocks(kv_again, seg_all)
        query_grad, kv_partial = attention_backward(
            queries, blocks, seg_blocks, seg_local, log_norm, context_grad, delta
        )
        kv_grad = lax.psum_scatter(
            kv_partial.astype(jnp.bfloat16), "group", scatter_dimension=0, tiled=True
        ).astype(jnp.float32)
        key_part = kv_grad[:, :width].reshape(head_shape)
        value_part = kv_grad[:, width:]
        query_back = unrotate(query_grad, cosine_table, sine_table).reshape(length, width)
        key_back = unrotate(key_part, cosine_table, sine_table).reshape(length, width)
        projected_grad = jnp.concatenate([query_back, key_back, value_part], axis=1).astype(
            jnp.bfloat16
        )
        project_bias_grad = jnp.sum(projected_grad.astype(jnp.float32), axis=0)
        project_weight_grad = contract_rows(token_low, projected_grad)
        input_grads.append(first_grad + times_transpose(projected_grad, params[0]))
        local_grads = (
            project_weight_grad,
            project_bias_grad,
            output_weight_grad,
            output_bias_grad,
            first_gain_grad,
            first_shift_grad,
            up_weight_grad,
            up_bias_grad,
            down_weight_grad,
            down_bias_grad,
            second_gain_grad,
            second_shift_grad,
            embed_weight_grad,
        )
        summed = (
            lax.psum_scatter(local_grads[0], ("group", "wide"), scatter_dimension=0, tiled=True),
            lax.psum_scatter(local_grads[1], ("group", "wide"), scatter_dimension=0, tiled=True),
            lax.psum_scatter(local_grads[2], ("group", "wide"), scatter_dimension=0, tiled=True),
            lax.psum_scatter(local_grads[3], ("group", "wide"), scatter_dimension=0, tiled=True),
            lax.psum_scatter(local_grads[4], ("group", "wide"), scatter_dimension=0, tiled=True),
            lax.psum_scatter(local_grads[5], ("group", "wide"), scatter_dimension=0, tiled=True),
            lax.psum_scatter(local_grads[6], ("group", "wide"), scatter_dimension=0, tiled=True),
            lax.psum_scatter(local_grads[7], ("group", "wide"), scatter_dimension=0, tiled=True),
            lax.psum_scatter(local_grads[8], ("group", "wide"), scatter_dimension=0, tiled=True),
            lax.psum_scatter(local_grads[9], ("group", "wide"), scatter_dimension=0, tiled=True),
            lax.psum_scatter(local_grads[10], ("group", "wide"), scatter_dimension=0, tiled=True),
            lax.psum_scatter(local_grads[11], ("group", "wide"), scatter_dimension=0, tiled=True),
            lax.psum_scatter(local_grads[12], ("group", "wide"), scatter_dimension=0, tiled=True),
        )
        grad_total = (
            summed
            if grad_total is None
            else tuple((total + part for total, part in zip(grad_total, summed)))
        )
    layer_out = jnp.stack(results)[:, None]
    embed_out = jnp.stack(embeddings)[:, None]
    token_grad = jnp.stack(input_grads)[:, None]
    return (
        layer_out,
        embed_out,
        token_grad,
        grad_total[0],
        grad_total[1],
        grad_total[2],
        grad_total[3],
        grad_total[4],
        grad_total[5],
        grad_total[6],
        grad_total[7],
        grad_total[8],
        grad_total[9],
        grad_total[10],
        grad_total[11],
        grad_total[12],
    )


MESH = pl.DeviceIdType.MESH
F32 = jnp.float32
BF16 = jnp.bfloat16
PLANE = 4
LINE = 4
GATHER_SEMS = 42
REDUCE_SEMS = 56
REDUCE_AHEAD = (3, 5, 7)
SMALL_ROWS = 16


def place():
    group = lax.axis_index("group")
    wide = lax.axis_index("wide")
    return (group, lax.rem(group, 2), group // 2, wide // 2, lax.rem(wide, 2))


def when(cond, act):
    if cond is True:
        act()
    else:
        pl.when(cond)(act)


def both(left, right):
    return right if left is True else jnp.logical_and(left, right)


def remote(src, dst, send_sem, recv_sem, device):
    return pltpu.make_async_remote_copy(
        src_ref=src,
        dst_ref=dst,
        send_sem=send_sem,
        recv_sem=recv_sem,
        device_id=device,
        device_id_type=MESH,
    )


def entry_barrier():
    g, x, y, z, c = place()
    devices = []
    for step in range(1, 8):
        other = lax.rem(g * 2 + c + step, 8)
        devices.append((other // 2, z * 2 + lax.rem(other, 2)))
    devices.append((g, lax.rem(z + 1, LINE) * 2 + c))
    devices.append((g, lax.rem(z + LINE - 1, LINE) * 2 + c))
    barrier = pltpu.get_barrier_semaphore()
    for device in devices:
        pl.semaphore_signal(barrier, inc=1, device_id=device, device_id_type=MESH)
    pl.semaphore_wait(barrier, len(devices))


class Sender:
    def __init__(self, send_sems, recv_sems):
        self.send_sems, self.recv_sems = send_sems, recv_sems
        self.pending, self.draining = [], False

    def copy(self, src, dst, index, device):
        return remote(src, dst, self.send_sems.at[index], self.recv_sems.at[index], device)

    def send(self, cond, src, dst, index, device):
        copy = self.copy(src, dst, index, device)
        when(cond, copy.wait_send if self.draining else copy.start)

    def post(self, cond, src, dst, index, device):
        self.send(cond, src, dst, index, device)
        self.pending.append((cond, src, dst, index, device))

    def land(self, ref, index, device):
        self.copy(ref, ref, index, device).wait_recv()

    def do(self, cond, act):
        if not self.draining:
            when(cond, act)

    def drain(self, ticks):
        self.draining = True
        for tick in ticks:
            tick()
        for call in self.pending:
            self.send(*call)


def near_items(z, distance):
    if distance == 0:
        return [(0, z, True)]
    return [
        (distance, jnp.maximum(z - distance, 0), z >= distance),
        (3 + distance, jnp.minimum(z + distance, LINE - 1), z + distance < LINE),
    ]


def gather_ticks(shards, fulls, splits, chunks, ahead, sender, local_sems):
    g, x, y, z, c = place()
    gx, gy, gd = g + 1 - 2 * x, g + 2 - 4 * y, 3 - g
    to_x, to_y, to_core = (gx, z * 2 + c), (gy, z * 2 + c), (g, z * 2 + 1 - c)
    above = (g, jnp.minimum(z + 1, LINE - 1) * 2 + c)
    below = (g, jnp.maximum(z - 1, 0) * 2 + c)

    def first(a, k):
        base = a * GATHER_SEMS
        for slot, zi, cond in near_items(z, k):
            region = fulls[a].at[g, zi, c]
            if k == 0:
                sender.do(
                    True, lambda: pltpu.make_async_copy(shards[a], region, local_sems.at[a]).start()
                )
                source = shards[a]
                sender.send(z < LINE - 1, source, region, base + 1, above)
                sender.send(z > 0, source, region, base + 4, below)
            else:
                source = region
                sender.do(cond, lambda: sender.land(region, base + slot, to_x))
                if k < LINE - 1:
                    if slot < 4:
                        sender.send(both(cond, z < LINE - 1), source, region, base + slot + 1, above)
                    else:
                        sender.send(both(cond, z > 0), source, region, base + slot + 1, below)
            sender.send(cond, source, region, base + 7 + slot, to_x)
            sender.send(cond, source, region, base + 14 + slot, to_y)

    def second(a, k):
        base, cut, rows = a * GATHER_SEMS, splits[a], fulls[a].shape[3]
        for slot, zi, cond in near_items(z, k):
            sender.do(cond, lambda: sender.land(fulls[a].at[gx, zi, c], base + 7 + slot, to_x))
            upper = fulls[a].at[gx, zi, c, 0:cut]
            sender.send(cond, upper, upper, base + 21 + slot, to_y)
            sender.do(cond, lambda: sender.land(fulls[a].at[gy, zi, c], base + 14 + slot, to_x))
            lower = fulls[a].at[gy, zi, c, cut:rows]
            sender.send(cond, lower, lower, base + 28 + slot, to_x)

    def third(a, k):
        base, cut, rows = a * GATHER_SEMS, splits[a], fulls[a].shape[3]
        if k == 0:
            sender.do(
                True,
                lambda: pltpu.make_async_copy(
                    shards[a], fulls[a].at[g, z, c], local_sems.at[a]
                ).wait(),
            )
        for slot, zi, cond in near_items(z, k):
            sender.do(cond, lambda: sender.land(fulls[a].at[gd, zi, c, 0:cut], base + 21 + slot, to_x))
            sender.do(cond, lambda: sender.land(fulls[a].at[gd, zi, c, cut:rows], base + 28 + slot, to_x))
            ring = fulls[a].at[:, zi, c]
            sender.send(cond, ring, ring, base + 35 + slot, to_core)

    def finish():
        for a in range(len(shards)):
            for k in range(LINE):
                for slot, zi, cond in near_items(z, k):
                    when(
                        cond,
                        lambda: sender.land(
                            fulls[a].at[:, zi, 1 - c], a * GATHER_SEMS + 35 + slot, to_x
                        ),
                    )

    def grouped(stage):
        def act(chunk, k):
            for a in chunk:
                stage(a, k)

        return act

    order = [(chunk, k) for chunk in chunks for k in range(LINE)]
    stages = [grouped(stage) for stage in (first, second, third)]
    return (staged(order, stages, (0,) + ahead), finish)


def staged(order, stages, delays):
    ticks = []
    for t in range(len(order) + delays[-1]):

        def tick(t=t):
            for stage, delay in zip(stages, delays):
                if 0 <= t - delay < len(order):
                    stage(*order[t - delay])

        ticks.append(tick)
    return ticks


def add_into(target, terms):
    rows, columns = target.shape
    step = min(columns, 512)

    def body(i, carry):
        cut = pl.ds(pl.multiple_of(i * step, step), step)
        value = terms[0][:, cut].astype(F32)
        for term in terms[1:]:
            value = value + term[:, cut].astype(F32)
        target[:, cut] = value.astype(target.dtype)
        return carry

    lax.fori_loop(0, columns // step, body, 0)


def reduce_ticks(grads, outs, splits, held, core_in, half_in, whole_in, rise_in, fall_in, sender, local_sems):
    g, x, y, z, c = place()
    gx, gy, gd = g + 1 - 2 * x, g + 2 - 4 * y, 3 - g
    to_x, to_y, to_core = (gx, z * 2 + c), (gy, z * 2 + c), (g, z * 2 + 1 - c)
    above = (g, jnp.minimum(z + 1, LINE - 1) * 2 + c)
    below = (g, jnp.maximum(z - 1, 0) * 2 + c)

    def far_items(k):
        items = near_items(z, k)
        if k == 0:
            return items
        return [(k,) + items[1][1:], (3 + k,) + items[0][1:]]

    def load(a, zi, slot):
        return pltpu.make_async_copy(
            grads[a].at[:, zi, c], held[a].at[zi], local_sems.at[a * 7 + slot]
        )

    def zeroth(a, k):
        base = a * REDUCE_SEMS
        for slot, zi, cond in far_items(k):
            sender.send(cond, grads[a].at[:, zi, 1 - c], core_in[a].at[zi], base + slot, to_core)
            sender.do(cond, lambda: load(a, zi, slot).start())

    def first(a, k):
        base, cut, rows = a * REDUCE_SEMS, splits[a], held[a].shape[2]
        for slot, zi, cond in far_items(k):

            def work():
                load(a, zi, slot).wait()
                sender.land(core_in[a].at[zi], base + slot, to_x)
                for j in range(PLANE):
                    add_into(held[a].at[zi, j], [held[a].at[zi, j], core_in[a].at[zi, j]])

            sender.do(cond, work)
            sender.send(
                cond, held[a].at[zi, gd, 0:cut], half_in[a].at[zi, 0:cut], base + 7 + slot, to_y
            )
            sender.send(
                cond, held[a].at[zi, gd, cut:rows], half_in[a].at[zi, cut:rows], base + 14 + slot, to_x
            )

    def second(a, k):
        base, cut, rows = a * REDUCE_SEMS, splits[a], held[a].shape[2]
        for slot, zi, cond in far_items(k):

            def upper():
                sender.land(half_in[a].at[zi, 0:cut], base + 7 + slot, to_x)
                mine = held[a].at[zi, gx, 0:cut]
                add_into(mine, [mine, half_in[a].at[zi, 0:cut]])

            sender.do(cond, upper)
            sender.send(cond, held[a].at[zi, gx], whole_in[a].at[zi, 0], base + 21 + slot, to_x)

            def lower():
                sender.land(half_in[a].at[zi, cut:rows], base + 14 + slot, to_x)
                mine = held[a].at[zi, gy, cut:rows]
                add_into(mine, [mine, half_in[a].at[zi, cut:rows]])

            sender.do(cond, lower)
            sender.send(cond, held[a].at[zi, gy], whole_in[a].at[zi, 1], base + 28 + slot, to_y)

    def third(a, k):
        base = a * REDUCE_SEMS
        for slot, zi, cond in far_items(k):
            mine = held[a].at[zi, g]
            terms = [mine, whole_in[a].at[zi, 0], whole_in[a].at[zi, 1]]
            rise, fall = rise_in[a].at[zi], fall_in[a].at[zi]

            def arrive():
                sender.land(whole_in[a].at[zi, 0], base + 21 + slot, to_x)
                sender.land(whole_in[a].at[zi, 1], base + 28 + slot, to_x)

            sender.do(cond, arrive)
            if k == 0:
                sender.do(z > 0, lambda: sender.land(rise, base + 36, to_x))
                sender.do(z < LINE - 1, lambda: sender.land(fall, base + 43, to_x))
                sender.do(z == 0, lambda: add_into(outs[a], terms + [fall]))
                sender.do(z == LINE - 1, lambda: add_into(outs[a], terms + [rise]))
                sender.do(
                    jnp.logical_and(z > 0, z < LINE - 1),
                    lambda: add_into(outs[a], terms + [rise, fall]),
                )
            else:
                going_up = slot < 4
                moved = rise if going_up else fall
                offset = base + (35 if going_up else 42)
                inner = (z > 0) if going_up else (z < LINE - 1)

                def join():
                    sender.land(moved, offset + k + 1, to_x)
                    add_into(mine, terms + [moved])

                if k < LINE - 1:
                    sender.do(both(cond, inner), join)
                sender.do(both(cond, jnp.logical_not(inner)), lambda: add_into(mine, terms))
                sender.send(cond, mine, moved, offset + k, above if going_up else below)

    order = [(a, k) for a in range(len(grads)) for k in (3, 2, 1, 0)]
    return staged(order, (zeroth, first, second, third), (0,) + REDUCE_AHEAD)


def exchange(sources, targets, outward, sender, base, local_sems, local_base):
    g, x, y, z, c = place()

    def partner(index):
        if outward:
            return (index * 2 + c, z * 2 + g // 2)
        return (2 * c + index, z * 2 + lax.rem(g, 2))

    def origin(index):
        if outward:
            return (2 * c + index, z * 2 + lax.rem(g, 2))
        return (index * 2 + c, z * 2 + g // 2)

    slot = lax.rem(g, 2) if outward else g // 2
    finals = []

    def post(i, index):
        chip, wide = partner(index)
        same = jnp.logical_and(chip == g, wide == z * 2 + c)
        other = jnp.logical_not(same)
        source, target = sources[i].at[index], targets[i].at[slot]
        at = base + i * 4

        def copy():
            return remote(
                source,
                target,
                sender.send_sems.at[at + 2 + index],
                sender.recv_sems.at[at + slot],
                (chip, wide),
            )

        when(
            same,
            lambda: pltpu.make_async_copy(source, target, local_sems.at[local_base + i]).start(),
        )
        when(other, lambda: copy().start())
        finals.append((other, lambda: copy().wait_send()))

    for i in range(len(sources)):
        for index in range(2):
            post(i, index)

    def arrive():
        for i in range(len(sources)):
            for index in range(2):
                chip, wide = origin(index)
                same = jnp.logical_and(chip == g, wide == z * 2 + c)
                target = targets[i].at[index]
                when(
                    same,
                    lambda: pltpu.make_async_copy(
                        sources[i].at[index], target, local_sems.at[local_base + i]
                    ).wait(),
                )
                when(
                    jnp.logical_not(same),
                    lambda: sender.land(target, base + i * 4 + index, (g, z * 2 + 1 - c)),
                )
        for other, final in finals:
            when(other, final)

    return arrive


def hbm():
    return pl.BlockSpec(memory_space=pltpu.HBM)


def vmem():
    return pl.BlockSpec(memory_space=pltpu.VMEM)


def chain(*ticks):
    def act():
        for tick in ticks:
            tick()

    return act


def run_with(ticks, steps, body):
    def act(i, carry):
        body(i)
        for j, tick in enumerate(ticks[:steps]):
            pl.when(i == j)(tick)
        return carry

    lax.fori_loop(0, steps, act, 0)
    for tick in ticks[steps:]:
        tick()


def reduce_kernel(count, moved, splits, *refs):
    grads, sources = refs[:count], refs[count : count + moved]
    refs = refs[count + moved :]
    outs, targets = refs[:count], refs[count : count + moved]
    refs = refs[count + moved :]
    scratch = [refs[i * count : (i + 1) * count] for i in range(6)]
    send_sems, recv_sems, local_sems = refs[6 * count :]
    sender = Sender(send_sems, recv_sems)
    entry_barrier()
    arrive = exchange(
        sources, targets, False, sender, count * REDUCE_SEMS, local_sems, count * 7
    )
    ticks = reduce_ticks(grads, outs, splits, *scratch, sender, local_sems)
    for tick in ticks:
        tick()
    arrive()
    sender.drain(ticks)


def reduce_grads(grads, splits, sources, collective_id):
    count, moved = len(grads), len(sources)
    semaphores = count * REDUCE_SEMS + moved * 4
    shapes = [g.shape[3:] for g in grads]
    scratch = []
    for lead in ((LINE, PLANE), (LINE, PLANE), (LINE,), (LINE, 2), (LINE,), (LINE,)):
        scratch += [pltpu.VMEM(lead + s, BF16) for s in shapes]
    results = pl.pallas_call(
        functools.partial(reduce_kernel, count, moved, splits),
        out_shape=[jax.ShapeDtypeStruct(s, F32) for s in shapes]
        + [jax.ShapeDtypeStruct(s.shape, s.dtype) for s in sources],
        in_specs=[hbm()] * count + [vmem()] * moved,
        out_specs=[vmem()] * count + [hbm()] * moved,
        scratch_shapes=scratch
        + [
            pltpu.SemaphoreType.DMA((semaphores,)),
            pltpu.SemaphoreType.DMA((semaphores,)),
            pltpu.SemaphoreType.DMA((count * 7 + moved,)),
        ],
        compiler_params=pltpu.CompilerParams(
            collective_id=collective_id, has_side_effects=True, vmem_limit_bytes=60 * 1024 * 1024
        ),
        name="reduce_grads",
    )(*grads, *sources)
    return (results[:count], results[count:])


def lane_half(shape, period, half):
    lanes = lax.broadcasted_iota(jnp.int32, shape, 1)
    return lax.rem(lanes, period) < half


def turn(values):
    first = lane_half(values.shape, HEAD_DIM, HEAD_DIM // 2)
    return jnp.where(
        first,
        -pltpu.roll(values, values.shape[1] - HEAD_DIM // 2, 1),
        pltpu.roll(values, HEAD_DIM // 2, 1),
    )


def dot_rows(left, right):
    return lax.dot_general(left, right, (((1,), (0,)), ((), ())), preferred_element_type=F32)


def dot_columns(left, right):
    return lax.dot_general(left, right, (((1,), (1,)), ((), ())), preferred_element_type=F32)


def attend_pair(
    query_ref, key_ref, value_ref, far_key_ref, far_value_ref, seg_ref, seg_near_ref, seg_far_ref, out_ref, norm_ref
):
    rows = query_ref.shape[0]
    first = lane_half((rows, 128), 128, HEAD_DIM)
    tile = 256
    for r in range(rows // tile):
        rs = pl.ds(r * tile, tile)
        query = query_ref[rs, :]
        low_half = first[:tile]
        seg = seg_ref[rs, 0:1]
        near, far = seg == seg_near_ref[...], seg == seg_far_ref[...]
        outs, norms = [], []
        for h in range(2):
            keep = low_half if h == 0 else jnp.logical_not(low_half)
            one = jnp.where(keep, query, jnp.zeros_like(query))
            near_scores = jnp.where(near, dot_columns(one, key_ref[...]), neg_large)
            far_scores = jnp.where(far, dot_columns(one, far_key_ref[...]), neg_large)
            top = jnp.maximum(
                jnp.max(near_scores, axis=1, keepdims=True), jnp.max(far_scores, axis=1, keepdims=True)
            )
            near_expon, far_expon = jnp.exp(near_scores - top), jnp.exp(far_scores - top)
            total = jnp.sum(near_expon, axis=1, keepdims=True) + jnp.sum(
                far_expon, axis=1, keepdims=True
            )
            mixed = dot_rows(near_expon.astype(BF16), value_ref[...]) + dot_rows(
                far_expon.astype(BF16), far_value_ref[...]
            )
            outs.append(mixed / total)
            norms.append(jnp.broadcast_to(top + jnp.log(total), (tile, 128)))
        out_ref[rs, :] = jnp.where(low_half, outs[0], outs[1]).astype(BF16)
        flipped = jnp.transpose(jnp.where(low_half, norms[0], norms[1]))
        norm_ref[0:1, rs] = flipped[0:1]
        norm_ref[1:2, rs] = flipped[HEAD_DIM : HEAD_DIM + 1]


def attend_back_kernel(
    query_ref, key_ref, value_ref, far_key_ref, far_value_ref, grad_ref, norm_ref,
    seg_ref, seg_near_ref, seg_far_ref, cosine_ref, sine_ref, far_cosine_ref, far_sine_ref,
    query_out, key_out, value_out, far_key_out, far_value_out,
):
    rows = query_ref.shape[0]
    low_half = lane_half((rows, 128), 128, HEAD_DIM)
    query, grad = query_ref[...], grad_ref[...]
    seg = seg_ref[...]
    sides = (
        (key_ref[...], value_ref[...], seg_near_ref[...]),
        (far_key_ref[...], far_value_ref[...], seg_far_ref[...]),
    )
    query_grads, key_grads, value_grads = [], [[], []], [[], []]
    for h in range(2):
        keep = low_half if h == 0 else jnp.logical_not(low_half)
        one = jnp.where(keep, query, jnp.zeros_like(query))
        one_grad = jnp.where(keep, grad, jnp.zeros_like(grad))
        norm = norm_ref[0, h : h + 1, :]
        kept = []
        delta = jnp.zeros((1, rows), F32)
        for key, value, seg_key in sides:
            scores = jnp.where(seg_key == seg, dot_columns(key, one), neg_large)
            probs = jnp.exp(scores - norm)
            product = probs * dot_columns(value, one_grad)
            delta = delta + jnp.sum(product, axis=0, keepdims=True)
            kept.append((probs, product))
        total = None
        for i, (key, value, seg_key) in enumerate(sides):
            probs, product = kept[i]
            score_grad = (product - probs * delta).astype(BF16)
            key_grads[i].append(dot_rows(score_grad, query))
            value_grads[i].append(dot_rows(probs.astype(BF16), grad))
            part = lax.dot_general(
                score_grad, key, (((0,), (0,)), ((), ())), preferred_element_type=F32
            )
            total = part if total is None else total + part
        query_grads.append(total)

    def join(pair):
        return jnp.where(low_half, pair[0], pair[1])

    def unturn(value, cosine, sine):
        return value * cosine - turn(value) * sine

    query_grad = join(query_grads) * HEAD_DIM ** (-0.5)
    query_out[...] = unturn(query_grad, cosine_ref[...], sine_ref[...]).astype(BF16)
    key_out[...] = unturn(join(key_grads[0]), cosine_ref[...], sine_ref[...])
    value_out[...] = join(value_grads[0])
    far_key_out[...] = unturn(join(key_grads[1]), far_cosine_ref[...], far_sine_ref[...]).astype(BF16)
    far_value_out[...] = join(value_grads[1]).astype(BF16)


def attend_back(qkv, far_kv, context_grad, norms, seg_row, seg_near, seg_far, tables):
    rows = qkv.shape[0]
    width = HEADS * HEAD_DIM
    pairs = width // 128
    block = lambda at: pl.BlockSpec((rows, 128), lambda h: (0, at + h))
    whole = lambda a: pl.BlockSpec(a.shape, lambda h: (0, 0))
    return pl.pallas_call(
        attend_back_kernel,
        out_shape=[
            jax.ShapeDtypeStruct((rows, width), BF16),
            jax.ShapeDtypeStruct((rows, width), F32),
            jax.ShapeDtypeStruct((rows, width), F32),
            jax.ShapeDtypeStruct((rows, width), BF16),
            jax.ShapeDtypeStruct((rows, width), BF16),
        ],
        grid=(pairs,),
        in_specs=[
            block(0),
            block(pairs),
            block(2 * pairs),
            block(0),
            block(pairs),
            block(0),
            pl.BlockSpec((1, 8, rows), lambda h: (h, 0, 0)),
            whole(seg_row),
            whole(seg_near),
            whole(seg_far),
        ]
        + [whole(t) for t in tables],
        out_specs=[block(0)] * 5,
        compiler_params=pltpu.CompilerParams(vmem_limit_bytes=60 * 1024 * 1024),
        name="attend_back",
    )(qkv, qkv, qkv, far_kv, far_kv, context_grad, norms, seg_row, seg_near, seg_far, *tables)


def plane_first_ticks(a, shard, full, cut, sender, local_sem):
    g, x, y, z, c = place()
    gx, gy, gd = g + 1 - 2 * x, g + 2 - 4 * y, 3 - g
    to_x, to_y, to_core = (gx, z * 2 + c), (gy, z * 2 + c), (g, z * 2 + 1 - c)
    above = (g, jnp.minimum(z + 1, LINE - 1) * 2 + c)
    below = (g, jnp.maximum(z - 1, 0) * 2 + c)
    base, rows = a * GATHER_SEMS, full.shape[3]
    own = full.at[g, z, c]

    def begin():
        sender.do(True, lambda: pltpu.make_async_copy(shard, own, local_sem).start())
        sender.send(True, shard, own, base + 7, to_x)
        sender.send(True, shard, own, base + 14, to_y)

    def middle():
        upper, lower = full.at[gx, z, c, 0:cut], full.at[gy, z, c, cut:rows]
        sender.do(True, lambda: sender.land(full.at[gx, z, c], base + 7, to_x))
        sender.send(True, upper, upper, base + 21, to_y)
        sender.do(True, lambda: sender.land(full.at[gy, z, c], base + 14, to_x))
        sender.send(True, lower, lower, base + 28, to_x)

    def along(k):
        def act():
            if k == 0:
                sender.do(True, lambda: pltpu.make_async_copy(shard, own, local_sem).wait())
                sender.do(True, lambda: sender.land(full.at[gd, z, c, 0:cut], base + 21, to_x))
                sender.do(True, lambda: sender.land(full.at[gd, z, c, cut:rows], base + 28, to_x))
            for slot, zi, cond in near_items(z, k):
                ring = full.at[:, zi, c]
                if k > 0:
                    sender.do(cond, lambda: sender.land(ring, base + slot, to_x))
                if k < LINE - 1:
                    if slot < 4:
                        sender.send(both(cond, z < LINE - 1), ring, ring, base + slot + 1, above)
                    if slot == 0 or slot >= 4:
                        going = 4 if slot == 0 else slot + 1
                        sender.send(both(cond, z > 0), ring, ring, base + going, below)
                sender.send(cond, ring, ring, base + 35 + slot, to_core)

        return act

    return [begin, middle] + [along(k) for k in range(LINE)]


def await_partner(a, full, sender):
    g, x, y, z, c = place()
    for k in range(LINE):
        for slot, zi, cond in near_items(z, k):
            when(
                cond,
                lambda: sender.land(
                    full.at[:, zi, 1 - c], a * GATHER_SEMS + 35 + slot, (g, z * 2 + 1 - c)
                ),
            )


def stretch(packed, vectors, sizes):
    shards = packed.shape[0] // 32
    for row, lane, size, target in vectors:
        pick_rows = lax.broadcasted_iota(jnp.int32, (shards, shards * 32), 0) * 32 + row
        pick = lax.broadcasted_iota(jnp.int32, (shards, shards * 32), 1) == pick_rows
        part = dot_rows(pick.astype(F32).astype(BF16), packed).astype(BF16)
        step = 1024

        def body(i, carry):
            at = pl.multiple_of(i * step, step)
            column = (lax.broadcasted_iota(jnp.int32, (1, step), 1) + i * step).astype(F32)
            shard = jnp.floor((column + 0.5) * (1.0 / size))
            lane_of = (column - shard * size + lane).astype(jnp.int32)
            spread = lax.broadcasted_iota(jnp.int32, (128, step), 0) == lane_of
            value = dot_rows(part, spread.astype(F32).astype(BF16))
            keep = lax.broadcasted_iota(jnp.int32, (shards, step), 0) == shard.astype(jnp.int32)
            target[:, pl.ds(at, step)] = jnp.sum(jnp.where(keep, value, 0.0), axis=0, keepdims=True)
            return carry

        lax.fori_loop(0, shards * size // step, body, 0)


def flat(value):
    return value.reshape(-1, value.shape[-1])


def row_mean(value):
    return jnp.mean(value, axis=1, keepdims=True)


def forward_kernel(*refs):
    shards, refs = refs[:6], refs[6:]
    (tokens, out_cot, embed_cot, segments, cosine, sine), refs = refs[:6], refs[6:]
    (
        project_out, token_out, qkv_out, far_out, context_out, norm, hidden_out, act_out, up_grad_out,
        down_grad_out, result_out, embed_cot_out, branch_grad_out, context_grad_out, first_grad_out,
        sums, seg_out, layer_back, embed_back,
    ), refs = refs[:19], refs[19:]
    fulls, refs = refs[:6], refs[6:]
    (
        token_in, cot_in, embed_cot_in, far_seg, seg_column, vectors, qkv, far, context, normed, rstd,
        hidden_low, act, slope, result_low, embedded, sum_grad, down_grad, branch_grad, context_grad,
        send_sems, recv_sems, local_sems,
    ) = refs
    project_w, embed_w, small_w, output_w, up_w, down_w = fulls
    g, x, y, z, c = place()
    partner = (g, z * 2 + 1 - c)
    rows, width = context.shape
    sender = Sender(send_sems, recv_sems)
    spare = 6 * GATHER_SEMS
    flushed = []

    def flush(source, target, index):
        copy = pltpu.make_async_copy(source, target, local_sems.at[10 + index])
        copy.start()
        flushed.append((source, target, index))

    entry_barrier()
    splits = [s.shape[0] // 2 for s in shards]
    early, unused = gather_ticks(shards, fulls, splits, [(0, 1, 2)], (1, 2), sender, local_sems)
    late, unused = gather_ticks(shards, fulls, splits, [(3,), (4,)], (3, 6), sender, local_sems)
    lines = plane_first_ticks(5, shards[5], down_w, splits[5], sender, local_sems.at[5])
    early[0]()
    sender.post(True, segments, far_seg, spare, partner)
    token_back = exchange([tokens], [token_in], True, sender, spare + 2, local_sems, 6)
    early[1]()
    lines[0]()
    early[2]()
    early[3]()
    lines[1]()
    early[4]()
    late[0]()
    early[5]()
    lines[2]()
    token_back()
    sender.land(far_seg, spare, partner)
    micro = g // 2
    own_ids = segments[pl.ds(micro, 1), :].astype(F32)
    far_ids = far_seg[pl.ds(micro, 1), :].astype(F32)
    ids = jnp.where(lax.rem(g, 2) == c, own_ids, far_ids)
    halves = (ids[:, :rows], ids[:, rows:])
    near_row = jnp.where(c == 0, halves[0], halves[1])
    far_row = jnp.where(c == 0, halves[1], halves[0])
    seg_out[0:1, :] = near_row
    seg_out[1:2, :] = far_row
    seg_column[...] = jnp.transpose(jnp.broadcast_to(near_row, (128, rows)))
    for a in range(3):
        await_partner(a, fulls[a], sender)
    flush(project_w, project_out, 0)
    flush(token_in, token_out, 1)
    vector = lambda i, size: vectors.at[i : i + 1, 0:size]
    stretch(
        flat(small_w[...]),
        (
            (0, 0, 96, vector(0, 3 * width)),
            (1, 0, 128, vector(1, 4 * width)),
            (2, 0, 32, vector(2, width)),
            (2, 32, 32, vector(3, width)),
            (2, 64, 32, vector(4, width)),
            (2, 96, 32, vector(5, width)),
            (3, 0, 32, vector(6, width)),
            (3, 32, 32, vector(7, width)),
        ),
        None,
    )
    tile = 512
    wide = qkv.shape[1] // tile

    def project_tile(i):
        t = lax.rem(i + 2, wide)
        cut = pl.ds(pl.multiple_of(t * tile, tile), tile)
        value = dot_rows(flat(token_in[...]), flat(project_w[:, :, :, :, cut]))
        value = value + vectors[0:1, cut]

        @pl.when(t < 4)
        def _():
            factor = jnp.where(t < 2, HEAD_DIM ** (-0.5), 1.0)
            for j in range(tile // 128):
                part = value[:, j * 128 : (j + 1) * 128]
                part = (part * cosine[...] + turn(part) * sine[...]) * factor
                qkv[:, pl.ds(pl.multiple_of(t * tile + j * 128, 128), 128)] = part.astype(BF16)

        @pl.when(t >= 4)
        def _():
            qkv[:, cut] = value.astype(BF16)

        pl.when(i == 3)(
            lambda: sender.copy(qkv.at[:, width:], far, spare + 1, partner).start()
        )

    run_with(late[1:5] + [chain(late[5], lines[3])], wide, project_tile)
    cot_back = exchange(
        [out_cot, embed_cot], [cot_in, embed_cot_in], True, sender, spare + 6, local_sems, 7
    )
    sender.land(far, spare + 1, partner)
    flush(qkv, qkv_out, 2)
    flush(far, far_out, 3)

    def attend_one(i):
        at = pl.multiple_of(i * 128, 128)
        cut = lambda ref, base: ref.at[:, pl.ds(base + at, 128)]
        attend_pair(
            cut(qkv, 0), cut(qkv, width), cut(qkv, 2 * width), cut(far, 0), cut(far, width),
            seg_column, seg_out.at[0:1], seg_out.at[1:2], cut(context, 0), norm.at[i],
        )

    run_with(late[6:13] + [chain(late[13], lines[4])], width // 128, attend_one)
    flush(context, context_out, 4)
    await_partner(3, output_w, sender)
    half = rows // 2
    output_weight, bias_o = lambda: flat(output_w[...]), vectors[2:3, 0:width]

    def hidden_of(cut):
        return normed[cut, :] * vectors[3:4, 0:width] + vectors[4:5, 0:width]

    def branch_tile(i):
        cut = pl.ds(pl.multiple_of(i * half, half), half)
        resid = dot_rows(context[cut, :], output_weight()) + vectors[2:3, 0:width]
        resid = resid + token_in[i].astype(F32)
        center = resid - row_mean(resid)
        scale = lax.rsqrt(row_mean(center * center) + eps_norm)
        normed[cut, :] = center * scale
        rstd[0, cut, :] = jnp.broadcast_to(scale, (half, 128))
        hidden_low[cut, :] = hidden_of(cut).astype(BF16)

    run_with([], 2, branch_tile)
    flush(hidden_low, hidden_out, 5)
    await_partner(4, up_w, sender)

    def up_tile(j):
        cut = pl.ds(pl.multiple_of(j * tile, tile), tile)
        value = dot_rows(hidden_low[...], flat(up_w[:, :, :, :, cut])) + vectors[1:2, cut]
        below = 0.5 + 0.5 * lax.erf(value * 0.7071067811865476)
        density = jnp.exp(-0.5 * value * value) * 0.3989422804014327
        act[:, cut] = (value * below).astype(BF16)
        slope[:, cut] = (below + value * density).astype(BF16)

    ff = act.shape[1]
    run_with([lambda: None, lambda: None, lines[5]], ff // tile, up_tile)
    flush(act, act_out, 6)
    await_partner(5, down_w, sender)
    cot_back()
    flush(embed_cot_in, embed_cot_out, 7)
    sums[...] = jnp.zeros_like(sums)

    def add_sum(row, value):
        sums[row : row + 1, 0:width] += jnp.sum(value, axis=0, keepdims=True)

    def norm_back(grads, row_normed, scale, gain):
        scaled = grads * gain
        return scale * (
            scaled - row_mean(scaled) - row_normed * row_mean(scaled * row_normed)
        )

    def down_tile(i):
        cut = pl.ds(pl.multiple_of(i * half, half), half)
        gain, shift = vectors[6:7, 0:width], vectors[7:8, 0:width]
        resid = dot_rows(act[cut, :], flat(down_w[...])) + vectors[5:6, 0:width]
        resid = resid + hidden_of(cut)
        center = resid - row_mean(resid)
        scale = lax.rsqrt(row_mean(center * center) + eps_norm)
        row_normed = center * scale
        low = (row_normed * gain + shift).astype(BF16)
        result_low[i] = low
        embed_full = flat(embed_w[...])
        embedded[i] = dot_rows(low, embed_full).astype(BF16)
        grads = cot_in[i].astype(F32) + dot_columns(embed_cot_in[i], embed_full)
        add_sum(6, grads * row_normed)
        add_sum(7, grads)
        total = norm_back(grads, row_normed, scale, gain)
        sum_grad[cut, :] = total
        low = total.astype(BF16)
        down_grad[cut, :] = low
        add_sum(5, low.astype(F32))

    run_with([], 2, down_tile)
    results_back = exchange(
        [result_low, embedded], [layer_back, embed_back], False, sender, spare + 14, local_sems, 1
    )
    flush(result_low, result_out, 8)
    flush(down_grad, down_grad_out, 9)

    def up_grad_tile(j):
        cut = pl.ds(pl.multiple_of(j * tile, tile), tile)
        part = flat(down_w[j // 2, pl.ds(lax.rem(j, 2) * 2, 2)])
        value = (dot_columns(down_grad[...], part) * slope[:, cut].astype(F32)).astype(BF16)
        slope[:, cut] = value
        sums[1:2, cut] = jnp.sum(value.astype(F32), axis=0, keepdims=True)

    run_with([], ff // tile, up_grad_tile)
    flush(slope, up_grad_out, 10)

    def first_tile(i):
        cut = pl.ds(pl.multiple_of(i * half, half), half)
        grads = sum_grad[cut, :] + dot_columns(slope[cut, :], flat(up_w[...]))
        row_normed = normed[cut, :]
        add_sum(3, grads * row_normed)
        add_sum(4, grads)
        total = norm_back(grads, row_normed, rstd[0, cut, 0:1], vectors[3:4, 0:width])
        sum_grad[cut, :] = total
        low = total.astype(BF16)
        branch_grad[cut, :] = low
        add_sum(2, low.astype(F32))
        context_grad[cut, :] = dot_columns(low, output_weight()).astype(BF16)

    run_with([], 2, first_tile)
    flush(sum_grad, first_grad_out, 11)
    flush(branch_grad, branch_grad_out, 12)
    flush(context_grad, context_grad_out, 13)
    results_back()
    sender.drain(early + late + lines)
    sender.copy(qkv.at[:, width:], far, spare + 1, partner).wait_send()
    for source, target, index in flushed:
        pltpu.make_async_copy(source, target, local_sems.at[10 + index]).wait()


def forward(shards, sources, segments, tables, ff):
    piece, width = sources[0].shape[1:]
    lanes = sources[2].shape[2]
    rows = 2 * piece
    semaphores = 6 * GATHER_SEMS + 32
    fulls = [(PLANE, LINE, 2) + s.shape for s in shards]
    shape = jax.ShapeDtypeStruct
    outs = [
        shape(fulls[0], BF16),
        shape((2, piece, width), BF16),
        shape((rows, 3 * width), BF16),
        shape((rows, 2 * width), BF16),
        shape((rows, width), BF16),
        shape((width // 128, 8, rows), F32),
        shape((rows, width), BF16),
        shape((rows, ff), BF16),
        shape((rows, ff), BF16),
        shape((rows, width), BF16),
        shape((2, piece, width), BF16),
        shape((2, piece, lanes), BF16),
        shape((rows, width), BF16),
        shape((rows, width), BF16),
        shape((rows, width), F32),
        shape((8, ff), F32),
        shape((8, rows), F32),
        shape((2, piece, width), BF16),
        shape((2, piece, lanes), BF16),
    ]
    spaces = [hbm()] * len(outs)
    for i in (5, 15, 16):
        spaces[i] = vmem()
    scratch = [pltpu.VMEM(f, BF16) for f in fulls] + [
        pltpu.VMEM((2, piece, width), BF16),
        pltpu.VMEM((2, piece, width), BF16),
        pltpu.VMEM((2, piece, lanes), BF16),
        pltpu.VMEM(segments.shape, jnp.int32),
        pltpu.VMEM((rows, 128), F32),
        pltpu.VMEM((8, ff), F32),
        pltpu.VMEM((rows, 3 * width), BF16),
        pltpu.VMEM((rows, 2 * width), BF16),
        pltpu.VMEM((rows, width), BF16),
        pltpu.VMEM((rows, width), F32),
        pltpu.VMEM((1, rows, 128), F32),
        pltpu.VMEM((rows, width), BF16),
        pltpu.VMEM((rows, ff), BF16),
        pltpu.VMEM((rows, ff), BF16),
        pltpu.VMEM((2, piece, width), BF16),
        pltpu.VMEM((2, piece, lanes), BF16),
        pltpu.VMEM((rows, width), F32),
        pltpu.VMEM((rows, width), BF16),
        pltpu.VMEM((rows, width), BF16),
        pltpu.VMEM((rows, width), BF16),
        pltpu.SemaphoreType.DMA((semaphores,)),
        pltpu.SemaphoreType.DMA((semaphores,)),
        pltpu.SemaphoreType.DMA((24,)),
    ]
    return pl.pallas_call(
        forward_kernel,
        out_shape=outs,
        in_specs=[hbm()] * 9 + [vmem()] * 3,
        out_specs=spaces,
        scratch_shapes=scratch,
        compiler_params=pltpu.CompilerParams(
            collective_id=1, has_side_effects=True, vmem_limit_bytes=67043328
        ),
        name="forward",
    )(*shards, *sources, segments, *tables)


def pair_tables(positions):
    cosine, sine = rotary_tables(positions)
    return (jnp.concatenate([cosine, cosine], axis=1), jnp.concatenate([sine, sine], axis=1))


def swap_cores(value, wide_size):
    pairs = [(w, w + 1 - 2 * (w % 2)) for w in range(wide_size)]
    return lax.ppermute(value, "wide", pairs)


def plane_device(
    tokens,
    segment_ids,
    project_weight,
    project_bias,
    output_weight,
    output_bias,
    first_gain,
    first_shift,
    up_weight,
    up_bias,
    down_weight,
    down_bias,
    second_gain,
    second_shift,
    embed_weight,
    out_cotangent,
    embed_cotangent,
):
    width = HEADS * HEAD_DIM
    piece = tokens.shape[2]
    rows = 2 * piece
    wide_size = 2 * LINE
    group = lax.axis_index("group")
    core = lax.rem(lax.axis_index("wide"), 2)
    devices = PLANE * LINE * 2
    lanes = embed_weight.shape[1]
    embed_rows = embed_weight.shape[0]
    small = None
    for row, lane, vector in (
        (0, 0, project_bias),
        (1, 0, up_bias),
        (2, 0, output_bias),
        (2, 32, first_gain),
        (2, 64, first_shift),
        (2, 96, down_bias),
        (3, 0, second_gain),
        (3, 32, second_shift),
    ):
        size = vector.shape[0]
        part = jnp.pad(
            vector.astype(F32)[None, :], ((row, 31 - row), (lane, lanes - lane - size))
        )
        small = part if small is None else small + part
    place_of = jnp.arange(rows)
    cosine, sine = pair_tables((core * rows + place_of).astype(F32))
    far_cosine, far_sine = pair_tables(((1 - core) * rows + place_of).astype(F32))
    (
        project_full, token_rows, qkv, far_kv, context_low, norms, hidden_low, act_low, up_grad,
        down_grad, result_low, embed_cot, branch_grad, context_grad, first_grad, sums, ids,
        layer_out, embed_out,
    ) = forward(
        [project_weight, embed_weight, small.astype(BF16), output_weight, up_weight, down_weight],
        [tokens[:, 0], out_cotangent[:, 0], embed_cotangent[:, 0]],
        segment_ids[:, 0],
        (cosine, sine),
        up_weight.shape[1],
    )
    project_full = project_full.reshape(width, 3 * width)
    token_rows = token_rows.reshape(rows, width)
    result_low = result_low.reshape(rows, width)
    embed_cot = embed_cot.reshape(rows, lanes)
    near_ids, far_ids = ids[0], ids[1]
    down_weight_grad = contract_rows(act_low, down_grad)
    up_weight_grad = contract_rows(hidden_low, up_grad)
    output_weight_grad = contract_rows(context_low, branch_grad)
    embed_weight_grad = contract_rows(result_low, embed_cot)
    query_back, key_near, value_near, key_far, value_far = attend_back(
        qkv,
        far_kv,
        context_grad,
        norms,
        near_ids[None, :],
        near_ids[:, None],
        far_ids[:, None],
        (cosine, sine, far_cosine, far_sine),
    )
    key_back = (key_near + swap_cores(key_far, wide_size).astype(F32)).astype(BF16)
    value_back = (value_near + swap_cores(value_far, wide_size).astype(F32)).astype(BF16)
    projected_grad = jnp.concatenate([query_back, key_back, value_back], axis=1)
    project_bias_grad = jnp.sum(projected_grad.astype(F32), axis=0)
    project_weight_grad = contract_rows(token_rows, projected_grad)
    token_grad = (first_grad + times_transpose(projected_grad, project_full)).astype(BF16)

    shares = [
        v.reshape(devices, -1)
        for v in (
            project_bias_grad,
            sums[2, :width],
            sums[3, :width],
            sums[4, :width],
            sums[1],
            sums[5, :width],
            sums[6, :width],
            sums[7, :width],
        )
    ]
    sizes = [v.shape[1] for v in shares]
    pad = SMALL_ROWS * lanes - sum(sizes)
    small_grads = jnp.pad(jnp.concatenate(shares, axis=1), ((0, 0), (0, pad)))
    small_grads = small_grads.reshape(devices, SMALL_ROWS, lanes)
    embed_grads = jnp.concatenate(
        [embed_weight_grad.reshape(devices, embed_rows, lanes), small_grads], axis=1
    )

    def spread(full):
        return full.astype(BF16).reshape(PLANE, LINE, 2, -1, full.shape[-1])

    grads = [
        spread(g)
        for g in (
            down_weight_grad,
            up_weight_grad,
            output_weight_grad,
            project_weight_grad,
            embed_grads,
        )
    ]
    splits = [g.shape[3] // 2 for g in grads[:4]] + [embed_rows]
    outs, moved = reduce_grads(
        grads,
        splits,
        [token_grad.reshape(2, piece, width)],
        3,
    )
    down_out, up_out, output_out, project_out, small_out = outs
    vector_out = small_out[embed_rows:].reshape(-1)
    parts, start = [], 0
    for size in sizes:
        parts.append(vector_out[start : start + size])
        start += size
    return (
        layer_out[:, None],
        embed_out[:, None],
        moved[0][:, None].astype(F32),
        project_out,
        parts[0],
        output_out,
        parts[1],
        parts[2],
        parts[3],
        up_out,
        parts[4],
        down_out,
        parts[5],
        parts[6],
        parts[7],
        small_out[:embed_rows],
    )


def choose_device(mesh):
    if mesh.shape["group"] == PLANE and mesh.shape["wide"] == 2 * LINE:
        return plane_device
    return general_device


def solution(mesh):
    in_specs = (
        P(None, "wide", "group", None),
        P(None, "wide", None),
        P(("group", "wide"), None),
        P(("group", "wide")),
        P(("group", "wide"), None),
        P(("group", "wide")),
        P(("group", "wide")),
        P(("group", "wide")),
        P(("group", "wide"), None),
        P(("group", "wide")),
        P(("group", "wide"), None),
        P(("group", "wide")),
        P(("group", "wide")),
        P(("group", "wide")),
        P(("group", "wide"), None),
        P(None, "wide", "group", None),
        P(None, "wide", "group", None),
    )
    out_specs = (
        P(None, "wide", "group", None),
        P(None, "wide", "group", None),
        P(None, "wide", "group", None),
        P(("group", "wide"), None),
        P(("group", "wide")),
        P(("group", "wide"), None),
        P(("group", "wide")),
        P(("group", "wide")),
        P(("group", "wide")),
        P(("group", "wide"), None),
        P(("group", "wide")),
        P(("group", "wide"), None),
        P(("group", "wide")),
        P(("group", "wide")),
        P(("group", "wide")),
        P(("group", "wide"), None),
    )
    return jax.shard_map(
        choose_device(mesh), mesh=mesh, in_specs=in_specs, out_specs=out_specs, check_vma=False
    )
```

```python
import functools

import jax
import jax.numpy as jnp
from jax import lax
from jax.experimental import pallas as pl
from jax.experimental.pallas import tpu as pltpu
from jax.sharding import PartitionSpec as P

HEADS = 16
HEAD_DIM = 64


eps_norm = 1e-05
neg_large = -1e30


def rotary_tables(positions):
    half_dim = HEAD_DIM // 2
    frequency = 10000.0 ** (-jnp.arange(half_dim, dtype=jnp.float32) * (2.0 / HEAD_DIM))
    angles = positions[:, None] * frequency[None, :]
    angles = jnp.concatenate([angles, angles], axis=1)
    return (jnp.cos(angles), jnp.sin(angles))


def rotate(values, cosine_table, sine_table):
    half_dim = HEAD_DIM // 2
    swapped = jnp.concatenate([-values[..., half_dim:], values[..., :half_dim]], axis=-1)
    return values * cosine_table[:, None, :] + swapped * sine_table[:, None, :]


def unrotate(grads, cosine_table, sine_table):
    half_dim = HEAD_DIM // 2
    scaled = grads * sine_table[:, None, :]
    swapped = jnp.concatenate([scaled[..., half_dim:], -scaled[..., :half_dim]], axis=-1)
    return grads * cosine_table[:, None, :] + swapped


def norm_forward(resid, gain, shift):
    center = resid - jnp.mean(resid, axis=-1, keepdims=True)
    spread = jnp.mean(center * center, axis=-1, keepdims=True)
    rstd_rows = lax.rsqrt(spread + eps_norm)
    normed = center * rstd_rows
    return (normed * gain + shift, normed, rstd_rows)


def norm_backward(grads, normed, rstd_rows, gain):
    scaled = grads * gain
    resid_grad = rstd_rows * (
        scaled
        - jnp.mean(scaled, axis=-1, keepdims=True)
        - normed * jnp.mean(scaled * normed, axis=-1, keepdims=True)
    )
    return (resid_grad, jnp.sum(grads * normed, axis=0), jnp.sum(grads, axis=0))


def contract_rows(left, right):
    return lax.dot_general(
        left, right, (((0,), (0,)), ((), ())), preferred_element_type=jnp.float32
    )


def times_transpose(left, right):
    return lax.dot_general(
        left, right, (((1,), (1,)), ((), ())), preferred_element_type=jnp.float32
    )


def gelu_slope(value):
    normal_cdf = 0.5 * (1.0 + lax.erf(value * 0.7071067811865476))
    density = jnp.exp(-0.5 * value * value) * 0.3989422804014327
    return normal_cdf + value * density


def key_blocks(kv_rows, seg_all):
    seq_len = kv_rows.shape[0]
    block_rows = min(512, seq_len)
    count = seq_len // block_rows
    return (
        kv_rows.reshape(count, block_rows, 2, HEADS, HEAD_DIM),
        seg_all.reshape(count, block_rows),
    )


def block_scores(queries, key_block, same):
    scores = jnp.einsum("qhd,khd->hqk", queries, key_block, preferred_element_type=jnp.float32)
    scores = scores * HEAD_DIM ** (-0.5)
    return jnp.where(same[None], scores, neg_large)


def attention_forward(queries, blocks, seg_blocks, seg_local):
    length = queries.shape[0]

    def norm_step(carry, pieces):
        kv_block, seg_block = pieces
        same = seg_local[:, None] == seg_block[None, :]

        def norm_update(running):
            run_max, run_sum = running
            scores = block_scores(queries, kv_block[:, 0], same)
            new_max = jnp.maximum(run_max, jnp.max(scores, axis=-1))
            new_sum = run_sum * jnp.exp(run_max - new_max) + jnp.sum(
                jnp.exp(scores - new_max[..., None]), axis=-1
            )
            return (new_max, new_sum)

        def norm_unchanged(running):
            return running

        return (lax.cond(jnp.any(same), norm_update, norm_unchanged, carry), None)

    start = (
        jnp.full((HEADS, length), neg_large, jnp.float32),
        jnp.zeros((HEADS, length), jnp.float32),
    )
    (run_max, run_sum), unused = lax.scan(norm_step, start, (blocks, seg_blocks))
    log_norm = run_max + jnp.log(run_sum)

    def value_step(total, pieces):
        kv_block, seg_block = pieces
        same = seg_local[:, None] == seg_block[None, :]

        def value_update(running):
            scores = block_scores(queries, kv_block[:, 0], same)
            weights = jnp.exp(scores - log_norm[..., None]).astype(jnp.bfloat16)
            return running + jnp.einsum(
                "hqk,khd->qhd", weights, kv_block[:, 1], preferred_element_type=jnp.float32
            )

        def value_unchanged(running):
            return running

        return (lax.cond(jnp.any(same), value_update, value_unchanged, total), None)

    context, unused = lax.scan(
        value_step, jnp.zeros(queries.shape, jnp.float32), (blocks, seg_blocks)
    )
    return (context, log_norm)


def attention_backward(queries, blocks, seg_blocks, seg_local, log_norm, context_grad, delta):

    def grad_step(query_grad, pieces):
        kv_block, seg_block = pieces
        same = seg_local[:, None] == seg_block[None, :]

        def work(running):
            scores = block_scores(queries, kv_block[:, 0], same)
            probs = jnp.exp(scores - log_norm[..., None])
            prob_grad = jnp.einsum(
                "qhd,khd->hqk", context_grad, kv_block[:, 1], preferred_element_type=jnp.float32
            )
            score_grad = (probs * (prob_grad - delta[..., None])).astype(jnp.bfloat16)
            running = running + jnp.einsum(
                "hqk,khd->qhd", score_grad, kv_block[:, 0], preferred_element_type=jnp.float32
            ) * HEAD_DIM ** (-0.5)
            prob_low = probs.astype(jnp.bfloat16)
            key_grad = jnp.einsum(
                "hqk,qhd->khd", score_grad, queries, preferred_element_type=jnp.float32
            ) * HEAD_DIM ** (-0.5)
            value_grad = jnp.einsum(
                "hqk,qhd->khd", prob_low, context_grad, preferred_element_type=jnp.float32
            )
            return (running, jnp.stack([key_grad, value_grad], axis=1))

        def skipped(running):
            return (running, jnp.zeros(kv_block.shape, jnp.float32))

        return lax.cond(jnp.any(same), work, skipped, query_grad)

    query_grad, kv_grad = lax.scan(
        grad_step, jnp.zeros(queries.shape, jnp.float32), (blocks, seg_blocks)
    )
    return (query_grad, kv_grad.reshape(-1, 2 * HEADS * HEAD_DIM))


def general_device(
    tokens,
    segment_ids,
    project_weight,
    project_bias,
    output_weight,
    output_bias,
    first_gain,
    first_shift,
    up_weight,
    up_bias,
    down_weight,
    down_bias,
    second_gain,
    second_shift,
    embed_weight,
    out_cotangent,
    embed_cotangent,
):
    shards = (
        project_weight,
        project_bias,
        output_weight,
        output_bias,
        first_gain,
        first_shift,
        up_weight,
        up_bias,
        down_weight,
        down_bias,
        second_gain,
        second_shift,
        embed_weight,
    )
    length = tokens.shape[2]
    width = HEADS * HEAD_DIM
    head_shape = (length, HEADS, HEAD_DIM)
    place = lax.axis_index("group")
    positions = (place * length + jnp.arange(length)).astype(jnp.float32)
    cosine_table, sine_table = rotary_tables(positions)
    grad_total = None
    results = []
    embeddings = []
    input_grads = []
    for micro_index in range(tokens.shape[0]):
        params = (
            lax.all_gather(shards[0], ("group", "wide"), axis=0, tiled=True),
            lax.all_gather(shards[1], ("group", "wide"), axis=0, tiled=True),
            lax.all_gather(shards[2], ("group", "wide"), axis=0, tiled=True),
            lax.all_gather(shards[3], ("group", "wide"), axis=0, tiled=True),
            lax.all_gather(shards[4], ("group", "wide"), axis=0, tiled=True),
            lax.all_gather(shards[5], ("group", "wide"), axis=0, tiled=True),
            lax.all_gather(shards[6], ("group", "wide"), axis=0, tiled=True),
            lax.all_gather(shards[7], ("group", "wide"), axis=0, tiled=True),
            lax.all_gather(shards[8], ("group", "wide"), axis=0, tiled=True),
            lax.all_gather(shards[9], ("group", "wide"), axis=0, tiled=True),
            lax.all_gather(shards[10], ("group", "wide"), axis=0, tiled=True),
            lax.all_gather(shards[11], ("group", "wide"), axis=0, tiled=True),
            lax.all_gather(shards[12], ("group", "wide"), axis=0, tiled=True),
        )
        seg_all = segment_ids[micro_index, 0]
        seg_local = lax.dynamic_slice_in_dim(seg_all, place * length, length)
        token_low = tokens[micro_index, 0]
        token_wide = token_low.astype(jnp.float32)
        projected = jnp.dot(token_low, params[0], preferred_element_type=jnp.float32) + params[
            1
        ].astype(jnp.float32)
        queries = rotate(projected[:, :width].reshape(head_shape), cosine_table, sine_table).astype(
            jnp.bfloat16
        )
        key_rows = rotate(
            projected[:, width : 2 * width].reshape(head_shape), cosine_table, sine_table
        ).astype(jnp.bfloat16)
        value_rows = projected[:, 2 * width :].astype(jnp.bfloat16)
        local_kv = jnp.concatenate([key_rows.reshape(length, width), value_rows], axis=1)
        kv_all = lax.all_gather(local_kv, "group", axis=0, tiled=True)
        blocks, seg_blocks = key_blocks(kv_all, seg_all)
        context, log_norm = attention_forward(queries, blocks, seg_blocks, seg_local)
        context_low = context.reshape(length, width).astype(jnp.bfloat16)
        branch = jnp.dot(context_low, params[2], preferred_element_type=jnp.float32) + params[
            3
        ].astype(jnp.float32)
        first_gain_wide = params[4].astype(jnp.float32)
        hidden, first_normed, first_rstd = norm_forward(
            token_wide + branch, first_gain_wide, params[5].astype(jnp.float32)
        )
        hidden_low = hidden.astype(jnp.bfloat16)
        up_value = jnp.dot(hidden_low, params[6], preferred_element_type=jnp.float32) + params[
            7
        ].astype(jnp.float32)
        act_low = jax.nn.gelu(up_value, approximate=False).astype(jnp.bfloat16)
        down_value = jnp.dot(act_low, params[8], preferred_element_type=jnp.float32) + params[
            9
        ].astype(jnp.float32)
        second_gain_wide = params[10].astype(jnp.float32)
        result, second_normed, second_rstd = norm_forward(
            hidden + down_value, second_gain_wide, params[11].astype(jnp.float32)
        )
        result_low = result.astype(jnp.bfloat16)
        embedded = jnp.dot(result_low, params[12], preferred_element_type=jnp.float32)
        results.append(result_low)
        embeddings.append(embedded.astype(jnp.bfloat16))
        params = (
            lax.all_gather(shards[0], ("group", "wide"), axis=0, tiled=True),
            lax.all_gather(shards[1], ("group", "wide"), axis=0, tiled=True),
            lax.all_gather(shards[2], ("group", "wide"), axis=0, tiled=True),
            lax.all_gather(shards[3], ("group", "wide"), axis=0, tiled=True),
            lax.all_gather(shards[4], ("group", "wide"), axis=0, tiled=True),
            lax.all_gather(shards[5], ("group", "wide"), axis=0, tiled=True),
            lax.all_gather(shards[6], ("group", "wide"), axis=0, tiled=True),
            lax.all_gather(shards[7], ("group", "wide"), axis=0, tiled=True),
            lax.all_gather(shards[8], ("group", "wide"), axis=0, tiled=True),
            lax.all_gather(shards[9], ("group", "wide"), axis=0, tiled=True),
            lax.all_gather(shards[10], ("group", "wide"), axis=0, tiled=True),
            lax.all_gather(shards[11], ("group", "wide"), axis=0, tiled=True),
            lax.all_gather(shards[12], ("group", "wide"), axis=0, tiled=True),
        )
        embed_cot = embed_cotangent[micro_index, 0]
        result_grad = out_cotangent[micro_index, 0].astype(jnp.float32) + times_transpose(
            embed_cot, params[12]
        )
        embed_weight_grad = contract_rows(result_low, embed_cot)
        sum_grad, second_gain_grad, second_shift_grad = norm_backward(
            result_grad, second_normed, second_rstd, second_gain_wide
        )
        down_grad = sum_grad.astype(jnp.bfloat16)
        down_bias_grad = jnp.sum(down_grad.astype(jnp.float32), axis=0)
        down_weight_grad = contract_rows(act_low, down_grad)
        up_grad = (times_transpose(down_grad, params[8]) * gelu_slope(up_value)).astype(
            jnp.bfloat16
        )
        up_bias_grad = jnp.sum(up_grad.astype(jnp.float32), axis=0)
        up_weight_grad = contract_rows(hidden_low, up_grad)
        hidden_grad = sum_grad + times_transpose(up_grad, params[6])
        first_grad, first_gain_grad, first_shift_grad = norm_backward(
            hidden_grad, first_normed, first_rstd, first_gain_wide
        )
        branch_grad = first_grad.astype(jnp.bfloat16)
        output_bias_grad = jnp.sum(branch_grad.astype(jnp.float32), axis=0)
        output_weight_grad = contract_rows(context_low, branch_grad)
        context_grad = (
            times_transpose(branch_grad, params[2]).astype(jnp.bfloat16).reshape(head_shape)
        )
        delta = jnp.transpose(jnp.sum(context_grad.astype(jnp.float32) * context, axis=-1))
        kv_again = lax.all_gather(local_kv, "group", axis=0, tiled=True)
        blocks, seg_blocks = key_blocks(kv_again, seg_all)
        query_grad, kv_partial = attention_backward(
            queries, blocks, seg_blocks, seg_local, log_norm, context_grad, delta
        )
        kv_grad = lax.psum_scatter(
            kv_partial.astype(jnp.bfloat16), "group", scatter_dimension=0, tiled=True
        ).astype(jnp.float32)
        key_part = kv_grad[:, :width].reshape(head_shape)
        value_part = kv_grad[:, width:]
        query_back = unrotate(query_grad, cosine_table, sine_table).reshape(length, width)
        key_back = unrotate(key_part, cosine_table, sine_table).reshape(length, width)
        projected_grad = jnp.concatenate([query_back, key_back, value_part], axis=1).astype(
            jnp.bfloat16
        )
        project_bias_grad = jnp.sum(projected_grad.astype(jnp.float32), axis=0)
        project_weight_grad = contract_rows(token_low, projected_grad)
        input_grads.append(first_grad + times_transpose(projected_grad, params[0]))
        local_grads = (
            project_weight_grad,
            project_bias_grad,
            output_weight_grad,
            output_bias_grad,
            first_gain_grad,
            first_shift_grad,
            up_weight_grad,
            up_bias_grad,
            down_weight_grad,
            down_bias_grad,
            second_gain_grad,
            second_shift_grad,
            embed_weight_grad,
        )
        summed = (
            lax.psum_scatter(local_grads[0], ("group", "wide"), scatter_dimension=0, tiled=True),
            lax.psum_scatter(local_grads[1], ("group", "wide"), scatter_dimension=0, tiled=True),
            lax.psum_scatter(local_grads[2], ("group", "wide"), scatter_dimension=0, tiled=True),
            lax.psum_scatter(local_grads[3], ("group", "wide"), scatter_dimension=0, tiled=True),
            lax.psum_scatter(local_grads[4], ("group", "wide"), scatter_dimension=0, tiled=True),
            lax.psum_scatter(local_grads[5], ("group", "wide"), scatter_dimension=0, tiled=True),
            lax.psum_scatter(local_grads[6], ("group", "wide"), scatter_dimension=0, tiled=True),
            lax.psum_scatter(local_grads[7], ("group", "wide"), scatter_dimension=0, tiled=True),
            lax.psum_scatter(local_grads[8], ("group", "wide"), scatter_dimension=0, tiled=True),
            lax.psum_scatter(local_grads[9], ("group", "wide"), scatter_dimension=0, tiled=True),
            lax.psum_scatter(local_grads[10], ("group", "wide"), scatter_dimension=0, tiled=True),
            lax.psum_scatter(local_grads[11], ("group", "wide"), scatter_dimension=0, tiled=True),
            lax.psum_scatter(local_grads[12], ("group", "wide"), scatter_dimension=0, tiled=True),
        )
        grad_total = (
            summed
            if grad_total is None
            else tuple((total + part for total, part in zip(grad_total, summed)))
        )
    layer_out = jnp.stack(results)[:, None]
    embed_out = jnp.stack(embeddings)[:, None]
    token_grad = jnp.stack(input_grads)[:, None]
    return (
        layer_out,
        embed_out,
        token_grad,
        grad_total[0],
        grad_total[1],
        grad_total[2],
        grad_total[3],
        grad_total[4],
        grad_total[5],
        grad_total[6],
        grad_total[7],
        grad_total[8],
        grad_total[9],
        grad_total[10],
        grad_total[11],
        grad_total[12],
    )


MESH = pl.DeviceIdType.MESH
F32 = jnp.float32
BF16 = jnp.bfloat16
PLANE = 4
LINE = 4
GATHER_SEMS = 42
REDUCE_SEMS = 56
MAIN_AHEAD = (1, 3, 5)
LATE_AHEAD = (1, 2, 3)


def place():
    group = lax.axis_index("group")
    wide = lax.axis_index("wide")
    return (group, lax.rem(group, 2), group // 2, wide // 2, lax.rem(wide, 2))


def when(cond, act):
    if cond is True:
        act()
    else:
        pl.when(cond)(act)


def both(left, right):
    return right if left is True else jnp.logical_and(left, right)


def remote(src, dst, send_sem, recv_sem, device):
    return pltpu.make_async_remote_copy(
        src_ref=src,
        dst_ref=dst,
        send_sem=send_sem,
        recv_sem=recv_sem,
        device_id=device,
        device_id_type=MESH,
    )


def entry_barrier():
    g, x, y, z, c = place()
    devices = []
    for step in range(1, 8):
        other = lax.rem(g * 2 + c + step, 8)
        devices.append((other // 2, z * 2 + lax.rem(other, 2)))
    devices.append((g, lax.rem(z + 1, LINE) * 2 + c))
    devices.append((g, lax.rem(z + LINE - 1, LINE) * 2 + c))
    barrier = pltpu.get_barrier_semaphore()
    for device in devices:
        pl.semaphore_signal(barrier, inc=1, device_id=device, device_id_type=MESH)
    pl.semaphore_wait(barrier, len(devices))


class Sender:
    def __init__(self, send_sems, recv_sems):
        self.send_sems, self.recv_sems = send_sems, recv_sems
        self.pending, self.draining = [], False

    def copy(self, src, dst, index, device):
        return remote(src, dst, self.send_sems.at[index], self.recv_sems.at[index], device)

    def send(self, cond, src, dst, index, device):
        copy = self.copy(src, dst, index, device)
        when(cond, copy.wait_send if self.draining else copy.start)

    def post(self, cond, src, dst, index, device):
        self.send(cond, src, dst, index, device)
        self.pending.append((cond, src, dst, index, device))

    def land(self, ref, index, device):
        self.copy(ref, ref, index, device).wait_recv()

    def do(self, cond, act):
        if not self.draining:
            when(cond, act)

    def drain(self, ticks):
        self.draining = True
        for tick in ticks:
            tick()
        for call in self.pending:
            self.send(*call)


def near_items(z, distance):
    if distance == 0:
        return [(0, z, True)]
    return [
        (distance, jnp.maximum(z - distance, 0), z >= distance),
        (3 + distance, jnp.minimum(z + distance, LINE - 1), z + distance < LINE),
    ]


def gather_ticks(shards, fulls, splits, chunks, ahead, sender, local_sems):
    g, x, y, z, c = place()
    gx, gy, gd = g + 1 - 2 * x, g + 2 - 4 * y, 3 - g
    to_x, to_y, to_core = (gx, z * 2 + c), (gy, z * 2 + c), (g, z * 2 + 1 - c)
    above = (g, jnp.minimum(z + 1, LINE - 1) * 2 + c)
    below = (g, jnp.maximum(z - 1, 0) * 2 + c)

    def first(a, k):
        base = a * GATHER_SEMS
        for slot, zi, cond in near_items(z, k):
            region = fulls[a].at[g, zi, c]
            if k == 0:
                sender.do(
                    True, lambda: pltpu.make_async_copy(shards[a], region, local_sems.at[a]).start()
                )
                source = shards[a]
                sender.send(z < LINE - 1, source, region, base + 1, above)
                sender.send(z > 0, source, region, base + 4, below)
            else:
                source = region
                sender.do(cond, lambda: sender.land(region, base + slot, to_x))
                if k < LINE - 1:
                    if slot < 4:
                        sender.send(both(cond, z < LINE - 1), source, region, base + slot + 1, above)
                    else:
                        sender.send(both(cond, z > 0), source, region, base + slot + 1, below)
            sender.send(cond, source, region, base + 7 + slot, to_x)
            sender.send(cond, source, region, base + 14 + slot, to_y)

    def second(a, k):
        base, cut, rows = a * GATHER_SEMS, splits[a], fulls[a].shape[3]
        for slot, zi, cond in near_items(z, k):
            sender.do(cond, lambda: sender.land(fulls[a].at[gx, zi, c], base + 7 + slot, to_x))
            upper = fulls[a].at[gx, zi, c, 0:cut]
            sender.send(cond, upper, upper, base + 21 + slot, to_y)
            sender.do(cond, lambda: sender.land(fulls[a].at[gy, zi, c], base + 14 + slot, to_x))
            lower = fulls[a].at[gy, zi, c, cut:rows]
            sender.send(cond, lower, lower, base + 28 + slot, to_x)

    def third(a, k):
        base, cut, rows = a * GATHER_SEMS, splits[a], fulls[a].shape[3]
        if k == 0:
            sender.do(
                True,
                lambda: pltpu.make_async_copy(
                    shards[a], fulls[a].at[g, z, c], local_sems.at[a]
                ).wait(),
            )
        for slot, zi, cond in near_items(z, k):
            sender.do(cond, lambda: sender.land(fulls[a].at[gd, zi, c, 0:cut], base + 21 + slot, to_x))
            sender.do(cond, lambda: sender.land(fulls[a].at[gd, zi, c, cut:rows], base + 28 + slot, to_x))
            ring = fulls[a].at[:, zi, c]
            sender.send(cond, ring, ring, base + 35 + slot, to_core)

    def finish():
        for a in range(len(shards)):
            for k in range(LINE):
                for slot, zi, cond in near_items(z, k):
                    when(
                        cond,
                        lambda: sender.land(
                            fulls[a].at[:, zi, 1 - c], a * GATHER_SEMS + 35 + slot, to_x
                        ),
                    )

    def grouped(stage):
        def act(chunk, k):
            for a in chunk:
                stage(a, k)

        return act

    order = [(chunk, k) for chunk in chunks for k in range(LINE)]
    stages = [grouped(stage) for stage in (first, second, third)]
    return (staged(order, stages, (0,) + ahead), finish)


def staged(order, stages, delays):
    ticks = []
    for t in range(len(order) + delays[-1]):

        def tick(t=t):
            for stage, delay in zip(stages, delays):
                if 0 <= t - delay < len(order):
                    stage(*order[t - delay])

        ticks.append(tick)
    return ticks


def add_into(target, terms):
    rows, columns = target.shape
    step = min(columns, 512)

    def body(i, carry):
        cut = pl.ds(pl.multiple_of(i * step, step), step)
        value = terms[0][:, cut].astype(F32)
        for term in terms[1:]:
            value = value + term[:, cut].astype(F32)
        target[:, cut] = value.astype(target.dtype)
        return carry

    lax.fori_loop(0, columns // step, body, 0)


def exchange(sources, targets, outward, sender, base, local_sems, local_base):
    g, x, y, z, c = place()

    def partner(index):
        if outward:
            return (index * 2 + c, z * 2 + g // 2)
        return (2 * c + index, z * 2 + lax.rem(g, 2))

    def origin(index):
        if outward:
            return (2 * c + index, z * 2 + lax.rem(g, 2))
        return (index * 2 + c, z * 2 + g // 2)

    slot = lax.rem(g, 2) if outward else g // 2
    finals = []

    def post(i, index):
        chip, wide = partner(index)
        same = jnp.logical_and(chip == g, wide == z * 2 + c)
        other = jnp.logical_not(same)
        source, target = sources[i].at[index], targets[i].at[slot]
        at = base + i * 4

        def copy():
            return remote(
                source,
                target,
                sender.send_sems.at[at + 2 + index],
                sender.recv_sems.at[at + slot],
                (chip, wide),
            )

        when(
            same,
            lambda: pltpu.make_async_copy(source, target, local_sems.at[local_base + i]).start(),
        )
        when(other, lambda: copy().start())
        finals.append((other, lambda: copy().wait_send()))

    for i in range(len(sources)):
        for index in range(2):
            post(i, index)

    def arrive():
        for i in range(len(sources)):
            for index in range(2):
                chip, wide = origin(index)
                same = jnp.logical_and(chip == g, wide == z * 2 + c)
                target = targets[i].at[index]
                when(
                    same,
                    lambda: pltpu.make_async_copy(
                        sources[i].at[index], target, local_sems.at[local_base + i]
                    ).wait(),
                )
                when(
                    jnp.logical_not(same),
                    lambda: sender.land(target, base + i * 4 + index, (g, z * 2 + 1 - c)),
                )
        for other, final in finals:
            when(other, final)

    return arrive


def hbm():
    return pl.BlockSpec(memory_space=pltpu.HBM)


def vmem():
    return pl.BlockSpec(memory_space=pltpu.VMEM)


def chain(*ticks):
    def act():
        for tick in ticks:
            tick()

    return act


def run_with(ticks, steps, body):
    def act(i, carry):
        body(i)
        for j, tick in enumerate(ticks[:steps]):
            pl.when(i == j)(tick)
        return carry

    lax.fori_loop(0, steps, act, 0)
    for tick in ticks[steps:]:
        tick()


def lane_half(shape, period, half):
    lanes = lax.broadcasted_iota(jnp.int32, shape, 1)
    return lax.rem(lanes, period) < half


def turn(values):
    first = lane_half(values.shape, HEAD_DIM, HEAD_DIM // 2)
    return jnp.where(
        first,
        -pltpu.roll(values, values.shape[1] - HEAD_DIM // 2, 1),
        pltpu.roll(values, HEAD_DIM // 2, 1),
    )


def dot_rows(left, right):
    return lax.dot_general(left, right, (((1,), (0,)), ((), ())), preferred_element_type=F32)


def dot_columns(left, right):
    return lax.dot_general(left, right, (((1,), (1,)), ((), ())), preferred_element_type=F32)


def attend_pair(
    query_ref, key_ref, value_ref, far_key_ref, far_value_ref, seg_ref, seg_near_ref, seg_far_ref, out_ref, norm_ref
):
    rows = query_ref.shape[0]
    first = lane_half((rows, 128), 128, HEAD_DIM)
    tile = 256
    for r in range(rows // tile):
        rs = pl.ds(r * tile, tile)
        query = query_ref[rs, :]
        low_half = first[:tile]
        seg = seg_ref[rs, 0:1]
        near, far = seg == seg_near_ref[...], seg == seg_far_ref[...]
        outs, norms = [], []
        for h in range(2):
            keep = low_half if h == 0 else jnp.logical_not(low_half)
            one = jnp.where(keep, query, jnp.zeros_like(query))
            near_scores = jnp.where(near, dot_columns(one, key_ref[...]), neg_large)
            far_scores = jnp.where(far, dot_columns(one, far_key_ref[...]), neg_large)
            top = jnp.maximum(
                jnp.max(near_scores, axis=1, keepdims=True), jnp.max(far_scores, axis=1, keepdims=True)
            )
            near_expon, far_expon = jnp.exp(near_scores - top), jnp.exp(far_scores - top)
            total = jnp.sum(near_expon, axis=1, keepdims=True) + jnp.sum(
                far_expon, axis=1, keepdims=True
            )
            mixed = dot_rows(near_expon.astype(BF16), value_ref[...]) + dot_rows(
                far_expon.astype(BF16), far_value_ref[...]
            )
            outs.append(mixed / total)
            norms.append(jnp.broadcast_to(top + jnp.log(total), (tile, 128)))
        out_ref[rs, :] = jnp.where(low_half, outs[0], outs[1]).astype(BF16)
        flipped = jnp.transpose(jnp.where(low_half, norms[0], norms[1]))
        norm_ref[0:1, rs] = flipped[0:1]
        norm_ref[1:2, rs] = flipped[HEAD_DIM : HEAD_DIM + 1]


def plane_first_ticks(a, shard, full, cut, sender, local_sem):
    g, x, y, z, c = place()
    gx, gy, gd = g + 1 - 2 * x, g + 2 - 4 * y, 3 - g
    to_x, to_y, to_core = (gx, z * 2 + c), (gy, z * 2 + c), (g, z * 2 + 1 - c)
    above = (g, jnp.minimum(z + 1, LINE - 1) * 2 + c)
    below = (g, jnp.maximum(z - 1, 0) * 2 + c)
    base, rows = a * GATHER_SEMS, full.shape[3]
    own = full.at[g, z, c]

    def begin():
        sender.do(True, lambda: pltpu.make_async_copy(shard, own, local_sem).start())
        sender.send(True, shard, own, base + 7, to_x)
        sender.send(True, shard, own, base + 14, to_y)

    def middle():
        upper, lower = full.at[gx, z, c, 0:cut], full.at[gy, z, c, cut:rows]
        sender.do(True, lambda: sender.land(full.at[gx, z, c], base + 7, to_x))
        sender.send(True, upper, upper, base + 21, to_y)
        sender.do(True, lambda: sender.land(full.at[gy, z, c], base + 14, to_x))
        sender.send(True, lower, lower, base + 28, to_x)

    def along(k):
        def act():
            if k == 0:
                sender.do(True, lambda: pltpu.make_async_copy(shard, own, local_sem).wait())
                sender.do(True, lambda: sender.land(full.at[gd, z, c, 0:cut], base + 21, to_x))
                sender.do(True, lambda: sender.land(full.at[gd, z, c, cut:rows], base + 28, to_x))
            for slot, zi, cond in near_items(z, k):
                ring = full.at[:, zi, c]
                if k > 0:
                    sender.do(cond, lambda: sender.land(ring, base + slot, to_x))
                if k < LINE - 1:
                    if slot < 4:
                        sender.send(both(cond, z < LINE - 1), ring, ring, base + slot + 1, above)
                    if slot == 0 or slot >= 4:
                        going = 4 if slot == 0 else slot + 1
                        sender.send(both(cond, z > 0), ring, ring, base + going, below)
                sender.send(cond, ring, ring, base + 35 + slot, to_core)

        return act

    return [begin, middle] + [along(k) for k in range(LINE)]


def await_partner(a, full, sender):
    g, x, y, z, c = place()
    for k in range(LINE):
        for slot, zi, cond in near_items(z, k):
            when(
                cond,
                lambda: sender.land(
                    full.at[:, zi, 1 - c], a * GATHER_SEMS + 35 + slot, (g, z * 2 + 1 - c)
                ),
            )


def stretch(packed, vectors, sizes):
    shards = packed.shape[0] // 32
    for row, lane, size, target in vectors:
        pick_rows = lax.broadcasted_iota(jnp.int32, (shards, shards * 32), 0) * 32 + row
        pick = lax.broadcasted_iota(jnp.int32, (shards, shards * 32), 1) == pick_rows
        part = dot_rows(pick.astype(F32).astype(BF16), packed).astype(BF16)
        step = 1024

        def body(i, carry):
            at = pl.multiple_of(i * step, step)
            column = (lax.broadcasted_iota(jnp.int32, (1, step), 1) + i * step).astype(F32)
            shard = jnp.floor((column + 0.5) * (1.0 / size))
            lane_of = (column - shard * size + lane).astype(jnp.int32)
            spread = lax.broadcasted_iota(jnp.int32, (128, step), 0) == lane_of
            value = dot_rows(part, spread.astype(F32).astype(BF16))
            keep = lax.broadcasted_iota(jnp.int32, (shards, step), 0) == shard.astype(jnp.int32)
            target[:, pl.ds(at, step)] = jnp.sum(jnp.where(keep, value, 0.0), axis=0, keepdims=True)
            return carry

        lax.fori_loop(0, shards * size // step, body, 0)


def flat(value):
    return value.reshape(-1, value.shape[-1])


def row_mean(value):
    return jnp.mean(value, axis=1, keepdims=True)


def forward_kernel(*refs):
    shards, refs = refs[:6], refs[6:]
    (tokens, out_cot, embed_cot, segments, cosine, sine), refs = refs[:6], refs[6:]
    (
        project_out, token_out, qkv_out, far_out, context_out, norm, hidden_out, act_out, up_grad_out,
        down_grad_out, result_out, embed_cot_out, branch_grad_out, context_grad_out, first_grad_out,
        sums, seg_out, layer_back, embed_back,
    ), refs = refs[:19], refs[19:]
    fulls, refs = refs[:6], refs[6:]
    (
        token_in, cot_in, embed_cot_in, far_seg, seg_column, vectors, qkv, far, context, normed, rstd,
        hidden_low, act, slope, result_low, embedded, sum_grad, down_grad, branch_grad, context_grad,
        send_sems, recv_sems, local_sems,
    ) = refs
    project_w, embed_w, small_w, output_w, up_w, down_w = fulls
    g, x, y, z, c = place()
    partner = (g, z * 2 + 1 - c)
    rows, width = context.shape
    sender = Sender(send_sems, recv_sems)
    spare = 6 * GATHER_SEMS
    flushed = []

    def flush(source, target, index):
        copy = pltpu.make_async_copy(source, target, local_sems.at[10 + index])
        copy.start()
        flushed.append((source, target, index))

    entry_barrier()
    splits = [s.shape[0] // 2 for s in shards]
    early, unused = gather_ticks(shards, fulls, splits, [(0, 1, 2)], (1, 2), sender, local_sems)
    late, unused = gather_ticks(shards, fulls, splits, [(3,), (4,)], (3, 6), sender, local_sems)
    lines = plane_first_ticks(5, shards[5], down_w, splits[5], sender, local_sems.at[5])
    early[0]()
    sender.post(True, segments, far_seg, spare, partner)
    token_back = exchange([tokens], [token_in], True, sender, spare + 2, local_sems, 6)
    early[1]()
    lines[0]()
    early[2]()
    early[3]()
    lines[1]()
    early[4]()
    late[0]()
    early[5]()
    lines[2]()
    token_back()
    sender.land(far_seg, spare, partner)
    micro = g // 2
    own_ids = segments[pl.ds(micro, 1), :].astype(F32)
    far_ids = far_seg[pl.ds(micro, 1), :].astype(F32)
    ids = jnp.where(lax.rem(g, 2) == c, own_ids, far_ids)
    halves = (ids[:, :rows], ids[:, rows:])
    near_row = jnp.where(c == 0, halves[0], halves[1])
    far_row = jnp.where(c == 0, halves[1], halves[0])
    seg_out[0:1, :] = near_row
    seg_out[1:2, :] = far_row
    seg_column[...] = jnp.transpose(jnp.broadcast_to(near_row, (128, rows)))
    for a in range(3):
        await_partner(a, fulls[a], sender)
    flush(project_w, project_out, 0)
    flush(token_in, token_out, 1)
    vector = lambda i, size: vectors.at[i : i + 1, 0:size]
    stretch(
        flat(small_w[...]),
        (
            (0, 0, 96, vector(0, 3 * width)),
            (1, 0, 128, vector(1, 4 * width)),
            (2, 0, 32, vector(2, width)),
            (2, 32, 32, vector(3, width)),
            (2, 64, 32, vector(4, width)),
            (2, 96, 32, vector(5, width)),
            (3, 0, 32, vector(6, width)),
            (3, 32, 32, vector(7, width)),
        ),
        None,
    )
    tile = 512
    wide = qkv.shape[1] // tile

    def project_tile(i):
        t = lax.rem(i + 2, wide)
        cut = pl.ds(pl.multiple_of(t * tile, tile), tile)
        value = dot_rows(flat(token_in[...]), flat(project_w[:, :, :, :, cut]))
        value = value + vectors[0:1, cut]

        @pl.when(t < 4)
        def _():
            factor = jnp.where(t < 2, HEAD_DIM ** (-0.5), 1.0)
            for j in range(tile // 128):
                part = value[:, j * 128 : (j + 1) * 128]
                part = (part * cosine[...] + turn(part) * sine[...]) * factor
                qkv[:, pl.ds(pl.multiple_of(t * tile + j * 128, 128), 128)] = part.astype(BF16)

        @pl.when(t >= 4)
        def _():
            qkv[:, cut] = value.astype(BF16)

        pl.when(i == 3)(
            lambda: sender.copy(qkv.at[:, width:], far, spare + 1, partner).start()
        )

    run_with(late[1:5] + [chain(late[5], lines[3])], wide, project_tile)
    cot_back = exchange(
        [out_cot, embed_cot], [cot_in, embed_cot_in], True, sender, spare + 6, local_sems, 7
    )
    sender.land(far, spare + 1, partner)
    flush(qkv, qkv_out, 2)
    flush(far, far_out, 3)

    def attend_one(i):
        at = pl.multiple_of(i * 128, 128)
        cut = lambda ref, base: ref.at[:, pl.ds(base + at, 128)]
        attend_pair(
            cut(qkv, 0), cut(qkv, width), cut(qkv, 2 * width), cut(far, 0), cut(far, width),
            seg_column, seg_out.at[0:1], seg_out.at[1:2], cut(context, 0), norm.at[i],
        )

    run_with(late[6:13] + [chain(late[13], lines[4])], width // 128, attend_one)
    flush(context, context_out, 4)
    await_partner(3, output_w, sender)
    half = rows // 2
    output_weight, bias_o = lambda: flat(output_w[...]), vectors[2:3, 0:width]

    def hidden_of(cut):
        return normed[cut, :] * vectors[3:4, 0:width] + vectors[4:5, 0:width]

    def branch_tile(i):
        cut = pl.ds(pl.multiple_of(i * half, half), half)
        resid = dot_rows(context[cut, :], output_weight()) + vectors[2:3, 0:width]
        resid = resid + token_in[i].astype(F32)
        center = resid - row_mean(resid)
        scale = lax.rsqrt(row_mean(center * center) + eps_norm)
        normed[cut, :] = center * scale
        rstd[0, cut, :] = jnp.broadcast_to(scale, (half, 128))
        hidden_low[cut, :] = hidden_of(cut).astype(BF16)

    run_with([], 2, branch_tile)
    flush(hidden_low, hidden_out, 5)
    await_partner(4, up_w, sender)

    def up_tile(j):
        cut = pl.ds(pl.multiple_of(j * tile, tile), tile)
        value = dot_rows(hidden_low[...], flat(up_w[:, :, :, :, cut])) + vectors[1:2, cut]
        below = 0.5 + 0.5 * lax.erf(value * 0.7071067811865476)
        density = jnp.exp(-0.5 * value * value) * 0.3989422804014327
        act[:, cut] = (value * below).astype(BF16)
        slope[:, cut] = (below + value * density).astype(BF16)

    ff = act.shape[1]
    run_with([lambda: None, lambda: None, lines[5]], ff // tile, up_tile)
    flush(act, act_out, 6)
    await_partner(5, down_w, sender)
    cot_back()
    flush(embed_cot_in, embed_cot_out, 7)
    sums[...] = jnp.zeros_like(sums)

    def add_sum(row, value):
        sums[row : row + 1, 0:width] += jnp.sum(value, axis=0, keepdims=True)

    def norm_back(grads, row_normed, scale, gain):
        scaled = grads * gain
        return scale * (
            scaled - row_mean(scaled) - row_normed * row_mean(scaled * row_normed)
        )

    def down_tile(i):
        cut = pl.ds(pl.multiple_of(i * half, half), half)
        gain, shift = vectors[6:7, 0:width], vectors[7:8, 0:width]
        resid = dot_rows(act[cut, :], flat(down_w[...])) + vectors[5:6, 0:width]
        resid = resid + hidden_of(cut)
        center = resid - row_mean(resid)
        scale = lax.rsqrt(row_mean(center * center) + eps_norm)
        row_normed = center * scale
        low = (row_normed * gain + shift).astype(BF16)
        result_low[i] = low
        embed_full = flat(embed_w[...])
        embedded[i] = dot_rows(low, embed_full).astype(BF16)
        grads = cot_in[i].astype(F32) + dot_columns(embed_cot_in[i], embed_full)
        add_sum(6, grads * row_normed)
        add_sum(7, grads)
        total = norm_back(grads, row_normed, scale, gain)
        sum_grad[cut, :] = total
        low = total.astype(BF16)
        down_grad[cut, :] = low
        add_sum(5, low.astype(F32))

    run_with([], 2, down_tile)
    results_back = exchange(
        [result_low, embedded], [layer_back, embed_back], False, sender, spare + 14, local_sems, 1
    )
    flush(result_low, result_out, 8)
    flush(down_grad, down_grad_out, 9)

    def up_grad_tile(j):
        cut = pl.ds(pl.multiple_of(j * tile, tile), tile)
        part = flat(down_w[j // 2, pl.ds(lax.rem(j, 2) * 2, 2)])
        value = (dot_columns(down_grad[...], part) * slope[:, cut].astype(F32)).astype(BF16)
        slope[:, cut] = value
        sums[1:2, cut] = jnp.sum(value.astype(F32), axis=0, keepdims=True)

    run_with([], ff // tile, up_grad_tile)
    flush(slope, up_grad_out, 10)

    def first_tile(i):
        cut = pl.ds(pl.multiple_of(i * half, half), half)
        grads = sum_grad[cut, :] + dot_columns(slope[cut, :], flat(up_w[...]))
        row_normed = normed[cut, :]
        add_sum(3, grads * row_normed)
        add_sum(4, grads)
        total = norm_back(grads, row_normed, rstd[0, cut, 0:1], vectors[3:4, 0:width])
        sum_grad[cut, :] = total
        low = total.astype(BF16)
        branch_grad[cut, :] = low
        add_sum(2, low.astype(F32))
        context_grad[cut, :] = dot_columns(low, output_weight()).astype(BF16)

    run_with([], 2, first_tile)
    flush(sum_grad, first_grad_out, 11)
    flush(branch_grad, branch_grad_out, 12)
    flush(context_grad, context_grad_out, 13)
    results_back()
    sender.drain(early + late + lines)
    sender.copy(qkv.at[:, width:], far, spare + 1, partner).wait_send()
    for source, target, index in flushed:
        pltpu.make_async_copy(source, target, local_sems.at[10 + index]).wait()


def forward(shards, sources, segments, tables, ff):
    piece, width = sources[0].shape[1:]
    lanes = sources[2].shape[2]
    rows = 2 * piece
    semaphores = 6 * GATHER_SEMS + 32
    fulls = [(PLANE, LINE, 2) + s.shape for s in shards]
    shape = jax.ShapeDtypeStruct
    outs = [
        shape(fulls[0], BF16),
        shape((2, piece, width), BF16),
        shape((rows, 3 * width), BF16),
        shape((rows, 2 * width), BF16),
        shape((rows, width), BF16),
        shape((width // 128, 8, rows), F32),
        shape((rows, width), BF16),
        shape((rows, ff), BF16),
        shape((rows, ff), BF16),
        shape((rows, width), BF16),
        shape((2, piece, width), BF16),
        shape((2, piece, lanes), BF16),
        shape((rows, width), BF16),
        shape((rows, width), BF16),
        shape((rows, width), F32),
        shape((8, ff), F32),
        shape((8, rows), F32),
        shape((2, piece, width), BF16),
        shape((2, piece, lanes), BF16),
    ]
    spaces = [hbm()] * len(outs)
    for i in (5, 15, 16):
        spaces[i] = vmem()
    scratch = [pltpu.VMEM(f, BF16) for f in fulls] + [
        pltpu.VMEM((2, piece, width), BF16),
        pltpu.VMEM((2, piece, width), BF16),
        pltpu.VMEM((2, piece, lanes), BF16),
        pltpu.VMEM(segments.shape, jnp.int32),
        pltpu.VMEM((rows, 128), F32),
        pltpu.VMEM((8, ff), F32),
        pltpu.VMEM((rows, 3 * width), BF16),
        pltpu.VMEM((rows, 2 * width), BF16),
        pltpu.VMEM((rows, width), BF16),
        pltpu.VMEM((rows, width), F32),
        pltpu.VMEM((1, rows, 128), F32),
        pltpu.VMEM((rows, width), BF16),
        pltpu.VMEM((rows, ff), BF16),
        pltpu.VMEM((rows, ff), BF16),
        pltpu.VMEM((2, piece, width), BF16),
        pltpu.VMEM((2, piece, lanes), BF16),
        pltpu.VMEM((rows, width), F32),
        pltpu.VMEM((rows, width), BF16),
        pltpu.VMEM((rows, width), BF16),
        pltpu.VMEM((rows, width), BF16),
        pltpu.SemaphoreType.DMA((semaphores,)),
        pltpu.SemaphoreType.DMA((semaphores,)),
        pltpu.SemaphoreType.DMA((24,)),
    ]
    return pl.pallas_call(
        forward_kernel,
        out_shape=outs,
        in_specs=[hbm()] * 9 + [vmem()] * 3,
        out_specs=spaces,
        scratch_shapes=scratch,
        compiler_params=pltpu.CompilerParams(
            collective_id=1, has_side_effects=True, vmem_limit_bytes=67043328
        ),
        name="forward",
    )(*shards, *sources, segments, *tables)


def attend_back_pair(
    query, key, value, far_key, far_value, grad, norm, seg_row, seg_near, seg_far, tables, summed
):
    rows = query.shape[0]
    tile = 256
    cosine, sine, far_cosine, far_sine = tables
    low_half = lane_half((rows, 128), 128, HEAD_DIM)
    query_low = lane_half((tile, 128), 128, HEAD_DIM)
    summed[...] = jnp.zeros_like(summed)

    def body(r, carry):
        rs = pl.ds(pl.multiple_of(r * tile, tile), tile)
        query_rows, grad_rows = query[rs, :], grad[rs, :]
        sides = ((key[...], value[...], seg_near), (far_key[...], far_value[...], seg_far))
        query_grads = []
        key_grads, value_grads = [[], []], [[], []]
        for h in range(2):
            keep = query_low if h == 0 else jnp.logical_not(query_low)
            one = jnp.where(keep, query_rows, jnp.zeros_like(query_rows))
            one_grad = jnp.where(keep, grad_rows, jnp.zeros_like(grad_rows))
            top = norm[h : h + 1, rs]
            kept = []
            delta = jnp.zeros((1, tile), F32)
            for keys, values, seg_key in sides:
                same = seg_key[:, 0:1] == seg_row[:, rs]
                scores = jnp.where(same, dot_columns(keys, one), neg_large)
                probs = jnp.exp(scores - top)
                product = probs * dot_columns(values, one_grad)
                delta = delta + jnp.sum(product, axis=0, keepdims=True)
                kept.append((probs, product))
            total = None
            for i, (keys, values, seg_key) in enumerate(sides):
                probs, product = kept[i]
                score_grad = (product - probs * delta).astype(BF16)
                key_grads[i].append(dot_rows(score_grad, query_rows))
                value_grads[i].append(dot_rows(probs.astype(BF16), grad_rows))
                part = contract_rows(score_grad, keys)
                total = part if total is None else total + part
            query_grads.append(total)
        for i in range(2):
            summed[i] += jnp.where(low_half, key_grads[i][0], key_grads[i][1])
            summed[2 + i] += jnp.where(low_half, value_grads[i][0], value_grads[i][1])
        joined = jnp.where(query_low, query_grads[0], query_grads[1]) * HEAD_DIM ** (-0.5)
        query[rs, :] = (joined * cosine[rs, :] - turn(joined) * sine[rs, :]).astype(BF16)
        return carry

    lax.fori_loop(0, rows // tile, body, 0)
    near, far = summed[0], summed[1]
    key[...] = (near * cosine[...] - turn(near) * sine[...]).astype(BF16)
    value[...] = summed[2].astype(BF16)
    far_key[...] = (far * far_cosine[...] - turn(far) * far_sine[...]).astype(BF16)
    far_value[...] = summed[3].astype(BF16)


def far_first(z, k):
    items = near_items(z, k)
    if k == 0:
        return items
    return [(k,) + items[1][1:], (3 + k,) + items[0][1:]]


def sum_ticks(arrays, chunks, ahead, sender):
    g, x, y, z, c = place()
    gx, gy, gd = g + 1 - 2 * x, g + 2 - 4 * y, 3 - g
    to_x, to_y, to_core = (gx, z * 2 + c), (gy, z * 2 + c), (g, z * 2 + 1 - c)
    above = (g, jnp.minimum(z + 1, LINE - 1) * 2 + c)
    below = (g, jnp.maximum(z - 1, 0) * 2 + c)

    def side_of(slot):
        return 0 if slot < 4 else 1

    def zeroth(a, k):
        array, base = arrays[a], a * REDUCE_SEMS
        for slot, zi, cond in far_first(z, k):
            buffer = array["send"].at[side_of(slot)]
            index = base + slot
            copy = lambda at, item: sender.copy(buffer, array["held"].at[item], base + at, to_core)
            if sender.draining:
                if slot in (0, 4) and not array["early"]:
                    when(cond, lambda: copy(slot, zi).wait_send())
                continue
            if slot == 0:
                when(z + 1 < LINE, lambda: copy(1, zi).wait_send())
            elif k < LINE - 1:
                before = z + k + 1 < LINE if slot < 4 else z >= k + 1
                when(before, lambda: copy(slot + 1, zi).wait_send())

            def work():
                array["product"](1 - c, zi, buffer, None)
                copy(slot, zi).start()

            if k == LINE - 1 and slot == k and array["after"] is not None:
                other = arrays[array["after"]]
                leave = lambda at: sender.copy(
                    other["send"].at[0], other["held"].at[0], array["after"] * REDUCE_SEMS + at, to_core
                )
                leave(0).wait_send()
                when(z >= 1, lambda: leave(4).wait_send())

            when(cond, work)

    def first(a, k):
        array, base = arrays[a], a * REDUCE_SEMS
        held, half_in = array["held"], array["half"]
        rows = held.shape[2]
        cut = rows // 2
        for slot, zi, cond in far_first(z, k):

            def work():
                sender.land(held.at[zi], base + slot, to_x)
                array["product"](c, zi, held.at[zi], held.at[zi])

            sender.do(cond, work)
            sender.send(cond, held.at[zi, gd, 0:cut], half_in.at[zi, 0:cut], base + 7 + slot, to_y)
            sender.send(
                cond, held.at[zi, gd, cut:rows], half_in.at[zi, cut:rows], base + 14 + slot, to_x
            )

    def second(a, k):
        array, base = arrays[a], a * REDUCE_SEMS
        held, half_in, whole_in = array["held"], array["half"], array["whole"]
        rows = held.shape[2]
        cut = rows // 2
        for slot, zi, cond in far_first(z, k):

            def upper():
                sender.land(half_in.at[zi, 0:cut], base + 7 + slot, to_x)
                mine = held.at[zi, gx, 0:cut]
                add_into(mine, [mine, half_in.at[zi, 0:cut]])

            sender.do(cond, upper)
            sender.send(cond, held.at[zi, gx], whole_in.at[zi, 0], base + 21 + slot, to_x)

            def lower():
                sender.land(half_in.at[zi, cut:rows], base + 14 + slot, to_x)
                mine = held.at[zi, gy, cut:rows]
                add_into(mine, [mine, half_in.at[zi, cut:rows]])

            sender.do(cond, lower)
            sender.send(cond, held.at[zi, gy], whole_in.at[zi, 1], base + 28 + slot, to_y)

    def third(a, k):
        array, base = arrays[a], a * REDUCE_SEMS
        held, whole_in, line_in, out = array["held"], array["whole"], array["line"], array["out"]
        for slot, zi, cond in far_first(z, k):
            mine = held.at[zi, g]
            terms = [mine, whole_in.at[zi, 0], whole_in.at[zi, 1]]

            def arrive():
                sender.land(whole_in.at[zi, 0], base + 21 + slot, to_x)
                sender.land(whole_in.at[zi, 1], base + 28 + slot, to_x)

            sender.do(cond, arrive)
            if k == 0:
                rise, fall = line_in.at[zi], line_in.at[LINE]
                sender.do(z > 0, lambda: sender.land(rise, base + 36, to_x))
                sender.do(z < LINE - 1, lambda: sender.land(fall, base + 43, to_x))
                sender.do(z == 0, lambda: add_into(out, terms + [fall]))
                sender.do(z == LINE - 1, lambda: add_into(out, terms + [rise]))
                sender.do(
                    jnp.logical_and(z > 0, z < LINE - 1),
                    lambda: add_into(out, terms + [rise, fall]),
                )
            else:
                going_up = slot < 4
                moved = line_in.at[zi]
                landing = line_in.at[LINE if k == 1 and not going_up else zi]
                offset = base + (35 if going_up else 42)
                inner = (z > 0) if going_up else (z < LINE - 1)

                def join():
                    sender.land(moved, offset + k + 1, to_x)
                    add_into(mine, terms + [moved])

                if k < LINE - 1:
                    sender.do(both(cond, inner), join)
                sender.do(both(cond, jnp.logical_not(inner)), lambda: add_into(mine, terms))
                sender.send(cond, mine, landing, offset + k, above if going_up else below)

    def grouped(stage):
        def act(chunk, k):
            for a in chunk:
                stage(a, k)

        return act

    order = [(chunk, k) for chunk in chunks for k in (3, 2, 1, 0)]
    stages = [grouped(stage) for stage in (zeroth, first, second, third)]
    return staged(order, stages, (0,) + ahead)


def gather_up(vectors, target):
    shards = PLANE * LINE * 2
    total = None
    for row in sorted({v[0] for v in vectors}):
        share = jnp.zeros((shards, 128), F32)
        for at, lane, size, source in vectors:
            if at != row:
                continue
            step = 1024

            def body(i, carry):
                cut = pl.ds(pl.multiple_of(i * step, step), step)
                column = (lax.broadcasted_iota(jnp.int32, (1, step), 1) + i * step).astype(F32)
                shard = jnp.floor((column + 0.5) * (1.0 / size))
                lane_of = (column - shard * size + lane).astype(jnp.int32)
                spread = lax.broadcasted_iota(jnp.int32, (128, step), 0) == lane_of
                keep = lax.broadcasted_iota(jnp.int32, (shards, step), 0) == shard.astype(jnp.int32)
                value = jnp.where(keep, source[:, cut], 0.0).astype(BF16)
                return carry + dot_columns(value, spread.astype(F32).astype(BF16))

            share = lax.fori_loop(0, shards * size // step, body, share)
        pick_rows = lax.broadcasted_iota(jnp.int32, (shards, shards * 32), 0) * 32 + row
        pick = lax.broadcasted_iota(jnp.int32, (shards, shards * 32), 1) == pick_rows
        part = contract_rows(pick.astype(F32).astype(BF16), share.astype(BF16))
        total = part if total is None else total + part
    target[...] = total.astype(BF16).reshape(target.shape)


def backward_kernel(*refs):
    (
        act_hbm, down_grad_hbm, hidden_hbm, up_grad_hbm, context_hbm, branch_grad_hbm, result_hbm,
        embed_cot_hbm, token_hbm, qkv_hbm, far_hbm, context_grad_hbm, first_grad_hbm, weight_hbm,
        norm, segs, sums, cosine, sine, far_cosine, far_sine,
    ), refs = refs[:21], refs[21:]
    outs, token_out, refs = refs[:6], refs[6], refs[7:]
    shared = lambda columns: refs[1].at[:, :, :, 0:columns]
    sends = (
        refs[0], refs[1], shared(branch_grad_hbm.shape[1]), refs[2], shared(qkv_hbm.shape[1]), refs[3]
    )
    helds, halves, wholes, lines = [refs[i * 6 - 2 : (i + 1) * 6 - 2] for i in range(1, 5)]
    (
        act, down_grad, up_grad, branch_grad, embed_cot, raw, turned_a, turned_b, turned_c, qkv, far,
        far_back, context_grad, seg_near, seg_far, vectors, shares, summed, token_in,
        send_sems, recv_sems, local_sems,
    ) = refs[28:]
    g, x, y, z, c = place()
    partner = (g, z * 2 + 1 - c)
    rows, width = branch_grad.shape
    ff = act.shape[1]
    sender = Sender(send_sems, recv_sems)
    spare = 6 * REDUCE_SEMS

    def load(source, target, index):
        copy = lambda: pltpu.make_async_copy(source, target, local_sems.at[index])
        copy().start()
        return lambda: copy().wait()

    waits = {
        "act": load(act_hbm, act, 0),
        "down": load(down_grad_hbm, down_grad, 1),
        "raw": load(hidden_hbm, raw, 2),
        "up": load(up_grad_hbm, up_grad, 3),
        "branch": load(branch_grad_hbm, branch_grad, 4),
        "embed": load(embed_cot_hbm, embed_cot, 5),
        "qkv": load(qkv_hbm, qkv, 6),
        "far": load(far_hbm, far, 7),
        "grad": load(context_grad_hbm, context_grad, 8),
        "first": load(first_grad_hbm, token_out, 9),
    }
    entry_barrier()

    def turn_over(target):
        for j in range(width // 128):
            block = jnp.transpose(flat(raw[:, :, j * 128 : (j + 1) * 128]))
            target[j // 2, (j % 2) * 2 : (j % 2) * 2 + 2] = block.reshape(2, 2, 32, rows)

    def product_of(turned, right):
        columns = right.shape[1]
        step = min(columns, 512)

        def act_on(parity, zi, target, base):
            left = flat(turned[:, zi, parity])

            def body(i, carry):
                cut = pl.ds(pl.multiple_of(i * step, step), step)
                value = dot_rows(left, right[:, cut]).reshape(PLANE, 32, step)
                if base is not None:
                    value = value + base[:, :, cut].astype(F32)
                target[:, :, cut] = value.astype(BF16)
                return carry

            lax.fori_loop(0, columns // step, body, 0)

        return act_on

    def down_product(parity, zi, target, base):
        def body(j, carry):
            at = ((j * LINE + zi) * 2 + parity) * 128
            left = act[:, pl.ds(pl.multiple_of(at, 128), 128)]
            value = contract_rows(left, down_grad[...])
            if base is not None:
                value = value + base[j].astype(F32)
            target[j] = value.astype(BF16)
            return carry

        lax.fori_loop(0, PLANE, body, 0)

    def share_product(parity, zi, target, base):
        value = shares[:, zi, parity].astype(F32)
        if base is not None:
            value = value + base[...].astype(F32)
        target[...] = value.astype(BF16)

    products = [
        down_product,
        product_of(turned_a, up_grad),
        product_of(turned_b, branch_grad),
        product_of(turned_c, embed_cot),
        product_of(turned_a, qkv),
        share_product,
    ]
    arrays = [
        {"product": p, "send": s, "held": h, "half": i, "whole": w, "line": l, "out": o}
        for p, s, h, i, w, l, o in zip(products, sends, helds, halves, wholes, lines, outs)
    ]
    for a, array in enumerate(arrays):
        array["after"] = {2: 1, 4: 2}.get(a)
        array["early"] = a in (1, 2)
    main = sum_ticks(arrays, [(0,), (1,), (2, 3)], MAIN_AHEAD, sender)
    late = sum_ticks(arrays, [(4, 5)], LATE_AHEAD, sender)
    waits["act"]()
    waits["down"]()
    main[0]()
    main[1]()
    waits["raw"]()
    turn_over(turned_a)
    load(context_hbm, raw, 2)
    main[2]()
    waits["up"]()
    main[3]()
    main[4]()
    waits["raw"]()
    turn_over(turned_b)
    load(result_hbm, raw, 2)
    main[5]()
    main[6]()
    waits["raw"]()
    turn_over(turned_c)
    load(token_hbm, raw, 2)
    waits["branch"]()
    waits["embed"]()
    main[7]()
    for name in ("qkv", "far", "grad"):
        waits[name]()
    seg_near[...] = jnp.transpose(jnp.broadcast_to(segs[0:1, :], (128, rows)))
    seg_far[...] = jnp.transpose(jnp.broadcast_to(segs[1:2, :], (128, rows)))

    def attend_one(i):
        at = pl.multiple_of(i * 128, 128)
        cut = lambda ref, base: ref.at[:, pl.ds(base + at, 128)]
        attend_back_pair(
            cut(qkv, 0), cut(qkv, width), cut(qkv, 2 * width), cut(far, 0), cut(far, width),
            cut(context_grad, 0), norm.at[i], segs.at[0:1], seg_near, seg_far,
            (cosine, sine, far_cosine, far_sine), summed,
        )

    run_with(main[8:16], width // 128, attend_one)
    sender.post(True, far, far_back, spare, partner)
    waits["raw"]()
    turn_over(turned_a)
    sender.land(far_back, spare, partner)
    tile = 512
    vectors[...] = jnp.zeros_like(vectors)

    def finish_tile(i):
        cut = pl.ds(pl.multiple_of(i * tile, tile), tile)

        @pl.when(i >= 2)
        def _():
            other = pl.ds(pl.multiple_of(jnp.maximum(i - 2, 0) * tile, tile), tile)
            qkv[:, cut] = (qkv[:, cut].astype(F32) + far_back[:, other].astype(F32)).astype(BF16)

        vectors[0:1, cut] = jnp.sum(qkv[:, cut].astype(F32), axis=0, keepdims=True)

    run_with([], 3 * width // tile, finish_tile)
    source = lambda i, size: (vectors if i == 0 else sums).at[i : i + 1, 0:size]
    gather_up(
        (
            (0, 0, 96, source(0, 3 * width)),
            (1, 0, 128, source(1, ff)),
            (2, 0, 32, source(2, width)),
            (2, 32, 32, source(3, width)),
            (2, 64, 32, source(4, width)),
            (2, 96, 32, source(5, width)),
            (3, 0, 32, source(6, width)),
            (3, 32, 32, source(7, width)),
        ),
        shares,
    )
    parts = 3 * width // tile

    def fetch(t):
        for r in range(2):
            at = ((t % 4) * 2 + r) * tile
            pltpu.make_async_copy(
                weight_hbm.at[r * rows : (r + 1) * rows, t * tile : (t + 1) * tile],
                act.at[:, at : at + tile],
                local_sems.at[10 + (t % 4) * 2 + r],
            ).start()

    def fetched(t):
        for r in range(2):
            at = ((t % 4) * 2 + r) * tile
            pltpu.make_async_copy(
                weight_hbm.at[r * rows : (r + 1) * rows, t * tile : (t + 1) * tile],
                act.at[:, at : at + tile],
                local_sems.at[10 + (t % 4) * 2 + r],
            ).wait()

    for t in range(4):
        fetch(t)
    for tick in late[:4]:
        tick()
    waits["first"]()
    for t in range(parts):
        fetched(t)
        for r in range(2):
            at = ((t % 4) * 2 + r) * tile
            half = token_out[:, r * tile : (r + 1) * tile]
            token_out[:, r * tile : (r + 1) * tile] = half + dot_columns(
                qkv[:, t * tile : (t + 1) * tile], act[:, at : at + tile]
            )
        if t + 4 < parts:
            fetch(t + 4)
    for i in range(2):
        raw[i] = token_out[i * (rows // 2) : (i + 1) * (rows // 2), :].astype(BF16)
    token_back = exchange([raw], [token_in], False, sender, spare + 2, local_sems, 18)
    for tick in main[16:] + late[4:]:
        tick()
    token_back()
    for i in range(2):
        token_out[i * (rows // 2) : (i + 1) * (rows // 2), :] = token_in[i].astype(F32)
    sender.drain(main + late)


def backward(operands, small_operands, shapes, rows, width, ff, lanes):
    shape = jax.ShapeDtypeStruct
    semaphores = 6 * REDUCE_SEMS + 16
    buffers = []
    for lead in ((2, PLANE), (LINE, PLANE), (LINE,), (LINE, 2), (LINE + 1,)):
        apart = shapes if lead != (2, PLANE) else [shapes[i] for i in (0, 1, 3, 5)]
        buffers += [pltpu.VMEM(lead + s, BF16) for s in apart]
    turned = pltpu.VMEM((PLANE, LINE, 2, 32, rows), BF16)
    piece = rows // 2
    scratch = buffers + [
        pltpu.VMEM((rows, ff), BF16),
        pltpu.VMEM((rows, width), BF16),
        pltpu.VMEM((rows, ff), BF16),
        pltpu.VMEM((rows, width), BF16),
        pltpu.VMEM((rows, lanes), BF16),
        pltpu.VMEM((2, piece, width), BF16),
        turned,
        turned,
        turned,
        pltpu.VMEM((rows, 3 * width), BF16),
        pltpu.VMEM((rows, 2 * width), BF16),
        pltpu.VMEM((rows, 2 * width), BF16),
        pltpu.VMEM((rows, width), BF16),
        pltpu.VMEM((rows, 128), F32),
        pltpu.VMEM((rows, 128), F32),
        pltpu.VMEM((8, ff), F32),
        pltpu.VMEM((PLANE, LINE, 2, 32, 128), BF16),
        pltpu.VMEM((4, rows, 128), F32),
        pltpu.VMEM((2, piece, width), BF16),
        pltpu.SemaphoreType.DMA((semaphores,)),
        pltpu.SemaphoreType.DMA((semaphores,)),
        pltpu.SemaphoreType.DMA((20,)),
    ]
    results = pl.pallas_call(
        backward_kernel,
        out_shape=[shape(s, F32) for s in shapes] + [shape((rows, width), F32)],
        in_specs=[hbm()] * len(operands) + [vmem()] * len(small_operands),
        out_specs=[vmem()] * 7,
        scratch_shapes=scratch,
        compiler_params=pltpu.CompilerParams(
            collective_id=2, has_side_effects=True, vmem_limit_bytes=67043328
        ),
        name="backward",
    )(*operands, *small_operands)
    return (results[:6], results[6])


def pair_tables(positions):
    cosine, sine = rotary_tables(positions)
    return (jnp.concatenate([cosine, cosine], axis=1), jnp.concatenate([sine, sine], axis=1))


def plane_device(
    tokens,
    segment_ids,
    project_weight,
    project_bias,
    output_weight,
    output_bias,
    first_gain,
    first_shift,
    up_weight,
    up_bias,
    down_weight,
    down_bias,
    second_gain,
    second_shift,
    embed_weight,
    out_cotangent,
    embed_cotangent,
):
    width = HEADS * HEAD_DIM
    piece = tokens.shape[2]
    rows = 2 * piece
    group = lax.axis_index("group")
    core = lax.rem(lax.axis_index("wide"), 2)
    lanes = embed_weight.shape[1]
    embed_rows = embed_weight.shape[0]
    small = None
    for row, lane, vector in (
        (0, 0, project_bias),
        (1, 0, up_bias),
        (2, 0, output_bias),
        (2, 32, first_gain),
        (2, 64, first_shift),
        (2, 96, down_bias),
        (3, 0, second_gain),
        (3, 32, second_shift),
    ):
        size = vector.shape[0]
        part = jnp.pad(
            vector.astype(F32)[None, :], ((row, 31 - row), (lane, lanes - lane - size))
        )
        small = part if small is None else small + part
    place_of = jnp.arange(rows)
    cosine, sine = pair_tables((core * rows + place_of).astype(F32))
    far_cosine, far_sine = pair_tables(((1 - core) * rows + place_of).astype(F32))
    (
        project_full, token_rows, qkv, far_kv, context_low, norms, hidden_low, act_low, up_grad,
        down_grad, result_low, embed_cot, branch_grad, context_grad, first_grad, sums, ids,
        layer_out, embed_out,
    ) = forward(
        [project_weight, embed_weight, small.astype(BF16), output_weight, up_weight, down_weight],
        [tokens[:, 0], out_cotangent[:, 0], embed_cotangent[:, 0]],
        segment_ids[:, 0],
        (cosine, sine),
        up_weight.shape[1],
    )
    shapes = [
        down_weight.shape,
        up_weight.shape,
        output_weight.shape,
        embed_weight.shape,
        project_weight.shape,
        small.shape,
    ]
    outs, token_grad = backward(
        (
            act_low, down_grad, hidden_low.reshape(2, piece, width), up_grad,
            context_low.reshape(2, piece, width), branch_grad, result_low,
            embed_cot.reshape(rows, lanes), token_rows, qkv, far_kv, context_grad, first_grad,
            project_full.reshape(width, 3 * width),
        ),
        (norms, ids, sums, cosine, sine, far_cosine, far_sine),
        shapes,
        rows,
        width,
        up_weight.shape[1],
        lanes,
    )
    down_out, up_out, output_out, embed_grad_out, project_out, small_out = outs
    return (
        layer_out[:, None],
        embed_out[:, None],
        token_grad.reshape(2, 1, piece, width),
        project_out,
        small_out[0, : project_bias.shape[0]],
        output_out,
        small_out[2, 0:32],
        small_out[2, 32:64],
        small_out[2, 64:96],
        up_out,
        small_out[1, : up_bias.shape[0]],
        down_out,
        small_out[2, 96:128],
        small_out[3, 0:32],
        small_out[3, 32:64],
        embed_grad_out,
    )


def choose_device(mesh):
    if mesh.shape["group"] == PLANE and mesh.shape["wide"] == 2 * LINE:
        return plane_device
    return general_device


def solution(mesh):
    in_specs = (
        P(None, "wide", "group", None),
        P(None, "wide", None),
        P(("group", "wide"), None),
        P(("group", "wide")),
        P(("group", "wide"), None),
        P(("group", "wide")),
        P(("group", "wide")),
        P(("group", "wide")),
        P(("group", "wide"), None),
        P(("group", "wide")),
        P(("group", "wide"), None),
        P(("group", "wide")),
        P(("group", "wide")),
        P(("group", "wide")),
        P(("group", "wide"), None),
        P(None, "wide", "group", None),
        P(None, "wide", "group", None),
    )
    out_specs = (
        P(None, "wide", "group", None),
        P(None, "wide", "group", None),
        P(None, "wide", "group", None),
        P(("group", "wide"), None),
        P(("group", "wide")),
        P(("group", "wide"), None),
        P(("group", "wide")),
        P(("group", "wide")),
        P(("group", "wide")),
        P(("group", "wide"), None),
        P(("group", "wide")),
        P(("group", "wide"), None),
        P(("group", "wide")),
        P(("group", "wide")),
        P(("group", "wide")),
        P(("group", "wide"), None),
    )
    return jax.shard_map(
        choose_device(mesh), mesh=mesh, in_specs=in_specs, out_specs=out_specs, check_vma=False
    )
```

```python
import functools

import jax
import jax.numpy as jnp
from jax import lax
from jax.experimental import pallas as pl
from jax.experimental.pallas import tpu as pltpu
from jax.sharding import PartitionSpec as P

HEADS = 16
HEAD_DIM = 64


eps_norm = 1e-05
neg_large = -1e30


def rotary_tables(positions):
    half_dim = HEAD_DIM // 2
    frequency = 10000.0 ** (-jnp.arange(half_dim, dtype=jnp.float32) * (2.0 / HEAD_DIM))
    angles = positions[:, None] * frequency[None, :]
    angles = jnp.concatenate([angles, angles], axis=1)
    return (jnp.cos(angles), jnp.sin(angles))


def rotate(values, cosine_table, sine_table):
    half_dim = HEAD_DIM // 2
    swapped = jnp.concatenate([-values[..., half_dim:], values[..., :half_dim]], axis=-1)
    return values * cosine_table[:, None, :] + swapped * sine_table[:, None, :]


def unrotate(grads, cosine_table, sine_table):
    half_dim = HEAD_DIM // 2
    scaled = grads * sine_table[:, None, :]
    swapped = jnp.concatenate([scaled[..., half_dim:], -scaled[..., :half_dim]], axis=-1)
    return grads * cosine_table[:, None, :] + swapped


def norm_forward(resid, gain, shift):
    center = resid - jnp.mean(resid, axis=-1, keepdims=True)
    spread = jnp.mean(center * center, axis=-1, keepdims=True)
    rstd_rows = lax.rsqrt(spread + eps_norm)
    normed = center * rstd_rows
    return (normed * gain + shift, normed, rstd_rows)


def norm_backward(grads, normed, rstd_rows, gain):
    scaled = grads * gain
    resid_grad = rstd_rows * (
        scaled
        - jnp.mean(scaled, axis=-1, keepdims=True)
        - normed * jnp.mean(scaled * normed, axis=-1, keepdims=True)
    )
    return (resid_grad, jnp.sum(grads * normed, axis=0), jnp.sum(grads, axis=0))


def contract_rows(left, right):
    return lax.dot_general(
        left, right, (((0,), (0,)), ((), ())), preferred_element_type=jnp.float32
    )


def times_transpose(left, right):
    return lax.dot_general(
        left, right, (((1,), (1,)), ((), ())), preferred_element_type=jnp.float32
    )


def gelu_slope(value):
    normal_cdf = 0.5 * (1.0 + lax.erf(value * 0.7071067811865476))
    density = jnp.exp(-0.5 * value * value) * 0.3989422804014327
    return normal_cdf + value * density


def key_blocks(kv_rows, seg_all):
    seq_len = kv_rows.shape[0]
    block_rows = min(512, seq_len)
    count = seq_len // block_rows
    return (
        kv_rows.reshape(count, block_rows, 2, HEADS, HEAD_DIM),
        seg_all.reshape(count, block_rows),
    )


def block_scores(queries, key_block, same):
    scores = jnp.einsum("qhd,khd->hqk", queries, key_block, preferred_element_type=jnp.float32)
    scores = scores * HEAD_DIM ** (-0.5)
    return jnp.where(same[None], scores, neg_large)


def attention_forward(queries, blocks, seg_blocks, seg_local):
    length = queries.shape[0]

    def norm_step(carry, pieces):
        kv_block, seg_block = pieces
        same = seg_local[:, None] == seg_block[None, :]

        def norm_update(running):
            run_max, run_sum = running
            scores = block_scores(queries, kv_block[:, 0], same)
            new_max = jnp.maximum(run_max, jnp.max(scores, axis=-1))
            new_sum = run_sum * jnp.exp(run_max - new_max) + jnp.sum(
                jnp.exp(scores - new_max[..., None]), axis=-1
            )
            return (new_max, new_sum)

        def norm_unchanged(running):
            return running

        return (lax.cond(jnp.any(same), norm_update, norm_unchanged, carry), None)

    start = (
        jnp.full((HEADS, length), neg_large, jnp.float32),
        jnp.zeros((HEADS, length), jnp.float32),
    )
    (run_max, run_sum), unused = lax.scan(norm_step, start, (blocks, seg_blocks))
    log_norm = run_max + jnp.log(run_sum)

    def value_step(total, pieces):
        kv_block, seg_block = pieces
        same = seg_local[:, None] == seg_block[None, :]

        def value_update(running):
            scores = block_scores(queries, kv_block[:, 0], same)
            weights = jnp.exp(scores - log_norm[..., None]).astype(jnp.bfloat16)
            return running + jnp.einsum(
                "hqk,khd->qhd", weights, kv_block[:, 1], preferred_element_type=jnp.float32
            )

        def value_unchanged(running):
            return running

        return (lax.cond(jnp.any(same), value_update, value_unchanged, total), None)

    context, unused = lax.scan(
        value_step, jnp.zeros(queries.shape, jnp.float32), (blocks, seg_blocks)
    )
    return (context, log_norm)


def attention_backward(queries, blocks, seg_blocks, seg_local, log_norm, context_grad, delta):

    def grad_step(query_grad, pieces):
        kv_block, seg_block = pieces
        same = seg_local[:, None] == seg_block[None, :]

        def work(running):
            scores = block_scores(queries, kv_block[:, 0], same)
            probs = jnp.exp(scores - log_norm[..., None])
            prob_grad = jnp.einsum(
                "qhd,khd->hqk", context_grad, kv_block[:, 1], preferred_element_type=jnp.float32
            )
            score_grad = (probs * (prob_grad - delta[..., None])).astype(jnp.bfloat16)
            running = running + jnp.einsum(
                "hqk,khd->qhd", score_grad, kv_block[:, 0], preferred_element_type=jnp.float32
            ) * HEAD_DIM ** (-0.5)
            prob_low = probs.astype(jnp.bfloat16)
            key_grad = jnp.einsum(
                "hqk,qhd->khd", score_grad, queries, preferred_element_type=jnp.float32
            ) * HEAD_DIM ** (-0.5)
            value_grad = jnp.einsum(
                "hqk,qhd->khd", prob_low, context_grad, preferred_element_type=jnp.float32
            )
            return (running, jnp.stack([key_grad, value_grad], axis=1))

        def skipped(running):
            return (running, jnp.zeros(kv_block.shape, jnp.float32))

        return lax.cond(jnp.any(same), work, skipped, query_grad)

    query_grad, kv_grad = lax.scan(
        grad_step, jnp.zeros(queries.shape, jnp.float32), (blocks, seg_blocks)
    )
    return (query_grad, kv_grad.reshape(-1, 2 * HEADS * HEAD_DIM))


def general_device(
    tokens,
    segment_ids,
    project_weight,
    project_bias,
    output_weight,
    output_bias,
    first_gain,
    first_shift,
    up_weight,
    up_bias,
    down_weight,
    down_bias,
    second_gain,
    second_shift,
    embed_weight,
    out_cotangent,
    embed_cotangent,
):
    shards = (
        project_weight,
        project_bias,
        output_weight,
        output_bias,
        first_gain,
        first_shift,
        up_weight,
        up_bias,
        down_weight,
        down_bias,
        second_gain,
        second_shift,
        embed_weight,
    )
    length = tokens.shape[2]
    width = HEADS * HEAD_DIM
    head_shape = (length, HEADS, HEAD_DIM)
    place = lax.axis_index("group")
    positions = (place * length + jnp.arange(length)).astype(jnp.float32)
    cosine_table, sine_table = rotary_tables(positions)
    grad_total = None
    results = []
    embeddings = []
    input_grads = []
    for micro_index in range(tokens.shape[0]):
        params = (
            lax.all_gather(shards[0], ("group", "wide"), axis=0, tiled=True),
            lax.all_gather(shards[1], ("group", "wide"), axis=0, tiled=True),
            lax.all_gather(shards[2], ("group", "wide"), axis=0, tiled=True),
            lax.all_gather(shards[3], ("group", "wide"), axis=0, tiled=True),
            lax.all_gather(shards[4], ("group", "wide"), axis=0, tiled=True),
            lax.all_gather(shards[5], ("group", "wide"), axis=0, tiled=True),
            lax.all_gather(shards[6], ("group", "wide"), axis=0, tiled=True),
            lax.all_gather(shards[7], ("group", "wide"), axis=0, tiled=True),
            lax.all_gather(shards[8], ("group", "wide"), axis=0, tiled=True),
            lax.all_gather(shards[9], ("group", "wide"), axis=0, tiled=True),
            lax.all_gather(shards[10], ("group", "wide"), axis=0, tiled=True),
            lax.all_gather(shards[11], ("group", "wide"), axis=0, tiled=True),
            lax.all_gather(shards[12], ("group", "wide"), axis=0, tiled=True),
        )
        seg_all = segment_ids[micro_index, 0]
        seg_local = lax.dynamic_slice_in_dim(seg_all, place * length, length)
        token_low = tokens[micro_index, 0]
        token_wide = token_low.astype(jnp.float32)
        projected = jnp.dot(token_low, params[0], preferred_element_type=jnp.float32) + params[
            1
        ].astype(jnp.float32)
        queries = rotate(projected[:, :width].reshape(head_shape), cosine_table, sine_table).astype(
            jnp.bfloat16
        )
        key_rows = rotate(
            projected[:, width : 2 * width].reshape(head_shape), cosine_table, sine_table
        ).astype(jnp.bfloat16)
        value_rows = projected[:, 2 * width :].astype(jnp.bfloat16)
        local_kv = jnp.concatenate([key_rows.reshape(length, width), value_rows], axis=1)
        kv_all = lax.all_gather(local_kv, "group", axis=0, tiled=True)
        blocks, seg_blocks = key_blocks(kv_all, seg_all)
        context, log_norm = attention_forward(queries, blocks, seg_blocks, seg_local)
        context_low = context.reshape(length, width).astype(jnp.bfloat16)
        branch = jnp.dot(context_low, params[2], preferred_element_type=jnp.float32) + params[
            3
        ].astype(jnp.float32)
        first_gain_wide = params[4].astype(jnp.float32)
        hidden, first_normed, first_rstd = norm_forward(
            token_wide + branch, first_gain_wide, params[5].astype(jnp.float32)
        )
        hidden_low = hidden.astype(jnp.bfloat16)
        up_value = jnp.dot(hidden_low, params[6], preferred_element_type=jnp.float32) + params[
            7
        ].astype(jnp.float32)
        act_low = jax.nn.gelu(up_value, approximate=False).astype(jnp.bfloat16)
        down_value = jnp.dot(act_low, params[8], preferred_element_type=jnp.float32) + params[
            9
        ].astype(jnp.float32)
        second_gain_wide = params[10].astype(jnp.float32)
        result, second_normed, second_rstd = norm_forward(
            hidden + down_value, second_gain_wide, params[11].astype(jnp.float32)
        )
        result_low = result.astype(jnp.bfloat16)
        embedded = jnp.dot(result_low, params[12], preferred_element_type=jnp.float32)
        results.append(result_low)
        embeddings.append(embedded.astype(jnp.bfloat16))
        params = (
            lax.all_gather(shards[0], ("group", "wide"), axis=0, tiled=True),
            lax.all_gather(shards[1], ("group", "wide"), axis=0, tiled=True),
            lax.all_gather(shards[2], ("group", "wide"), axis=0, tiled=True),
            lax.all_gather(shards[3], ("group", "wide"), axis=0, tiled=True),
            lax.all_gather(shards[4], ("group", "wide"), axis=0, tiled=True),
            lax.all_gather(shards[5], ("group", "wide"), axis=0, tiled=True),
            lax.all_gather(shards[6], ("group", "wide"), axis=0, tiled=True),
            lax.all_gather(shards[7], ("group", "wide"), axis=0, tiled=True),
            lax.all_gather(shards[8], ("group", "wide"), axis=0, tiled=True),
            lax.all_gather(shards[9], ("group", "wide"), axis=0, tiled=True),
            lax.all_gather(shards[10], ("group", "wide"), axis=0, tiled=True),
            lax.all_gather(shards[11], ("group", "wide"), axis=0, tiled=True),
            lax.all_gather(shards[12], ("group", "wide"), axis=0, tiled=True),
        )
        embed_cot = embed_cotangent[micro_index, 0]
        result_grad = out_cotangent[micro_index, 0].astype(jnp.float32) + times_transpose(
            embed_cot, params[12]
        )
        embed_weight_grad = contract_rows(result_low, embed_cot)
        sum_grad, second_gain_grad, second_shift_grad = norm_backward(
            result_grad, second_normed, second_rstd, second_gain_wide
        )
        down_grad = sum_grad.astype(jnp.bfloat16)
        down_bias_grad = jnp.sum(down_grad.astype(jnp.float32), axis=0)
        down_weight_grad = contract_rows(act_low, down_grad)
        up_grad = (times_transpose(down_grad, params[8]) * gelu_slope(up_value)).astype(
            jnp.bfloat16
        )
        up_bias_grad = jnp.sum(up_grad.astype(jnp.float32), axis=0)
        up_weight_grad = contract_rows(hidden_low, up_grad)
        hidden_grad = sum_grad + times_transpose(up_grad, params[6])
        first_grad, first_gain_grad, first_shift_grad = norm_backward(
            hidden_grad, first_normed, first_rstd, first_gain_wide
        )
        branch_grad = first_grad.astype(jnp.bfloat16)
        output_bias_grad = jnp.sum(branch_grad.astype(jnp.float32), axis=0)
        output_weight_grad = contract_rows(context_low, branch_grad)
        context_grad = (
            times_transpose(branch_grad, params[2]).astype(jnp.bfloat16).reshape(head_shape)
        )
        delta = jnp.transpose(jnp.sum(context_grad.astype(jnp.float32) * context, axis=-1))
        kv_again = lax.all_gather(local_kv, "group", axis=0, tiled=True)
        blocks, seg_blocks = key_blocks(kv_again, seg_all)
        query_grad, kv_partial = attention_backward(
            queries, blocks, seg_blocks, seg_local, log_norm, context_grad, delta
        )
        kv_grad = lax.psum_scatter(
            kv_partial.astype(jnp.bfloat16), "group", scatter_dimension=0, tiled=True
        ).astype(jnp.float32)
        key_part = kv_grad[:, :width].reshape(head_shape)
        value_part = kv_grad[:, width:]
        query_back = unrotate(query_grad, cosine_table, sine_table).reshape(length, width)
        key_back = unrotate(key_part, cosine_table, sine_table).reshape(length, width)
        projected_grad = jnp.concatenate([query_back, key_back, value_part], axis=1).astype(
            jnp.bfloat16
        )
        project_bias_grad = jnp.sum(projected_grad.astype(jnp.float32), axis=0)
        project_weight_grad = contract_rows(token_low, projected_grad)
        input_grads.append(first_grad + times_transpose(projected_grad, params[0]))
        local_grads = (
            project_weight_grad,
            project_bias_grad,
            output_weight_grad,
            output_bias_grad,
            first_gain_grad,
            first_shift_grad,
            up_weight_grad,
            up_bias_grad,
            down_weight_grad,
            down_bias_grad,
            second_gain_grad,
            second_shift_grad,
            embed_weight_grad,
        )
        summed = (
            lax.psum_scatter(local_grads[0], ("group", "wide"), scatter_dimension=0, tiled=True),
            lax.psum_scatter(local_grads[1], ("group", "wide"), scatter_dimension=0, tiled=True),
            lax.psum_scatter(local_grads[2], ("group", "wide"), scatter_dimension=0, tiled=True),
            lax.psum_scatter(local_grads[3], ("group", "wide"), scatter_dimension=0, tiled=True),
            lax.psum_scatter(local_grads[4], ("group", "wide"), scatter_dimension=0, tiled=True),
            lax.psum_scatter(local_grads[5], ("group", "wide"), scatter_dimension=0, tiled=True),
            lax.psum_scatter(local_grads[6], ("group", "wide"), scatter_dimension=0, tiled=True),
            lax.psum_scatter(local_grads[7], ("group", "wide"), scatter_dimension=0, tiled=True),
            lax.psum_scatter(local_grads[8], ("group", "wide"), scatter_dimension=0, tiled=True),
            lax.psum_scatter(local_grads[9], ("group", "wide"), scatter_dimension=0, tiled=True),
            lax.psum_scatter(local_grads[10], ("group", "wide"), scatter_dimension=0, tiled=True),
            lax.psum_scatter(local_grads[11], ("group", "wide"), scatter_dimension=0, tiled=True),
            lax.psum_scatter(local_grads[12], ("group", "wide"), scatter_dimension=0, tiled=True),
        )
        grad_total = (
            summed
            if grad_total is None
            else tuple((total + part for total, part in zip(grad_total, summed)))
        )
    layer_out = jnp.stack(results)[:, None]
    embed_out = jnp.stack(embeddings)[:, None]
    token_grad = jnp.stack(input_grads)[:, None]
    return (
        layer_out,
        embed_out,
        token_grad,
        grad_total[0],
        grad_total[1],
        grad_total[2],
        grad_total[3],
        grad_total[4],
        grad_total[5],
        grad_total[6],
        grad_total[7],
        grad_total[8],
        grad_total[9],
        grad_total[10],
        grad_total[11],
        grad_total[12],
    )


MESH = pl.DeviceIdType.MESH
F32 = jnp.float32
BF16 = jnp.bfloat16
PLANE = 4
LINE = 4
GATHER_SEMS = 42
REDUCE_SEMS = 56
MAIN_AHEAD = (1, 3, 5)
LATE_AHEAD = (1, 2, 3)
FORWARD_PARTS = ((True, ((0, 0, 4, 0, 2, ), (1, 0, 4, 0, 4, ), (2, 0, 4, 0, 4, ), ), ), (False, ((0, 0, 4, 2, 4, ), ), ), (True, ((3, 0, 4, 0, 4, ), ), ), (True, ((4, 0, 4, 0, 4, ), ), ), (False, ((5, 0, 2, 0, 4, ), ), ), (True, ((5, 2, 4, 0, 4, ), ), ), )
FORWARD_STEPS = (((1003, 1, 1002, 20005, 2001, 0, 3, 2, 2000, 3001, 41, 1202, 10, 12, 4002, 42, 1103, 2041, 23, 2010, 2003, 3000, 2012, 20003, 1401, 3003, 2023, 51, 3041, 20, 2043, 1404, 2020, 20002, 52, 33, 1400, 53, 43, 113, 2013, 2033, 2052, 2032, 32, 3012, 1410, 1441, 4003, 222, 62, 202, 2042, 3010, 153, 2212, 143, 3002, 103, 2222, 4103, 63, 22, 133, 242, 252, 1424, 1451, 2051, 2002, 232, 3051, 2113, 4202, 1420, 262, 2232, 2133, 1414, 13, 2143, 3113, 163, 123, 1444, 5001, 3103, 3020, 1454, 212, 5002, 3023, 3053, 354, 2022, 2242, 2314, 334, 2053, 4401, 21005, 2334, 324, 344, 3052, 3013, 1464, 1434, 5000, 314, 304, 4400, 2103, 3202, 364, 900, 1900, 2062, 20900, 2153, ), ), ((), ), ((3033, 2202, 2252, ), (), (2123, ), (23004, 3063, 3032, 2063, 3043, ), (3042, ), (3153, 2344, 5010, 5041, 23900, ), ), ((3252, 5043, 5053, 5052, 4441, 3062, 3022, 2304, ), (5013, 5022, 3212, 5023, 4410, ), (3133, 2163, 3304, 3242, 3232, 3222, ), (3143, ), (5051, 3163, 2354, 5020, 3123, 2262, 2324, 21003, 5012, 5042, 3354, ), (3262, 5153, 4404, ), (3334, 3314, 5242, 5063, 4451, 5032, 5033, 2364, ), (4414, 3324, 2900, 3344, 21002, 5062, 4420, 5003, 3364, ), ), ((), (5143, 5113, 3900, 4454, 5232, 5222, 5212, ), ), ((4424, 5133, 5123, 5252, ), (), (4464, ), (5202, 4434, 5103, 5334, 5344, 5262, 5163, ), (4444, 5314, 5324, ), (5304, 5364, 5354, ), (), (4900, 5900, 21900, ), ), ((), (22003, 22005, ), ), ((), (), (), (), (22002, ), (), (), (), ), ((), (22900, ), ), )


def place():
    group = lax.axis_index("group")
    wide = lax.axis_index("wide")
    return (group, lax.rem(group, 2), group // 2, wide // 2, lax.rem(wide, 2))


def when(cond, act):
    if cond is True:
        act()
    else:
        pl.when(cond)(act)


def both(left, right):
    return right if left is True else jnp.logical_and(left, right)


def remote(src, dst, send_sem, recv_sem, device):
    return pltpu.make_async_remote_copy(
        src_ref=src,
        dst_ref=dst,
        send_sem=send_sem,
        recv_sem=recv_sem,
        device_id=device,
        device_id_type=MESH,
    )


def entry_barrier():
    g, x, y, z, c = place()
    devices = []
    for step in range(1, 8):
        other = lax.rem(g * 2 + c + step, 8)
        devices.append((other // 2, z * 2 + lax.rem(other, 2)))
    devices.append((g, lax.rem(z + 1, LINE) * 2 + c))
    devices.append((g, lax.rem(z + LINE - 1, LINE) * 2 + c))
    barrier = pltpu.get_barrier_semaphore()
    for device in devices:
        pl.semaphore_signal(barrier, inc=1, device_id=device, device_id_type=MESH)
    pl.semaphore_wait(barrier, len(devices))


class Sender:
    def __init__(self, send_sems, recv_sems):
        self.send_sems, self.recv_sems = send_sems, recv_sems
        self.pending, self.draining = [], False

    def copy(self, src, dst, index, device):
        return remote(src, dst, self.send_sems.at[index], self.recv_sems.at[index], device)

    def send(self, cond, src, dst, index, device):
        copy = self.copy(src, dst, index, device)
        when(cond, copy.wait_send if self.draining else copy.start)

    def post(self, cond, src, dst, index, device):
        self.send(cond, src, dst, index, device)
        self.pending.append((cond, src, dst, index, device))

    def land(self, ref, index, device):
        self.copy(ref, ref, index, device).wait_recv()

    def do(self, cond, act):
        if not self.draining:
            when(cond, act)

    def drain(self, ticks):
        self.draining = True
        for tick in ticks:
            tick()
        for call in self.pending:
            self.send(*call)


def near_items(z, distance):
    if distance == 0:
        return [(0, z, True)]
    return [
        (distance, jnp.maximum(z - distance, 0), z >= distance),
        (3 + distance, jnp.minimum(z + distance, LINE - 1), z + distance < LINE),
    ]


class Gather:
    def __init__(self, parts, sender, local_sems):
        self.parts, self.sender, self.local_sems = parts, sender, local_sems
        self.seen = set()
        g, x, y, z, c = place()
        self.g, self.z, self.c = g, z, c
        self.gx, self.gy, self.gd = g + 1 - 2 * x, g + 2 - 4 * y, 3 - g
        self.devices = (
            (g, jnp.minimum(z + 1, LINE - 1) * 2 + c),
            (g, jnp.maximum(z - 1, 0) * 2 + c),
            (self.gx, z * 2 + c),
            (self.gy, z * 2 + c),
            (g, z * 2 + 1 - c),
        )
        for part in parts:
            for member in part[1]:
                self.own(member).start()

    def window(self, member, g, zi, c, rows=None):
        shard, full, top, count, left, columns, index = member
        first, last = (0, count) if rows is None else rows
        return full.at[g, zi, c, top + first : top + last, left : left + columns]

    def shard(self, member):
        shard, full, top, count, left, columns, index = member
        return shard.at[top : top + count, left : left + columns]

    def own(self, member):
        return pltpu.make_async_copy(
            self.shard(member),
            self.window(member, self.g, self.z, self.c),
            self.local_sems.at[member[6]],
        )

    def ring(self, member, zi, c):
        shard, full, top, count, left, columns, index = member
        return full.at[:, zi, c, top : top + count, left : left + columns]

    def item(self, slot):
        z = self.z
        if slot == 0:
            return z, True
        if slot < 4:
            return jnp.maximum(z - slot, 0), z >= slot
        return jnp.minimum(z + slot - 3, LINE - 1), z + slot - 3 < LINE

    def land(self, cond, ref, index):
        self.sender.do(cond, lambda: self.sender.land(ref, index, self.devices[4]))

    def arrivals(self, part, event, slot):
        zi, cond = self.item(slot)
        line = self.parts[part][0]
        for member in self.parts[part][1]:
            base, half, rows = member[6] * GATHER_SEMS, member[3] // 2, member[3]
            diagonal = lambda: (
                self.land(cond, self.window(member, self.gd, zi, self.c, (0, half)), base + 21 + slot),
                self.land(cond, self.window(member, self.gd, zi, self.c, (half, rows)), base + 28 + slot),
            )
            if event == 0 and slot > 0:
                self.land(cond, self.window(member, self.g, zi, self.c), base + slot)
            elif event == 1:
                self.land(cond, self.window(member, self.gx, zi, self.c), base + 7 + slot)
            elif event == 2:
                self.land(cond, self.window(member, self.gy, zi, self.c), base + 14 + slot)
            elif event == 3 or (event == 4 and slot == 0):
                diagonal()
                if slot == 0:
                    self.sender.do(True, lambda: self.own(member).wait())
            elif event == 4:
                self.land(cond, self.ring(member, zi, self.c), base + slot)

    def step(self, part, event, slot, link):
        if (part, event, slot) not in self.seen:
            self.seen.add((part, event, slot))
            self.arrivals(part, event, slot)
        zi, cond = self.item(slot)
        z, device = self.z, self.devices[link]
        for member in self.parts[part][1]:
            base, half, rows = member[6] * GATHER_SEMS, member[3] // 2, member[3]
            if link == 0:
                cond_here, index = both(cond, z < LINE - 1), base + slot + 1
            elif link == 1:
                cond_here, index = both(cond, z > 0), base + (4 if slot == 0 else slot + 1)
            else:
                cond_here = cond
                index = base + slot + ({2: 7, 3: 14} if event == 0 else {3: 21, 2: 28, 4: 35})[link]
            if event == 0:
                target = self.window(member, self.g, zi, self.c)
                source = self.shard(member) if slot == 0 else target
            elif event == 1:
                source = target = self.window(member, self.gx, zi, self.c, (0, half))
            elif event == 2:
                source = target = self.window(member, self.gy, zi, self.c, (half, rows))
            else:
                source = target = self.ring(member, zi, self.c)
            self.sender.send(cond_here, source, target, index, device)

    def finish(self, part):
        for member in self.parts[part][1]:
            for slot in range(7):
                zi, cond = self.item(slot)
                self.land(cond, self.ring(member, zi, 1 - self.c), member[6] * GATHER_SEMS + 35 + slot)


def staged(order, stages, delays):
    ticks = []
    for t in range(len(order) + delays[-1]):

        def tick(t=t):
            for stage, delay in zip(stages, delays):
                if 0 <= t - delay < len(order):
                    stage(*order[t - delay])

        ticks.append(tick)
    return ticks


def add_into(target, terms):
    rows, columns = target.shape
    step = min(columns, 512)

    def body(i, carry):
        cut = pl.ds(pl.multiple_of(i * step, step), step)
        value = terms[0][:, cut].astype(F32)
        for term in terms[1:]:
            value = value + term[:, cut].astype(F32)
        target[:, cut] = value.astype(target.dtype)
        return carry

    lax.fori_loop(0, columns // step, body, 0)


class Exchange:
    def __init__(self, sources, targets, outward, sender, base, local_sems, local_base):
        self.sources, self.targets, self.outward = sources, targets, outward
        self.sender, self.base = sender, base
        self.local_sems, self.local_base = local_sems, local_base
        self.started = False
        g, x, y, z, c = place()
        self.g, self.z, self.c = g, z, c
        self.neighbours = {2: g + 1 - 2 * x, 3: g + 2 - 4 * y, 5: 3 - g}

    def device(self, index, outward):
        g, z, c = self.g, self.z, self.c
        if outward:
            return (index * 2 + c, z * 2 + g // 2)
        return (2 * c + index, z * 2 + lax.rem(g, 2))

    def same(self, device):
        return jnp.logical_and(device[0] == self.g, device[1] == self.z * 2 + self.c)

    def local(self, i, index, slot):
        return pltpu.make_async_copy(
            self.sources[i].at[index],
            self.targets[i].at[slot],
            self.local_sems.at[self.local_base + i],
        )

    def step(self, link):
        slot = lax.rem(self.g, 2) if self.outward else self.g // 2
        first = not self.started and not self.sender.draining
        self.started = True
        for i in range(len(self.sources)):
            for index in range(2):
                device = self.device(index, self.outward)
                if first:
                    when(self.same(device), lambda: self.local(i, index, slot).start())
                copy = remote(
                    self.sources[i].at[index],
                    self.targets[i].at[slot],
                    self.sender.send_sems.at[self.base + i * 4 + 2 + index],
                    self.sender.recv_sems.at[self.base + i * 4 + slot],
                    device,
                )
                cond = device[0] == self.neighbours[link]
                if link == 2:
                    here = jnp.logical_and(device[0] == self.g, device[1] != self.z * 2 + self.c)
                    cond = jnp.logical_or(cond, here)
                when(cond, copy.wait_send if self.sender.draining else copy.start)

    def arrive(self):
        for i in range(len(self.sources)):
            for index in range(2):
                device = self.device(index, not self.outward)
                target = self.targets[i].at[index]
                when(self.same(device), lambda: self.local(i, index, index).wait())
                when(
                    jnp.logical_not(self.same(device)),
                    lambda: self.sender.land(
                        target, self.base + i * 4 + index, (self.g, self.z * 2 + 1 - self.c)
                    ),
                )


def hbm():
    return pl.BlockSpec(memory_space=pltpu.HBM)


def vmem():
    return pl.BlockSpec(memory_space=pltpu.VMEM)


def chain(*ticks):
    def act():
        for tick in ticks:
            tick()

    return act


def run_with(ticks, steps, body):
    def act(i, carry):
        body(i)
        for j, tick in enumerate(ticks[:steps]):
            pl.when(i == j)(tick)
        return carry

    lax.fori_loop(0, steps, act, 0)
    for tick in ticks[steps:]:
        tick()


def lane_half(shape, period, half):
    lanes = lax.broadcasted_iota(jnp.int32, shape, 1)
    return lax.rem(lanes, period) < half


def turn(values):
    first = lane_half(values.shape, HEAD_DIM, HEAD_DIM // 2)
    return jnp.where(
        first,
        -pltpu.roll(values, values.shape[1] - HEAD_DIM // 2, 1),
        pltpu.roll(values, HEAD_DIM // 2, 1),
    )


def dot_rows(left, right):
    return lax.dot_general(left, right, (((1,), (0,)), ((), ())), preferred_element_type=F32)


def dot_columns(left, right):
    return lax.dot_general(left, right, (((1,), (1,)), ((), ())), preferred_element_type=F32)


def attend_pair(
    query_ref, key_ref, value_ref, far_key_ref, far_value_ref, seg_ref, seg_near_ref, seg_far_ref, out_ref, norm_ref
):
    rows = query_ref.shape[0]
    first = lane_half((rows, 128), 128, HEAD_DIM)
    tile = 256
    for r in range(rows // tile):
        rs = pl.ds(r * tile, tile)
        query = query_ref[rs, :]
        low_half = first[:tile]
        seg = seg_ref[rs, 0:1]
        near, far = seg == seg_near_ref[...], seg == seg_far_ref[...]
        outs, norms = [], []
        for h in range(2):
            keep = low_half if h == 0 else jnp.logical_not(low_half)
            one = jnp.where(keep, query, jnp.zeros_like(query))
            near_scores = jnp.where(near, dot_columns(one, key_ref[...]), neg_large)
            far_scores = jnp.where(far, dot_columns(one, far_key_ref[...]), neg_large)
            top = jnp.maximum(
                jnp.max(near_scores, axis=1, keepdims=True), jnp.max(far_scores, axis=1, keepdims=True)
            )
            near_expon, far_expon = jnp.exp(near_scores - top), jnp.exp(far_scores - top)
            total = jnp.sum(near_expon, axis=1, keepdims=True) + jnp.sum(
                far_expon, axis=1, keepdims=True
            )
            mixed = dot_rows(near_expon.astype(BF16), value_ref[...]) + dot_rows(
                far_expon.astype(BF16), far_value_ref[...]
            )
            outs.append(mixed / total)
            norms.append(jnp.broadcast_to(top + jnp.log(total), (tile, 128)))
        out_ref[rs, :] = jnp.where(low_half, outs[0], outs[1]).astype(BF16)
        flipped = jnp.transpose(jnp.where(low_half, norms[0], norms[1]))
        norm_ref[0:1, rs] = flipped[0:1]
        norm_ref[1:2, rs] = flipped[HEAD_DIM : HEAD_DIM + 1]


def stretch(packed, vectors, sizes):
    shards = packed.shape[0] // 32
    for row, lane, size, target in vectors:
        pick_rows = lax.broadcasted_iota(jnp.int32, (shards, shards * 32), 0) * 32 + row
        pick = lax.broadcasted_iota(jnp.int32, (shards, shards * 32), 1) == pick_rows
        part = dot_rows(pick.astype(F32).astype(BF16), packed).astype(BF16)
        step = 1024

        def body(i, carry):
            at = pl.multiple_of(i * step, step)
            column = (lax.broadcasted_iota(jnp.int32, (1, step), 1) + i * step).astype(F32)
            shard = jnp.floor((column + 0.5) * (1.0 / size))
            lane_of = (column - shard * size + lane).astype(jnp.int32)
            spread = lax.broadcasted_iota(jnp.int32, (128, step), 0) == lane_of
            value = dot_rows(part, spread.astype(F32).astype(BF16))
            keep = lax.broadcasted_iota(jnp.int32, (shards, step), 0) == shard.astype(jnp.int32)
            target[:, pl.ds(at, step)] = jnp.sum(jnp.where(keep, value, 0.0), axis=0, keepdims=True)
            return carry

        lax.fori_loop(0, shards * size // step, body, 0)


def flat(value):
    return value.reshape(-1, value.shape[-1])


def row_mean(value):
    return jnp.mean(value, axis=1, keepdims=True)


def forward_kernel(*refs):
    shards, refs = refs[:6], refs[6:]
    (tokens, out_cot, embed_cot, segments, cosine, sine), refs = refs[:6], refs[6:]
    (
        project_out, token_out, qkv_out, far_out, context_out, norm, hidden_out, act_out, up_grad_out,
        down_grad_out, result_out, embed_cot_out, branch_grad_out, context_grad_out, first_grad_out,
        sums, seg_out, layer_back, embed_back,
    ), refs = refs[:19], refs[19:]
    fulls, refs = refs[:6], refs[6:]
    (
        token_in, cot_in, embed_cot_in, far_seg, seg_column, vectors, qkv, far, context, normed, rstd,
        hidden_low, act, slope, result_low, embedded, sum_grad, down_grad, branch_grad, context_grad,
        send_sems, recv_sems, local_sems,
    ) = refs
    project_w, embed_w, small_w, output_w, up_w, down_w = fulls
    g, x, y, z, c = place()
    partner = (g, z * 2 + 1 - c)
    rows, width = context.shape
    sender = Sender(send_sems, recv_sems)
    spare = sum(len(p[1]) for p in FORWARD_PARTS) * GATHER_SEMS
    flushed = []

    def flush(source, target, index):
        copy = pltpu.make_async_copy(source, target, local_sems.at[40 + index])
        copy.start()
        flushed.append((source, target, index))

    entry_barrier()
    parts = []
    for line, members in FORWARD_PARTS:
        rows_of = []
        for array, first_row, last_row, first_column, last_column in members:
            height, breadth = shards[array].shape
            top, left = first_row * height // 4, first_column * breadth // 4
            rows_of.append(
                (
                    shards[array],
                    fulls[array],
                    top,
                    last_row * height // 4 - top,
                    left,
                    last_column * breadth // 4 - left,
                    sum(len(p[1]) for p in parts) + len(rows_of),
                )
            )
        parts.append((line, rows_of))
    plan = Gather(parts, sender, local_sems)
    exchanges = {
        20: Exchange([tokens], [token_in], True, sender, spare + 2, local_sems, 20),
        21: Exchange(
            [out_cot, embed_cot], [cot_in, embed_cot_in], True, sender, spare + 6, local_sems, 21
        ),
        22: Exchange(
            [result_low, embedded], [layer_back, embed_back], False, sender, spare + 14, local_sems, 23
        ),
    }

    def perform(steps):
        def act():
            for step in steps:
                part, event, slot, link = step // 1000, step // 100 % 10, step // 10 % 10, step % 10
                if part == 23:
                    if event == 9:
                        sender.do(True, lambda: sender.land(far, spare + 1, partner))
                    else:
                        sender.send(True, qkv.at[:, width:], far, spare + 1, partner)
                elif part >= 20:
                    if event != 9:
                        exchanges[part].step(link)
                    elif not sender.draining:
                        exchanges[part].arrive()
                elif event == 9:
                    plan.finish(part)
                else:
                    plan.step(part, event, slot, link)

        return act

    ticks = [[perform(steps) for steps in phase] for phase in FORWARD_STEPS]
    sender.post(True, segments, far_seg, spare, partner)
    ticks[0][0]()
    sender.land(far_seg, spare, partner)
    micro = g // 2
    own_ids = segments[pl.ds(micro, 1), :].astype(F32)
    far_ids = far_seg[pl.ds(micro, 1), :].astype(F32)
    ids = jnp.where(lax.rem(g, 2) == c, own_ids, far_ids)
    halves = (ids[:, :rows], ids[:, rows:])
    near_row = jnp.where(c == 0, halves[0], halves[1])
    far_row = jnp.where(c == 0, halves[1], halves[0])
    seg_out[0:1, :] = near_row
    seg_out[1:2, :] = far_row
    seg_column[...] = jnp.transpose(jnp.broadcast_to(near_row, (128, rows)))
    flush(project_w, project_out, 0)
    flush(token_in, token_out, 1)
    vector = lambda i, size: vectors.at[i : i + 1, 0:size]
    stretch(
        flat(small_w[...]),
        (
            (0, 0, 96, vector(0, 3 * width)),
            (1, 0, 128, vector(1, 4 * width)),
            (2, 0, 32, vector(2, width)),
            (2, 32, 32, vector(3, width)),
            (2, 64, 32, vector(4, width)),
            (2, 96, 32, vector(5, width)),
            (3, 0, 32, vector(6, width)),
            (3, 32, 32, vector(7, width)),
        ),
        None,
    )
    tile = 512
    wide = qkv.shape[1] // tile

    def project_tile(i):
        t = lax.rem(i + 2, wide)
        cut = pl.ds(pl.multiple_of(t * tile, tile), tile)
        value = dot_rows(flat(token_in[...]), flat(project_w[:, :, :, :, cut]))
        value = value + vectors[0:1, cut]

        @pl.when(t < 4)
        def _():
            factor = jnp.where(t < 2, HEAD_DIM ** (-0.5), 1.0)
            for j in range(tile // 128):
                part = value[:, j * 128 : (j + 1) * 128]
                part = (part * cosine[...] + turn(part) * sine[...]) * factor
                qkv[:, pl.ds(pl.multiple_of(t * tile + j * 128, 128), 128)] = part.astype(BF16)

        @pl.when(t >= 4)
        def _():
            qkv[:, cut] = value.astype(BF16)

    ticks[1][0]()
    run_with(ticks[2], wide, project_tile)
    flush(qkv, qkv_out, 2)
    flush(far, far_out, 3)

    def attend_one(i):
        at = pl.multiple_of(i * 128, 128)
        cut = lambda ref, base: ref.at[:, pl.ds(base + at, 128)]
        attend_pair(
            cut(qkv, 0), cut(qkv, width), cut(qkv, 2 * width), cut(far, 0), cut(far, width),
            seg_column, seg_out.at[0:1], seg_out.at[1:2], cut(context, 0), norm.at[i],
        )

    run_with(ticks[3], width // 128, attend_one)
    flush(context, context_out, 4)
    half = rows // 2
    output_weight, bias_o = lambda: flat(output_w[...]), vectors[2:3, 0:width]

    def hidden_of(cut):
        return normed[cut, :] * vectors[3:4, 0:width] + vectors[4:5, 0:width]

    def branch_tile(i):
        cut = pl.ds(pl.multiple_of(i * half, half), half)
        resid = dot_rows(context[cut, :], output_weight()) + vectors[2:3, 0:width]
        resid = resid + token_in[i].astype(F32)
        center = resid - row_mean(resid)
        scale = lax.rsqrt(row_mean(center * center) + eps_norm)
        normed[cut, :] = center * scale
        rstd[0, cut, :] = jnp.broadcast_to(scale, (half, 128))
        hidden_low[cut, :] = hidden_of(cut).astype(BF16)

    run_with(ticks[4], 2, branch_tile)
    flush(hidden_low, hidden_out, 5)

    def up_tile(j):
        cut = pl.ds(pl.multiple_of(j * tile, tile), tile)
        value = dot_rows(hidden_low[...], flat(up_w[:, :, :, :, cut])) + vectors[1:2, cut]
        below = 0.5 + 0.5 * lax.erf(value * 0.7071067811865476)
        density = jnp.exp(-0.5 * value * value) * 0.3989422804014327
        act[:, cut] = (value * below).astype(BF16)
        slope[:, cut] = (below + value * density).astype(BF16)

    ff = act.shape[1]
    run_with(ticks[5], ff // tile, up_tile)
    flush(act, act_out, 6)
    flush(embed_cot_in, embed_cot_out, 7)
    sums[...] = jnp.zeros_like(sums)

    def add_sum(row, value):
        sums[row : row + 1, 0:width] += jnp.sum(value, axis=0, keepdims=True)

    def norm_back(grads, row_normed, scale, gain):
        scaled = grads * gain
        return scale * (
            scaled - row_mean(scaled) - row_normed * row_mean(scaled * row_normed)
        )

    def down_tile(i):
        cut = pl.ds(pl.multiple_of(i * half, half), half)
        gain, shift = vectors[6:7, 0:width], vectors[7:8, 0:width]
        resid = dot_rows(act[cut, :], flat(down_w[...])) + vectors[5:6, 0:width]
        resid = resid + hidden_of(cut)
        center = resid - row_mean(resid)
        scale = lax.rsqrt(row_mean(center * center) + eps_norm)
        row_normed = center * scale
        low = (row_normed * gain + shift).astype(BF16)
        result_low[i] = low
        embed_full = flat(embed_w[...])
        embedded[i] = dot_rows(low, embed_full).astype(BF16)
        grads = cot_in[i].astype(F32) + dot_columns(embed_cot_in[i], embed_full)
        add_sum(6, grads * row_normed)
        add_sum(7, grads)
        total = norm_back(grads, row_normed, scale, gain)
        sum_grad[cut, :] = total
        low = total.astype(BF16)
        down_grad[cut, :] = low
        add_sum(5, low.astype(F32))

    run_with(ticks[6], 2, down_tile)
    flush(result_low, result_out, 8)
    flush(down_grad, down_grad_out, 9)

    def up_grad_tile(j):
        cut = pl.ds(pl.multiple_of(j * tile, tile), tile)
        part = flat(down_w[j // 2, pl.ds(lax.rem(j, 2) * 2, 2)])
        value = (dot_columns(down_grad[...], part) * slope[:, cut].astype(F32)).astype(BF16)
        slope[:, cut] = value
        sums[1:2, cut] = jnp.sum(value.astype(F32), axis=0, keepdims=True)

    run_with(ticks[7], ff // tile, up_grad_tile)
    flush(slope, up_grad_out, 10)

    def first_tile(i):
        cut = pl.ds(pl.multiple_of(i * half, half), half)
        grads = sum_grad[cut, :] + dot_columns(slope[cut, :], flat(up_w[...]))
        row_normed = normed[cut, :]
        add_sum(3, grads * row_normed)
        add_sum(4, grads)
        total = norm_back(grads, row_normed, rstd[0, cut, 0:1], vectors[3:4, 0:width])
        sum_grad[cut, :] = total
        low = total.astype(BF16)
        branch_grad[cut, :] = low
        add_sum(2, low.astype(F32))
        context_grad[cut, :] = dot_columns(low, output_weight()).astype(BF16)

    run_with(ticks[8], 2, first_tile)
    flush(sum_grad, first_grad_out, 11)
    flush(branch_grad, branch_grad_out, 12)
    flush(context_grad, context_grad_out, 13)
    sender.drain([tick for phase in ticks for tick in phase])
    for source, target, index in flushed:
        pltpu.make_async_copy(source, target, local_sems.at[40 + index]).wait()


def forward(shards, sources, segments, tables, ff):
    piece, width = sources[0].shape[1:]
    lanes = sources[2].shape[2]
    rows = 2 * piece
    semaphores = sum(len(p[1]) for p in FORWARD_PARTS) * GATHER_SEMS + 32
    fulls = [(PLANE, LINE, 2) + s.shape for s in shards]
    shape = jax.ShapeDtypeStruct
    outs = [
        shape(fulls[0], BF16),
        shape((2, piece, width), BF16),
        shape((rows, 3 * width), BF16),
        shape((rows, 2 * width), BF16),
        shape((rows, width), BF16),
        shape((width // 128, 8, rows), F32),
        shape((rows, width), BF16),
        shape((rows, ff), BF16),
        shape((rows, ff), BF16),
        shape((rows, width), BF16),
        shape((2, piece, width), BF16),
        shape((2, piece, lanes), BF16),
        shape((rows, width), BF16),
        shape((rows, width), BF16),
        shape((rows, width), F32),
        shape((8, ff), F32),
        shape((8, rows), F32),
        shape((2, piece, width), BF16),
        shape((2, piece, lanes), BF16),
    ]
    spaces = [hbm()] * len(outs)
    for i in (5, 15, 16):
        spaces[i] = vmem()
    scratch = [pltpu.VMEM(f, BF16) for f in fulls] + [
        pltpu.VMEM((2, piece, width), BF16),
        pltpu.VMEM((2, piece, width), BF16),
        pltpu.VMEM((2, piece, lanes), BF16),
        pltpu.VMEM(segments.shape, jnp.int32),
        pltpu.VMEM((rows, 128), F32),
        pltpu.VMEM((8, ff), F32),
        pltpu.VMEM((rows, 3 * width), BF16),
        pltpu.VMEM((rows, 2 * width), BF16),
        pltpu.VMEM((rows, width), BF16),
        pltpu.VMEM((rows, width), F32),
        pltpu.VMEM((1, rows, 128), F32),
        pltpu.VMEM((rows, width), BF16),
        pltpu.VMEM((rows, ff), BF16),
        pltpu.VMEM((rows, ff), BF16),
        pltpu.VMEM((2, piece, width), BF16),
        pltpu.VMEM((2, piece, lanes), BF16),
        pltpu.VMEM((rows, width), F32),
        pltpu.VMEM((rows, width), BF16),
        pltpu.VMEM((rows, width), BF16),
        pltpu.VMEM((rows, width), BF16),
        pltpu.SemaphoreType.DMA((semaphores,)),
        pltpu.SemaphoreType.DMA((semaphores,)),
        pltpu.SemaphoreType.DMA((60,)),
    ]
    return pl.pallas_call(
        forward_kernel,
        out_shape=outs,
        in_specs=[hbm()] * 9 + [vmem()] * 3,
        out_specs=spaces,
        scratch_shapes=scratch,
        compiler_params=pltpu.CompilerParams(
            collective_id=1, has_side_effects=True, vmem_limit_bytes=67043328
        ),
        name="forward",
    )(*shards, *sources, segments, *tables)


def attend_back_pair(
    query, key, value, far_key, far_value, grad, norm, seg_row, seg_near, seg_far, tables, summed
):
    rows = query.shape[0]
    tile = 256
    cosine, sine, far_cosine, far_sine = tables
    low_half = lane_half((rows, 128), 128, HEAD_DIM)
    query_low = lane_half((tile, 128), 128, HEAD_DIM)
    summed[...] = jnp.zeros_like(summed)

    def body(r, carry):
        rs = pl.ds(pl.multiple_of(r * tile, tile), tile)
        query_rows, grad_rows = query[rs, :], grad[rs, :]
        sides = ((key[...], value[...], seg_near), (far_key[...], far_value[...], seg_far))
        query_grads = []
        key_grads, value_grads = [[], []], [[], []]
        for h in range(2):
            keep = query_low if h == 0 else jnp.logical_not(query_low)
            one = jnp.where(keep, query_rows, jnp.zeros_like(query_rows))
            one_grad = jnp.where(keep, grad_rows, jnp.zeros_like(grad_rows))
            top = norm[h : h + 1, rs]
            kept = []
            delta = jnp.zeros((1, tile), F32)
            for keys, values, seg_key in sides:
                same = seg_key[:, 0:1] == seg_row[:, rs]
                scores = jnp.where(same, dot_columns(keys, one), neg_large)
                probs = jnp.exp(scores - top)
                product = probs * dot_columns(values, one_grad)
                delta = delta + jnp.sum(product, axis=0, keepdims=True)
                kept.append((probs, product))
            total = None
            for i, (keys, values, seg_key) in enumerate(sides):
                probs, product = kept[i]
                score_grad = (product - probs * delta).astype(BF16)
                key_grads[i].append(dot_rows(score_grad, query_rows))
                value_grads[i].append(dot_rows(probs.astype(BF16), grad_rows))
                part = contract_rows(score_grad, keys)
                total = part if total is None else total + part
            query_grads.append(total)
        for i in range(2):
            summed[i] += jnp.where(low_half, key_grads[i][0], key_grads[i][1])
            summed[2 + i] += jnp.where(low_half, value_grads[i][0], value_grads[i][1])
        joined = jnp.where(query_low, query_grads[0], query_grads[1]) * HEAD_DIM ** (-0.5)
        query[rs, :] = (joined * cosine[rs, :] - turn(joined) * sine[rs, :]).astype(BF16)
        return carry

    lax.fori_loop(0, rows // tile, body, 0)
    near, far = summed[0], summed[1]
    key[...] = (near * cosine[...] - turn(near) * sine[...]).astype(BF16)
    value[...] = summed[2].astype(BF16)
    far_key[...] = (far * far_cosine[...] - turn(far) * far_sine[...]).astype(BF16)
    far_value[...] = summed[3].astype(BF16)


def far_first(z, k):
    items = near_items(z, k)
    if k == 0:
        return items
    return [(k,) + items[1][1:], (3 + k,) + items[0][1:]]


def sum_ticks(arrays, chunks, ahead, sender):
    g, x, y, z, c = place()
    gx, gy, gd = g + 1 - 2 * x, g + 2 - 4 * y, 3 - g
    to_x, to_y, to_core = (gx, z * 2 + c), (gy, z * 2 + c), (g, z * 2 + 1 - c)
    above = (g, jnp.minimum(z + 1, LINE - 1) * 2 + c)
    below = (g, jnp.maximum(z - 1, 0) * 2 + c)

    def side_of(slot):
        return 0 if slot < 4 else 1

    def zeroth(a, k):
        array, base = arrays[a], a * REDUCE_SEMS
        for slot, zi, cond in far_first(z, k):
            buffer = array["send"].at[side_of(slot)]
            index = base + slot
            copy = lambda at, item: sender.copy(buffer, array["held"].at[item], base + at, to_core)
            if sender.draining:
                if slot in (0, 4) and not array["early"]:
                    when(cond, lambda: copy(slot, zi).wait_send())
                continue
            if slot == 0:
                when(z + 1 < LINE, lambda: copy(1, zi).wait_send())
            elif k < LINE - 1:
                before = z + k + 1 < LINE if slot < 4 else z >= k + 1
                when(before, lambda: copy(slot + 1, zi).wait_send())

            def work():
                array["product"](1 - c, zi, buffer, None)
                copy(slot, zi).start()

            if k == LINE - 1 and slot == k and array["after"] is not None:
                other = arrays[array["after"]]
                leave = lambda at: sender.copy(
                    other["send"].at[0], other["held"].at[0], array["after"] * REDUCE_SEMS + at, to_core
                )
                leave(0).wait_send()
                when(z >= 1, lambda: leave(4).wait_send())

            when(cond, work)

    def first(a, k):
        array, base = arrays[a], a * REDUCE_SEMS
        held, half_in = array["held"], array["half"]
        rows = held.shape[2]
        cut = rows // 2
        for slot, zi, cond in far_first(z, k):

            def work():
                sender.land(held.at[zi], base + slot, to_x)
                array["product"](c, zi, held.at[zi], held.at[zi])

            sender.do(cond, work)
            sender.send(cond, held.at[zi, gd, 0:cut], half_in.at[zi, 0:cut], base + 7 + slot, to_y)
            sender.send(
                cond, held.at[zi, gd, cut:rows], half_in.at[zi, cut:rows], base + 14 + slot, to_x
            )

    def second(a, k):
        array, base = arrays[a], a * REDUCE_SEMS
        held, half_in, whole_in = array["held"], array["half"], array["whole"]
        rows = held.shape[2]
        cut = rows // 2
        for slot, zi, cond in far_first(z, k):

            def upper():
                sender.land(half_in.at[zi, 0:cut], base + 7 + slot, to_x)
                mine = held.at[zi, gx, 0:cut]
                add_into(mine, [mine, half_in.at[zi, 0:cut]])

            sender.do(cond, upper)
            sender.send(cond, held.at[zi, gx], whole_in.at[zi, 0], base + 21 + slot, to_x)

            def lower():
                sender.land(half_in.at[zi, cut:rows], base + 14 + slot, to_x)
                mine = held.at[zi, gy, cut:rows]
                add_into(mine, [mine, half_in.at[zi, cut:rows]])

            sender.do(cond, lower)
            sender.send(cond, held.at[zi, gy], whole_in.at[zi, 1], base + 28 + slot, to_y)

    def third(a, k):
        array, base = arrays[a], a * REDUCE_SEMS
        held, whole_in, line_in, out = array["held"], array["whole"], array["line"], array["out"]
        for slot, zi, cond in far_first(z, k):
            mine = held.at[zi, g]
            terms = [mine, whole_in.at[zi, 0], whole_in.at[zi, 1]]

            def arrive():
                sender.land(whole_in.at[zi, 0], base + 21 + slot, to_x)
                sender.land(whole_in.at[zi, 1], base + 28 + slot, to_x)

            sender.do(cond, arrive)
            if k == 0:
                rise, fall = line_in.at[zi], line_in.at[LINE]
                sender.do(z > 0, lambda: sender.land(rise, base + 36, to_x))
                sender.do(z < LINE - 1, lambda: sender.land(fall, base + 43, to_x))
                sender.do(z == 0, lambda: add_into(out, terms + [fall]))
                sender.do(z == LINE - 1, lambda: add_into(out, terms + [rise]))
                sender.do(
                    jnp.logical_and(z > 0, z < LINE - 1),
                    lambda: add_into(out, terms + [rise, fall]),
                )
            else:
                going_up = slot < 4
                moved = line_in.at[zi]
                landing = line_in.at[LINE if k == 1 and not going_up else zi]
                offset = base + (35 if going_up else 42)
                inner = (z > 0) if going_up else (z < LINE - 1)

                def join():
                    sender.land(moved, offset + k + 1, to_x)
                    add_into(mine, terms + [moved])

                if k < LINE - 1:
                    sender.do(both(cond, inner), join)
                sender.do(both(cond, jnp.logical_not(inner)), lambda: add_into(mine, terms))
                sender.send(cond, mine, landing, offset + k, above if going_up else below)

    def grouped(stage):
        def act(chunk, k):
            for a in chunk:
                stage(a, k)

        return act

    order = [(chunk, k) for chunk in chunks for k in (3, 2, 1, 0)]
    stages = [grouped(stage) for stage in (zeroth, first, second, third)]
    return staged(order, stages, (0,) + ahead)


def gather_up(vectors, target):
    shards = PLANE * LINE * 2
    total = None
    for row in sorted({v[0] for v in vectors}):
        share = jnp.zeros((shards, 128), F32)
        for at, lane, size, source in vectors:
            if at != row:
                continue
            step = 1024

            def body(i, carry):
                cut = pl.ds(pl.multiple_of(i * step, step), step)
                column = (lax.broadcasted_iota(jnp.int32, (1, step), 1) + i * step).astype(F32)
                shard = jnp.floor((column + 0.5) * (1.0 / size))
                lane_of = (column - shard * size + lane).astype(jnp.int32)
                spread = lax.broadcasted_iota(jnp.int32, (128, step), 0) == lane_of
                keep = lax.broadcasted_iota(jnp.int32, (shards, step), 0) == shard.astype(jnp.int32)
                value = jnp.where(keep, source[:, cut], 0.0).astype(BF16)
                return carry + dot_columns(value, spread.astype(F32).astype(BF16))

            share = lax.fori_loop(0, shards * size // step, body, share)
        pick_rows = lax.broadcasted_iota(jnp.int32, (shards, shards * 32), 0) * 32 + row
        pick = lax.broadcasted_iota(jnp.int32, (shards, shards * 32), 1) == pick_rows
        part = contract_rows(pick.astype(F32).astype(BF16), share.astype(BF16))
        total = part if total is None else total + part
    target[...] = total.astype(BF16).reshape(target.shape)


def backward_kernel(*refs):
    (
        act_hbm, down_grad_hbm, hidden_hbm, up_grad_hbm, context_hbm, branch_grad_hbm, result_hbm,
        embed_cot_hbm, token_hbm, qkv_hbm, far_hbm, context_grad_hbm, first_grad_hbm, weight_hbm,
        norm, segs, sums, cosine, sine, far_cosine, far_sine,
    ), refs = refs[:21], refs[21:]
    outs, token_out, refs = refs[:6], refs[6], refs[7:]
    shared = lambda columns: refs[1].at[:, :, :, 0:columns]
    sends = (
        refs[0], refs[1], shared(branch_grad_hbm.shape[1]), refs[2], shared(qkv_hbm.shape[1]), refs[3]
    )
    helds, halves, wholes, lines = [refs[i * 6 - 2 : (i + 1) * 6 - 2] for i in range(1, 5)]
    (
        act, down_grad, up_grad, branch_grad, embed_cot, raw, turned_a, turned_b, turned_c, qkv, far,
        far_back, context_grad, seg_near, seg_far, vectors, shares, summed, token_in,
        send_sems, recv_sems, local_sems,
    ) = refs[28:]
    g, x, y, z, c = place()
    partner = (g, z * 2 + 1 - c)
    rows, width = branch_grad.shape
    ff = act.shape[1]
    sender = Sender(send_sems, recv_sems)
    spare = 6 * REDUCE_SEMS

    def load(source, target, index):
        copy = lambda: pltpu.make_async_copy(source, target, local_sems.at[index])
        copy().start()
        return lambda: copy().wait()

    waits = {
        "act": load(act_hbm, act, 0),
        "down": load(down_grad_hbm, down_grad, 1),
        "raw": load(hidden_hbm, raw, 2),
        "up": load(up_grad_hbm, up_grad, 3),
        "branch": load(branch_grad_hbm, branch_grad, 4),
        "embed": load(embed_cot_hbm, embed_cot, 5),
        "qkv": load(qkv_hbm, qkv, 6),
        "far": load(far_hbm, far, 7),
        "grad": load(context_grad_hbm, context_grad, 8),
        "first": load(first_grad_hbm, token_out, 9),
    }
    entry_barrier()

    def turn_over(target):
        for j in range(width // 128):
            block = jnp.transpose(flat(raw[:, :, j * 128 : (j + 1) * 128]))
            target[j // 2, (j % 2) * 2 : (j % 2) * 2 + 2] = block.reshape(2, 2, 32, rows)

    def product_of(turned, right):
        columns = right.shape[1]
        step = min(columns, 512)

        def act_on(parity, zi, target, base):
            left = flat(turned[:, zi, parity])

            def body(i, carry):
                cut = pl.ds(pl.multiple_of(i * step, step), step)
                value = dot_rows(left, right[:, cut]).reshape(PLANE, 32, step)
                if base is not None:
                    value = value + base[:, :, cut].astype(F32)
                target[:, :, cut] = value.astype(BF16)
                return carry

            lax.fori_loop(0, columns // step, body, 0)

        return act_on

    def down_product(parity, zi, target, base):
        def body(j, carry):
            at = ((j * LINE + zi) * 2 + parity) * 128
            left = act[:, pl.ds(pl.multiple_of(at, 128), 128)]
            value = contract_rows(left, down_grad[...])
            if base is not None:
                value = value + base[j].astype(F32)
            target[j] = value.astype(BF16)
            return carry

        lax.fori_loop(0, PLANE, body, 0)

    def share_product(parity, zi, target, base):
        value = shares[:, zi, parity].astype(F32)
        if base is not None:
            value = value + base[...].astype(F32)
        target[...] = value.astype(BF16)

    products = [
        down_product,
        product_of(turned_a, up_grad),
        product_of(turned_b, branch_grad),
        product_of(turned_c, embed_cot),
        product_of(turned_a, qkv),
        share_product,
    ]
    arrays = [
        {"product": p, "send": s, "held": h, "half": i, "whole": w, "line": l, "out": o}
        for p, s, h, i, w, l, o in zip(products, sends, helds, halves, wholes, lines, outs)
    ]
    for a, array in enumerate(arrays):
        array["after"] = {2: 1, 4: 2}.get(a)
        array["early"] = a in (1, 2)
    main = sum_ticks(arrays, [(0,), (1,), (2, 3)], MAIN_AHEAD, sender)
    late = sum_ticks(arrays, [(4, 5)], LATE_AHEAD, sender)
    waits["act"]()
    waits["down"]()
    main[0]()
    main[1]()
    waits["raw"]()
    turn_over(turned_a)
    load(context_hbm, raw, 2)
    main[2]()
    waits["up"]()
    main[3]()
    main[4]()
    waits["raw"]()
    turn_over(turned_b)
    load(result_hbm, raw, 2)
    main[5]()
    main[6]()
    waits["raw"]()
    turn_over(turned_c)
    load(token_hbm, raw, 2)
    waits["branch"]()
    waits["embed"]()
    main[7]()
    for name in ("qkv", "far", "grad"):
        waits[name]()
    seg_near[...] = jnp.transpose(jnp.broadcast_to(segs[0:1, :], (128, rows)))
    seg_far[...] = jnp.transpose(jnp.broadcast_to(segs[1:2, :], (128, rows)))

    def attend_one(i):
        at = pl.multiple_of(i * 128, 128)
        cut = lambda ref, base: ref.at[:, pl.ds(base + at, 128)]
        attend_back_pair(
            cut(qkv, 0), cut(qkv, width), cut(qkv, 2 * width), cut(far, 0), cut(far, width),
            cut(context_grad, 0), norm.at[i], segs.at[0:1], seg_near, seg_far,
            (cosine, sine, far_cosine, far_sine), summed,
        )

    run_with(main[8:16], width // 128, attend_one)
    sender.post(True, far, far_back, spare, partner)
    waits["raw"]()
    turn_over(turned_a)
    sender.land(far_back, spare, partner)
    tile = 512
    vectors[...] = jnp.zeros_like(vectors)

    def finish_tile(i):
        cut = pl.ds(pl.multiple_of(i * tile, tile), tile)

        @pl.when(i >= 2)
        def _():
            other = pl.ds(pl.multiple_of(jnp.maximum(i - 2, 0) * tile, tile), tile)
            qkv[:, cut] = (qkv[:, cut].astype(F32) + far_back[:, other].astype(F32)).astype(BF16)

        vectors[0:1, cut] = jnp.sum(qkv[:, cut].astype(F32), axis=0, keepdims=True)

    run_with([], 3 * width // tile, finish_tile)
    source = lambda i, size: (vectors if i == 0 else sums).at[i : i + 1, 0:size]
    gather_up(
        (
            (0, 0, 96, source(0, 3 * width)),
            (1, 0, 128, source(1, ff)),
            (2, 0, 32, source(2, width)),
            (2, 32, 32, source(3, width)),
            (2, 64, 32, source(4, width)),
            (2, 96, 32, source(5, width)),
            (3, 0, 32, source(6, width)),
            (3, 32, 32, source(7, width)),
        ),
        shares,
    )
    parts = 3 * width // tile

    def fetch(t):
        for r in range(2):
            at = ((t % 4) * 2 + r) * tile
            pltpu.make_async_copy(
                weight_hbm.at[r * rows : (r + 1) * rows, t * tile : (t + 1) * tile],
                act.at[:, at : at + tile],
                local_sems.at[10 + (t % 4) * 2 + r],
            ).start()

    def fetched(t):
        for r in range(2):
            at = ((t % 4) * 2 + r) * tile
            pltpu.make_async_copy(
                weight_hbm.at[r * rows : (r + 1) * rows, t * tile : (t + 1) * tile],
                act.at[:, at : at + tile],
                local_sems.at[10 + (t % 4) * 2 + r],
            ).wait()

    for t in range(4):
        fetch(t)
    for tick in late[:4]:
        tick()
    waits["first"]()
    for t in range(parts):
        fetched(t)
        for r in range(2):
            at = ((t % 4) * 2 + r) * tile
            half = token_out[:, r * tile : (r + 1) * tile]
            token_out[:, r * tile : (r + 1) * tile] = half + dot_columns(
                qkv[:, t * tile : (t + 1) * tile], act[:, at : at + tile]
            )
        if t + 4 < parts:
            fetch(t + 4)
    for i in range(2):
        raw[i] = token_out[i * (rows // 2) : (i + 1) * (rows // 2), :].astype(BF16)
    token_back = Exchange([raw], [token_in], False, sender, spare + 2, local_sems, 18)
    for link in (5, 2, 3):
        token_back.step(link)
    for tick in main[16:] + late[4:]:
        tick()
    token_back.arrive()
    for i in range(2):
        token_out[i * (rows // 2) : (i + 1) * (rows // 2), :] = token_in[i].astype(F32)
    sender.drain(main + late + [lambda: [token_back.step(link) for link in (5, 2, 3)]])


def backward(operands, small_operands, shapes, rows, width, ff, lanes):
    shape = jax.ShapeDtypeStruct
    semaphores = 6 * REDUCE_SEMS + 16
    buffers = []
    for lead in ((2, PLANE), (LINE, PLANE), (LINE,), (LINE, 2), (LINE + 1,)):
        apart = shapes if lead != (2, PLANE) else [shapes[i] for i in (0, 1, 3, 5)]
        buffers += [pltpu.VMEM(lead + s, BF16) for s in apart]
    turned = pltpu.VMEM((PLANE, LINE, 2, 32, rows), BF16)
    piece = rows // 2
    scratch = buffers + [
        pltpu.VMEM((rows, ff), BF16),
        pltpu.VMEM((rows, width), BF16),
        pltpu.VMEM((rows, ff), BF16),
        pltpu.VMEM((rows, width), BF16),
        pltpu.VMEM((rows, lanes), BF16),
        pltpu.VMEM((2, piece, width), BF16),
        turned,
        turned,
        turned,
        pltpu.VMEM((rows, 3 * width), BF16),
        pltpu.VMEM((rows, 2 * width), BF16),
        pltpu.VMEM((rows, 2 * width), BF16),
        pltpu.VMEM((rows, width), BF16),
        pltpu.VMEM((rows, 128), F32),
        pltpu.VMEM((rows, 128), F32),
        pltpu.VMEM((8, ff), F32),
        pltpu.VMEM((PLANE, LINE, 2, 32, 128), BF16),
        pltpu.VMEM((4, rows, 128), F32),
        pltpu.VMEM((2, piece, width), BF16),
        pltpu.SemaphoreType.DMA((semaphores,)),
        pltpu.SemaphoreType.DMA((semaphores,)),
        pltpu.SemaphoreType.DMA((20,)),
    ]
    results = pl.pallas_call(
        backward_kernel,
        out_shape=[shape(s, F32) for s in shapes] + [shape((rows, width), F32)],
        in_specs=[hbm()] * len(operands) + [vmem()] * len(small_operands),
        out_specs=[vmem()] * 7,
        scratch_shapes=scratch,
        compiler_params=pltpu.CompilerParams(
            collective_id=2, has_side_effects=True, vmem_limit_bytes=67043328
        ),
        name="backward",
    )(*operands, *small_operands)
    return (results[:6], results[6])


def pair_tables(positions):
    cosine, sine = rotary_tables(positions)
    return (jnp.concatenate([cosine, cosine], axis=1), jnp.concatenate([sine, sine], axis=1))


def plane_device(
    tokens,
    segment_ids,
    project_weight,
    project_bias,
    output_weight,
    output_bias,
    first_gain,
    first_shift,
    up_weight,
    up_bias,
    down_weight,
    down_bias,
    second_gain,
    second_shift,
    embed_weight,
    out_cotangent,
    embed_cotangent,
):
    width = HEADS * HEAD_DIM
    piece = tokens.shape[2]
    rows = 2 * piece
    group = lax.axis_index("group")
    core = lax.rem(lax.axis_index("wide"), 2)
    lanes = embed_weight.shape[1]
    embed_rows = embed_weight.shape[0]
    small = None
    for row, lane, vector in (
        (0, 0, project_bias),
        (1, 0, up_bias),
        (2, 0, output_bias),
        (2, 32, first_gain),
        (2, 64, first_shift),
        (2, 96, down_bias),
        (3, 0, second_gain),
        (3, 32, second_shift),
    ):
        size = vector.shape[0]
        part = jnp.pad(
            vector.astype(F32)[None, :], ((row, 31 - row), (lane, lanes - lane - size))
        )
        small = part if small is None else small + part
    place_of = jnp.arange(rows)
    cosine, sine = pair_tables((core * rows + place_of).astype(F32))
    far_cosine, far_sine = pair_tables(((1 - core) * rows + place_of).astype(F32))
    (
        project_full, token_rows, qkv, far_kv, context_low, norms, hidden_low, act_low, up_grad,
        down_grad, result_low, embed_cot, branch_grad, context_grad, first_grad, sums, ids,
        layer_out, embed_out,
    ) = forward(
        [project_weight, embed_weight, small.astype(BF16), output_weight, up_weight, down_weight],
        [tokens[:, 0], out_cotangent[:, 0], embed_cotangent[:, 0]],
        segment_ids[:, 0],
        (cosine, sine),
        up_weight.shape[1],
    )
    shapes = [
        down_weight.shape,
        up_weight.shape,
        output_weight.shape,
        embed_weight.shape,
        project_weight.shape,
        small.shape,
    ]
    outs, token_grad = backward(
        (
            act_low, down_grad, hidden_low.reshape(2, piece, width), up_grad,
            context_low.reshape(2, piece, width), branch_grad, result_low,
            embed_cot.reshape(rows, lanes), token_rows, qkv, far_kv, context_grad, first_grad,
            project_full.reshape(width, 3 * width),
        ),
        (norms, ids, sums, cosine, sine, far_cosine, far_sine),
        shapes,
        rows,
        width,
        up_weight.shape[1],
        lanes,
    )
    down_out, up_out, output_out, embed_grad_out, project_out, small_out = outs
    return (
        layer_out[:, None],
        embed_out[:, None],
        token_grad.reshape(2, 1, piece, width),
        project_out,
        small_out[0, : project_bias.shape[0]],
        output_out,
        small_out[2, 0:32],
        small_out[2, 32:64],
        small_out[2, 64:96],
        up_out,
        small_out[1, : up_bias.shape[0]],
        down_out,
        small_out[2, 96:128],
        small_out[3, 0:32],
        small_out[3, 32:64],
        embed_grad_out,
    )


def choose_device(mesh):
    if mesh.shape["group"] == PLANE and mesh.shape["wide"] == 2 * LINE:
        return plane_device
    return general_device


def solution(mesh):
    in_specs = (
        P(None, "wide", "group", None),
        P(None, "wide", None),
        P(("group", "wide"), None),
        P(("group", "wide")),
        P(("group", "wide"), None),
        P(("group", "wide")),
        P(("group", "wide")),
        P(("group", "wide")),
        P(("group", "wide"), None),
        P(("group", "wide")),
        P(("group", "wide"), None),
        P(("group", "wide")),
        P(("group", "wide")),
        P(("group", "wide")),
        P(("group", "wide"), None),
        P(None, "wide", "group", None),
        P(None, "wide", "group", None),
    )
    out_specs = (
        P(None, "wide", "group", None),
        P(None, "wide", "group", None),
        P(None, "wide", "group", None),
        P(("group", "wide"), None),
        P(("group", "wide")),
        P(("group", "wide"), None),
        P(("group", "wide")),
        P(("group", "wide")),
        P(("group", "wide")),
        P(("group", "wide"), None),
        P(("group", "wide")),
        P(("group", "wide"), None),
        P(("group", "wide")),
        P(("group", "wide")),
        P(("group", "wide")),
        P(("group", "wide"), None),
    )
    return jax.shard_map(
        choose_device(mesh), mesh=mesh, in_specs=in_specs, out_specs=out_specs, check_vma=False
    )
```

```python
import functools

import jax
import jax.numpy as jnp
from jax import lax
from jax.experimental import pallas as pl
from jax.experimental.pallas import tpu as pltpu
from jax.sharding import PartitionSpec as P

HEADS = 16
HEAD_DIM = 64


eps_norm = 1e-05
neg_large = -1e30


def rotary_tables(positions):
    half_dim = HEAD_DIM // 2
    frequency = 10000.0 ** (-jnp.arange(half_dim, dtype=jnp.float32) * (2.0 / HEAD_DIM))
    angles = positions[:, None] * frequency[None, :]
    angles = jnp.concatenate([angles, angles], axis=1)
    return (jnp.cos(angles), jnp.sin(angles))


def rotate(values, cosine_table, sine_table):
    half_dim = HEAD_DIM // 2
    swapped = jnp.concatenate([-values[..., half_dim:], values[..., :half_dim]], axis=-1)
    return values * cosine_table[:, None, :] + swapped * sine_table[:, None, :]


def unrotate(grads, cosine_table, sine_table):
    half_dim = HEAD_DIM // 2
    scaled = grads * sine_table[:, None, :]
    swapped = jnp.concatenate([scaled[..., half_dim:], -scaled[..., :half_dim]], axis=-1)
    return grads * cosine_table[:, None, :] + swapped


def norm_forward(resid, gain, shift):
    center = resid - jnp.mean(resid, axis=-1, keepdims=True)
    spread = jnp.mean(center * center, axis=-1, keepdims=True)
    rstd_rows = lax.rsqrt(spread + eps_norm)
    normed = center * rstd_rows
    return (normed * gain + shift, normed, rstd_rows)


def norm_backward(grads, normed, rstd_rows, gain):
    scaled = grads * gain
    resid_grad = rstd_rows * (
        scaled
        - jnp.mean(scaled, axis=-1, keepdims=True)
        - normed * jnp.mean(scaled * normed, axis=-1, keepdims=True)
    )
    return (resid_grad, jnp.sum(grads * normed, axis=0), jnp.sum(grads, axis=0))


def contract_rows(left, right):
    return lax.dot_general(
        left, right, (((0,), (0,)), ((), ())), preferred_element_type=jnp.float32
    )


def times_transpose(left, right):
    return lax.dot_general(
        left, right, (((1,), (1,)), ((), ())), preferred_element_type=jnp.float32
    )


def gelu_slope(value):
    normal_cdf = 0.5 * (1.0 + lax.erf(value * 0.7071067811865476))
    density = jnp.exp(-0.5 * value * value) * 0.3989422804014327
    return normal_cdf + value * density


def key_blocks(kv_rows, seg_all):
    seq_len = kv_rows.shape[0]
    block_rows = min(512, seq_len)
    count = seq_len // block_rows
    return (
        kv_rows.reshape(count, block_rows, 2, HEADS, HEAD_DIM),
        seg_all.reshape(count, block_rows),
    )


def block_scores(queries, key_block, same):
    scores = jnp.einsum("qhd,khd->hqk", queries, key_block, preferred_element_type=jnp.float32)
    scores = scores * HEAD_DIM ** (-0.5)
    return jnp.where(same[None], scores, neg_large)


def attention_forward(queries, blocks, seg_blocks, seg_local):
    length = queries.shape[0]

    def norm_step(carry, pieces):
        kv_block, seg_block = pieces
        same = seg_local[:, None] == seg_block[None, :]

        def norm_update(running):
            run_max, run_sum = running
            scores = block_scores(queries, kv_block[:, 0], same)
            new_max = jnp.maximum(run_max, jnp.max(scores, axis=-1))
            new_sum = run_sum * jnp.exp(run_max - new_max) + jnp.sum(
                jnp.exp(scores - new_max[..., None]), axis=-1
            )
            return (new_max, new_sum)

        def norm_unchanged(running):
            return running

        return (lax.cond(jnp.any(same), norm_update, norm_unchanged, carry), None)

    start = (
        jnp.full((HEADS, length), neg_large, jnp.float32),
        jnp.zeros((HEADS, length), jnp.float32),
    )
    (run_max, run_sum), unused = lax.scan(norm_step, start, (blocks, seg_blocks))
    log_norm = run_max + jnp.log(run_sum)

    def value_step(total, pieces):
        kv_block, seg_block = pieces
        same = seg_local[:, None] == seg_block[None, :]

        def value_update(running):
            scores = block_scores(queries, kv_block[:, 0], same)
            weights = jnp.exp(scores - log_norm[..., None]).astype(jnp.bfloat16)
            return running + jnp.einsum(
                "hqk,khd->qhd", weights, kv_block[:, 1], preferred_element_type=jnp.float32
            )

        def value_unchanged(running):
            return running

        return (lax.cond(jnp.any(same), value_update, value_unchanged, total), None)

    context, unused = lax.scan(
        value_step, jnp.zeros(queries.shape, jnp.float32), (blocks, seg_blocks)
    )
    return (context, log_norm)


def attention_backward(queries, blocks, seg_blocks, seg_local, log_norm, context_grad, delta):

    def grad_step(query_grad, pieces):
        kv_block, seg_block = pieces
        same = seg_local[:, None] == seg_block[None, :]

        def work(running):
            scores = block_scores(queries, kv_block[:, 0], same)
            probs = jnp.exp(scores - log_norm[..., None])
            prob_grad = jnp.einsum(
                "qhd,khd->hqk", context_grad, kv_block[:, 1], preferred_element_type=jnp.float32
            )
            score_grad = (probs * (prob_grad - delta[..., None])).astype(jnp.bfloat16)
            running = running + jnp.einsum(
                "hqk,khd->qhd", score_grad, kv_block[:, 0], preferred_element_type=jnp.float32
            ) * HEAD_DIM ** (-0.5)
            prob_low = probs.astype(jnp.bfloat16)
            key_grad = jnp.einsum(
                "hqk,qhd->khd", score_grad, queries, preferred_element_type=jnp.float32
            ) * HEAD_DIM ** (-0.5)
            value_grad = jnp.einsum(
                "hqk,qhd->khd", prob_low, context_grad, preferred_element_type=jnp.float32
            )
            return (running, jnp.stack([key_grad, value_grad], axis=1))

        def skipped(running):
            return (running, jnp.zeros(kv_block.shape, jnp.float32))

        return lax.cond(jnp.any(same), work, skipped, query_grad)

    query_grad, kv_grad = lax.scan(
        grad_step, jnp.zeros(queries.shape, jnp.float32), (blocks, seg_blocks)
    )
    return (query_grad, kv_grad.reshape(-1, 2 * HEADS * HEAD_DIM))


def general_device(
    tokens,
    segment_ids,
    project_weight,
    project_bias,
    output_weight,
    output_bias,
    first_gain,
    first_shift,
    up_weight,
    up_bias,
    down_weight,
    down_bias,
    second_gain,
    second_shift,
    embed_weight,
    out_cotangent,
    embed_cotangent,
):
    shards = (
        project_weight,
        project_bias,
        output_weight,
        output_bias,
        first_gain,
        first_shift,
        up_weight,
        up_bias,
        down_weight,
        down_bias,
        second_gain,
        second_shift,
        embed_weight,
    )
    length = tokens.shape[2]
    width = HEADS * HEAD_DIM
    head_shape = (length, HEADS, HEAD_DIM)
    place = lax.axis_index("group")
    positions = (place * length + jnp.arange(length)).astype(jnp.float32)
    cosine_table, sine_table = rotary_tables(positions)
    grad_total = None
    results = []
    embeddings = []
    input_grads = []
    for micro_index in range(tokens.shape[0]):
        params = (
            lax.all_gather(shards[0], ("group", "wide"), axis=0, tiled=True),
            lax.all_gather(shards[1], ("group", "wide"), axis=0, tiled=True),
            lax.all_gather(shards[2], ("group", "wide"), axis=0, tiled=True),
            lax.all_gather(shards[3], ("group", "wide"), axis=0, tiled=True),
            lax.all_gather(shards[4], ("group", "wide"), axis=0, tiled=True),
            lax.all_gather(shards[5], ("group", "wide"), axis=0, tiled=True),
            lax.all_gather(shards[6], ("group", "wide"), axis=0, tiled=True),
            lax.all_gather(shards[7], ("group", "wide"), axis=0, tiled=True),
            lax.all_gather(shards[8], ("group", "wide"), axis=0, tiled=True),
            lax.all_gather(shards[9], ("group", "wide"), axis=0, tiled=True),
            lax.all_gather(shards[10], ("group", "wide"), axis=0, tiled=True),
            lax.all_gather(shards[11], ("group", "wide"), axis=0, tiled=True),
            lax.all_gather(shards[12], ("group", "wide"), axis=0, tiled=True),
        )
        seg_all = segment_ids[micro_index, 0]
        seg_local = lax.dynamic_slice_in_dim(seg_all, place * length, length)
        token_low = tokens[micro_index, 0]
        token_wide = token_low.astype(jnp.float32)
        projected = jnp.dot(token_low, params[0], preferred_element_type=jnp.float32) + params[
            1
        ].astype(jnp.float32)
        queries = rotate(projected[:, :width].reshape(head_shape), cosine_table, sine_table).astype(
            jnp.bfloat16
        )
        key_rows = rotate(
            projected[:, width : 2 * width].reshape(head_shape), cosine_table, sine_table
        ).astype(jnp.bfloat16)
        value_rows = projected[:, 2 * width :].astype(jnp.bfloat16)
        local_kv = jnp.concatenate([key_rows.reshape(length, width), value_rows], axis=1)
        kv_all = lax.all_gather(local_kv, "group", axis=0, tiled=True)
        blocks, seg_blocks = key_blocks(kv_all, seg_all)
        context, log_norm = attention_forward(queries, blocks, seg_blocks, seg_local)
        context_low = context.reshape(length, width).astype(jnp.bfloat16)
        branch = jnp.dot(context_low, params[2], preferred_element_type=jnp.float32) + params[
            3
        ].astype(jnp.float32)
        first_gain_wide = params[4].astype(jnp.float32)
        hidden, first_normed, first_rstd = norm_forward(
            token_wide + branch, first_gain_wide, params[5].astype(jnp.float32)
        )
        hidden_low = hidden.astype(jnp.bfloat16)
        up_value = jnp.dot(hidden_low, params[6], preferred_element_type=jnp.float32) + params[
            7
        ].astype(jnp.float32)
        act_low = jax.nn.gelu(up_value, approximate=False).astype(jnp.bfloat16)
        down_value = jnp.dot(act_low, params[8], preferred_element_type=jnp.float32) + params[
            9
        ].astype(jnp.float32)
        second_gain_wide = params[10].astype(jnp.float32)
        result, second_normed, second_rstd = norm_forward(
            hidden + down_value, second_gain_wide, params[11].astype(jnp.float32)
        )
        result_low = result.astype(jnp.bfloat16)
        embedded = jnp.dot(result_low, params[12], preferred_element_type=jnp.float32)
        results.append(result_low)
        embeddings.append(embedded.astype(jnp.bfloat16))
        params = (
            lax.all_gather(shards[0], ("group", "wide"), axis=0, tiled=True),
            lax.all_gather(shards[1], ("group", "wide"), axis=0, tiled=True),
            lax.all_gather(shards[2], ("group", "wide"), axis=0, tiled=True),
            lax.all_gather(shards[3], ("group", "wide"), axis=0, tiled=True),
            lax.all_gather(shards[4], ("group", "wide"), axis=0, tiled=True),
            lax.all_gather(shards[5], ("group", "wide"), axis=0, tiled=True),
            lax.all_gather(shards[6], ("group", "wide"), axis=0, tiled=True),
            lax.all_gather(shards[7], ("group", "wide"), axis=0, tiled=True),
            lax.all_gather(shards[8], ("group", "wide"), axis=0, tiled=True),
            lax.all_gather(shards[9], ("group", "wide"), axis=0, tiled=True),
            lax.all_gather(shards[10], ("group", "wide"), axis=0, tiled=True),
            lax.all_gather(shards[11], ("group", "wide"), axis=0, tiled=True),
            lax.all_gather(shards[12], ("group", "wide"), axis=0, tiled=True),
        )
        embed_cot = embed_cotangent[micro_index, 0]
        result_grad = out_cotangent[micro_index, 0].astype(jnp.float32) + times_transpose(
            embed_cot, params[12]
        )
        embed_weight_grad = contract_rows(result_low, embed_cot)
        sum_grad, second_gain_grad, second_shift_grad = norm_backward(
            result_grad, second_normed, second_rstd, second_gain_wide
        )
        down_grad = sum_grad.astype(jnp.bfloat16)
        down_bias_grad = jnp.sum(down_grad.astype(jnp.float32), axis=0)
        down_weight_grad = contract_rows(act_low, down_grad)
        up_grad = (times_transpose(down_grad, params[8]) * gelu_slope(up_value)).astype(
            jnp.bfloat16
        )
        up_bias_grad = jnp.sum(up_grad.astype(jnp.float32), axis=0)
        up_weight_grad = contract_rows(hidden_low, up_grad)
        hidden_grad = sum_grad + times_transpose(up_grad, params[6])
        first_grad, first_gain_grad, first_shift_grad = norm_backward(
            hidden_grad, first_normed, first_rstd, first_gain_wide
        )
        branch_grad = first_grad.astype(jnp.bfloat16)
        output_bias_grad = jnp.sum(branch_grad.astype(jnp.float32), axis=0)
        output_weight_grad = contract_rows(context_low, branch_grad)
        context_grad = (
            times_transpose(branch_grad, params[2]).astype(jnp.bfloat16).reshape(head_shape)
        )
        delta = jnp.transpose(jnp.sum(context_grad.astype(jnp.float32) * context, axis=-1))
        kv_again = lax.all_gather(local_kv, "group", axis=0, tiled=True)
        blocks, seg_blocks = key_blocks(kv_again, seg_all)
        query_grad, kv_partial = attention_backward(
            queries, blocks, seg_blocks, seg_local, log_norm, context_grad, delta
        )
        kv_grad = lax.psum_scatter(
            kv_partial.astype(jnp.bfloat16), "group", scatter_dimension=0, tiled=True
        ).astype(jnp.float32)
        key_part = kv_grad[:, :width].reshape(head_shape)
        value_part = kv_grad[:, width:]
        query_back = unrotate(query_grad, cosine_table, sine_table).reshape(length, width)
        key_back = unrotate(key_part, cosine_table, sine_table).reshape(length, width)
        projected_grad = jnp.concatenate([query_back, key_back, value_part], axis=1).astype(
            jnp.bfloat16
        )
        project_bias_grad = jnp.sum(projected_grad.astype(jnp.float32), axis=0)
        project_weight_grad = contract_rows(token_low, projected_grad)
        input_grads.append(first_grad + times_transpose(projected_grad, params[0]))
        local_grads = (
            project_weight_grad,
            project_bias_grad,
            output_weight_grad,
            output_bias_grad,
            first_gain_grad,
            first_shift_grad,
            up_weight_grad,
            up_bias_grad,
            down_weight_grad,
            down_bias_grad,
            second_gain_grad,
            second_shift_grad,
            embed_weight_grad,
        )
        summed = (
            lax.psum_scatter(local_grads[0], ("group", "wide"), scatter_dimension=0, tiled=True),
            lax.psum_scatter(local_grads[1], ("group", "wide"), scatter_dimension=0, tiled=True),
            lax.psum_scatter(local_grads[2], ("group", "wide"), scatter_dimension=0, tiled=True),
            lax.psum_scatter(local_grads[3], ("group", "wide"), scatter_dimension=0, tiled=True),
            lax.psum_scatter(local_grads[4], ("group", "wide"), scatter_dimension=0, tiled=True),
            lax.psum_scatter(local_grads[5], ("group", "wide"), scatter_dimension=0, tiled=True),
            lax.psum_scatter(local_grads[6], ("group", "wide"), scatter_dimension=0, tiled=True),
            lax.psum_scatter(local_grads[7], ("group", "wide"), scatter_dimension=0, tiled=True),
            lax.psum_scatter(local_grads[8], ("group", "wide"), scatter_dimension=0, tiled=True),
            lax.psum_scatter(local_grads[9], ("group", "wide"), scatter_dimension=0, tiled=True),
            lax.psum_scatter(local_grads[10], ("group", "wide"), scatter_dimension=0, tiled=True),
            lax.psum_scatter(local_grads[11], ("group", "wide"), scatter_dimension=0, tiled=True),
            lax.psum_scatter(local_grads[12], ("group", "wide"), scatter_dimension=0, tiled=True),
        )
        grad_total = (
            summed
            if grad_total is None
            else tuple((total + part for total, part in zip(grad_total, summed)))
        )
    layer_out = jnp.stack(results)[:, None]
    embed_out = jnp.stack(embeddings)[:, None]
    token_grad = jnp.stack(input_grads)[:, None]
    return (
        layer_out,
        embed_out,
        token_grad,
        grad_total[0],
        grad_total[1],
        grad_total[2],
        grad_total[3],
        grad_total[4],
        grad_total[5],
        grad_total[6],
        grad_total[7],
        grad_total[8],
        grad_total[9],
        grad_total[10],
        grad_total[11],
        grad_total[12],
    )


MESH = pl.DeviceIdType.MESH
F32 = jnp.float32
BF16 = jnp.bfloat16
PLANE = 4
LINE = 4
GATHER_SEMS = 42
REDUCE_SEMS = 42
REDUCE_KINDS = {
    "core": 0, "upper": 4, "lower": 8, "row": 12, "column": 16, "line": 20, "hop": 25,
    "own upper": 29, "own lower": 30, "own row": 31, "own column": 32, "ring line": 33, "ring hop": 38,
}
FORWARD_PARTS = ((True, ((0, 0, 4, 0, 2, ), (1, 0, 4, 0, 4, ), (2, 0, 4, 0, 4, ), ), ), (False, ((0, 0, 4, 2, 4, ), ), ), (True, ((3, 0, 4, 0, 4, ), ), ), (True, ((4, 0, 4, 0, 4, ), ), ), (False, ((5, 0, 2, 0, 4, ), ), ), (True, ((5, 2, 4, 0, 4, ), ), ), )
FORWARD_STEPS = (((1003, 1, 1002, 20005, 2001, 0, 3, 2, 2000, 3001, 41, 1202, 10, 12, 4002, 42, 1103, 2041, 23, 2010, 2003, 3000, 2012, 20003, 1401, 3003, 2023, 51, 3041, 20, 2043, 1404, 2020, 20002, 52, 33, 1400, 53, 43, 113, 2013, 2033, 2052, 2032, 32, 3012, 1410, 1441, 4003, 222, 62, 202, 2042, 3010, 153, 2212, 143, 3002, 103, 2222, 4103, 63, 22, 133, 242, 252, 1424, 1451, 2051, 2002, 232, 3051, 2113, 4202, 1420, 262, 2232, 2133, 1414, 13, 2143, 3113, 163, 123, 1444, 5001, 3103, 3020, 1454, 212, 5002, 3023, 3053, 354, 2022, 2242, 2314, 334, 2053, 4401, 21005, 2334, 324, 344, 3052, 3013, 1464, 1434, 5000, 314, 304, 4400, 2103, 3202, 364, 900, 1900, 2062, 20900, 2153, ), ), ((), ), ((3033, 2202, 2252, ), (), (2123, ), (23004, 3063, 3032, 2063, 3043, ), (3042, ), (3153, 2344, 5010, 5041, 23900, ), ), ((3252, 5043, 5053, 5052, 4441, 3062, 3022, 2304, ), (5013, 5022, 3212, 5023, 4410, ), (3133, 2163, 3304, 3242, 3232, 3222, ), (3143, ), (5051, 3163, 2354, 5020, 3123, 2262, 2324, 21003, 5012, 5042, 3354, ), (3262, 5153, 4404, ), (3334, 3314, 5242, 5063, 4451, 5032, 5033, 2364, ), (4414, 3324, 2900, 3344, 21002, 5062, 4420, 5003, 3364, ), ), ((), (5143, 5113, 3900, 4454, 5232, 5222, 5212, ), ), ((4424, 5133, 5123, 5252, ), (), (4464, ), (5202, 4434, 5103, 5334, 5344, 5262, 5163, ), (4444, 5314, 5324, ), (5304, 5364, 5354, ), (), (4900, 5900, 21900, ), ), ((), (22003, 22005, ), ), ((), (), (), (), (22002, ), (), (), (), ), ((), (22900, ), ), )
BACKWARD_STEPS = ((900, 0, 901, ), ((10, 100, 1, 902, 110, 300, ), (101, 301, 11, ), (200, 201, ), (111, 210, 211, 400, ), (20, 303, 310, ), (), (311, 212, 401, ), (), ), (911, 302, 903, 904, 213, 21, 909, 410, 905, 120, 30, 312, 411, 203, 31, 313, 221, 202, 320, 130, 530, 131, 930, 920, 906, 531, 231, 321, 330, 121, 40, 41, 230, 412, 921, 332, 232, 331, 922, 923, 532, 220, 323, 924, 140, 925, 907, 141, 912, 233, 240, 420, 340, 430, 241, 341, 322, 413, 402, 222, 243, 533, 223, 910, 440, 421, 333, 431, 432, 403, 422, 343, 242, 630, 342, 730, 441, 442, 908, 433, 830, 423, 443, ), )


def place():
    group = lax.axis_index("group")
    wide = lax.axis_index("wide")
    return (group, lax.rem(group, 2), group // 2, wide // 2, lax.rem(wide, 2))


def when(cond, act):
    if cond is True:
        act()
    else:
        pl.when(cond)(act)


def both(left, right):
    return right if left is True else jnp.logical_and(left, right)


def remote(src, dst, send_sem, recv_sem, device):
    return pltpu.make_async_remote_copy(
        src_ref=src,
        dst_ref=dst,
        send_sem=send_sem,
        recv_sem=recv_sem,
        device_id=device,
        device_id_type=MESH,
    )


def entry_barrier():
    g, x, y, z, c = place()
    devices = []
    for step in range(1, 8):
        other = lax.rem(g * 2 + c + step, 8)
        devices.append((other // 2, z * 2 + lax.rem(other, 2)))
    devices.append((g, lax.rem(z + 1, LINE) * 2 + c))
    devices.append((g, lax.rem(z + LINE - 1, LINE) * 2 + c))
    barrier = pltpu.get_barrier_semaphore()
    for device in devices:
        pl.semaphore_signal(barrier, inc=1, device_id=device, device_id_type=MESH)
    pl.semaphore_wait(barrier, len(devices))


class Sender:
    def __init__(self, send_sems, recv_sems):
        self.send_sems, self.recv_sems = send_sems, recv_sems
        self.pending, self.draining = [], False

    def copy(self, src, dst, index, device):
        return remote(src, dst, self.send_sems.at[index], self.recv_sems.at[index], device)

    def send(self, cond, src, dst, index, device):
        copy = self.copy(src, dst, index, device)
        when(cond, copy.wait_send if self.draining else copy.start)

    def post(self, cond, src, dst, index, device):
        self.send(cond, src, dst, index, device)
        self.pending.append((cond, src, dst, index, device))

    def land(self, ref, index, device):
        self.copy(ref, ref, index, device).wait_recv()

    def do(self, cond, act):
        if not self.draining:
            when(cond, act)

    def drain(self, ticks):
        self.draining = True
        for tick in ticks:
            tick()
        for call in self.pending:
            self.send(*call)


def near_items(z, distance):
    if distance == 0:
        return [(0, z, True)]
    return [
        (distance, jnp.maximum(z - distance, 0), z >= distance),
        (3 + distance, jnp.minimum(z + distance, LINE - 1), z + distance < LINE),
    ]


class Gather:
    def __init__(self, parts, sender, local_sems):
        self.parts, self.sender, self.local_sems = parts, sender, local_sems
        self.seen = set()
        g, x, y, z, c = place()
        self.g, self.z, self.c = g, z, c
        self.gx, self.gy, self.gd = g + 1 - 2 * x, g + 2 - 4 * y, 3 - g
        self.devices = (
            (g, jnp.minimum(z + 1, LINE - 1) * 2 + c),
            (g, jnp.maximum(z - 1, 0) * 2 + c),
            (self.gx, z * 2 + c),
            (self.gy, z * 2 + c),
            (g, z * 2 + 1 - c),
        )
        for part in parts:
            for member in part[1]:
                self.own(member).start()

    def window(self, member, g, zi, c, rows=None):
        shard, full, top, count, left, columns, index = member
        first, last = (0, count) if rows is None else rows
        return full.at[g, zi, c, top + first : top + last, left : left + columns]

    def shard(self, member):
        shard, full, top, count, left, columns, index = member
        return shard.at[top : top + count, left : left + columns]

    def own(self, member):
        return pltpu.make_async_copy(
            self.shard(member),
            self.window(member, self.g, self.z, self.c),
            self.local_sems.at[member[6]],
        )

    def ring(self, member, zi, c):
        shard, full, top, count, left, columns, index = member
        return full.at[:, zi, c, top : top + count, left : left + columns]

    def item(self, slot):
        z = self.z
        if slot == 0:
            return z, True
        if slot < 4:
            return jnp.maximum(z - slot, 0), z >= slot
        return jnp.minimum(z + slot - 3, LINE - 1), z + slot - 3 < LINE

    def land(self, cond, ref, index):
        self.sender.do(cond, lambda: self.sender.land(ref, index, self.devices[4]))

    def arrivals(self, part, event, slot):
        zi, cond = self.item(slot)
        line = self.parts[part][0]
        for member in self.parts[part][1]:
            base, half, rows = member[6] * GATHER_SEMS, member[3] // 2, member[3]
            diagonal = lambda: (
                self.land(cond, self.window(member, self.gd, zi, self.c, (0, half)), base + 21 + slot),
                self.land(cond, self.window(member, self.gd, zi, self.c, (half, rows)), base + 28 + slot),
            )
            if event == 0 and slot > 0:
                self.land(cond, self.window(member, self.g, zi, self.c), base + slot)
            elif event == 1:
                self.land(cond, self.window(member, self.gx, zi, self.c), base + 7 + slot)
            elif event == 2:
                self.land(cond, self.window(member, self.gy, zi, self.c), base + 14 + slot)
            elif event == 3 or (event == 4 and slot == 0):
                diagonal()
                if slot == 0:
                    self.sender.do(True, lambda: self.own(member).wait())
            elif event == 4:
                self.land(cond, self.ring(member, zi, self.c), base + slot)

    def step(self, part, event, slot, link):
        if (part, event, slot) not in self.seen:
            self.seen.add((part, event, slot))
            self.arrivals(part, event, slot)
        zi, cond = self.item(slot)
        z, device = self.z, self.devices[link]
        for member in self.parts[part][1]:
            base, half, rows = member[6] * GATHER_SEMS, member[3] // 2, member[3]
            if link == 0:
                cond_here, index = both(cond, z < LINE - 1), base + slot + 1
            elif link == 1:
                cond_here, index = both(cond, z > 0), base + (4 if slot == 0 else slot + 1)
            else:
                cond_here = cond
                index = base + slot + ({2: 7, 3: 14} if event == 0 else {3: 21, 2: 28, 4: 35})[link]
            if event == 0:
                target = self.window(member, self.g, zi, self.c)
                source = self.shard(member) if slot == 0 else target
            elif event == 1:
                source = target = self.window(member, self.gx, zi, self.c, (0, half))
            elif event == 2:
                source = target = self.window(member, self.gy, zi, self.c, (half, rows))
            else:
                source = target = self.ring(member, zi, self.c)
            self.sender.send(cond_here, source, target, index, device)

    def finish(self, part):
        for member in self.parts[part][1]:
            for slot in range(7):
                zi, cond = self.item(slot)
                self.land(cond, self.ring(member, zi, 1 - self.c), member[6] * GATHER_SEMS + 35 + slot)


def staged(order, stages, delays):
    ticks = []
    for t in range(len(order) + delays[-1]):

        def tick(t=t):
            for stage, delay in zip(stages, delays):
                if 0 <= t - delay < len(order):
                    stage(*order[t - delay])

        ticks.append(tick)
    return ticks


def add_into(target, terms):
    rows, columns = target.shape
    step = min(columns, 512)

    def body(i, carry):
        cut = pl.ds(pl.multiple_of(i * step, step), step)
        value = terms[0][:, cut].astype(F32)
        for term in terms[1:]:
            value = value + term[:, cut].astype(F32)
        target[:, cut] = value.astype(target.dtype)
        return carry

    lax.fori_loop(0, columns // step, body, 0)


class Exchange:
    def __init__(self, sources, targets, outward, sender, base, local_sems, local_base):
        self.sources, self.targets, self.outward = sources, targets, outward
        self.sender, self.base = sender, base
        self.local_sems, self.local_base = local_sems, local_base
        self.started = False
        g, x, y, z, c = place()
        self.g, self.z, self.c = g, z, c
        self.neighbours = {2: g + 1 - 2 * x, 3: g + 2 - 4 * y, 5: 3 - g}

    def device(self, index, outward):
        g, z, c = self.g, self.z, self.c
        if outward:
            return (index * 2 + c, z * 2 + g // 2)
        return (2 * c + index, z * 2 + lax.rem(g, 2))

    def same(self, device):
        return jnp.logical_and(device[0] == self.g, device[1] == self.z * 2 + self.c)

    def local(self, i, index, slot):
        return pltpu.make_async_copy(
            self.sources[i].at[index],
            self.targets[i].at[slot],
            self.local_sems.at[self.local_base + i],
        )

    def step(self, link):
        slot = lax.rem(self.g, 2) if self.outward else self.g // 2
        first = not self.started and not self.sender.draining
        self.started = True
        for i in range(len(self.sources)):
            for index in range(2):
                device = self.device(index, self.outward)
                if first:
                    when(self.same(device), lambda: self.local(i, index, slot).start())
                copy = remote(
                    self.sources[i].at[index],
                    self.targets[i].at[slot],
                    self.sender.send_sems.at[self.base + i * 4 + 2 + index],
                    self.sender.recv_sems.at[self.base + i * 4 + slot],
                    device,
                )
                cond = device[0] == self.neighbours[link]
                if link == 2:
                    here = jnp.logical_and(device[0] == self.g, device[1] != self.z * 2 + self.c)
                    cond = jnp.logical_or(cond, here)
                when(cond, copy.wait_send if self.sender.draining else copy.start)

    def arrive(self):
        for i in range(len(self.sources)):
            for index in range(2):
                device = self.device(index, not self.outward)
                target = self.targets[i].at[index]
                when(self.same(device), lambda: self.local(i, index, index).wait())
                when(
                    jnp.logical_not(self.same(device)),
                    lambda: self.sender.land(
                        target, self.base + i * 4 + index, (self.g, self.z * 2 + 1 - self.c)
                    ),
                )


def hbm():
    return pl.BlockSpec(memory_space=pltpu.HBM)


def vmem():
    return pl.BlockSpec(memory_space=pltpu.VMEM)


def chain(*ticks):
    def act():
        for tick in ticks:
            tick()

    return act


def run_with(ticks, steps, body):
    def act(i, carry):
        body(i)
        for j, tick in enumerate(ticks[:steps]):
            pl.when(i == j)(tick)
        return carry

    lax.fori_loop(0, steps, act, 0)
    for tick in ticks[steps:]:
        tick()


def lane_half(shape, period, half):
    lanes = lax.broadcasted_iota(jnp.int32, shape, 1)
    return lax.rem(lanes, period) < half


def turn(values):
    first = lane_half(values.shape, HEAD_DIM, HEAD_DIM // 2)
    return jnp.where(
        first,
        -pltpu.roll(values, values.shape[1] - HEAD_DIM // 2, 1),
        pltpu.roll(values, HEAD_DIM // 2, 1),
    )


def dot_rows(left, right):
    return lax.dot_general(left, right, (((1,), (0,)), ((), ())), preferred_element_type=F32)


def dot_columns(left, right):
    return lax.dot_general(left, right, (((1,), (1,)), ((), ())), preferred_element_type=F32)


def attend_pair(
    query_ref, key_ref, value_ref, far_key_ref, far_value_ref, seg_ref, seg_near_ref, seg_far_ref, out_ref, norm_ref
):
    rows = query_ref.shape[0]
    first = lane_half((rows, 128), 128, HEAD_DIM)
    tile = 256
    for r in range(rows // tile):
        rs = pl.ds(r * tile, tile)
        query = query_ref[rs, :]
        low_half = first[:tile]
        seg = seg_ref[rs, 0:1]
        near, far = seg == seg_near_ref[...], seg == seg_far_ref[...]
        outs, norms = [], []
        for h in range(2):
            keep = low_half if h == 0 else jnp.logical_not(low_half)
            one = jnp.where(keep, query, jnp.zeros_like(query))
            near_scores = jnp.where(near, dot_columns(one, key_ref[...]), neg_large)
            far_scores = jnp.where(far, dot_columns(one, far_key_ref[...]), neg_large)
            top = jnp.maximum(
                jnp.max(near_scores, axis=1, keepdims=True), jnp.max(far_scores, axis=1, keepdims=True)
            )
            near_expon, far_expon = jnp.exp(near_scores - top), jnp.exp(far_scores - top)
            total = jnp.sum(near_expon, axis=1, keepdims=True) + jnp.sum(
                far_expon, axis=1, keepdims=True
            )
            mixed = dot_rows(near_expon.astype(BF16), value_ref[...]) + dot_rows(
                far_expon.astype(BF16), far_value_ref[...]
            )
            outs.append(mixed / total)
            norms.append(jnp.broadcast_to(top + jnp.log(total), (tile, 128)))
        out_ref[rs, :] = jnp.where(low_half, outs[0], outs[1]).astype(BF16)
        flipped = jnp.transpose(jnp.where(low_half, norms[0], norms[1]))
        norm_ref[0:1, rs] = flipped[0:1]
        norm_ref[1:2, rs] = flipped[HEAD_DIM : HEAD_DIM + 1]


def stretch(packed, vectors, sizes):
    shards = packed.shape[0] // 32
    for row, lane, size, target in vectors:
        pick_rows = lax.broadcasted_iota(jnp.int32, (shards, shards * 32), 0) * 32 + row
        pick = lax.broadcasted_iota(jnp.int32, (shards, shards * 32), 1) == pick_rows
        part = dot_rows(pick.astype(F32).astype(BF16), packed).astype(BF16)
        step = 1024

        def body(i, carry):
            at = pl.multiple_of(i * step, step)
            column = (lax.broadcasted_iota(jnp.int32, (1, step), 1) + i * step).astype(F32)
            shard = jnp.floor((column + 0.5) * (1.0 / size))
            lane_of = (column - shard * size + lane).astype(jnp.int32)
            spread = lax.broadcasted_iota(jnp.int32, (128, step), 0) == lane_of
            value = dot_rows(part, spread.astype(F32).astype(BF16))
            keep = lax.broadcasted_iota(jnp.int32, (shards, step), 0) == shard.astype(jnp.int32)
            target[:, pl.ds(at, step)] = jnp.sum(jnp.where(keep, value, 0.0), axis=0, keepdims=True)
            return carry

        lax.fori_loop(0, shards * size // step, body, 0)


def flat(value):
    return value.reshape(-1, value.shape[-1])


def row_mean(value):
    return jnp.mean(value, axis=1, keepdims=True)


def forward_kernel(*refs):
    shards, refs = refs[:6], refs[6:]
    (tokens, out_cot, embed_cot, segments, cosine, sine), refs = refs[:6], refs[6:]
    (
        project_out, token_out, qkv_out, far_out, context_out, norm, hidden_out, act_out, up_grad_out,
        down_grad_out, result_out, embed_cot_out, branch_grad_out, context_grad_out, first_grad_out,
        sums, seg_out, layer_back, embed_back,
    ), refs = refs[:19], refs[19:]
    fulls, refs = refs[:6], refs[6:]
    (
        token_in, cot_in, embed_cot_in, far_seg, seg_column, vectors, qkv, far, context, normed, rstd,
        hidden_low, act, slope, result_low, embedded, sum_grad, down_grad, branch_grad, context_grad,
        send_sems, recv_sems, local_sems,
    ) = refs
    project_w, embed_w, small_w, output_w, up_w, down_w = fulls
    g, x, y, z, c = place()
    partner = (g, z * 2 + 1 - c)
    rows, width = context.shape
    sender = Sender(send_sems, recv_sems)
    spare = sum(len(p[1]) for p in FORWARD_PARTS) * GATHER_SEMS
    flushed = []

    def flush(source, target, index):
        copy = pltpu.make_async_copy(source, target, local_sems.at[40 + index])
        copy.start()
        flushed.append((source, target, index))

    entry_barrier()
    parts = []
    for line, members in FORWARD_PARTS:
        rows_of = []
        for array, first_row, last_row, first_column, last_column in members:
            height, breadth = shards[array].shape
            top, left = first_row * height // 4, first_column * breadth // 4
            rows_of.append(
                (
                    shards[array],
                    fulls[array],
                    top,
                    last_row * height // 4 - top,
                    left,
                    last_column * breadth // 4 - left,
                    sum(len(p[1]) for p in parts) + len(rows_of),
                )
            )
        parts.append((line, rows_of))
    plan = Gather(parts, sender, local_sems)
    exchanges = {
        20: Exchange([tokens], [token_in], True, sender, spare + 2, local_sems, 20),
        21: Exchange(
            [out_cot, embed_cot], [cot_in, embed_cot_in], True, sender, spare + 6, local_sems, 21
        ),
        22: Exchange(
            [result_low, embedded], [layer_back, embed_back], False, sender, spare + 14, local_sems, 23
        ),
    }

    def perform(steps):
        def act():
            for step in steps:
                part, event, slot, link = step // 1000, step // 100 % 10, step // 10 % 10, step % 10
                if part == 23:
                    if event == 9:
                        sender.do(True, lambda: sender.land(far, spare + 1, partner))
                    else:
                        sender.send(True, qkv.at[:, width:], far, spare + 1, partner)
                elif part >= 20:
                    if event != 9:
                        exchanges[part].step(link)
                    elif not sender.draining:
                        exchanges[part].arrive()
                elif event == 9:
                    plan.finish(part)
                else:
                    plan.step(part, event, slot, link)

        return act

    ticks = [[perform(steps) for steps in phase] for phase in FORWARD_STEPS]
    sender.post(True, segments, far_seg, spare, partner)
    ticks[0][0]()
    sender.land(far_seg, spare, partner)
    micro = g // 2
    own_ids, far_ids = segments[micro].astype(F32), far_seg[micro].astype(F32)
    ids = jnp.where(lax.rem(g, 2) == c, own_ids, far_ids)
    halves = (ids[:, :rows], ids[:, rows:])
    near_row = jnp.where(c == 0, halves[0], halves[1])
    far_row = jnp.where(c == 0, halves[1], halves[0])
    seg_out[0:1, :] = near_row
    seg_out[1:2, :] = far_row
    seg_column[...] = jnp.transpose(jnp.broadcast_to(near_row, (128, rows)))
    flush(project_w, project_out, 0)
    flush(token_in, token_out, 1)
    vector = lambda i, size: vectors.at[i : i + 1, 0:size]
    stretch(
        flat(small_w[...]),
        (
            (0, 0, 96, vector(0, 3 * width)),
            (1, 0, 128, vector(1, 4 * width)),
            (2, 0, 32, vector(2, width)),
            (2, 32, 32, vector(3, width)),
            (2, 64, 32, vector(4, width)),
            (2, 96, 32, vector(5, width)),
            (3, 0, 32, vector(6, width)),
            (3, 32, 32, vector(7, width)),
        ),
        None,
    )
    tile = 512
    wide = qkv.shape[1] // tile

    def project_tile(i):
        t = lax.rem(i + 2, wide)
        cut = pl.ds(pl.multiple_of(t * tile, tile), tile)
        value = dot_rows(flat(token_in[...]), flat(project_w[:, :, :, :, cut]))
        value = value + vectors[0:1, cut]

        @pl.when(t < 4)
        def _():
            factor = jnp.where(t < 2, HEAD_DIM ** (-0.5), 1.0)
            for j in range(tile // 128):
                part = value[:, j * 128 : (j + 1) * 128]
                part = (part * cosine[...] + turn(part) * sine[...]) * factor
                qkv[:, pl.ds(pl.multiple_of(t * tile + j * 128, 128), 128)] = part.astype(BF16)

        @pl.when(t >= 4)
        def _():
            qkv[:, cut] = value.astype(BF16)

    ticks[1][0]()
    run_with(ticks[2], wide, project_tile)
    flush(qkv, qkv_out, 2)
    flush(far, far_out, 3)

    def attend_one(i):
        at = pl.multiple_of(i * 128, 128)
        cut = lambda ref, base: ref.at[:, pl.ds(base + at, 128)]
        attend_pair(
            cut(qkv, 0), cut(qkv, width), cut(qkv, 2 * width), cut(far, 0), cut(far, width),
            seg_column, seg_out.at[0:1], seg_out.at[1:2], cut(context, 0), norm.at[i],
        )

    run_with(ticks[3], width // 128, attend_one)
    flush(context, context_out, 4)
    half = rows // 2
    output_weight, bias_o = lambda: flat(output_w[...]), vectors[2:3, 0:width]

    def hidden_of(cut):
        return normed[cut, :] * vectors[3:4, 0:width] + vectors[4:5, 0:width]

    def branch_tile(i):
        cut = pl.ds(pl.multiple_of(i * half, half), half)
        resid = dot_rows(context[cut, :], output_weight()) + vectors[2:3, 0:width]
        resid = resid + token_in[i].astype(F32)
        center = resid - row_mean(resid)
        scale = lax.rsqrt(row_mean(center * center) + eps_norm)
        normed[cut, :] = center * scale
        rstd[0, cut, :] = jnp.broadcast_to(scale, (half, 128))
        hidden_low[cut, :] = hidden_of(cut).astype(BF16)

    run_with(ticks[4], 2, branch_tile)
    flush(hidden_low, hidden_out, 5)

    def up_tile(j):
        cut = pl.ds(pl.multiple_of(j * tile, tile), tile)
        value = dot_rows(hidden_low[...], flat(up_w[:, :, :, :, cut])) + vectors[1:2, cut]
        below = 0.5 + 0.5 * lax.erf(value * 0.7071067811865476)
        density = jnp.exp(-0.5 * value * value) * 0.3989422804014327
        act[:, cut] = (value * below).astype(BF16)
        slope[:, cut] = (below + value * density).astype(BF16)

    ff = act.shape[1]
    run_with(ticks[5], ff // tile, up_tile)
    flush(act, act_out, 6)
    flush(embed_cot_in, embed_cot_out, 7)
    sums[...] = jnp.zeros_like(sums)

    def add_sum(row, value):
        sums[row : row + 1, 0:width] += jnp.sum(value, axis=0, keepdims=True)

    def norm_back(grads, row_normed, scale, gain):
        scaled = grads * gain
        return scale * (
            scaled - row_mean(scaled) - row_normed * row_mean(scaled * row_normed)
        )

    def down_tile(i):
        cut = pl.ds(pl.multiple_of(i * half, half), half)
        gain, shift = vectors[6:7, 0:width], vectors[7:8, 0:width]
        resid = dot_rows(act[cut, :], flat(down_w[...])) + vectors[5:6, 0:width]
        resid = resid + hidden_of(cut)
        center = resid - row_mean(resid)
        scale = lax.rsqrt(row_mean(center * center) + eps_norm)
        row_normed = center * scale
        low = (row_normed * gain + shift).astype(BF16)
        result_low[i] = low
        embed_full = flat(embed_w[...])
        embedded[i] = dot_rows(low, embed_full).astype(BF16)
        grads = cot_in[i].astype(F32) + dot_columns(embed_cot_in[i], embed_full)
        add_sum(6, grads * row_normed)
        add_sum(7, grads)
        total = norm_back(grads, row_normed, scale, gain)
        sum_grad[cut, :] = total
        low = total.astype(BF16)
        down_grad[cut, :] = low
        add_sum(5, low.astype(F32))

    run_with(ticks[6], 2, down_tile)
    flush(result_low, result_out, 8)
    flush(down_grad, down_grad_out, 9)

    def up_grad_tile(j):
        cut = pl.ds(pl.multiple_of(j * tile, tile), tile)
        part = flat(down_w[j // 2, pl.ds(lax.rem(j, 2) * 2, 2)])
        value = (dot_columns(down_grad[...], part) * slope[:, cut].astype(F32)).astype(BF16)
        slope[:, cut] = value
        sums[1:2, cut] = jnp.sum(value.astype(F32), axis=0, keepdims=True)

    run_with(ticks[7], ff // tile, up_grad_tile)
    flush(slope, up_grad_out, 10)

    def first_tile(i):
        cut = pl.ds(pl.multiple_of(i * half, half), half)
        grads = sum_grad[cut, :] + dot_columns(slope[cut, :], flat(up_w[...]))
        row_normed = normed[cut, :]
        add_sum(3, grads * row_normed)
        add_sum(4, grads)
        total = norm_back(grads, row_normed, rstd[0, cut, 0:1], vectors[3:4, 0:width])
        sum_grad[cut, :] = total
        low = total.astype(BF16)
        branch_grad[cut, :] = low
        add_sum(2, low.astype(F32))
        context_grad[cut, :] = dot_columns(low, output_weight()).astype(BF16)

    run_with(ticks[8], 2, first_tile)
    flush(sum_grad, first_grad_out, 11)
    flush(branch_grad, branch_grad_out, 12)
    flush(context_grad, context_grad_out, 13)
    sender.drain([tick for phase in ticks for tick in phase])
    for source, target, index in flushed:
        pltpu.make_async_copy(source, target, local_sems.at[40 + index]).wait()


def forward(shards, sources, segments, tables, ff):
    piece, width = sources[0].shape[1:]
    lanes = sources[2].shape[2]
    rows = 2 * piece
    semaphores = sum(len(p[1]) for p in FORWARD_PARTS) * GATHER_SEMS + 32
    fulls = [(PLANE, LINE, 2) + s.shape for s in shards]
    shape = jax.ShapeDtypeStruct
    outs = [
        shape(fulls[0], BF16),
        shape((2, piece, width), BF16),
        shape((rows, 3 * width), BF16),
        shape((rows, 2 * width), BF16),
        shape((rows, width), BF16),
        shape((width // 128, 8, rows), F32),
        shape((rows, width), BF16),
        shape((rows, ff), BF16),
        shape((rows, ff), BF16),
        shape((rows, width), BF16),
        shape((2, piece, width), BF16),
        shape((2, piece, lanes), BF16),
        shape((rows, width), BF16),
        shape((rows, width), BF16),
        shape((rows, width), F32),
        shape((8, ff), F32),
        shape((8, rows), F32),
        shape((2, piece, width), BF16),
        shape((2, piece, lanes), BF16),
    ]
    spaces = [hbm()] * len(outs)
    for i in (5, 15, 16):
        spaces[i] = vmem()
    scratch = [pltpu.VMEM(f, BF16) for f in fulls] + [
        pltpu.VMEM((2, piece, width), BF16),
        pltpu.VMEM((2, piece, width), BF16),
        pltpu.VMEM((2, piece, lanes), BF16),
        pltpu.VMEM(segments.shape, jnp.int32),
        pltpu.VMEM((rows, 128), F32),
        pltpu.VMEM((8, ff), F32),
        pltpu.VMEM((rows, 3 * width), BF16),
        pltpu.VMEM((rows, 2 * width), BF16),
        pltpu.VMEM((rows, width), BF16),
        pltpu.VMEM((rows, width), F32),
        pltpu.VMEM((1, rows, 128), F32),
        pltpu.VMEM((rows, width), BF16),
        pltpu.VMEM((rows, ff), BF16),
        pltpu.VMEM((rows, ff), BF16),
        pltpu.VMEM((2, piece, width), BF16),
        pltpu.VMEM((2, piece, lanes), BF16),
        pltpu.VMEM((rows, width), F32),
        pltpu.VMEM((rows, width), BF16),
        pltpu.VMEM((rows, width), BF16),
        pltpu.VMEM((rows, width), BF16),
        pltpu.SemaphoreType.DMA((semaphores,)),
        pltpu.SemaphoreType.DMA((semaphores,)),
        pltpu.SemaphoreType.DMA((60,)),
    ]
    return pl.pallas_call(
        forward_kernel,
        out_shape=outs,
        in_specs=[hbm()] * 9 + [vmem()] * 3,
        out_specs=spaces,
        scratch_shapes=scratch,
        compiler_params=pltpu.CompilerParams(
            collective_id=1, has_side_effects=True, vmem_limit_bytes=67043328
        ),
        name="forward",
    )(*shards, *sources, segments, *tables)


def attend_back_pair(
    query, key, value, far_key, far_value, grad, norm, seg_row, seg_near, seg_far, tables, summed
):
    rows = query.shape[0]
    tile = 256
    cosine, sine, shift = tables
    low_half = lane_half((rows, 128), 128, HEAD_DIM)
    query_low = lane_half((tile, 128), 128, HEAD_DIM)
    for total in summed:
        total[...] = jnp.zeros_like(total)

    def body(r, carry):
        rs = pl.ds(pl.multiple_of(r * tile, tile), tile)
        query_rows, grad_rows = query[rs, :], grad[rs, :]
        sides = ((key[...], value[...], seg_near), (far_key[...], far_value[...], seg_far))
        query_grads = []
        key_grads, value_grads = [[], []], [[], []]
        for h in range(2):
            keep = query_low if h == 0 else jnp.logical_not(query_low)
            one = jnp.where(keep, query_rows, jnp.zeros_like(query_rows))
            one_grad = jnp.where(keep, grad_rows, jnp.zeros_like(grad_rows))
            top = norm[h : h + 1, rs]
            kept = []
            delta = jnp.zeros((1, tile), F32)
            for keys, values, seg_key in sides:
                same = seg_key[:, 0:1] == seg_row[:, rs]
                scores = jnp.where(same, dot_columns(keys, one), neg_large)
                probs = jnp.exp(scores - top)
                product = probs * dot_columns(values, one_grad)
                delta = delta + jnp.sum(product, axis=0, keepdims=True)
                kept.append((probs, product))
            total = None
            for i, (keys, values, seg_key) in enumerate(sides):
                probs, product = kept[i]
                score_grad = (product - probs * delta).astype(BF16)
                key_grads[i].append(dot_rows(score_grad, query_rows))
                value_grads[i].append(dot_rows(probs.astype(BF16), grad_rows))
                part = contract_rows(score_grad, keys)
                total = part if total is None else total + part
            query_grads.append(total)
        for i in range(2):
            summed[i][...] += jnp.where(low_half, key_grads[i][0], key_grads[i][1])
            summed[2 + i][...] += jnp.where(low_half, value_grads[i][0], value_grads[i][1])
        joined = jnp.where(query_low, query_grads[0], query_grads[1]) * HEAD_DIM ** (-0.5)
        query[rs, :] = (joined * cosine[rs, :] - turn(joined) * sine[rs, :]).astype(BF16)
        return carry

    lax.fori_loop(0, rows // tile, body, 0)
    near, far = summed[0][...], summed[1][...]
    far_cosine = cosine[...] * shift[0:1, :] - sine[...] * shift[1:2, :]
    far_sine = sine[...] * shift[0:1, :] + cosine[...] * shift[1:2, :]
    key[...] = (near * cosine[...] - turn(near) * sine[...]).astype(BF16)
    value[...] = summed[2][...].astype(BF16)
    far_key[...] = (far * far_cosine - turn(far) * far_sine).astype(BF16)
    far_value[...] = summed[3][...].astype(BF16)


class Reduce:
    def __init__(self, arrays, sender):
        self.arrays, self.sender = arrays, sender
        g, x, y, z, c = place()
        self.g, self.z, self.c = g, z, c
        self.gx, self.gy, self.gd = g + 1 - 2 * x, g + 2 - 4 * y, 3 - g
        self.to_x, self.to_y = (self.gx, z * 2 + c), (self.gy, z * 2 + c)
        self.to_core = (g, z * 2 + 1 - c)
        lower = z < 2
        even = lax.rem(z, 2) == 0
        third = jnp.where(even, z + 1, z - 1)
        self.order = (jnp.where(lower, 3, 0), jnp.where(lower, 2, 1), third, z)
        self.rising = (lower, lower, even)

    def index(self, a, kind, i=0):
        return a * REDUCE_SEMS + REDUCE_KINDS[kind] + i

    def start(self, a, p):
        array, sender = self.arrays[a], self.sender

        def copy(b, i):
            other = self.arrays[b]
            return sender.copy(
                other["send"].at[i % 2],
                other["held"].at[self.order[i]],
                self.index(b, "core", i),
                self.to_core,
            )

        if sender.draining:
            if p == 1 and a not in (1, 2):
                copy(a, 2).wait_send()
                copy(a, 3).wait_send()
            return
        before = (a, 0) if p == 1 else {2: (1, 2), 3: (2, 2)}.get(a)
        if before is not None:
            copy(before[0], before[1]).wait_send()
            copy(before[0], before[1] + 1).wait_send()
        zs = self.order[2 * p : 2 * p + 2]
        array["product"](1 - self.c, zs, (array["send"].at[0], array["send"].at[1]), False)
        copy(a, 2 * p).start()
        copy(a, 2 * p + 1).start()

    def meet(self, a, p):
        array, sender = self.arrays[a], self.sender
        held, half_in, low = array["held"], array["half"], array["low"]
        rows, columns = held.shape[2:]
        cut = rows // 2
        zs = self.order[2 * p : 2 * p + 2]

        def work():
            for i in range(2):
                sender.land(held.at[zs[i]], self.index(a, "core", 2 * p + i), self.to_x)
            array["product"](self.c, zs, (held.at[zs[0]], held.at[zs[1]]), True)

        sender.do(True, work)
        for i in range(2):
            block = held.at[zs[i], self.gd]
            sender.send(
                True, block.at[0:cut, low:columns], half_in.at[zs[i], 0:cut],
                self.index(a, "upper", 2 * p + i), self.to_y,
            )
            sender.send(
                True, block.at[cut:rows, low:columns], half_in.at[zs[i], cut:rows],
                self.index(a, "lower", 2 * p + i), self.to_x,
            )

    def turn(self, a, i, upper):
        array, sender = self.arrays[a], self.sender
        held, half_in, whole_in, low = array["held"], array["half"], array["whole"], array["low"]
        rows, columns = held.shape[2:]
        zi, cut = self.order[i], rows // 2
        first, last = (0, cut) if upper else (cut, rows)
        block = held.at[zi, self.gx if upper else self.gy, :, low:columns]

        def work():
            arrived = half_in.at[zi, first:last]
            sender.land(arrived, self.index(a, "upper" if upper else "lower", i), self.to_x)
            add_into(block.at[first:last], [block.at[first:last], arrived])

        sender.do(True, work)
        sender.send(
            True, block, whole_in.at[zi, 0 if upper else 1],
            self.index(a, "row" if upper else "column", i), self.to_x if upper else self.to_y,
        )

    def pass_on(self, i, source, lines, recv_kind, send_kind, a):
        z, zi = self.z, self.order[i]
        up = self.rising[i]
        slot = jnp.where(jnp.logical_and(jnp.logical_not(up), zi == z - 1), LINE, zi)
        copy = remote(
            source,
            lines.at[slot],
            self.sender.send_sems.at[self.index(a, send_kind, i)],
            self.sender.recv_sems.at[self.index(a, recv_kind) + slot],
            (self.g, jnp.where(up, z + 1, z - 1) * 2 + self.c),
        )
        if self.sender.draining:
            copy.wait_send()
        else:
            copy.start()

    def inner(self, i):
        return jnp.logical_or(
            jnp.logical_and(self.rising[i], self.z > 0),
            jnp.logical_and(jnp.logical_not(self.rising[i]), self.z < LINE - 1),
        )

    def along(self, a, i):
        array, sender = self.arrays[a], self.sender
        whole_in, lines, low = array["whole"], array["line"], array["low"]
        columns, zi, z = array["held"].shape[3], self.order[i], self.z
        mine = array["held"].at[zi, self.g, :, low:columns]
        terms = [mine, whole_in.at[zi, 0], whole_in.at[zi, 1]]
        arrived = self.index(a, "line")

        def work():
            sender.land(whole_in.at[zi, 0], self.index(a, "row", i), self.to_x)
            sender.land(whole_in.at[zi, 1], self.index(a, "column", i), self.to_x)
            if i < 3:
                inner = self.inner(i)

                def join():
                    sender.land(lines.at[zi], arrived + zi, self.to_x)
                    add_into(mine, terms + [lines.at[zi]])

                pl.when(inner)(join)
                pl.when(jnp.logical_not(inner))(lambda: add_into(mine, terms))
            else:
                self.close(lines, arrived, terms, array["out"].at[:, low:columns])

        sender.do(True, work)
        if i < 3:
            self.pass_on(i, mine, lines, "line", "hop", a)

    def close(self, lines, arrived, terms, target):
        z, sender = self.z, self.sender
        rise, fall = lines.at[z], lines.at[LINE]
        pl.when(z > 0)(lambda: sender.land(rise, arrived + z, self.to_x))
        pl.when(z < LINE - 1)(lambda: sender.land(fall, arrived + LINE, self.to_x))
        pl.when(z == 0)(lambda: add_into(target, terms + [fall]))
        pl.when(z == LINE - 1)(lambda: add_into(target, terms + [rise]))
        pl.when(jnp.logical_and(z > 0, z < LINE - 1))(
            lambda: add_into(target, terms + [rise, fall])
        )

    def along_first(self, a, i):
        array, sender = self.arrays[a], self.sender
        low, rings, zi, z = array["low"], array["rings"], self.order[i], self.z
        mine = array["held"].at[zi, :, :, 0:low]
        arrived = self.index(a, "ring line")

        def add(slots):
            for j in range(PLANE):
                block = array["held"].at[zi, j, :, 0:low]
                add_into(block, [block] + [rings.at[slot, j] for slot in slots])

        def work():
            if i < 3:

                def join():
                    sender.land(rings.at[zi], arrived + zi, self.to_x)
                    add([zi])

                pl.when(self.inner(i))(join)
                return
            pl.when(z > 0)(lambda: sender.land(rings.at[z], arrived + z, self.to_x))
            pl.when(z < LINE - 1)(lambda: sender.land(rings.at[LINE], arrived + LINE, self.to_x))
            pl.when(z == 0)(lambda: add([LINE]))
            pl.when(z == LINE - 1)(lambda: add([z]))
            pl.when(jnp.logical_and(z > 0, z < LINE - 1))(lambda: add([z, LINE]))

        sender.do(True, work)
        if i < 3:
            self.pass_on(i, mine, rings, "ring line", "ring hop", a)
            return
        block, half_in = array["held"].at[z, self.gd, :, 0:low], array["own half"]
        rows = half_in.shape[0]
        cut = rows // 2
        sender.send(
            True, block.at[0:cut], half_in.at[0:cut], self.index(a, "own upper"), self.to_y
        )
        sender.send(
            True, block.at[cut:rows], half_in.at[cut:rows], self.index(a, "own lower"), self.to_x
        )

    def turn_own(self, a, upper):
        array, sender = self.arrays[a], self.sender
        low, half_in = array["low"], array["own half"]
        rows = half_in.shape[0]
        first, last = (0, rows // 2) if upper else (rows // 2, rows)
        block = array["held"].at[self.z, self.gx if upper else self.gy, :, 0:low]

        def work():
            arrived = half_in.at[first:last]
            sender.land(arrived, self.index(a, "own upper" if upper else "own lower"), self.to_x)
            add_into(block.at[first:last], [block.at[first:last], arrived])

        sender.do(True, work)
        sender.send(
            True, block, array["own whole"].at[0 if upper else 1],
            self.index(a, "own row" if upper else "own column"),
            self.to_x if upper else self.to_y,
        )

    def close_own(self, a):
        array, sender = self.arrays[a], self.sender
        low, whole_in = array["low"], array["own whole"]

        def work():
            sender.land(whole_in.at[0], self.index(a, "own row"), self.to_x)
            sender.land(whole_in.at[1], self.index(a, "own column"), self.to_x)
            mine = array["held"].at[self.z, self.g, :, 0:low]
            add_into(array["out"].at[:, 0:low], [mine, whole_in.at[0], whole_in.at[1]])

        sender.do(True, work)

    def step(self, code):
        kind, a, i = code // 100, code // 10 % 10, code % 10
        if kind == 0:
            self.start(a, i)
        elif kind == 1:
            self.meet(a, i)
        elif kind in (2, 3):
            self.turn(a, i, kind == 2)
        elif kind == 4:
            self.along(a, i)
        elif kind == 5:
            self.along_first(a, i)
        elif kind in (6, 7):
            self.turn_own(a, kind == 6)
        else:
            self.close_own(a)


def gather_up(vectors, target):
    shards = PLANE * LINE * 2
    total = None
    for row in sorted({v[0] for v in vectors}):
        share = jnp.zeros((shards, 128), F32)
        for at, lane, size, source in vectors:
            if at != row:
                continue
            step = 1024

            def body(i, carry):
                cut = pl.ds(pl.multiple_of(i * step, step), step)
                column = (lax.broadcasted_iota(jnp.int32, (1, step), 1) + i * step).astype(F32)
                shard = jnp.floor((column + 0.5) * (1.0 / size))
                lane_of = (column - shard * size + lane).astype(jnp.int32)
                spread = lax.broadcasted_iota(jnp.int32, (128, step), 0) == lane_of
                keep = lax.broadcasted_iota(jnp.int32, (shards, step), 0) == shard.astype(jnp.int32)
                value = jnp.where(keep, source[:, cut], 0.0).astype(BF16)
                return carry + dot_columns(value, spread.astype(F32).astype(BF16))

            share = lax.fori_loop(0, shards * size // step, body, share)
        pick_rows = lax.broadcasted_iota(jnp.int32, (shards, shards * 32), 0) * 32 + row
        pick = lax.broadcasted_iota(jnp.int32, (shards, shards * 32), 1) == pick_rows
        part = contract_rows(pick.astype(F32).astype(BF16), share.astype(BF16))
        total = part if total is None else total + part
    target[...] = total.astype(BF16).reshape(target.shape)


def backward_kernel(*refs):
    (
        act_hbm, down_grad_hbm, hidden_hbm, up_grad_hbm, context_hbm, branch_grad_hbm, result_hbm,
        embed_cot_hbm, token_hbm, qkv_hbm, far_hbm, context_grad_hbm, first_grad_hbm, weight_hbm,
        norm, segs, sums, cosine, sine, shift,
    ), refs = refs[:20], refs[20:]
    outs, token_in, refs = refs[:5], refs[5], refs[6:]
    (send_d, send_u, send_s), refs = refs[:3], refs[3:]
    helds, halves, wholes, lines = [refs[i * 5 : (i + 1) * 5] for i in range(4)]
    (
        rings, own_half, own_whole,
        act, down_grad, up_grad, branch_grad, embed_cot, raw, turned_a, turned_b, qkv, far,
        far_back, context_grad, seg_near, seg_far, vectors, shares, token_out,
        send_sems, recv_sems, local_sems,
    ) = refs[20:]
    g, x, y, z, c = place()
    partner = (g, z * 2 + 1 - c)
    rows, width = branch_grad.shape
    ff = act.shape[1]
    sender = Sender(send_sems, recv_sems)
    spare = 5 * REDUCE_SEMS

    def load(source, target, index):
        copy = lambda: pltpu.make_async_copy(source, target, local_sems.at[index])
        copy().start()
        return lambda: copy().wait()

    waits = {
        "act": load(act_hbm, act, 0),
        "down": load(down_grad_hbm, down_grad, 1),
        "raw": load(hidden_hbm, raw, 2),
        "up": load(up_grad_hbm, up_grad, 3),
        "branch": load(branch_grad_hbm, branch_grad, 4),
        "embed": load(embed_cot_hbm, embed_cot, 5),
        "qkv": load(qkv_hbm, qkv, 6),
        "far": load(far_hbm, far, 7),
        "grad": load(context_grad_hbm, context_grad, 8),
    }
    entry_barrier()

    def turn_over(target):
        for j in range(width // 128):
            block = jnp.transpose(flat(raw[:, :, j * 128 : (j + 1) * 128]))
            target[j // 2, (j % 2) * 2 : (j % 2) * 2 + 2] = block.reshape(2, 2, 32, rows)

    def product_of(turned, right):
        columns = right.shape[1]
        step = min(columns, 512)

        def act_on(parity, zs, targets, added):
            left = jnp.concatenate([flat(turned[:, zi, parity]) for zi in zs], axis=0)

            def body(i, carry):
                cut = pl.ds(pl.multiple_of(i * step, step), step)
                value = dot_rows(left, right[:, cut]).reshape(2, PLANE, 32, step)
                for j, target in enumerate(targets):
                    part = value[j]
                    if added:
                        part = part + target[:, :, cut].astype(F32)
                    target[:, :, cut] = part.astype(BF16)
                return carry

            lax.fori_loop(0, columns // step, body, 0)

        return act_on

    def down_product(parity, zs, targets, added):
        def body(j, carry):
            pieces = []
            for zi in zs:
                at = ((j * LINE + zi) * 2 + parity) * 128
                pieces.append(act[:, pl.ds(pl.multiple_of(at, 128), 128)])
            value = contract_rows(jnp.concatenate(pieces, axis=1), down_grad[...])
            for i, target in enumerate(targets):
                part = value[i * 128 : (i + 1) * 128]
                if added:
                    part = part + target[j].astype(F32)
                target[j] = part.astype(BF16)
            return carry

        lax.fori_loop(0, PLANE, body, 0)

    def share_product(parity, zs, targets, added):
        for zi, target in zip(zs, targets):
            value = shares[:, zi, parity]
            if added:
                value = (value.astype(F32) + target[...].astype(F32)).astype(BF16)
            target[...] = value

    shared = lambda columns: send_u.at[:, :, :, 0:columns]
    sends = (send_d, send_u, shared(width), shared(3 * width), send_s)
    products = [
        down_product,
        product_of(turned_a, up_grad),
        product_of(turned_b, branch_grad),
        product_of(turned_a, qkv),
        share_product,
    ]
    arrays = [
        {"product": p, "send": s, "held": h, "half": i, "whole": w, "line": l, "out": o, "low": 0}
        for p, s, h, i, w, l, o in zip(products, sends, helds, halves, wholes, lines, outs)
    ]
    arrays[3].update(
        {"low": rings.shape[3], "rings": rings, "own half": own_half, "own whole": own_whole}
    )
    plan = Reduce(arrays, sender)
    token_back = Exchange([raw], [token_in], False, sender, spare + 2, local_sems, 18)
    parts, tile = 3 * width // 512, 512

    def fetch(t, begin):
        for r in range(2):
            at = ((t % 4) * 2 + r) * tile
            copy = pltpu.make_async_copy(
                weight_hbm.at[r * rows : (r + 1) * rows, t * tile : (t + 1) * tile],
                act.at[:, at : at + tile],
                local_sems.at[10 + (t % 4) * 2 + r],
            )
            copy.start() if begin else copy.wait()

    def fetched(t):
        fetch(t, False)
        for r in range(2):
            at = ((t % 4) * 2 + r) * tile
            half = token_out[:, r * tile : (r + 1) * tile]
            token_out[:, r * tile : (r + 1) * tile] = half + dot_columns(
                qkv[:, t * tile : (t + 1) * tile], act[:, at : at + tile]
            )
        if t + 4 < parts:
            fetch(t + 4, True)

    def turn_hidden():
        waits["raw"]()
        turn_over(turned_a)
        load(context_hbm, raw, 2)

    def turn_context():
        waits["raw"]()
        turn_over(turned_b)
        load(result_hbm, raw, 2)

    def embed_share():
        waits["raw"]()
        waits["embed"]()
        value = contract_rows(flat(raw[...]), embed_cot[...]).astype(BF16)
        shares[:, :, :, 0:32, :] = value.reshape(PLANE, LINE, 2, 32, 128)
        load(token_hbm, raw, 2)

    def before_attention():
        for name in ("qkv", "far", "grad"):
            waits[name]()
        seg_near[...] = jnp.transpose(jnp.broadcast_to(segs[0:1, :], (128, rows)))
        seg_far[...] = jnp.transpose(jnp.broadcast_to(segs[1:2, :], (128, rows)))

    def turn_tokens():
        waits["raw"]()
        turn_over(turned_a)
        for t in range(4):
            fetch(t, True)

    def finish_tile(i):
        cut = pl.ds(pl.multiple_of(i * tile, tile), tile)

        @pl.when(i >= 2)
        def _():
            other = pl.ds(pl.multiple_of(jnp.maximum(i - 2, 0) * tile, tile), tile)
            qkv[:, cut] = (qkv[:, cut].astype(F32) + far_back[:, other].astype(F32)).astype(BF16)

        vectors[0:1, cut] = jnp.sum(qkv[:, cut].astype(F32), axis=0, keepdims=True)

    def other_shares():
        source = lambda i, size: (vectors if i == 0 else sums).at[i : i + 1, 0:size]
        gather_up(
            (
                (0, 0, 96, source(0, 3 * width)),
                (1, 0, 128, source(1, ff)),
                (2, 0, 32, source(2, width)),
                (2, 32, 32, source(3, width)),
                (2, 64, 32, source(4, width)),
                (2, 96, 32, source(5, width)),
                (3, 0, 32, source(6, width)),
                (3, 32, 32, source(7, width)),
            ),
            shares.at[:, :, :, 32:64, :],
        )

    def round_tokens():
        for i in range(2):
            raw[i] = token_out[i * (rows // 2) : (i + 1) * (rows // 2), :].astype(BF16)

    def attend_one(i):
        at = pl.multiple_of(i * 128, 128)
        cut = lambda ref, base: ref.at[:, pl.ds(base + at, 128)]
        attend_back_pair(
            cut(qkv, 0), cut(qkv, width), cut(qkv, 2 * width), cut(far, 0), cut(far, width),
            cut(context_grad, 0), norm.at[i], segs.at[0:1], seg_near, seg_far,
            (cosine, sine, shift), [token_out.at[:, j * 128 : (j + 1) * 128] for j in range(4)],
        )

    first_copy = pltpu.make_async_copy(first_grad_hbm, token_out, local_sems.at[9])
    others = {
        900: lambda: (waits["act"](), waits["down"]()),
        901: lambda: (turn_hidden(), waits["up"]()),
        902: lambda: (turn_context(), waits["branch"]()),
        903: embed_share,
        904: turn_tokens,
        905: lambda: lax.fori_loop(0, parts, lambda i, carry: (finish_tile(i), carry)[1], 0),
        906: other_shares,
        907: round_tokens,
        908: lambda: None,
        909: lambda: sender.land(far_back, spare, partner),
        910: token_back.arrive,
        930: first_copy.wait,
    }
    for t in range(parts):
        others[920 + t] = lambda t=t: fetched(t)

    def perform(steps):
        def act_on():
            for step in steps:
                if step == 911:
                    sender.do(True, first_copy.start)
                    sender.send(True, far, far_back, spare, partner)
                elif step == 912:
                    for link in (5, 2, 3):
                        token_back.step(link)
                elif step >= 900:
                    if not sender.draining:
                        others[step]()
                else:
                    plan.step(step)

        return act_on

    first, middle, last = BACKWARD_STEPS
    ticks = [perform(steps) for steps in (first,) + middle + (last,)]
    ticks[0]()
    before_attention()
    run_with(ticks[1:-1], width // 128, attend_one)
    ticks[-1]()
    sender.drain(ticks)


def backward(operands, small_operands, shapes, rows, width, ff, lanes):
    shape = jax.ShapeDtypeStruct
    semaphores = 5 * REDUCE_SEMS + 16
    ring = (shapes[3][0], shapes[3][1] // 2)
    buffers = [pltpu.VMEM((2, PLANE) + shapes[i], BF16) for i in (0, 1, 4)]
    apart = shapes[:3] + [ring] + shapes[4:]
    buffers += [pltpu.VMEM((LINE, PLANE) + s, BF16) for s in shapes]
    for lead in ((LINE,), (LINE, 2), (LINE + 1,)):
        buffers += [pltpu.VMEM(lead + s, BF16) for s in apart]
    turned = pltpu.VMEM((PLANE, LINE, 2, 32, rows), BF16)
    piece = rows // 2
    scratch = buffers + [
        pltpu.VMEM((LINE + 1, PLANE) + ring, BF16),
        pltpu.VMEM(ring, BF16),
        pltpu.VMEM((2,) + ring, BF16),
        pltpu.VMEM((rows, ff), BF16),
        pltpu.VMEM((rows, width), BF16),
        pltpu.VMEM((rows, ff), BF16),
        pltpu.VMEM((rows, width), BF16),
        pltpu.VMEM((rows, lanes), BF16),
        pltpu.VMEM((2, piece, width), BF16),
        turned,
        turned,
        pltpu.VMEM((rows, 3 * width), BF16),
        pltpu.VMEM((rows, 2 * width), BF16),
        pltpu.VMEM((rows, 2 * width), BF16),
        pltpu.VMEM((rows, width), BF16),
        pltpu.VMEM((rows, 128), F32),
        pltpu.VMEM((rows, 128), F32),
        pltpu.VMEM((1, 3 * width), F32),
        pltpu.VMEM((PLANE, LINE, 2, 64, 128), BF16),
        pltpu.VMEM((rows, width), F32),
        pltpu.SemaphoreType.DMA((semaphores,)),
        pltpu.SemaphoreType.DMA((semaphores,)),
        pltpu.SemaphoreType.DMA((20,)),
    ]
    results = pl.pallas_call(
        backward_kernel,
        out_shape=[shape(s, F32) for s in shapes] + [shape((2, piece, width), BF16)],
        in_specs=[hbm()] * len(operands) + [vmem()] * len(small_operands),
        out_specs=[vmem()] * 6,
        scratch_shapes=scratch,
        compiler_params=pltpu.CompilerParams(
            collective_id=2, has_side_effects=True, vmem_limit_bytes=67043328
        ),
        name="backward",
    )(*operands, *small_operands)
    return (results[:5], results[5])


def pair_tables(positions):
    lanes = lax.broadcasted_iota(jnp.int32, (positions.shape[0], 2 * HEAD_DIM), 1)
    place_in_half = lax.rem(lanes, HEAD_DIM // 2).astype(F32)
    angles = positions[:, None] * 10000.0 ** (-place_in_half * (2.0 / HEAD_DIM))
    return (jnp.cos(angles), jnp.sin(angles))


def deliver_kernel(count, vectors, *refs):
    sources, small, token, refs = refs[:count], refs[count], refs[count + 1], refs[count + 2 :]
    targets, small_out, token_out, refs = (
        refs[:count], refs[count : count + 1 + len(vectors)], refs[count + 1 + len(vectors)],
        refs[count + 2 + len(vectors) :],
    )
    held, sems = refs[:count], refs[count]
    inward = [
        pltpu.make_async_copy(s, h, sems.at[i]) for i, (s, h) in enumerate(zip(sources, held))
    ]
    outward = [
        pltpu.make_async_copy(h, t, sems.at[count + i])
        for i, (h, t) in enumerate(zip(held, targets))
    ]
    for copy in inward:
        copy.start()
    small_out[0][...] = small[: small_out[0].shape[0], :]
    top = small_out[0].shape[0]
    for target, (row, lane, size) in zip(small_out[1:], vectors):
        target[...] = small[top + row : top + row + 1, lane : lane + size]
    token_out[...] = token[...].astype(F32)
    for arrived, leave in zip(inward, outward):
        arrived.wait()
        leave.start()
    for copy in outward:
        copy.wait()


def deliver(arrays, small, token, embed_rows, vectors):
    shape = jax.ShapeDtypeStruct
    count = len(arrays)
    outs = [shape(a.shape, a.dtype) for a in arrays]
    outs += [shape((embed_rows, small.shape[1]), F32)]
    outs += [shape((1, size), F32) for row, lane, size in vectors]
    outs += [shape(token.shape, F32)]
    results = pl.pallas_call(
        functools.partial(deliver_kernel, count, vectors),
        out_shape=outs,
        in_specs=[hbm()] * count + [vmem()] * 2,
        out_specs=[hbm()] * count + [vmem()] * (2 + len(vectors)),
        scratch_shapes=[pltpu.VMEM(a.shape, a.dtype) for a in arrays]
        + [pltpu.SemaphoreType.DMA((2 * count,))],
        compiler_params=pltpu.CompilerParams(vmem_limit_bytes=67043328),
        name="deliver",
    )(*arrays, small, token)
    middle = [r.reshape(-1) for r in results[count + 1 : -1]]
    return (results[:count], results[count], middle, results[-1])


def plane_device(
    tokens,
    segment_ids,
    project_weight,
    project_bias,
    output_weight,
    output_bias,
    first_gain,
    first_shift,
    up_weight,
    up_bias,
    down_weight,
    down_bias,
    second_gain,
    second_shift,
    embed_weight,
    out_cotangent,
    embed_cotangent,
):
    width = HEADS * HEAD_DIM
    piece = tokens.shape[2]
    rows = 2 * piece
    group = lax.axis_index("group")
    core = lax.rem(lax.axis_index("wide"), 2)
    lanes = embed_weight.shape[1]
    embed_rows = embed_weight.shape[0]
    small = None
    for row, lane, vector in (
        (0, 0, project_bias),
        (1, 0, up_bias),
        (2, 0, output_bias),
        (2, 32, first_gain),
        (2, 64, first_shift),
        (2, 96, down_bias),
        (3, 0, second_gain),
        (3, 32, second_shift),
    ):
        size = vector.shape[0]
        part = jnp.pad(
            vector.astype(F32)[None, :], ((row, 31 - row), (lane, lanes - lane - size))
        )
        small = part if small is None else small + part
    place_of = jnp.arange(rows)
    cosine, sine = pair_tables((core * rows + place_of).astype(F32))
    step_cosine, step_sine = pair_tables(jnp.full((1,), rows, F32))
    step_sine = step_sine * (1 - 2 * core).astype(F32)
    shift = jnp.concatenate([step_cosine, step_sine] + [jnp.zeros_like(step_sine)] * 6)
    (
        project_full, token_rows, qkv, far_kv, context_low, norms, hidden_low, act_low, up_grad,
        down_grad, result_low, embed_cot, branch_grad, context_grad, first_grad, sums, ids,
        layer_out, embed_out,
    ) = forward(
        [project_weight, embed_weight, small.astype(BF16), output_weight, up_weight, down_weight],
        [tokens[:, 0], out_cotangent[:, 0], embed_cotangent[:, 0]],
        segment_ids,
        (cosine, sine),
        up_weight.shape[1],
    )
    shapes = [
        down_weight.shape,
        up_weight.shape,
        output_weight.shape,
        project_weight.shape,
        (embed_rows + small.shape[0], lanes),
    ]
    outs, token_low = backward(
        (
            act_low, down_grad, hidden_low.reshape(2, piece, width), up_grad,
            context_low.reshape(2, piece, width), branch_grad, result_low,
            embed_cot.reshape(rows, lanes), token_rows, qkv, far_kv, context_grad, first_grad,
            project_full.reshape(width, 3 * width),
        ),
        (norms, ids, sums, cosine, sine, shift),
        shapes,
        rows,
        width,
        up_weight.shape[1],
        lanes,
    )
    vectors = (
        (0, 0, 96), (2, 0, 32), (2, 32, 32), (2, 64, 32), (1, 0, 128), (2, 96, 32), (3, 0, 32), (3, 32, 32),
    )
    arrays, embed_grad, parts, token_grad = deliver(
        (layer_out, embed_out) + tuple(outs[:4]), outs[4], token_low, embed_rows, vectors
    )
    return (
        arrays[0][:, None],
        arrays[1][:, None],
        token_grad[:, None],
        arrays[5],
        parts[0],
        arrays[4],
        parts[1],
        parts[2],
        parts[3],
        arrays[3],
        parts[4],
        arrays[2],
        parts[5],
        parts[6],
        parts[7],
        embed_grad,
    )


def choose_device(mesh):
    if mesh.shape["group"] == PLANE and mesh.shape["wide"] == 2 * LINE:
        return plane_device
    return general_device


def solution(mesh):
    in_specs = (
        P(None, "wide", "group", None),
        P(None, "wide", None),
        P(("group", "wide"), None),
        P(("group", "wide")),
        P(("group", "wide"), None),
        P(("group", "wide")),
        P(("group", "wide")),
        P(("group", "wide")),
        P(("group", "wide"), None),
        P(("group", "wide")),
        P(("group", "wide"), None),
        P(("group", "wide")),
        P(("group", "wide")),
        P(("group", "wide")),
        P(("group", "wide"), None),
        P(None, "wide", "group", None),
        P(None, "wide", "group", None),
    )
    out_specs = (
        P(None, "wide", "group", None),
        P(None, "wide", "group", None),
        P(None, "wide", "group", None),
        P(("group", "wide"), None),
        P(("group", "wide")),
        P(("group", "wide"), None),
        P(("group", "wide")),
        P(("group", "wide")),
        P(("group", "wide")),
        P(("group", "wide"), None),
        P(("group", "wide")),
        P(("group", "wide"), None),
        P(("group", "wide")),
        P(("group", "wide")),
        P(("group", "wide")),
        P(("group", "wide"), None),
    )
    return jax.shard_map(
        choose_device(mesh), mesh=mesh, in_specs=in_specs, out_specs=out_specs, check_vma=False
    )
```

```python
import functools
from types import SimpleNamespace

import jax
import jax.numpy as jnp
from jax import lax
from jax.experimental import pallas as pl
from jax.experimental.pallas import tpu as pltpu
from jax.sharding import PartitionSpec as P

HEADS = 16
HEAD_DIM = 64


eps_norm = 1e-05
neg_large = -1e30


def rotary_tables(positions):
    half_dim = HEAD_DIM // 2
    frequency = 10000.0 ** (-jnp.arange(half_dim, dtype=jnp.float32) * (2.0 / HEAD_DIM))
    angles = positions[:, None] * frequency[None, :]
    angles = jnp.concatenate([angles, angles], axis=1)
    return (jnp.cos(angles), jnp.sin(angles))


def rotate(values, cosine_table, sine_table):
    half_dim = HEAD_DIM // 2
    swapped = jnp.concatenate([-values[..., half_dim:], values[..., :half_dim]], axis=-1)
    return values * cosine_table[:, None, :] + swapped * sine_table[:, None, :]


def unrotate(grads, cosine_table, sine_table):
    half_dim = HEAD_DIM // 2
    scaled = grads * sine_table[:, None, :]
    swapped = jnp.concatenate([scaled[..., half_dim:], -scaled[..., :half_dim]], axis=-1)
    return grads * cosine_table[:, None, :] + swapped


def norm_forward(resid, gain, shift):
    center = resid - jnp.mean(resid, axis=-1, keepdims=True)
    spread = jnp.mean(center * center, axis=-1, keepdims=True)
    rstd_rows = lax.rsqrt(spread + eps_norm)
    normed = center * rstd_rows
    return (normed * gain + shift, normed, rstd_rows)


def norm_backward(grads, normed, rstd_rows, gain):
    scaled = grads * gain
    resid_grad = rstd_rows * (
        scaled
        - jnp.mean(scaled, axis=-1, keepdims=True)
        - normed * jnp.mean(scaled * normed, axis=-1, keepdims=True)
    )
    return (resid_grad, jnp.sum(grads * normed, axis=0), jnp.sum(grads, axis=0))


def contract_rows(left, right):
    return lax.dot_general(
        left, right, (((0,), (0,)), ((), ())), preferred_element_type=jnp.float32
    )


def times_transpose(left, right):
    return lax.dot_general(
        left, right, (((1,), (1,)), ((), ())), preferred_element_type=jnp.float32
    )


def gelu_slope(value):
    normal_cdf = 0.5 * (1.0 + lax.erf(value * 0.7071067811865476))
    density = jnp.exp(-0.5 * value * value) * 0.3989422804014327
    return normal_cdf + value * density


def key_blocks(kv_rows, seg_all):
    seq_len = kv_rows.shape[0]
    block_rows = min(512, seq_len)
    count = seq_len // block_rows
    return (
        kv_rows.reshape(count, block_rows, 2, HEADS, HEAD_DIM),
        seg_all.reshape(count, block_rows),
    )


def block_scores(queries, key_block, same):
    scores = jnp.einsum("qhd,khd->hqk", queries, key_block, preferred_element_type=jnp.float32)
    scores = scores * HEAD_DIM ** (-0.5)
    return jnp.where(same[None], scores, neg_large)


def attention_forward(queries, blocks, seg_blocks, seg_local):
    length = queries.shape[0]

    def norm_step(carry, pieces):
        kv_block, seg_block = pieces
        same = seg_local[:, None] == seg_block[None, :]

        def norm_update(running):
            run_max, run_sum = running
            scores = block_scores(queries, kv_block[:, 0], same)
            new_max = jnp.maximum(run_max, jnp.max(scores, axis=-1))
            new_sum = run_sum * jnp.exp(run_max - new_max) + jnp.sum(
                jnp.exp(scores - new_max[..., None]), axis=-1
            )
            return (new_max, new_sum)

        def norm_unchanged(running):
            return running

        return (lax.cond(jnp.any(same), norm_update, norm_unchanged, carry), None)

    start = (
        jnp.full((HEADS, length), neg_large, jnp.float32),
        jnp.zeros((HEADS, length), jnp.float32),
    )
    (run_max, run_sum), unused = lax.scan(norm_step, start, (blocks, seg_blocks))
    log_norm = run_max + jnp.log(run_sum)

    def value_step(total, pieces):
        kv_block, seg_block = pieces
        same = seg_local[:, None] == seg_block[None, :]

        def value_update(running):
            scores = block_scores(queries, kv_block[:, 0], same)
            weights = jnp.exp(scores - log_norm[..., None]).astype(jnp.bfloat16)
            return running + jnp.einsum(
                "hqk,khd->qhd", weights, kv_block[:, 1], preferred_element_type=jnp.float32
            )

        def value_unchanged(running):
            return running

        return (lax.cond(jnp.any(same), value_update, value_unchanged, total), None)

    context, unused = lax.scan(
        value_step, jnp.zeros(queries.shape, jnp.float32), (blocks, seg_blocks)
    )
    return (context, log_norm)


def attention_backward(queries, blocks, seg_blocks, seg_local, log_norm, context_grad, delta):

    def grad_step(query_grad, pieces):
        kv_block, seg_block = pieces
        same = seg_local[:, None] == seg_block[None, :]

        def work(running):
            scores = block_scores(queries, kv_block[:, 0], same)
            probs = jnp.exp(scores - log_norm[..., None])
            prob_grad = jnp.einsum(
                "qhd,khd->hqk", context_grad, kv_block[:, 1], preferred_element_type=jnp.float32
            )
            score_grad = (probs * (prob_grad - delta[..., None])).astype(jnp.bfloat16)
            running = running + jnp.einsum(
                "hqk,khd->qhd", score_grad, kv_block[:, 0], preferred_element_type=jnp.float32
            ) * HEAD_DIM ** (-0.5)
            prob_low = probs.astype(jnp.bfloat16)
            key_grad = jnp.einsum(
                "hqk,qhd->khd", score_grad, queries, preferred_element_type=jnp.float32
            ) * HEAD_DIM ** (-0.5)
            value_grad = jnp.einsum(
                "hqk,qhd->khd", prob_low, context_grad, preferred_element_type=jnp.float32
            )
            return (running, jnp.stack([key_grad, value_grad], axis=1))

        def skipped(running):
            return (running, jnp.zeros(kv_block.shape, jnp.float32))

        return lax.cond(jnp.any(same), work, skipped, query_grad)

    query_grad, kv_grad = lax.scan(
        grad_step, jnp.zeros(queries.shape, jnp.float32), (blocks, seg_blocks)
    )
    return (query_grad, kv_grad.reshape(-1, 2 * HEADS * HEAD_DIM))


def general_device(
    tokens,
    segment_ids,
    project_weight,
    project_bias,
    output_weight,
    output_bias,
    first_gain,
    first_shift,
    up_weight,
    up_bias,
    down_weight,
    down_bias,
    second_gain,
    second_shift,
    embed_weight,
    out_cotangent,
    embed_cotangent,
):
    shards = (
        project_weight,
        project_bias,
        output_weight,
        output_bias,
        first_gain,
        first_shift,
        up_weight,
        up_bias,
        down_weight,
        down_bias,
        second_gain,
        second_shift,
        embed_weight,
    )
    length = tokens.shape[2]
    width = HEADS * HEAD_DIM
    head_shape = (length, HEADS, HEAD_DIM)
    place = lax.axis_index("group")
    positions = (place * length + jnp.arange(length)).astype(jnp.float32)
    cosine_table, sine_table = rotary_tables(positions)
    grad_total = None
    results = []
    embeddings = []
    input_grads = []
    for micro_index in range(tokens.shape[0]):
        params = (
            lax.all_gather(shards[0], ("group", "wide"), axis=0, tiled=True),
            lax.all_gather(shards[1], ("group", "wide"), axis=0, tiled=True),
            lax.all_gather(shards[2], ("group", "wide"), axis=0, tiled=True),
            lax.all_gather(shards[3], ("group", "wide"), axis=0, tiled=True),
            lax.all_gather(shards[4], ("group", "wide"), axis=0, tiled=True),
            lax.all_gather(shards[5], ("group", "wide"), axis=0, tiled=True),
            lax.all_gather(shards[6], ("group", "wide"), axis=0, tiled=True),
            lax.all_gather(shards[7], ("group", "wide"), axis=0, tiled=True),
            lax.all_gather(shards[8], ("group", "wide"), axis=0, tiled=True),
            lax.all_gather(shards[9], ("group", "wide"), axis=0, tiled=True),
            lax.all_gather(shards[10], ("group", "wide"), axis=0, tiled=True),
            lax.all_gather(shards[11], ("group", "wide"), axis=0, tiled=True),
            lax.all_gather(shards[12], ("group", "wide"), axis=0, tiled=True),
        )
        seg_all = segment_ids[micro_index, 0]
        seg_local = lax.dynamic_slice_in_dim(seg_all, place * length, length)
        token_low = tokens[micro_index, 0]
        token_wide = token_low.astype(jnp.float32)
        projected = jnp.dot(token_low, params[0], preferred_element_type=jnp.float32) + params[
            1
        ].astype(jnp.float32)
        queries = rotate(projected[:, :width].reshape(head_shape), cosine_table, sine_table).astype(
            jnp.bfloat16
        )
        key_rows = rotate(
            projected[:, width : 2 * width].reshape(head_shape), cosine_table, sine_table
        ).astype(jnp.bfloat16)
        value_rows = projected[:, 2 * width :].astype(jnp.bfloat16)
        local_kv = jnp.concatenate([key_rows.reshape(length, width), value_rows], axis=1)
        kv_all = lax.all_gather(local_kv, "group", axis=0, tiled=True)
        blocks, seg_blocks = key_blocks(kv_all, seg_all)
        context, log_norm = attention_forward(queries, blocks, seg_blocks, seg_local)
        context_low = context.reshape(length, width).astype(jnp.bfloat16)
        branch = jnp.dot(context_low, params[2], preferred_element_type=jnp.float32) + params[
            3
        ].astype(jnp.float32)
        first_gain_wide = params[4].astype(jnp.float32)
        hidden, first_normed, first_rstd = norm_forward(
            token_wide + branch, first_gain_wide, params[5].astype(jnp.float32)
        )
        hidden_low = hidden.astype(jnp.bfloat16)
        up_value = jnp.dot(hidden_low, params[6], preferred_element_type=jnp.float32) + params[
            7
        ].astype(jnp.float32)
        act_low = jax.nn.gelu(up_value, approximate=False).astype(jnp.bfloat16)
        down_value = jnp.dot(act_low, params[8], preferred_element_type=jnp.float32) + params[
            9
        ].astype(jnp.float32)
        second_gain_wide = params[10].astype(jnp.float32)
        result, second_normed, second_rstd = norm_forward(
            hidden + down_value, second_gain_wide, params[11].astype(jnp.float32)
        )
        result_low = result.astype(jnp.bfloat16)
        embedded = jnp.dot(result_low, params[12], preferred_element_type=jnp.float32)
        results.append(result_low)
        embeddings.append(embedded.astype(jnp.bfloat16))
        params = (
            lax.all_gather(shards[0], ("group", "wide"), axis=0, tiled=True),
            lax.all_gather(shards[1], ("group", "wide"), axis=0, tiled=True),
            lax.all_gather(shards[2], ("group", "wide"), axis=0, tiled=True),
            lax.all_gather(shards[3], ("group", "wide"), axis=0, tiled=True),
            lax.all_gather(shards[4], ("group", "wide"), axis=0, tiled=True),
            lax.all_gather(shards[5], ("group", "wide"), axis=0, tiled=True),
            lax.all_gather(shards[6], ("group", "wide"), axis=0, tiled=True),
            lax.all_gather(shards[7], ("group", "wide"), axis=0, tiled=True),
            lax.all_gather(shards[8], ("group", "wide"), axis=0, tiled=True),
            lax.all_gather(shards[9], ("group", "wide"), axis=0, tiled=True),
            lax.all_gather(shards[10], ("group", "wide"), axis=0, tiled=True),
            lax.all_gather(shards[11], ("group", "wide"), axis=0, tiled=True),
            lax.all_gather(shards[12], ("group", "wide"), axis=0, tiled=True),
        )
        embed_cot = embed_cotangent[micro_index, 0]
        result_grad = out_cotangent[micro_index, 0].astype(jnp.float32) + times_transpose(
            embed_cot, params[12]
        )
        embed_weight_grad = contract_rows(result_low, embed_cot)
        sum_grad, second_gain_grad, second_shift_grad = norm_backward(
            result_grad, second_normed, second_rstd, second_gain_wide
        )
        down_grad = sum_grad.astype(jnp.bfloat16)
        down_bias_grad = jnp.sum(down_grad.astype(jnp.float32), axis=0)
        down_weight_grad = contract_rows(act_low, down_grad)
        up_grad = (times_transpose(down_grad, params[8]) * gelu_slope(up_value)).astype(
            jnp.bfloat16
        )
        up_bias_grad = jnp.sum(up_grad.astype(jnp.float32), axis=0)
        up_weight_grad = contract_rows(hidden_low, up_grad)
        hidden_grad = sum_grad + times_transpose(up_grad, params[6])
        first_grad, first_gain_grad, first_shift_grad = norm_backward(
            hidden_grad, first_normed, first_rstd, first_gain_wide
        )
        branch_grad = first_grad.astype(jnp.bfloat16)
        output_bias_grad = jnp.sum(branch_grad.astype(jnp.float32), axis=0)
        output_weight_grad = contract_rows(context_low, branch_grad)
        context_grad = (
            times_transpose(branch_grad, params[2]).astype(jnp.bfloat16).reshape(head_shape)
        )
        delta = jnp.transpose(jnp.sum(context_grad.astype(jnp.float32) * context, axis=-1))
        kv_again = lax.all_gather(local_kv, "group", axis=0, tiled=True)
        blocks, seg_blocks = key_blocks(kv_again, seg_all)
        query_grad, kv_partial = attention_backward(
            queries, blocks, seg_blocks, seg_local, log_norm, context_grad, delta
        )
        kv_grad = lax.psum_scatter(
            kv_partial.astype(jnp.bfloat16), "group", scatter_dimension=0, tiled=True
        ).astype(jnp.float32)
        key_part = kv_grad[:, :width].reshape(head_shape)
        value_part = kv_grad[:, width:]
        query_back = unrotate(query_grad, cosine_table, sine_table).reshape(length, width)
        key_back = unrotate(key_part, cosine_table, sine_table).reshape(length, width)
        projected_grad = jnp.concatenate([query_back, key_back, value_part], axis=1).astype(
            jnp.bfloat16
        )
        project_bias_grad = jnp.sum(projected_grad.astype(jnp.float32), axis=0)
        project_weight_grad = contract_rows(token_low, projected_grad)
        input_grads.append(first_grad + times_transpose(projected_grad, params[0]))
        local_grads = (
            project_weight_grad,
            project_bias_grad,
            output_weight_grad,
            output_bias_grad,
            first_gain_grad,
            first_shift_grad,
            up_weight_grad,
            up_bias_grad,
            down_weight_grad,
            down_bias_grad,
            second_gain_grad,
            second_shift_grad,
            embed_weight_grad,
        )
        summed = (
            lax.psum_scatter(local_grads[0], ("group", "wide"), scatter_dimension=0, tiled=True),
            lax.psum_scatter(local_grads[1], ("group", "wide"), scatter_dimension=0, tiled=True),
            lax.psum_scatter(local_grads[2], ("group", "wide"), scatter_dimension=0, tiled=True),
            lax.psum_scatter(local_grads[3], ("group", "wide"), scatter_dimension=0, tiled=True),
            lax.psum_scatter(local_grads[4], ("group", "wide"), scatter_dimension=0, tiled=True),
            lax.psum_scatter(local_grads[5], ("group", "wide"), scatter_dimension=0, tiled=True),
            lax.psum_scatter(local_grads[6], ("group", "wide"), scatter_dimension=0, tiled=True),
            lax.psum_scatter(local_grads[7], ("group", "wide"), scatter_dimension=0, tiled=True),
            lax.psum_scatter(local_grads[8], ("group", "wide"), scatter_dimension=0, tiled=True),
            lax.psum_scatter(local_grads[9], ("group", "wide"), scatter_dimension=0, tiled=True),
            lax.psum_scatter(local_grads[10], ("group", "wide"), scatter_dimension=0, tiled=True),
            lax.psum_scatter(local_grads[11], ("group", "wide"), scatter_dimension=0, tiled=True),
            lax.psum_scatter(local_grads[12], ("group", "wide"), scatter_dimension=0, tiled=True),
        )
        grad_total = (
            summed
            if grad_total is None
            else tuple((total + part for total, part in zip(grad_total, summed)))
        )
    layer_out = jnp.stack(results)[:, None]
    embed_out = jnp.stack(embeddings)[:, None]
    token_grad = jnp.stack(input_grads)[:, None]
    return (
        layer_out,
        embed_out,
        token_grad,
        grad_total[0],
        grad_total[1],
        grad_total[2],
        grad_total[3],
        grad_total[4],
        grad_total[5],
        grad_total[6],
        grad_total[7],
        grad_total[8],
        grad_total[9],
        grad_total[10],
        grad_total[11],
        grad_total[12],
    )


MESH = pl.DeviceIdType.MESH
F32 = jnp.float32
BF16 = jnp.bfloat16
PLANE = 4
LINE = 4
GATHER_SEMS = 42
REDUCE_SEMS = 42
CORE, UPPER, LOWER, ROW, COLUMN, ARRIVED, HOP = 0, 4, 8, 12, 16, 20, 25
OWN_UPPER, OWN_LOWER, OWN_ROW, OWN_COLUMN, RING_ARRIVED, RING_HOP = 29, 30, 31, 32, 33, 38
FORWARD_PARTS = ((True, ((0, 0, 4, 0, 2, ), (1, 0, 4, 0, 4, ), (2, 0, 4, 0, 4, ), ), ), (False, ((0, 0, 4, 2, 4, ), ), ), (True, ((3, 0, 4, 0, 4, ), ), ), (True, ((4, 0, 4, 0, 4, ), ), ), (False, ((5, 0, 2, 0, 4, ), ), ), (True, ((5, 2, 4, 0, 4, ), ), ), )
FORWARD_STEPS = (((1003, 1, 1002, 20005, 2001, 0, 3, 2, 2000, 3001, 41, 1202, 10, 12, 4002, 42, 1103, 2041, 23, 2010, 2003, 3000, 2012, 20003, 1401, 3003, 2023, 51, 3041, 20, 2043, 1404, 2020, 20002, 52, 33, 1400, 53, 43, 113, 2013, 2033, 2052, 2032, 32, 3012, 1410, 1441, 4003, 222, 62, 202, 2042, 3010, 153, 2212, 143, 3002, 103, 2222, 4103, 63, 22, 133, 242, 252, 1424, 1451, 2051, 2002, 232, 3051, 2113, 4202, 1420, 262, 2232, 2133, 1414, 13, 2143, 3113, 163, 123, 1444, 5001, 3103, 3020, 1454, 212, 5002, 3023, 3053, 354, 2022, 2242, 2314, 334, 2053, 4401, 21005, 2334, 324, 344, 3052, 3013, 1464, 1434, 5000, 314, 304, 4400, 2103, 3202, 364, 900, 1900, 2062, 20900, 2153, ), ), ((), ), ((3033, 2202, 2252, ), (), (2123, ), (23004, 3063, 3032, 2063, 3043, ), (3042, ), (3153, 2344, 5010, 5041, 23900, ), ), ((3252, 5043, 5053, 5052, 4441, 3062, 3022, 2304, ), (5013, 5022, 3212, 5023, 4410, ), (3133, 2163, 3304, 3242, 3232, 3222, ), (3143, ), (5051, 3163, 2354, 5020, 3123, 2262, 2324, 21003, 5012, 5042, 3354, ), (3262, 5153, 4404, ), (3334, 3314, 5242, 5063, 4451, 5032, 5033, 2364, ), (4414, 3324, 2900, 3344, 21002, 5062, 4420, 5003, 3364, ), ), ((), (5143, 5113, 3900, 4454, 5232, 5222, 5212, ), ), ((4424, 5133, 5123, 5252, ), (), (4464, ), (5202, 4434, 5103, 5334, 5344, 5262, 5163, ), (4444, 5314, 5324, ), (5304, 5364, 5354, ), (), (4900, 5900, 21900, ), ), ((), (22003, 22005, ), ), ((), (), (), (), (22002, ), (), (), (), ), ((), (22900, ), ), )
BACKWARD_STEPS = ((900, 0, 901, 10, 902, 100, 110, 11, 1, 20, 200, 300, ), ((101, 210, 111, ), (), (212, 310, 311, 303, 400, 120, 202, 302, ), (), (211, ), (201, ), (410, 312, 220, ), (), ), (911, 221, 411, 21, 301, 320, 903, 904, 909, 412, 121, 213, 905, 30, 323, 313, 420, 401, 203, 906, 130, 40, 530, 41, 31, 322, 230, 930, 920, 140, 223, 331, 231, 330, 921, 141, 131, 531, 922, 923, 342, 321, 430, 241, 532, 240, 232, 340, 343, 242, 924, 333, 222, 925, 907, 912, 421, 422, 332, 402, 533, 341, 630, 413, 423, 440, 233, 243, 431, 432, 730, 441, 442, 403, 910, 908, 433, 830, 443, ), )


def place():
    group = lax.axis_index("group")
    wide = lax.axis_index("wide")
    return (group, lax.rem(group, 2), group // 2, wide // 2, lax.rem(wide, 2))


def when(cond, act):
    if cond is True:
        act()
    else:
        pl.when(cond)(act)


def both(left, right):
    return right if left is True else jnp.logical_and(left, right)


def remote(src, dst, send_sem, recv_sem, device):
    return pltpu.make_async_remote_copy(
        src_ref=src,
        dst_ref=dst,
        send_sem=send_sem,
        recv_sem=recv_sem,
        device_id=device,
        device_id_type=MESH,
    )


def entry_barrier():
    g, x, y, z, c = place()
    devices = []
    for step in range(1, 8):
        other = lax.rem(g * 2 + c + step, 8)
        devices.append((other // 2, z * 2 + lax.rem(other, 2)))
    devices.append((g, lax.rem(z + 1, LINE) * 2 + c))
    devices.append((g, lax.rem(z + LINE - 1, LINE) * 2 + c))
    barrier = pltpu.get_barrier_semaphore()
    for device in devices:
        pl.semaphore_signal(barrier, inc=1, device_id=device, device_id_type=MESH)
    pl.semaphore_wait(barrier, len(devices))


class Sender:
    def __init__(self, send_sems, recv_sems):
        self.send_sems, self.recv_sems = send_sems, recv_sems
        self.pending, self.draining = [], False

    def copy(self, src, dst, index, device):
        return remote(src, dst, self.send_sems.at[index], self.recv_sems.at[index], device)

    def send(self, cond, src, dst, index, device):
        copy = self.copy(src, dst, index, device)
        when(cond, copy.wait_send if self.draining else copy.start)

    def post(self, cond, src, dst, index, device):
        self.send(cond, src, dst, index, device)
        self.pending.append((cond, src, dst, index, device))

    def land(self, ref, index, device):
        self.copy(ref, ref, index, device).wait_recv()

    def do(self, cond, act):
        if not self.draining:
            when(cond, act)

    def drain(self, ticks):
        self.draining = True
        for tick in ticks:
            tick()
        for call in self.pending:
            self.send(*call)


def near_items(z, distance):
    if distance == 0:
        return [(0, z, True)]
    return [
        (distance, jnp.maximum(z - distance, 0), z >= distance),
        (3 + distance, jnp.minimum(z + distance, LINE - 1), z + distance < LINE),
    ]


class Gather:
    def __init__(self, parts, sender, local_sems):
        self.parts, self.sender, self.local_sems = parts, sender, local_sems
        self.seen = set()
        g, x, y, z, c = place()
        self.g, self.z, self.c = g, z, c
        self.gx, self.gy, self.gd = g + 1 - 2 * x, g + 2 - 4 * y, 3 - g
        self.devices = (
            (g, jnp.minimum(z + 1, LINE - 1) * 2 + c),
            (g, jnp.maximum(z - 1, 0) * 2 + c),
            (self.gx, z * 2 + c),
            (self.gy, z * 2 + c),
            (g, z * 2 + 1 - c),
        )
        for part in parts:
            for member in part[1]:
                self.own(member).start()

    def window(self, member, g, zi, c, rows=None):
        shard, full, top, count, left, columns, index = member
        first, last = (0, count) if rows is None else rows
        return full.at[g, zi, c, top + first : top + last, left : left + columns]

    def shard(self, member):
        shard, full, top, count, left, columns, index = member
        return shard.at[top : top + count, left : left + columns]

    def own(self, member):
        return pltpu.make_async_copy(
            self.shard(member),
            self.window(member, self.g, self.z, self.c),
            self.local_sems.at[member[6]],
        )

    def ring(self, member, zi, c):
        shard, full, top, count, left, columns, index = member
        return full.at[:, zi, c, top : top + count, left : left + columns]

    def item(self, slot):
        z = self.z
        if slot == 0:
            return z, True
        if slot < 4:
            return jnp.maximum(z - slot, 0), z >= slot
        return jnp.minimum(z + slot - 3, LINE - 1), z + slot - 3 < LINE

    def land(self, cond, ref, index):
        self.sender.do(cond, lambda: self.sender.land(ref, index, self.devices[4]))

    def arrivals(self, part, event, slot):
        zi, cond = self.item(slot)
        line = self.parts[part][0]
        for member in self.parts[part][1]:
            base, half, rows = member[6] * GATHER_SEMS, member[3] // 2, member[3]
            diagonal = lambda: (
                self.land(cond, self.window(member, self.gd, zi, self.c, (0, half)), base + 21 + slot),
                self.land(cond, self.window(member, self.gd, zi, self.c, (half, rows)), base + 28 + slot),
            )
            if event == 0 and slot > 0:
                self.land(cond, self.window(member, self.g, zi, self.c), base + slot)
            elif event == 1:
                self.land(cond, self.window(member, self.gx, zi, self.c), base + 7 + slot)
            elif event == 2:
                self.land(cond, self.window(member, self.gy, zi, self.c), base + 14 + slot)
            elif event == 3 or (event == 4 and slot == 0):
                diagonal()
                if slot == 0:
                    self.sender.do(True, lambda: self.own(member).wait())
            elif event == 4:
                self.land(cond, self.ring(member, zi, self.c), base + slot)

    def step(self, part, event, slot, link):
        if (part, event, slot) not in self.seen:
            self.seen.add((part, event, slot))
            self.arrivals(part, event, slot)
        zi, cond = self.item(slot)
        z, device = self.z, self.devices[link]
        for member in self.parts[part][1]:
            base, half, rows = member[6] * GATHER_SEMS, member[3] // 2, member[3]
            if link == 0:
                cond_here, index = both(cond, z < LINE - 1), base + slot + 1
            elif link == 1:
                cond_here, index = both(cond, z > 0), base + (4 if slot == 0 else slot + 1)
            else:
                cond_here = cond
                index = base + slot + ({2: 7, 3: 14} if event == 0 else {3: 21, 2: 28, 4: 35})[link]
            if event == 0:
                target = self.window(member, self.g, zi, self.c)
                source = self.shard(member) if slot == 0 else target
            elif event == 1:
                source = target = self.window(member, self.gx, zi, self.c, (0, half))
            elif event == 2:
                source = target = self.window(member, self.gy, zi, self.c, (half, rows))
            else:
                source = target = self.ring(member, zi, self.c)
            self.sender.send(cond_here, source, target, index, device)

    def finish(self, part):
        for member in self.parts[part][1]:
            for slot in range(7):
                zi, cond = self.item(slot)
                self.land(cond, self.ring(member, zi, 1 - self.c), member[6] * GATHER_SEMS + 35 + slot)


def staged(order, stages, delays):
    ticks = []
    for t in range(len(order) + delays[-1]):

        def tick(t=t):
            for stage, delay in zip(stages, delays):
                if 0 <= t - delay < len(order):
                    stage(*order[t - delay])

        ticks.append(tick)
    return ticks


def add_into(target, terms):
    rows, columns = target.shape
    step = min(columns, 512)

    def body(i, carry):
        cut = pl.ds(pl.multiple_of(i * step, step), step)
        value = terms[0][:, cut].astype(F32)
        for term in terms[1:]:
            value = value + term[:, cut].astype(F32)
        target[:, cut] = value.astype(target.dtype)
        return carry

    lax.fori_loop(0, columns // step, body, 0)


class Exchange:
    def __init__(self, sources, targets, outward, sender, base, local_sems, local_base):
        self.sources, self.targets, self.outward = sources, targets, outward
        self.sender, self.base = sender, base
        self.local_sems, self.local_base = local_sems, local_base
        self.started = False
        g, x, y, z, c = place()
        self.g, self.z, self.c = g, z, c
        self.neighbours = {2: g + 1 - 2 * x, 3: g + 2 - 4 * y, 5: 3 - g}

    def device(self, index, outward):
        g, z, c = self.g, self.z, self.c
        if outward:
            return (index * 2 + c, z * 2 + g // 2)
        return (2 * c + index, z * 2 + lax.rem(g, 2))

    def same(self, device):
        return jnp.logical_and(device[0] == self.g, device[1] == self.z * 2 + self.c)

    def local(self, i, index, slot):
        return pltpu.make_async_copy(
            self.sources[i].at[index],
            self.targets[i].at[slot],
            self.local_sems.at[self.local_base + i],
        )

    def step(self, link):
        slot = lax.rem(self.g, 2) if self.outward else self.g // 2
        first = not self.started and not self.sender.draining
        self.started = True
        for i in range(len(self.sources)):
            for index in range(2):
                device = self.device(index, self.outward)
                if first:
                    when(self.same(device), lambda: self.local(i, index, slot).start())
                copy = remote(
                    self.sources[i].at[index],
                    self.targets[i].at[slot],
                    self.sender.send_sems.at[self.base + i * 4 + 2 + index],
                    self.sender.recv_sems.at[self.base + i * 4 + slot],
                    device,
                )
                cond = device[0] == self.neighbours[link]
                if link == 2:
                    here = jnp.logical_and(device[0] == self.g, device[1] != self.z * 2 + self.c)
                    cond = jnp.logical_or(cond, here)
                when(cond, copy.wait_send if self.sender.draining else copy.start)

    def arrive(self):
        for i in range(len(self.sources)):
            for index in range(2):
                device = self.device(index, not self.outward)
                target = self.targets[i].at[index]
                when(self.same(device), lambda: self.local(i, index, index).wait())
                when(
                    jnp.logical_not(self.same(device)),
                    lambda: self.sender.land(
                        target, self.base + i * 4 + index, (self.g, self.z * 2 + 1 - self.c)
                    ),
                )


def hbm():
    return pl.BlockSpec(memory_space=pltpu.HBM)


def vmem():
    return pl.BlockSpec(memory_space=pltpu.VMEM)


def chain(*ticks):
    def act():
        for tick in ticks:
            tick()

    return act


def run_with(ticks, steps, body):
    def act(i, carry):
        body(i)
        for j, tick in enumerate(ticks[:steps]):
            pl.when(i == j)(tick)
        return carry

    lax.fori_loop(0, steps, act, 0)
    for tick in ticks[steps:]:
        tick()


def lane_half(shape, period, half):
    lanes = lax.broadcasted_iota(jnp.int32, shape, 1)
    return lax.rem(lanes, period) < half


def turn(values):
    first = lane_half(values.shape, HEAD_DIM, HEAD_DIM // 2)
    return jnp.where(
        first,
        -pltpu.roll(values, values.shape[1] - HEAD_DIM // 2, 1),
        pltpu.roll(values, HEAD_DIM // 2, 1),
    )


def dot_rows(left, right):
    return lax.dot_general(left, right, (((1,), (0,)), ((), ())), preferred_element_type=F32)


def dot_columns(left, right):
    return lax.dot_general(left, right, (((1,), (1,)), ((), ())), preferred_element_type=F32)


def attend_pair(
    query_ref, key_ref, value_ref, far_key_ref, far_value_ref, seg_ref, seg_near_ref, seg_far_ref, out_ref, norm_ref
):
    rows = query_ref.shape[0]
    first = lane_half((rows, 128), 128, HEAD_DIM)
    tile = 256
    for r in range(rows // tile):
        rs = pl.ds(r * tile, tile)
        query = query_ref[rs, :]
        low_half = first[:tile]
        seg = seg_ref[rs, 0:1]
        near, far = seg == seg_near_ref[...], seg == seg_far_ref[...]
        outs, norms = [], []
        for h in range(2):
            keep = low_half if h == 0 else jnp.logical_not(low_half)
            one = jnp.where(keep, query, jnp.zeros_like(query))
            near_scores = jnp.where(near, dot_columns(one, key_ref[...]), neg_large)
            far_scores = jnp.where(far, dot_columns(one, far_key_ref[...]), neg_large)
            top = jnp.maximum(
                jnp.max(near_scores, axis=1, keepdims=True), jnp.max(far_scores, axis=1, keepdims=True)
            )
            near_expon, far_expon = jnp.exp(near_scores - top), jnp.exp(far_scores - top)
            total = jnp.sum(near_expon, axis=1, keepdims=True) + jnp.sum(
                far_expon, axis=1, keepdims=True
            )
            mixed = dot_rows(near_expon.astype(BF16), value_ref[...]) + dot_rows(
                far_expon.astype(BF16), far_value_ref[...]
            )
            outs.append(mixed / total)
            norms.append(jnp.broadcast_to(top + jnp.log(total), (tile, 128)))
        out_ref[rs, :] = jnp.where(low_half, outs[0], outs[1]).astype(BF16)
        flipped = jnp.transpose(jnp.where(low_half, norms[0], norms[1]))
        norm_ref[0:1, rs] = flipped[0:1]
        norm_ref[1:2, rs] = flipped[HEAD_DIM : HEAD_DIM + 1]


def stretch(packed, vectors, sizes):
    shards = packed.shape[0] // 32
    for row, lane, size, target in vectors:
        pick_rows = lax.broadcasted_iota(jnp.int32, (shards, shards * 32), 0) * 32 + row
        pick = lax.broadcasted_iota(jnp.int32, (shards, shards * 32), 1) == pick_rows
        part = dot_rows(pick.astype(F32).astype(BF16), packed).astype(BF16)
        step = 1024

        def body(i, carry):
            at = pl.multiple_of(i * step, step)
            column = (lax.broadcasted_iota(jnp.int32, (1, step), 1) + i * step).astype(F32)
            shard = jnp.floor((column + 0.5) * (1.0 / size))
            lane_of = (column - shard * size + lane).astype(jnp.int32)
            spread = lax.broadcasted_iota(jnp.int32, (128, step), 0) == lane_of
            value = dot_rows(part, spread.astype(F32).astype(BF16))
            keep = lax.broadcasted_iota(jnp.int32, (shards, step), 0) == shard.astype(jnp.int32)
            target[:, pl.ds(at, step)] = jnp.sum(jnp.where(keep, value, 0.0), axis=0, keepdims=True)
            return carry

        lax.fori_loop(0, shards * size // step, body, 0)


def flat(value):
    return value.reshape(-1, value.shape[-1])


def row_mean(value):
    return jnp.mean(value, axis=1, keepdims=True)


def forward_kernel(*refs):
    shards, refs = refs[:6], refs[6:]
    (tokens, out_cot, embed_cot, segments, cosine, sine), refs = refs[:6], refs[6:]
    (
        project_out, token_out, qkv_out, far_out, context_out, norm, hidden_out, act_out, up_grad_out,
        down_grad_out, result_out, embed_cot_out, branch_grad_out, context_grad_out, first_grad_out,
        sums, seg_out, layer_back, embed_back,
    ), refs = refs[:19], refs[19:]
    fulls, refs = refs[:6], refs[6:]
    (
        token_in, cot_in, embed_cot_in, far_seg, seg_column, vectors, qkv, far, context, normed, rstd,
        hidden_low, act, slope, result_low, embedded, sum_grad, down_grad, branch_grad, context_grad,
        send_sems, recv_sems, local_sems,
    ) = refs
    project_w, embed_w, small_w, output_w, up_w, down_w = fulls
    g, x, y, z, c = place()
    partner = (g, z * 2 + 1 - c)
    rows, width = context.shape
    sender = Sender(send_sems, recv_sems)
    spare = sum(len(p[1]) for p in FORWARD_PARTS) * GATHER_SEMS
    flushed = []

    def flush(source, target, index):
        copy = pltpu.make_async_copy(source, target, local_sems.at[40 + index])
        copy.start()
        flushed.append((source, target, index))

    entry_barrier()
    parts = []
    for line, members in FORWARD_PARTS:
        rows_of = []
        for array, first_row, last_row, first_column, last_column in members:
            height, breadth = shards[array].shape
            top, left = first_row * height // 4, first_column * breadth // 4
            rows_of.append(
                (
                    shards[array],
                    fulls[array],
                    top,
                    last_row * height // 4 - top,
                    left,
                    last_column * breadth // 4 - left,
                    sum(len(p[1]) for p in parts) + len(rows_of),
                )
            )
        parts.append((line, rows_of))
    plan = Gather(parts, sender, local_sems)
    exchanges = {
        20: Exchange([tokens], [token_in], True, sender, spare + 2, local_sems, 20),
        21: Exchange(
            [out_cot, embed_cot], [cot_in, embed_cot_in], True, sender, spare + 6, local_sems, 21
        ),
        22: Exchange(
            [result_low, embedded], [layer_back, embed_back], False, sender, spare + 14, local_sems, 23
        ),
    }

    def perform(steps):
        def act():
            for step in steps:
                part, event, slot, link = step // 1000, step // 100 % 10, step // 10 % 10, step % 10
                if part == 23:
                    if event == 9:
                        sender.do(True, lambda: sender.land(far, spare + 1, partner))
                    else:
                        sender.send(True, qkv.at[:, width:], far, spare + 1, partner)
                elif part >= 20:
                    if event != 9:
                        exchanges[part].step(link)
                    elif not sender.draining:
                        exchanges[part].arrive()
                elif event == 9:
                    plan.finish(part)
                else:
                    plan.step(part, event, slot, link)

        return act

    ticks = [[perform(steps) for steps in phase] for phase in FORWARD_STEPS]
    sender.post(True, segments, far_seg, spare, partner)
    ticks[0][0]()
    sender.land(far_seg, spare, partner)
    micro = g // 2
    own_ids, far_ids = segments[micro].astype(F32), far_seg[micro].astype(F32)
    ids = jnp.where(lax.rem(g, 2) == c, own_ids, far_ids)
    halves = (ids[:, :rows], ids[:, rows:])
    near_row = jnp.where(c == 0, halves[0], halves[1])
    far_row = jnp.where(c == 0, halves[1], halves[0])
    seg_out[0:1, :] = near_row
    seg_out[1:2, :] = far_row
    seg_column[...] = jnp.transpose(jnp.broadcast_to(near_row, (128, rows)))
    flush(project_w, project_out, 0)
    flush(token_in, token_out, 1)
    vector = lambda i, size: vectors.at[i : i + 1, 0:size]
    stretch(
        flat(small_w[...]),
        (
            (0, 0, 96, vector(0, 3 * width)),
            (1, 0, 128, vector(1, 4 * width)),
            (2, 0, 32, vector(2, width)),
            (2, 32, 32, vector(3, width)),
            (2, 64, 32, vector(4, width)),
            (2, 96, 32, vector(5, width)),
            (3, 0, 32, vector(6, width)),
            (3, 32, 32, vector(7, width)),
        ),
        None,
    )
    tile = 512
    wide = qkv.shape[1] // tile

    def project_tile(i):
        t = lax.rem(i + 2, wide)
        cut = pl.ds(pl.multiple_of(t * tile, tile), tile)
        value = dot_rows(flat(token_in[...]), flat(project_w[:, :, :, :, cut]))
        value = value + vectors[0:1, cut]

        @pl.when(t < 4)
        def _():
            factor = jnp.where(t < 2, HEAD_DIM ** (-0.5), 1.0)
            for j in range(tile // 128):
                part = value[:, j * 128 : (j + 1) * 128]
                part = (part * cosine[...] + turn(part) * sine[...]) * factor
                qkv[:, pl.ds(pl.multiple_of(t * tile + j * 128, 128), 128)] = part.astype(BF16)

        @pl.when(t >= 4)
        def _():
            qkv[:, cut] = value.astype(BF16)

    ticks[1][0]()
    run_with(ticks[2], wide, project_tile)
    flush(qkv, qkv_out, 2)
    flush(far, far_out, 3)

    def attend_one(i):
        at = pl.multiple_of(i * 128, 128)
        cut = lambda ref, base: ref.at[:, pl.ds(base + at, 128)]
        attend_pair(
            cut(qkv, 0), cut(qkv, width), cut(qkv, 2 * width), cut(far, 0), cut(far, width),
            seg_column, seg_out.at[0:1], seg_out.at[1:2], cut(context, 0), norm.at[i],
        )

    run_with(ticks[3], width // 128, attend_one)
    flush(context, context_out, 4)
    half = rows // 2
    output_weight, bias_o = lambda: flat(output_w[...]), vectors[2:3, 0:width]

    def hidden_of(cut):
        return normed[cut, :] * vectors[3:4, 0:width] + vectors[4:5, 0:width]

    def branch_tile(i):
        cut = pl.ds(pl.multiple_of(i * half, half), half)
        resid = dot_rows(context[cut, :], output_weight()) + vectors[2:3, 0:width]
        resid = resid + token_in[i].astype(F32)
        center = resid - row_mean(resid)
        scale = lax.rsqrt(row_mean(center * center) + eps_norm)
        normed[cut, :] = center * scale
        rstd[0, cut, :] = jnp.broadcast_to(scale, (half, 128))
        hidden_low[cut, :] = hidden_of(cut).astype(BF16)

    run_with(ticks[4], 2, branch_tile)
    flush(hidden_low, hidden_out, 5)

    def up_tile(j):
        cut = pl.ds(pl.multiple_of(j * tile, tile), tile)
        value = dot_rows(hidden_low[...], flat(up_w[:, :, :, :, cut])) + vectors[1:2, cut]
        below = 0.5 + 0.5 * lax.erf(value * 0.7071067811865476)
        density = jnp.exp(-0.5 * value * value) * 0.3989422804014327
        act[:, cut] = (value * below).astype(BF16)
        slope[:, cut] = (below + value * density).astype(BF16)

    ff = act.shape[1]
    run_with(ticks[5], ff // tile, up_tile)
    flush(act, act_out, 6)
    flush(embed_cot_in, embed_cot_out, 7)
    sums[...] = jnp.zeros_like(sums)

    def add_sum(row, value):
        sums[row : row + 1, 0:width] += jnp.sum(value, axis=0, keepdims=True)

    def norm_back(grads, row_normed, scale, gain):
        scaled = grads * gain
        return scale * (
            scaled - row_mean(scaled) - row_normed * row_mean(scaled * row_normed)
        )

    def down_tile(i):
        cut = pl.ds(pl.multiple_of(i * half, half), half)
        gain, shift = vectors[6:7, 0:width], vectors[7:8, 0:width]
        resid = dot_rows(act[cut, :], flat(down_w[...])) + vectors[5:6, 0:width]
        resid = resid + hidden_of(cut)
        center = resid - row_mean(resid)
        scale = lax.rsqrt(row_mean(center * center) + eps_norm)
        row_normed = center * scale
        low = (row_normed * gain + shift).astype(BF16)
        result_low[i] = low
        embed_full = flat(embed_w[...])
        embedded[i] = dot_rows(low, embed_full).astype(BF16)
        grads = cot_in[i].astype(F32) + dot_columns(embed_cot_in[i], embed_full)
        add_sum(6, grads * row_normed)
        add_sum(7, grads)
        total = norm_back(grads, row_normed, scale, gain)
        sum_grad[cut, :] = total
        low = total.astype(BF16)
        down_grad[cut, :] = low
        add_sum(5, low.astype(F32))

    run_with(ticks[6], 2, down_tile)
    flush(result_low, result_out, 8)
    flush(down_grad, down_grad_out, 9)

    def up_grad_tile(j):
        cut = pl.ds(pl.multiple_of(j * tile, tile), tile)
        part = flat(down_w[j // 2, pl.ds(lax.rem(j, 2) * 2, 2)])
        value = (dot_columns(down_grad[...], part) * slope[:, cut].astype(F32)).astype(BF16)
        slope[:, cut] = value
        sums[1:2, cut] = jnp.sum(value.astype(F32), axis=0, keepdims=True)

    run_with(ticks[7], ff // tile, up_grad_tile)
    flush(slope, up_grad_out, 10)

    def first_tile(i):
        cut = pl.ds(pl.multiple_of(i * half, half), half)
        grads = sum_grad[cut, :] + dot_columns(slope[cut, :], flat(up_w[...]))
        row_normed = normed[cut, :]
        add_sum(3, grads * row_normed)
        add_sum(4, grads)
        total = norm_back(grads, row_normed, rstd[0, cut, 0:1], vectors[3:4, 0:width])
        sum_grad[cut, :] = total
        low = total.astype(BF16)
        branch_grad[cut, :] = low
        add_sum(2, low.astype(F32))
        context_grad[cut, :] = dot_columns(low, output_weight()).astype(BF16)

    run_with(ticks[8], 2, first_tile)
    flush(sum_grad, first_grad_out, 11)
    flush(branch_grad, branch_grad_out, 12)
    flush(context_grad, context_grad_out, 13)
    sender.drain([tick for phase in ticks for tick in phase])
    for source, target, index in flushed:
        pltpu.make_async_copy(source, target, local_sems.at[40 + index]).wait()


def forward(shards, sources, segments, tables, ff):
    piece, width = sources[0].shape[1:]
    lanes = sources[2].shape[2]
    rows = 2 * piece
    semaphores = sum(len(p[1]) for p in FORWARD_PARTS) * GATHER_SEMS + 32
    fulls = [(PLANE, LINE, 2) + s.shape for s in shards]
    shape = jax.ShapeDtypeStruct
    outs = [
        shape(fulls[0], BF16),
        shape((2, piece, width), BF16),
        shape((rows, 3 * width), BF16),
        shape((rows, 2 * width), BF16),
        shape((rows, width), BF16),
        shape((width // 128, 8, rows), F32),
        shape((rows, width), BF16),
        shape((rows, ff), BF16),
        shape((rows, ff), BF16),
        shape((rows, width), BF16),
        shape((2, piece, width), BF16),
        shape((2, piece, lanes), BF16),
        shape((rows, width), BF16),
        shape((rows, width), BF16),
        shape((rows, width), F32),
        shape((8, ff), F32),
        shape((8, rows), F32),
        shape((2, piece, width), BF16),
        shape((2, piece, lanes), BF16),
    ]
    spaces = [hbm()] * len(outs)
    for i in (5, 15, 16):
        spaces[i] = vmem()
    scratch = [pltpu.VMEM(f, BF16) for f in fulls] + [
        pltpu.VMEM((2, piece, width), BF16),
        pltpu.VMEM((2, piece, width), BF16),
        pltpu.VMEM((2, piece, lanes), BF16),
        pltpu.VMEM(segments.shape, jnp.int32),
        pltpu.VMEM((rows, 128), F32),
        pltpu.VMEM((8, ff), F32),
        pltpu.VMEM((rows, 3 * width), BF16),
        pltpu.VMEM((rows, 2 * width), BF16),
        pltpu.VMEM((rows, width), BF16),
        pltpu.VMEM((rows, width), F32),
        pltpu.VMEM((1, rows, 128), F32),
        pltpu.VMEM((rows, width), BF16),
        pltpu.VMEM((rows, ff), BF16),
        pltpu.VMEM((rows, ff), BF16),
        pltpu.VMEM((2, piece, width), BF16),
        pltpu.VMEM((2, piece, lanes), BF16),
        pltpu.VMEM((rows, width), F32),
        pltpu.VMEM((rows, width), BF16),
        pltpu.VMEM((rows, width), BF16),
        pltpu.VMEM((rows, width), BF16),
        pltpu.SemaphoreType.DMA((semaphores,)),
        pltpu.SemaphoreType.DMA((semaphores,)),
        pltpu.SemaphoreType.DMA((60,)),
    ]
    return pl.pallas_call(
        forward_kernel,
        out_shape=outs,
        in_specs=[hbm()] * 9 + [vmem()] * 3,
        out_specs=spaces,
        scratch_shapes=scratch,
        compiler_params=pltpu.CompilerParams(
            collective_id=1, has_side_effects=True, vmem_limit_bytes=67043328
        ),
        name="forward",
    )(*shards, *sources, segments, *tables)


def attend_back_pair(
    query, key, value, far_key, far_value, grad, norm, seg_row, seg_near, seg_far, tables, summed
):
    rows = query.shape[0]
    tile = 256
    cosine, sine, shift = tables
    low_half = lane_half((rows, 128), 128, HEAD_DIM)
    query_low = lane_half((tile, 128), 128, HEAD_DIM)
    for total in summed:
        total[...] = jnp.zeros_like(total)

    def body(r, carry):
        rs = pl.ds(pl.multiple_of(r * tile, tile), tile)
        query_rows, grad_rows = query[rs, :], grad[rs, :]
        sides = ((key[...], value[...], seg_near), (far_key[...], far_value[...], seg_far))
        query_grads = []
        key_grads, value_grads = [[], []], [[], []]
        for h in range(2):
            keep = query_low if h == 0 else jnp.logical_not(query_low)
            one = jnp.where(keep, query_rows, jnp.zeros_like(query_rows))
            one_grad = jnp.where(keep, grad_rows, jnp.zeros_like(grad_rows))
            top = norm[h : h + 1, rs]
            kept = []
            delta = jnp.zeros((1, tile), F32)
            for keys, values, seg_key in sides:
                same = seg_key[:, 0:1] == seg_row[:, rs]
                scores = jnp.where(same, dot_columns(keys, one), neg_large)
                probs = jnp.exp(scores - top)
                product = probs * dot_columns(values, one_grad)
                delta = delta + jnp.sum(product, axis=0, keepdims=True)
                kept.append((probs, product))
            total = None
            for i, (keys, values, seg_key) in enumerate(sides):
                probs, product = kept[i]
                score_grad = (product - probs * delta).astype(BF16)
                key_grads[i].append(dot_rows(score_grad, query_rows))
                value_grads[i].append(dot_rows(probs.astype(BF16), grad_rows))
                part = contract_rows(score_grad, keys)
                total = part if total is None else total + part
            query_grads.append(total)
        for i in range(2):
            summed[i][...] += jnp.where(low_half, key_grads[i][0], key_grads[i][1])
            summed[2 + i][...] += jnp.where(low_half, value_grads[i][0], value_grads[i][1])
        joined = jnp.where(query_low, query_grads[0], query_grads[1]) * HEAD_DIM ** (-0.5)
        query[rs, :] = (joined * cosine[rs, :] - turn(joined) * sine[rs, :]).astype(BF16)
        return carry

    lax.fori_loop(0, rows // tile, body, 0)
    near, far = summed[0][...], summed[1][...]
    far_cosine = cosine[...] * shift[0:1, :] - sine[...] * shift[1:2, :]
    far_sine = sine[...] * shift[0:1, :] + cosine[...] * shift[1:2, :]
    key[...] = (near * cosine[...] - turn(near) * sine[...]).astype(BF16)
    value[...] = summed[2][...].astype(BF16)
    far_key[...] = (far * far_cosine - turn(far) * far_sine).astype(BF16)
    far_value[...] = summed[3][...].astype(BF16)


class Reduce:
    def __init__(self, arrays, sender):
        self.arrays, self.sender = arrays, sender
        g, x, y, z, c = place()
        self.g, self.z, self.c = g, z, c
        self.gx, self.gy, self.gd = g + 1 - 2 * x, g + 2 - 4 * y, 3 - g
        self.to_x, self.to_y = (self.gx, z * 2 + c), (self.gy, z * 2 + c)
        self.to_core = (g, z * 2 + 1 - c)
        lower = z < 2
        even = lax.rem(z, 2) == 0
        third = jnp.where(even, z + 1, z - 1)
        self.order = (jnp.where(lower, 3, 0), jnp.where(lower, 2, 1), third, z)
        self.rising = (lower, lower, even)

    def index(self, a, kind, i=0):
        return a * REDUCE_SEMS + kind + i

    def start(self, a, p):
        array, sender = self.arrays[a], self.sender

        def copy(b, i):
            other = self.arrays[b]
            return sender.copy(
                other.send.at[i % 2],
                other.held.at[self.order[i]],
                self.index(b, CORE, i),
                self.to_core,
            )

        if sender.draining:
            if p == 1 and a not in (1, 2):
                copy(a, 2).wait_send()
                copy(a, 3).wait_send()
            return
        before = (a, 0) if p == 1 else {2: (1, 2), 3: (2, 2)}.get(a)
        if before is not None:
            copy(before[0], before[1]).wait_send()
            copy(before[0], before[1] + 1).wait_send()
        zs = self.order[2 * p : 2 * p + 2]
        array.product(1 - self.c, zs, (array.send.at[0], array.send.at[1]), False)
        copy(a, 2 * p).start()
        copy(a, 2 * p + 1).start()

    def meet(self, a, p):
        array, sender = self.arrays[a], self.sender
        held, half_in, low = array.held, array.half, array.low
        rows, columns = held.shape[2:]
        cut = rows // 2
        zs = self.order[2 * p : 2 * p + 2]

        def work():
            for i in range(2):
                sender.land(held.at[zs[i]], self.index(a, CORE, 2 * p + i), self.to_x)
            array.product(self.c, zs, (held.at[zs[0]], held.at[zs[1]]), True)

        sender.do(True, work)
        for i in range(2):
            block = held.at[zs[i], self.gd]
            sender.send(
                True, block.at[0:cut, low:columns], half_in.at[zs[i], 0:cut],
                self.index(a, UPPER, 2 * p + i), self.to_y,
            )
            sender.send(
                True, block.at[cut:rows, low:columns], half_in.at[zs[i], cut:rows],
                self.index(a, LOWER, 2 * p + i), self.to_x,
            )

    def turn(self, a, i, upper):
        array, sender = self.arrays[a], self.sender
        held, half_in, whole_in, low = array.held, array.half, array.whole, array.low
        rows, columns = held.shape[2:]
        zi, cut = self.order[i], rows // 2
        first, last = (0, cut) if upper else (cut, rows)
        block = held.at[zi, self.gx if upper else self.gy, :, low:columns]

        def work():
            arrived = half_in.at[zi, first:last]
            sender.land(arrived, self.index(a, UPPER if upper else LOWER, i), self.to_x)
            add_into(block.at[first:last], [block.at[first:last], arrived])

        sender.do(True, work)
        sender.send(
            True, block, whole_in.at[zi, 0 if upper else 1],
            self.index(a, ROW if upper else COLUMN, i), self.to_x if upper else self.to_y,
        )

    def pass_on(self, i, source, lines, recv_kind, send_kind, a):
        z, zi = self.z, self.order[i]
        up = self.rising[i]
        slot = jnp.where(jnp.logical_and(jnp.logical_not(up), zi == z - 1), LINE, zi)
        copy = remote(
            source,
            lines.at[slot],
            self.sender.send_sems.at[self.index(a, send_kind, i)],
            self.sender.recv_sems.at[self.index(a, recv_kind) + slot],
            (self.g, jnp.where(up, z + 1, z - 1) * 2 + self.c),
        )
        if self.sender.draining:
            copy.wait_send()
        else:
            copy.start()

    def inner(self, i):
        return jnp.logical_or(
            jnp.logical_and(self.rising[i], self.z > 0),
            jnp.logical_and(jnp.logical_not(self.rising[i]), self.z < LINE - 1),
        )

    def along(self, a, i):
        array, sender = self.arrays[a], self.sender
        whole_in, lines, low = array.whole, array.line, array.low
        columns, zi, z = array.held.shape[3], self.order[i], self.z
        mine = array.held.at[zi, self.g, :, low:columns]
        terms = [mine, whole_in.at[zi, 0], whole_in.at[zi, 1]]
        arrived = self.index(a, ARRIVED)

        def work():
            sender.land(whole_in.at[zi, 0], self.index(a, ROW, i), self.to_x)
            sender.land(whole_in.at[zi, 1], self.index(a, COLUMN, i), self.to_x)
            if i < 3:
                inner = self.inner(i)

                def join():
                    sender.land(lines.at[zi], arrived + zi, self.to_x)
                    add_into(mine, terms + [lines.at[zi]])

                pl.when(inner)(join)
                pl.when(jnp.logical_not(inner))(lambda: add_into(mine, terms))
            else:
                self.close(lines, arrived, terms, array.out.at[:, low:columns])

        sender.do(True, work)
        if i < 3:
            self.pass_on(i, mine, lines, ARRIVED, HOP, a)

    def close(self, lines, arrived, terms, target):
        z, sender = self.z, self.sender
        rise, fall = lines.at[z], lines.at[LINE]
        pl.when(z > 0)(lambda: sender.land(rise, arrived + z, self.to_x))
        pl.when(z < LINE - 1)(lambda: sender.land(fall, arrived + LINE, self.to_x))
        pl.when(z == 0)(lambda: add_into(target, terms + [fall]))
        pl.when(z == LINE - 1)(lambda: add_into(target, terms + [rise]))
        pl.when(jnp.logical_and(z > 0, z < LINE - 1))(
            lambda: add_into(target, terms + [rise, fall])
        )

    def along_first(self, a, i):
        array, sender = self.arrays[a], self.sender
        low, rings, zi, z = array.low, array.rings, self.order[i], self.z
        mine = array.held.at[zi, :, :, 0:low]
        arrived = self.index(a, RING_ARRIVED)

        def add(slots):
            for j in range(PLANE):
                block = array.held.at[zi, j, :, 0:low]
                add_into(block, [block] + [rings.at[slot, j] for slot in slots])

        def work():
            if i < 3:

                def join():
                    sender.land(rings.at[zi], arrived + zi, self.to_x)
                    add([zi])

                pl.when(self.inner(i))(join)
                return
            pl.when(z > 0)(lambda: sender.land(rings.at[z], arrived + z, self.to_x))
            pl.when(z < LINE - 1)(lambda: sender.land(rings.at[LINE], arrived + LINE, self.to_x))
            pl.when(z == 0)(lambda: add([LINE]))
            pl.when(z == LINE - 1)(lambda: add([z]))
            pl.when(jnp.logical_and(z > 0, z < LINE - 1))(lambda: add([z, LINE]))

        sender.do(True, work)
        if i < 3:
            self.pass_on(i, mine, rings, RING_ARRIVED, RING_HOP, a)
            return
        block, half_in = array.held.at[z, self.gd, :, 0:low], array.own_half
        rows = half_in.shape[0]
        cut = rows // 2
        sender.send(
            True, block.at[0:cut], half_in.at[0:cut], self.index(a, OWN_UPPER), self.to_y
        )
        sender.send(
            True, block.at[cut:rows], half_in.at[cut:rows], self.index(a, OWN_LOWER), self.to_x
        )

    def turn_own(self, a, upper):
        array, sender = self.arrays[a], self.sender
        low, half_in = array.low, array.own_half
        rows = half_in.shape[0]
        first, last = (0, rows // 2) if upper else (rows // 2, rows)
        block = array.held.at[self.z, self.gx if upper else self.gy, :, 0:low]

        def work():
            arrived = half_in.at[first:last]
            sender.land(arrived, self.index(a, OWN_UPPER if upper else OWN_LOWER), self.to_x)
            add_into(block.at[first:last], [block.at[first:last], arrived])

        sender.do(True, work)
        sender.send(
            True, block, array.own_whole.at[0 if upper else 1],
            self.index(a, OWN_ROW if upper else OWN_COLUMN),
            self.to_x if upper else self.to_y,
        )

    def close_own(self, a):
        array, sender = self.arrays[a], self.sender
        low, whole_in = array.low, array.own_whole

        def work():
            sender.land(whole_in.at[0], self.index(a, OWN_ROW), self.to_x)
            sender.land(whole_in.at[1], self.index(a, OWN_COLUMN), self.to_x)
            mine = array.held.at[self.z, self.g, :, 0:low]
            add_into(array.out.at[:, 0:low], [mine, whole_in.at[0], whole_in.at[1]])

        sender.do(True, work)

    def step(self, code):
        kind, a, i = code // 100, code // 10 % 10, code % 10
        if kind == 0:
            self.start(a, i)
        elif kind == 1:
            self.meet(a, i)
        elif kind in (2, 3):
            self.turn(a, i, kind == 2)
        elif kind == 4:
            self.along(a, i)
        elif kind == 5:
            self.along_first(a, i)
        elif kind in (6, 7):
            self.turn_own(a, kind == 6)
        else:
            self.close_own(a)


def gather_up(vectors, target):
    shards = PLANE * LINE * 2
    total = None
    for row in sorted({v[0] for v in vectors}):
        share = jnp.zeros((shards, 128), F32)
        for at, lane, size, source in vectors:
            if at != row:
                continue
            step = 1024

            def body(i, carry):
                cut = pl.ds(pl.multiple_of(i * step, step), step)
                column = (lax.broadcasted_iota(jnp.int32, (1, step), 1) + i * step).astype(F32)
                shard = jnp.floor((column + 0.5) * (1.0 / size))
                lane_of = (column - shard * size + lane).astype(jnp.int32)
                spread = lax.broadcasted_iota(jnp.int32, (128, step), 0) == lane_of
                keep = lax.broadcasted_iota(jnp.int32, (shards, step), 0) == shard.astype(jnp.int32)
                value = jnp.where(keep, source[:, cut], 0.0).astype(BF16)
                return carry + dot_columns(value, spread.astype(F32).astype(BF16))

            share = lax.fori_loop(0, shards * size // step, body, share)
        pick_rows = lax.broadcasted_iota(jnp.int32, (shards, shards * 32), 0) * 32 + row
        pick = lax.broadcasted_iota(jnp.int32, (shards, shards * 32), 1) == pick_rows
        part = contract_rows(pick.astype(F32).astype(BF16), share.astype(BF16))
        total = part if total is None else total + part
    target[...] = total.astype(BF16).reshape(target.shape)


def backward_kernel(*refs):
    (
        act_hbm, down_grad_hbm, hidden_hbm, up_grad_hbm, context_hbm, branch_grad_hbm, result_hbm,
        embed_cot_hbm, token_hbm, qkv_hbm, far_hbm, context_grad_hbm, first_grad_hbm, weight_hbm,
        norm, segs, sums, cosine, sine, shift,
    ), refs = refs[:20], refs[20:]
    outs, token_in, refs = refs[:5], refs[5], refs[6:]
    (send_d, send_u, send_s), refs = refs[:3], refs[3:]
    helds, halves, wholes, lines = [refs[i * 5 : (i + 1) * 5] for i in range(4)]
    (
        rings, own_half, own_whole,
        act, down_grad, up_grad, branch_grad, embed_cot, raw, turned_a, turned_b, qkv, far,
        far_back, context_grad, seg_near, seg_far, vectors, shares, token_out,
        send_sems, recv_sems, local_sems,
    ) = refs[20:]
    g, x, y, z, c = place()
    partner = (g, z * 2 + 1 - c)
    rows, width = branch_grad.shape
    ff = act.shape[1]
    sender = Sender(send_sems, recv_sems)
    spare = 5 * REDUCE_SEMS

    def load(source, target, index):
        copy = lambda: pltpu.make_async_copy(source, target, local_sems.at[index])
        copy().start()
        return lambda: copy().wait()

    wait_act = load(act_hbm, act, 0)
    wait_down = load(down_grad_hbm, down_grad, 1)
    wait_raw = load(hidden_hbm, raw, 2)
    wait_up = load(up_grad_hbm, up_grad, 3)
    wait_branch = load(branch_grad_hbm, branch_grad, 4)
    wait_embed = load(embed_cot_hbm, embed_cot, 5)
    wait_qkv = load(qkv_hbm, qkv, 6)
    wait_far = load(far_hbm, far, 7)
    wait_grad = load(context_grad_hbm, context_grad, 8)
    entry_barrier()

    def turn_over(target):
        for j in range(width // 128):
            block = jnp.transpose(flat(raw[:, :, j * 128 : (j + 1) * 128]))
            target[j // 2, (j % 2) * 2 : (j % 2) * 2 + 2] = block.reshape(2, 2, 32, rows)

    def product_of(turned, right):
        columns = right.shape[1]
        step = min(columns, 512)

        def act_on(parity, zs, targets, added):
            left = jnp.concatenate([flat(turned[:, zi, parity]) for zi in zs], axis=0)

            def body(i, carry):
                cut = pl.ds(pl.multiple_of(i * step, step), step)
                value = dot_rows(left, right[:, cut]).reshape(2, PLANE, 32, step)
                for j, target in enumerate(targets):
                    part = value[j]
                    if added:
                        part = part + target[:, :, cut].astype(F32)
                    target[:, :, cut] = part.astype(BF16)
                return carry

            lax.fori_loop(0, columns // step, body, 0)

        return act_on

    def down_product(parity, zs, targets, added):
        def body(j, carry):
            pieces = []
            for zi in zs:
                at = ((j * LINE + zi) * 2 + parity) * 128
                pieces.append(act[:, pl.ds(pl.multiple_of(at, 128), 128)])
            value = contract_rows(jnp.concatenate(pieces, axis=1), down_grad[...])
            for i, target in enumerate(targets):
                part = value[i * 128 : (i + 1) * 128]
                if added:
                    part = part + target[j].astype(F32)
                target[j] = part.astype(BF16)
            return carry

        lax.fori_loop(0, PLANE, body, 0)

    def share_product(parity, zs, targets, added):
        for zi, target in zip(zs, targets):
            value = shares[:, zi, parity]
            if added:
                value = (value.astype(F32) + target[...].astype(F32)).astype(BF16)
            target[...] = value

    shared = lambda columns: send_u.at[:, :, :, 0:columns]
    sends = (send_d, send_u, shared(width), shared(3 * width), send_s)
    products = [
        down_product,
        product_of(turned_a, up_grad),
        product_of(turned_b, branch_grad),
        product_of(turned_a, qkv),
        share_product,
    ]
    arrays = [
        SimpleNamespace(product=p, send=s, held=h, half=i, whole=w, line=l, out=o, low=0)
        for p, s, h, i, w, l, o in zip(products, sends, helds, halves, wholes, lines, outs)
    ]
    arrays[3].low, arrays[3].rings = rings.shape[3], rings
    arrays[3].own_half, arrays[3].own_whole = own_half, own_whole
    plan = Reduce(arrays, sender)
    token_back = Exchange([raw], [token_in], False, sender, spare + 2, local_sems, 18)
    parts, tile = 3 * width // 512, 512

    def fetch(t, begin):
        for r in range(2):
            at = ((t % 4) * 2 + r) * tile
            copy = pltpu.make_async_copy(
                weight_hbm.at[r * rows : (r + 1) * rows, t * tile : (t + 1) * tile],
                act.at[:, at : at + tile],
                local_sems.at[10 + (t % 4) * 2 + r],
            )
            copy.start() if begin else copy.wait()

    def fetched(t):
        fetch(t, False)
        for r in range(2):
            at = ((t % 4) * 2 + r) * tile
            half = token_out[:, r * tile : (r + 1) * tile]
            token_out[:, r * tile : (r + 1) * tile] = half + dot_columns(
                qkv[:, t * tile : (t + 1) * tile], act[:, at : at + tile]
            )
        if t + 4 < parts:
            fetch(t + 4, True)

    def turn_hidden():
        wait_raw()
        turn_over(turned_a)
        load(context_hbm, raw, 2)

    def turn_context():
        wait_raw()
        turn_over(turned_b)
        load(result_hbm, raw, 2)

    def embed_share():
        wait_raw()
        wait_embed()
        value = contract_rows(flat(raw[...]), embed_cot[...]).astype(BF16)
        shares[:, :, :, 0:32, :] = value.reshape(PLANE, LINE, 2, 32, 128)
        load(token_hbm, raw, 2)

    def before_attention():
        wait_qkv()
        wait_far()
        wait_grad()
        seg_near[...] = jnp.transpose(jnp.broadcast_to(segs[0:1, :], (128, rows)))
        seg_far[...] = jnp.transpose(jnp.broadcast_to(segs[1:2, :], (128, rows)))

    def turn_tokens():
        wait_raw()
        turn_over(turned_a)
        for t in range(4):
            fetch(t, True)

    def finish_tile(i):
        cut = pl.ds(pl.multiple_of(i * tile, tile), tile)

        @pl.when(i >= 2)
        def _():
            other = pl.ds(pl.multiple_of(jnp.maximum(i - 2, 0) * tile, tile), tile)
            qkv[:, cut] = (qkv[:, cut].astype(F32) + far_back[:, other].astype(F32)).astype(BF16)

        vectors[0:1, cut] = jnp.sum(qkv[:, cut].astype(F32), axis=0, keepdims=True)

    def other_shares():
        source = lambda i, size: (vectors if i == 0 else sums).at[i : i + 1, 0:size]
        gather_up(
            (
                (0, 0, 96, source(0, 3 * width)),
                (1, 0, 128, source(1, ff)),
                (2, 0, 32, source(2, width)),
                (2, 32, 32, source(3, width)),
                (2, 64, 32, source(4, width)),
                (2, 96, 32, source(5, width)),
                (3, 0, 32, source(6, width)),
                (3, 32, 32, source(7, width)),
            ),
            shares.at[:, :, :, 32:64, :],
        )

    def round_tokens():
        for i in range(2):
            raw[i] = token_out[i * (rows // 2) : (i + 1) * (rows // 2), :].astype(BF16)

    def attend_one(i):
        at = pl.multiple_of(i * 128, 128)
        cut = lambda ref, base: ref.at[:, pl.ds(base + at, 128)]
        attend_back_pair(
            cut(qkv, 0), cut(qkv, width), cut(qkv, 2 * width), cut(far, 0), cut(far, width),
            cut(context_grad, 0), norm.at[i], segs.at[0:1], seg_near, seg_far,
            (cosine, sine, shift), [token_out.at[:, j * 128 : (j + 1) * 128] for j in range(4)],
        )

    first_copy = pltpu.make_async_copy(first_grad_hbm, token_out, local_sems.at[9])
    others = {
        900: lambda: (wait_act(), wait_down()),
        901: lambda: (turn_hidden(), wait_up()),
        902: lambda: (turn_context(), wait_branch()),
        903: embed_share,
        904: turn_tokens,
        905: lambda: lax.fori_loop(0, parts, lambda i, carry: (finish_tile(i), carry)[1], 0),
        906: other_shares,
        907: round_tokens,
        908: lambda: None,
        909: lambda: sender.land(far_back, spare, partner),
        910: token_back.arrive,
        930: first_copy.wait,
    }
    for t in range(parts):
        others[920 + t] = lambda t=t: fetched(t)

    def perform(steps):
        def act_on():
            for step in steps:
                if step == 911:
                    sender.do(True, first_copy.start)
                    sender.send(True, far, far_back, spare, partner)
                elif step == 912:
                    for link in (5, 2, 3):
                        token_back.step(link)
                elif step >= 900:
                    if not sender.draining:
                        others[step]()
                else:
                    plan.step(step)

        return act_on

    first, middle, last = BACKWARD_STEPS
    ticks = [perform(steps) for steps in (first,) + middle + (last,)]
    ticks[0]()
    before_attention()
    run_with(ticks[1:-1], width // 128, attend_one)
    ticks[-1]()
    sender.drain(ticks)


def backward(operands, small_operands, shapes, rows, width, ff, lanes):
    shape = jax.ShapeDtypeStruct
    semaphores = 5 * REDUCE_SEMS + 16
    ring = (shapes[3][0], shapes[3][1] // 2)
    buffers = [pltpu.VMEM((2, PLANE) + shapes[i], BF16) for i in (0, 1, 4)]
    apart = shapes[:3] + [ring] + shapes[4:]
    buffers += [pltpu.VMEM((LINE, PLANE) + s, BF16) for s in shapes]
    for lead in ((LINE,), (LINE, 2), (LINE + 1,)):
        buffers += [pltpu.VMEM(lead + s, BF16) for s in apart]
    turned = pltpu.VMEM((PLANE, LINE, 2, 32, rows), BF16)
    piece = rows // 2
    scratch = buffers + [
        pltpu.VMEM((LINE + 1, PLANE) + ring, BF16),
        pltpu.VMEM(ring, BF16),
        pltpu.VMEM((2,) + ring, BF16),
        pltpu.VMEM((rows, ff), BF16),
        pltpu.VMEM((rows, width), BF16),
        pltpu.VMEM((rows, ff), BF16),
        pltpu.VMEM((rows, width), BF16),
        pltpu.VMEM((rows, lanes), BF16),
        pltpu.VMEM((2, piece, width), BF16),
        turned,
        turned,
        pltpu.VMEM((rows, 3 * width), BF16),
        pltpu.VMEM((rows, 2 * width), BF16),
        pltpu.VMEM((rows, 2 * width), BF16),
        pltpu.VMEM((rows, width), BF16),
        pltpu.VMEM((rows, 128), F32),
        pltpu.VMEM((rows, 128), F32),
        pltpu.VMEM((1, 3 * width), F32),
        pltpu.VMEM((PLANE, LINE, 2, 64, 128), BF16),
        pltpu.VMEM((rows, width), F32),
        pltpu.SemaphoreType.DMA((semaphores,)),
        pltpu.SemaphoreType.DMA((semaphores,)),
        pltpu.SemaphoreType.DMA((20,)),
    ]
    results = pl.pallas_call(
        backward_kernel,
        out_shape=[shape(s, F32) for s in shapes] + [shape((2, piece, width), BF16)],
        in_specs=[hbm()] * len(operands) + [vmem()] * len(small_operands),
        out_specs=[vmem()] * 6,
        scratch_shapes=scratch,
        compiler_params=pltpu.CompilerParams(
            collective_id=2, has_side_effects=True, vmem_limit_bytes=67043328
        ),
        name="backward",
    )(*operands, *small_operands)
    return (results[:5], results[5])


def pair_tables(positions):
    lanes = lax.broadcasted_iota(jnp.int32, (positions.shape[0], 2 * HEAD_DIM), 1)
    place_in_half = lax.rem(lanes, HEAD_DIM // 2).astype(F32)
    angles = positions[:, None] * 10000.0 ** (-place_in_half * (2.0 / HEAD_DIM))
    return (jnp.cos(angles), jnp.sin(angles))


def deliver_kernel(count, vectors, *refs):
    sources, small, token, refs = refs[:count], refs[count], refs[count + 1], refs[count + 2 :]
    targets, small_out, token_out, refs = (
        refs[:count], refs[count : count + 1 + len(vectors)], refs[count + 1 + len(vectors)],
        refs[count + 2 + len(vectors) :],
    )
    held, sems = refs[:count], refs[count]
    inward = [
        pltpu.make_async_copy(s, h, sems.at[i]) for i, (s, h) in enumerate(zip(sources, held))
    ]
    outward = [
        pltpu.make_async_copy(h, t, sems.at[count + i])
        for i, (h, t) in enumerate(zip(held, targets))
    ]
    for copy in inward:
        copy.start()
    small_out[0][...] = small[: small_out[0].shape[0], :]
    top = small_out[0].shape[0]
    for target, (row, lane, size) in zip(small_out[1:], vectors):
        target[...] = small[top + row : top + row + 1, lane : lane + size]
    token_out[...] = token[...].astype(F32)
    for arrived, leave in zip(inward, outward):
        arrived.wait()
        leave.start()
    for copy in outward:
        copy.wait()


def deliver(arrays, small, token, embed_rows, vectors):
    shape = jax.ShapeDtypeStruct
    count = len(arrays)
    outs = [shape(a.shape, a.dtype) for a in arrays]
    outs += [shape((embed_rows, small.shape[1]), F32)]
    outs += [shape((1, size), F32) for row, lane, size in vectors]
    outs += [shape(token.shape, F32)]
    results = pl.pallas_call(
        functools.partial(deliver_kernel, count, vectors),
        out_shape=outs,
        in_specs=[hbm()] * count + [vmem()] * 2,
        out_specs=[hbm()] * count + [vmem()] * (2 + len(vectors)),
        scratch_shapes=[pltpu.VMEM(a.shape, a.dtype) for a in arrays]
        + [pltpu.SemaphoreType.DMA((2 * count,))],
        compiler_params=pltpu.CompilerParams(vmem_limit_bytes=67043328),
        name="deliver",
    )(*arrays, small, token)
    middle = [r.reshape(-1) for r in results[count + 1 : -1]]
    return (results[:count], results[count], middle, results[-1])


def plane_device(
    tokens,
    segment_ids,
    project_weight,
    project_bias,
    output_weight,
    output_bias,
    first_gain,
    first_shift,
    up_weight,
    up_bias,
    down_weight,
    down_bias,
    second_gain,
    second_shift,
    embed_weight,
    out_cotangent,
    embed_cotangent,
):
    width = HEADS * HEAD_DIM
    piece = tokens.shape[2]
    rows = 2 * piece
    group = lax.axis_index("group")
    core = lax.rem(lax.axis_index("wide"), 2)
    lanes = embed_weight.shape[1]
    embed_rows = embed_weight.shape[0]
    small = None
    for row, lane, vector in (
        (0, 0, project_bias),
        (1, 0, up_bias),
        (2, 0, output_bias),
        (2, 32, first_gain),
        (2, 64, first_shift),
        (2, 96, down_bias),
        (3, 0, second_gain),
        (3, 32, second_shift),
    ):
        size = vector.shape[0]
        part = jnp.pad(
            vector.astype(F32)[None, :], ((row, 31 - row), (lane, lanes - lane - size))
        )
        small = part if small is None else small + part
    place_of = jnp.arange(rows)
    cosine, sine = pair_tables((core * rows + place_of).astype(F32))
    step_cosine, step_sine = pair_tables(jnp.full((1,), rows, F32))
    step_sine = step_sine * (1 - 2 * core).astype(F32)
    shift = jnp.concatenate([step_cosine, step_sine] + [jnp.zeros_like(step_sine)] * 6)
    (
        project_full, token_rows, qkv, far_kv, context_low, norms, hidden_low, act_low, up_grad,
        down_grad, result_low, embed_cot, branch_grad, context_grad, first_grad, sums, ids,
        layer_out, embed_out,
    ) = forward(
        [project_weight, embed_weight, small.astype(BF16), output_weight, up_weight, down_weight],
        [tokens[:, 0], out_cotangent[:, 0], embed_cotangent[:, 0]],
        segment_ids,
        (cosine, sine),
        up_weight.shape[1],
    )
    shapes = [
        down_weight.shape,
        up_weight.shape,
        output_weight.shape,
        project_weight.shape,
        (embed_rows + small.shape[0], lanes),
    ]
    outs, token_low = backward(
        (
            act_low, down_grad, hidden_low.reshape(2, piece, width), up_grad,
            context_low.reshape(2, piece, width), branch_grad, result_low,
            embed_cot.reshape(rows, lanes), token_rows, qkv, far_kv, context_grad, first_grad,
            project_full.reshape(width, 3 * width),
        ),
        (norms, ids, sums, cosine, sine, shift),
        shapes,
        rows,
        width,
        up_weight.shape[1],
        lanes,
    )
    vectors = (
        (0, 0, 96), (2, 0, 32), (2, 32, 32), (2, 64, 32), (1, 0, 128), (2, 96, 32), (3, 0, 32), (3, 32, 32),
    )
    arrays, embed_grad, parts, token_grad = deliver(
        (layer_out, embed_out) + tuple(outs[:4]), outs[4], token_low, embed_rows, vectors
    )
    return (
        arrays[0][:, None],
        arrays[1][:, None],
        token_grad[:, None],
        arrays[5],
        parts[0],
        arrays[4],
        parts[1],
        parts[2],
        parts[3],
        arrays[3],
        parts[4],
        arrays[2],
        parts[5],
        parts[6],
        parts[7],
        embed_grad,
    )


def choose_device(mesh):
    if mesh.shape["group"] == PLANE and mesh.shape["wide"] == 2 * LINE:
        return plane_device
    return general_device


def solution(mesh):
    in_specs = (
        P(None, "wide", "group", None),
        P(None, "wide", None),
        P(("group", "wide"), None),
        P(("group", "wide")),
        P(("group", "wide"), None),
        P(("group", "wide")),
        P(("group", "wide")),
        P(("group", "wide")),
        P(("group", "wide"), None),
        P(("group", "wide")),
        P(("group", "wide"), None),
        P(("group", "wide")),
        P(("group", "wide")),
        P(("group", "wide")),
        P(("group", "wide"), None),
        P(None, "wide", "group", None),
        P(None, "wide", "group", None),
    )
    out_specs = (
        P(None, "wide", "group", None),
        P(None, "wide", "group", None),
        P(None, "wide", "group", None),
        P(("group", "wide"), None),
        P(("group", "wide")),
        P(("group", "wide"), None),
        P(("group", "wide")),
        P(("group", "wide")),
        P(("group", "wide")),
        P(("group", "wide"), None),
        P(("group", "wide")),
        P(("group", "wide"), None),
        P(("group", "wide")),
        P(("group", "wide")),
        P(("group", "wide")),
        P(("group", "wide"), None),
    )
    return jax.shard_map(
        choose_device(mesh), mesh=mesh, in_specs=in_specs, out_specs=out_specs, check_vma=False
    )
```

```python
import functools
from types import SimpleNamespace

import jax
import jax.numpy as jnp
from jax import lax
from jax.experimental import pallas as pl
from jax.experimental.pallas import tpu as pltpu
from jax.sharding import PartitionSpec as P

HEADS = 16
HEAD_DIM = 64


eps_norm = 1e-05
neg_large = -1e30


def rotary_tables(positions):
    half_dim = HEAD_DIM // 2
    frequency = 10000.0 ** (-jnp.arange(half_dim, dtype=jnp.float32) * (2.0 / HEAD_DIM))
    angles = positions[:, None] * frequency[None, :]
    angles = jnp.concatenate([angles, angles], axis=1)
    return (jnp.cos(angles), jnp.sin(angles))


def rotate(values, cosine_table, sine_table):
    half_dim = HEAD_DIM // 2
    swapped = jnp.concatenate([-values[..., half_dim:], values[..., :half_dim]], axis=-1)
    return values * cosine_table[:, None, :] + swapped * sine_table[:, None, :]


def unrotate(grads, cosine_table, sine_table):
    half_dim = HEAD_DIM // 2
    scaled = grads * sine_table[:, None, :]
    swapped = jnp.concatenate([scaled[..., half_dim:], -scaled[..., :half_dim]], axis=-1)
    return grads * cosine_table[:, None, :] + swapped


def norm_forward(resid, gain, shift):
    center = resid - jnp.mean(resid, axis=-1, keepdims=True)
    spread = jnp.mean(center * center, axis=-1, keepdims=True)
    rstd_rows = lax.rsqrt(spread + eps_norm)
    normed = center * rstd_rows
    return (normed * gain + shift, normed, rstd_rows)


def norm_backward(grads, normed, rstd_rows, gain):
    scaled = grads * gain
    resid_grad = rstd_rows * (
        scaled
        - jnp.mean(scaled, axis=-1, keepdims=True)
        - normed * jnp.mean(scaled * normed, axis=-1, keepdims=True)
    )
    return (resid_grad, jnp.sum(grads * normed, axis=0), jnp.sum(grads, axis=0))


def contract_rows(left, right):
    return lax.dot_general(
        left, right, (((0,), (0,)), ((), ())), preferred_element_type=jnp.float32
    )


def times_transpose(left, right):
    return lax.dot_general(
        left, right, (((1,), (1,)), ((), ())), preferred_element_type=jnp.float32
    )


def gelu_slope(value):
    normal_cdf = 0.5 * (1.0 + lax.erf(value * 0.7071067811865476))
    density = jnp.exp(-0.5 * value * value) * 0.3989422804014327
    return normal_cdf + value * density


def key_blocks(kv_rows, seg_all):
    seq_len = kv_rows.shape[0]
    block_rows = min(512, seq_len)
    count = seq_len // block_rows
    return (
        kv_rows.reshape(count, block_rows, 2, HEADS, HEAD_DIM),
        seg_all.reshape(count, block_rows),
    )


def block_scores(queries, key_block, same):
    scores = jnp.einsum("qhd,khd->hqk", queries, key_block, preferred_element_type=jnp.float32)
    scores = scores * HEAD_DIM ** (-0.5)
    return jnp.where(same[None], scores, neg_large)


def attention_forward(queries, blocks, seg_blocks, seg_local):
    length = queries.shape[0]

    def norm_step(carry, pieces):
        kv_block, seg_block = pieces
        same = seg_local[:, None] == seg_block[None, :]

        def norm_update(running):
            run_max, run_sum = running
            scores = block_scores(queries, kv_block[:, 0], same)
            new_max = jnp.maximum(run_max, jnp.max(scores, axis=-1))
            new_sum = run_sum * jnp.exp(run_max - new_max) + jnp.sum(
                jnp.exp(scores - new_max[..., None]), axis=-1
            )
            return (new_max, new_sum)

        def norm_unchanged(running):
            return running

        return (lax.cond(jnp.any(same), norm_update, norm_unchanged, carry), None)

    start = (
        jnp.full((HEADS, length), neg_large, jnp.float32),
        jnp.zeros((HEADS, length), jnp.float32),
    )
    (run_max, run_sum), unused = lax.scan(norm_step, start, (blocks, seg_blocks))
    log_norm = run_max + jnp.log(run_sum)

    def value_step(total, pieces):
        kv_block, seg_block = pieces
        same = seg_local[:, None] == seg_block[None, :]

        def value_update(running):
            scores = block_scores(queries, kv_block[:, 0], same)
            weights = jnp.exp(scores - log_norm[..., None]).astype(jnp.bfloat16)
            return running + jnp.einsum(
                "hqk,khd->qhd", weights, kv_block[:, 1], preferred_element_type=jnp.float32
            )

        def value_unchanged(running):
            return running

        return (lax.cond(jnp.any(same), value_update, value_unchanged, total), None)

    context, unused = lax.scan(
        value_step, jnp.zeros(queries.shape, jnp.float32), (blocks, seg_blocks)
    )
    return (context, log_norm)


def attention_backward(queries, blocks, seg_blocks, seg_local, log_norm, context_grad, delta):

    def grad_step(query_grad, pieces):
        kv_block, seg_block = pieces
        same = seg_local[:, None] == seg_block[None, :]

        def work(running):
            scores = block_scores(queries, kv_block[:, 0], same)
            probs = jnp.exp(scores - log_norm[..., None])
            prob_grad = jnp.einsum(
                "qhd,khd->hqk", context_grad, kv_block[:, 1], preferred_element_type=jnp.float32
            )
            score_grad = (probs * (prob_grad - delta[..., None])).astype(jnp.bfloat16)
            running = running + jnp.einsum(
                "hqk,khd->qhd", score_grad, kv_block[:, 0], preferred_element_type=jnp.float32
            ) * HEAD_DIM ** (-0.5)
            prob_low = probs.astype(jnp.bfloat16)
            key_grad = jnp.einsum(
                "hqk,qhd->khd", score_grad, queries, preferred_element_type=jnp.float32
            ) * HEAD_DIM ** (-0.5)
            value_grad = jnp.einsum(
                "hqk,qhd->khd", prob_low, context_grad, preferred_element_type=jnp.float32
            )
            return (running, jnp.stack([key_grad, value_grad], axis=1))

        def skipped(running):
            return (running, jnp.zeros(kv_block.shape, jnp.float32))

        return lax.cond(jnp.any(same), work, skipped, query_grad)

    query_grad, kv_grad = lax.scan(
        grad_step, jnp.zeros(queries.shape, jnp.float32), (blocks, seg_blocks)
    )
    return (query_grad, kv_grad.reshape(-1, 2 * HEADS * HEAD_DIM))


def general_device(
    tokens,
    segment_ids,
    project_weight,
    project_bias,
    output_weight,
    output_bias,
    first_gain,
    first_shift,
    up_weight,
    up_bias,
    down_weight,
    down_bias,
    second_gain,
    second_shift,
    embed_weight,
    out_cotangent,
    embed_cotangent,
):
    shards = (
        project_weight,
        project_bias,
        output_weight,
        output_bias,
        first_gain,
        first_shift,
        up_weight,
        up_bias,
        down_weight,
        down_bias,
        second_gain,
        second_shift,
        embed_weight,
    )
    length = tokens.shape[2]
    width = HEADS * HEAD_DIM
    head_shape = (length, HEADS, HEAD_DIM)
    place = lax.axis_index("group")
    positions = (place * length + jnp.arange(length)).astype(jnp.float32)
    cosine_table, sine_table = rotary_tables(positions)
    grad_total = None
    results = []
    embeddings = []
    input_grads = []
    for micro_index in range(tokens.shape[0]):
        params = (
            lax.all_gather(shards[0], ("group", "wide"), axis=0, tiled=True),
            lax.all_gather(shards[1], ("group", "wide"), axis=0, tiled=True),
            lax.all_gather(shards[2], ("group", "wide"), axis=0, tiled=True),
            lax.all_gather(shards[3], ("group", "wide"), axis=0, tiled=True),
            lax.all_gather(shards[4], ("group", "wide"), axis=0, tiled=True),
            lax.all_gather(shards[5], ("group", "wide"), axis=0, tiled=True),
            lax.all_gather(shards[6], ("group", "wide"), axis=0, tiled=True),
            lax.all_gather(shards[7], ("group", "wide"), axis=0, tiled=True),
            lax.all_gather(shards[8], ("group", "wide"), axis=0, tiled=True),
            lax.all_gather(shards[9], ("group", "wide"), axis=0, tiled=True),
            lax.all_gather(shards[10], ("group", "wide"), axis=0, tiled=True),
            lax.all_gather(shards[11], ("group", "wide"), axis=0, tiled=True),
            lax.all_gather(shards[12], ("group", "wide"), axis=0, tiled=True),
        )
        seg_all = segment_ids[micro_index, 0]
        seg_local = lax.dynamic_slice_in_dim(seg_all, place * length, length)
        token_low = tokens[micro_index, 0]
        token_wide = token_low.astype(jnp.float32)
        projected = jnp.dot(token_low, params[0], preferred_element_type=jnp.float32) + params[
            1
        ].astype(jnp.float32)
        queries = rotate(projected[:, :width].reshape(head_shape), cosine_table, sine_table).astype(
            jnp.bfloat16
        )
        key_rows = rotate(
            projected[:, width : 2 * width].reshape(head_shape), cosine_table, sine_table
        ).astype(jnp.bfloat16)
        value_rows = projected[:, 2 * width :].astype(jnp.bfloat16)
        local_kv = jnp.concatenate([key_rows.reshape(length, width), value_rows], axis=1)
        kv_all = lax.all_gather(local_kv, "group", axis=0, tiled=True)
        blocks, seg_blocks = key_blocks(kv_all, seg_all)
        context, log_norm = attention_forward(queries, blocks, seg_blocks, seg_local)
        context_low = context.reshape(length, width).astype(jnp.bfloat16)
        branch = jnp.dot(context_low, params[2], preferred_element_type=jnp.float32) + params[
            3
        ].astype(jnp.float32)
        first_gain_wide = params[4].astype(jnp.float32)
        hidden, first_normed, first_rstd = norm_forward(
            token_wide + branch, first_gain_wide, params[5].astype(jnp.float32)
        )
        hidden_low = hidden.astype(jnp.bfloat16)
        up_value = jnp.dot(hidden_low, params[6], preferred_element_type=jnp.float32) + params[
            7
        ].astype(jnp.float32)
        act_low = jax.nn.gelu(up_value, approximate=False).astype(jnp.bfloat16)
        down_value = jnp.dot(act_low, params[8], preferred_element_type=jnp.float32) + params[
            9
        ].astype(jnp.float32)
        second_gain_wide = params[10].astype(jnp.float32)
        result, second_normed, second_rstd = norm_forward(
            hidden + down_value, second_gain_wide, params[11].astype(jnp.float32)
        )
        result_low = result.astype(jnp.bfloat16)
        embedded = jnp.dot(result_low, params[12], preferred_element_type=jnp.float32)
        results.append(result_low)
        embeddings.append(embedded.astype(jnp.bfloat16))
        params = (
            lax.all_gather(shards[0], ("group", "wide"), axis=0, tiled=True),
            lax.all_gather(shards[1], ("group", "wide"), axis=0, tiled=True),
            lax.all_gather(shards[2], ("group", "wide"), axis=0, tiled=True),
            lax.all_gather(shards[3], ("group", "wide"), axis=0, tiled=True),
            lax.all_gather(shards[4], ("group", "wide"), axis=0, tiled=True),
            lax.all_gather(shards[5], ("group", "wide"), axis=0, tiled=True),
            lax.all_gather(shards[6], ("group", "wide"), axis=0, tiled=True),
            lax.all_gather(shards[7], ("group", "wide"), axis=0, tiled=True),
            lax.all_gather(shards[8], ("group", "wide"), axis=0, tiled=True),
            lax.all_gather(shards[9], ("group", "wide"), axis=0, tiled=True),
            lax.all_gather(shards[10], ("group", "wide"), axis=0, tiled=True),
            lax.all_gather(shards[11], ("group", "wide"), axis=0, tiled=True),
            lax.all_gather(shards[12], ("group", "wide"), axis=0, tiled=True),
        )
        embed_cot = embed_cotangent[micro_index, 0]
        result_grad = out_cotangent[micro_index, 0].astype(jnp.float32) + times_transpose(
            embed_cot, params[12]
        )
        embed_weight_grad = contract_rows(result_low, embed_cot)
        sum_grad, second_gain_grad, second_shift_grad = norm_backward(
            result_grad, second_normed, second_rstd, second_gain_wide
        )
        down_grad = sum_grad.astype(jnp.bfloat16)
        down_bias_grad = jnp.sum(down_grad.astype(jnp.float32), axis=0)
        down_weight_grad = contract_rows(act_low, down_grad)
        up_grad = (times_transpose(down_grad, params[8]) * gelu_slope(up_value)).astype(
            jnp.bfloat16
        )
        up_bias_grad = jnp.sum(up_grad.astype(jnp.float32), axis=0)
        up_weight_grad = contract_rows(hidden_low, up_grad)
        hidden_grad = sum_grad + times_transpose(up_grad, params[6])
        first_grad, first_gain_grad, first_shift_grad = norm_backward(
            hidden_grad, first_normed, first_rstd, first_gain_wide
        )
        branch_grad = first_grad.astype(jnp.bfloat16)
        output_bias_grad = jnp.sum(branch_grad.astype(jnp.float32), axis=0)
        output_weight_grad = contract_rows(context_low, branch_grad)
        context_grad = (
            times_transpose(branch_grad, params[2]).astype(jnp.bfloat16).reshape(head_shape)
        )
        delta = jnp.transpose(jnp.sum(context_grad.astype(jnp.float32) * context, axis=-1))
        kv_again = lax.all_gather(local_kv, "group", axis=0, tiled=True)
        blocks, seg_blocks = key_blocks(kv_again, seg_all)
        query_grad, kv_partial = attention_backward(
            queries, blocks, seg_blocks, seg_local, log_norm, context_grad, delta
        )
        kv_grad = lax.psum_scatter(
            kv_partial.astype(jnp.bfloat16), "group", scatter_dimension=0, tiled=True
        ).astype(jnp.float32)
        key_part = kv_grad[:, :width].reshape(head_shape)
        value_part = kv_grad[:, width:]
        query_back = unrotate(query_grad, cosine_table, sine_table).reshape(length, width)
        key_back = unrotate(key_part, cosine_table, sine_table).reshape(length, width)
        projected_grad = jnp.concatenate([query_back, key_back, value_part], axis=1).astype(
            jnp.bfloat16
        )
        project_bias_grad = jnp.sum(projected_grad.astype(jnp.float32), axis=0)
        project_weight_grad = contract_rows(token_low, projected_grad)
        input_grads.append(first_grad + times_transpose(projected_grad, params[0]))
        local_grads = (
            project_weight_grad,
            project_bias_grad,
            output_weight_grad,
            output_bias_grad,
            first_gain_grad,
            first_shift_grad,
            up_weight_grad,
            up_bias_grad,
            down_weight_grad,
            down_bias_grad,
            second_gain_grad,
            second_shift_grad,
            embed_weight_grad,
        )
        summed = (
            lax.psum_scatter(local_grads[0], ("group", "wide"), scatter_dimension=0, tiled=True),
            lax.psum_scatter(local_grads[1], ("group", "wide"), scatter_dimension=0, tiled=True),
            lax.psum_scatter(local_grads[2], ("group", "wide"), scatter_dimension=0, tiled=True),
            lax.psum_scatter(local_grads[3], ("group", "wide"), scatter_dimension=0, tiled=True),
            lax.psum_scatter(local_grads[4], ("group", "wide"), scatter_dimension=0, tiled=True),
            lax.psum_scatter(local_grads[5], ("group", "wide"), scatter_dimension=0, tiled=True),
            lax.psum_scatter(local_grads[6], ("group", "wide"), scatter_dimension=0, tiled=True),
            lax.psum_scatter(local_grads[7], ("group", "wide"), scatter_dimension=0, tiled=True),
            lax.psum_scatter(local_grads[8], ("group", "wide"), scatter_dimension=0, tiled=True),
            lax.psum_scatter(local_grads[9], ("group", "wide"), scatter_dimension=0, tiled=True),
            lax.psum_scatter(local_grads[10], ("group", "wide"), scatter_dimension=0, tiled=True),
            lax.psum_scatter(local_grads[11], ("group", "wide"), scatter_dimension=0, tiled=True),
            lax.psum_scatter(local_grads[12], ("group", "wide"), scatter_dimension=0, tiled=True),
        )
        grad_total = (
            summed
            if grad_total is None
            else tuple((total + part for total, part in zip(grad_total, summed)))
        )
    layer_out = jnp.stack(results)[:, None]
    embed_out = jnp.stack(embeddings)[:, None]
    token_grad = jnp.stack(input_grads)[:, None]
    return (
        layer_out,
        embed_out,
        token_grad,
        grad_total[0],
        grad_total[1],
        grad_total[2],
        grad_total[3],
        grad_total[4],
        grad_total[5],
        grad_total[6],
        grad_total[7],
        grad_total[8],
        grad_total[9],
        grad_total[10],
        grad_total[11],
        grad_total[12],
    )


MESH = pl.DeviceIdType.MESH
F32 = jnp.float32
BF16 = jnp.bfloat16
PLANE = 4
LINE = 4
GATHER_SEMS = 42
REDUCE_SEMS = 42
CORE, UPPER, LOWER, ROW, COLUMN, ARRIVED, HOP = 0, 4, 8, 12, 16, 20, 25
OWN_UPPER, OWN_LOWER, OWN_ROW, OWN_COLUMN, RING_ARRIVED, RING_HOP = 29, 30, 31, 32, 33, 38
PACKED_AT = ((0, 0), (1, 0), (2, 0), (2, 32), (2, 64), (2, 96), (3, 0), (3, 32))
FORWARD_PARTS = ((True, ((0, 0, 4, 0, 2, ), (1, 0, 4, 0, 4, ), (2, 0, 4, 0, 4, ), ), ), (False, ((0, 0, 4, 2, 4, ), ), ), (True, ((3, 0, 4, 0, 4, ), ), ), (True, ((4, 0, 4, 0, 4, ), ), ), (False, ((5, 0, 2, 0, 4, ), ), ), (True, ((5, 2, 4, 0, 4, ), ), ), )
FORWARD_STEPS = (((1003, 1, 1002, 20005, 2001, 0, 3, 2, 2000, 3001, 41, 1202, 10, 12, 4002, 42, 1103, 2041, 23, 2010, 2003, 3000, 2012, 20003, 1401, 3003, 2023, 51, 3041, 20, 2043, 1404, 2020, 20002, 52, 33, 1400, 53, 43, 113, 2013, 2033, 2052, 2032, 32, 3012, 1410, 1441, 4003, 222, 62, 202, 2042, 3010, 153, 2212, 143, 3002, 103, 2222, 4103, 63, 22, 133, 242, 252, 1424, 1451, 2051, 2002, 232, 3051, 2113, 4202, 1420, 262, 2232, 2133, 1414, 13, 2143, 3113, 163, 123, 1444, 5001, 3103, 3020, 1454, 212, 5002, 3023, 3053, 354, 2022, 2242, 2314, 334, 2053, 4401, 21005, 2334, 324, 344, 3052, 3013, 1464, 1434, 5000, 314, 304, 4400, 2103, 3202, 364, 900, 1900, 2062, 20900, 2153, ), ), ((), ), ((3033, 2202, 2252, ), (), (2123, ), (23004, 3063, 3032, 2063, 3043, ), (3042, ), (3153, 2344, 5010, 5041, 23900, ), ), ((3252, 5043, 5053, 5052, 4441, 3062, 3022, 2304, ), (5013, 5022, 3212, 5023, 4410, ), (3133, 2163, 3304, 3242, 3232, 3222, ), (3143, ), (5051, 3163, 2354, 5020, 3123, 2262, 2324, 21003, 5012, 5042, 3354, ), (3262, 5153, 4404, ), (3334, 3314, 5242, 5063, 4451, 5032, 5033, 2364, ), (4414, 3324, 2900, 3344, 21002, 5062, 4420, 5003, 3364, ), ), ((), (5143, 5113, 3900, 4454, 5232, 5222, 5212, ), ), ((4424, 5133, 5123, 5252, ), (), (4464, ), (5202, 4434, 5103, 5334, 5344, 5262, 5163, ), (4444, 5314, 5324, ), (5304, 5364, 5354, ), (), (4900, 5900, 21900, ), ), ((), (22003, 22005, ), ), ((), (), (), (), (22002, ), (), (), (), ), ((), (22900, ), ), )
BACKWARD_STEPS = ((900, 0, 901, ), ((10, 100, 1, 902, 110, 300, ), (101, 301, 11, ), (200, 201, ), (111, 210, 211, 400, ), (20, 303, 310, ), (), (311, 212, 401, ), (), ), (911, 302, 903, 904, 213, 21, 909, 410, 905, 120, 30, 312, 411, 203, 31, 313, 221, 202, 320, 130, 530, 131, 930, 920, 906, 531, 231, 321, 330, 121, 40, 41, 230, 412, 921, 332, 232, 331, 922, 923, 532, 220, 323, 924, 140, 925, 907, 141, 912, 233, 240, 420, 340, 430, 241, 341, 322, 413, 402, 222, 243, 533, 223, 910, 440, 421, 333, 431, 432, 403, 422, 343, 242, 630, 342, 730, 441, 442, 908, 433, 830, 423, 443, ), )


def place():
    group = lax.axis_index("group")
    wide = lax.axis_index("wide")
    return (group, lax.rem(group, 2), group // 2, wide // 2, lax.rem(wide, 2))


def when(cond, act):
    if cond is True:
        act()
    else:
        pl.when(cond)(act)


def both(left, right):
    return right if left is True else jnp.logical_and(left, right)


def remote(src, dst, send_sem, recv_sem, device):
    return pltpu.make_async_remote_copy(
        src_ref=src,
        dst_ref=dst,
        send_sem=send_sem,
        recv_sem=recv_sem,
        device_id=device,
        device_id_type=MESH,
    )


def entry_barrier():
    g, x, y, z, c = place()
    devices = []
    for step in range(1, 8):
        other = lax.rem(g * 2 + c + step, 8)
        devices.append((other // 2, z * 2 + lax.rem(other, 2)))
    devices.append((g, lax.rem(z + 1, LINE) * 2 + c))
    devices.append((g, lax.rem(z + LINE - 1, LINE) * 2 + c))
    barrier = pltpu.get_barrier_semaphore()
    for device in devices:
        pl.semaphore_signal(barrier, inc=1, device_id=device, device_id_type=MESH)
    pl.semaphore_wait(barrier, len(devices))


class Sender:
    def __init__(self, send_sems, recv_sems):
        self.send_sems, self.recv_sems = send_sems, recv_sems
        self.pending, self.draining = [], False

    def copy(self, src, dst, index, device):
        return remote(src, dst, self.send_sems.at[index], self.recv_sems.at[index], device)

    def send(self, cond, src, dst, index, device):
        copy = self.copy(src, dst, index, device)
        when(cond, copy.wait_send if self.draining else copy.start)

    def post(self, cond, src, dst, index, device):
        self.send(cond, src, dst, index, device)
        self.pending.append((cond, src, dst, index, device))

    def land(self, ref, index, device):
        self.copy(ref, ref, index, device).wait_recv()

    def do(self, cond, act):
        if not self.draining:
            when(cond, act)

    def drain(self, ticks):
        self.draining = True
        for tick in ticks:
            tick()
        for call in self.pending:
            self.send(*call)


def near_items(z, distance):
    if distance == 0:
        return [(0, z, True)]
    return [
        (distance, jnp.maximum(z - distance, 0), z >= distance),
        (3 + distance, jnp.minimum(z + distance, LINE - 1), z + distance < LINE),
    ]


class Gather:
    def __init__(self, parts, sender, local_sems):
        self.parts, self.sender, self.local_sems = parts, sender, local_sems
        self.seen = set()
        g, x, y, z, c = place()
        self.g, self.z, self.c = g, z, c
        self.gx, self.gy, self.gd = g + 1 - 2 * x, g + 2 - 4 * y, 3 - g
        self.devices = (
            (g, jnp.minimum(z + 1, LINE - 1) * 2 + c),
            (g, jnp.maximum(z - 1, 0) * 2 + c),
            (self.gx, z * 2 + c),
            (self.gy, z * 2 + c),
            (g, z * 2 + 1 - c),
        )
        for part in parts:
            for member in part[1]:
                self.own(member).start()

    def window(self, member, g, zi, c, rows=None):
        shard, full, top, count, left, columns, index = member
        first, last = (0, count) if rows is None else rows
        return full.at[g, zi, c, top + first : top + last, left : left + columns]

    def shard(self, member):
        shard, full, top, count, left, columns, index = member
        return shard.at[top : top + count, left : left + columns]

    def own(self, member):
        return pltpu.make_async_copy(
            self.shard(member),
            self.window(member, self.g, self.z, self.c),
            self.local_sems.at[member[6]],
        )

    def ring(self, member, zi, c):
        shard, full, top, count, left, columns, index = member
        return full.at[:, zi, c, top : top + count, left : left + columns]

    def item(self, slot):
        z = self.z
        if slot == 0:
            return z, True
        if slot < 4:
            return jnp.maximum(z - slot, 0), z >= slot
        return jnp.minimum(z + slot - 3, LINE - 1), z + slot - 3 < LINE

    def land(self, cond, ref, index):
        self.sender.do(cond, lambda: self.sender.land(ref, index, self.devices[4]))

    def arrivals(self, part, event, slot):
        zi, cond = self.item(slot)
        line = self.parts[part][0]
        for member in self.parts[part][1]:
            base, half, rows = member[6] * GATHER_SEMS, member[3] // 2, member[3]
            diagonal = lambda: (
                self.land(cond, self.window(member, self.gd, zi, self.c, (0, half)), base + 21 + slot),
                self.land(cond, self.window(member, self.gd, zi, self.c, (half, rows)), base + 28 + slot),
            )
            if event == 0 and slot > 0:
                self.land(cond, self.window(member, self.g, zi, self.c), base + slot)
            elif event == 1:
                self.land(cond, self.window(member, self.gx, zi, self.c), base + 7 + slot)
            elif event == 2:
                self.land(cond, self.window(member, self.gy, zi, self.c), base + 14 + slot)
            elif event == 3 or (event == 4 and slot == 0):
                diagonal()
                if slot == 0:
                    self.sender.do(True, lambda: self.own(member).wait())
            elif event == 4:
                self.land(cond, self.ring(member, zi, self.c), base + slot)

    def step(self, part, event, slot, link):
        if (part, event, slot) not in self.seen:
            self.seen.add((part, event, slot))
            self.arrivals(part, event, slot)
        zi, cond = self.item(slot)
        z, device = self.z, self.devices[link]
        for member in self.parts[part][1]:
            base, half, rows = member[6] * GATHER_SEMS, member[3] // 2, member[3]
            if link == 0:
                cond_here, index = both(cond, z < LINE - 1), base + slot + 1
            elif link == 1:
                cond_here, index = both(cond, z > 0), base + (4 if slot == 0 else slot + 1)
            else:
                cond_here = cond
                index = base + slot + ({2: 7, 3: 14} if event == 0 else {3: 21, 2: 28, 4: 35})[link]
            if event == 0:
                target = self.window(member, self.g, zi, self.c)
                source = self.shard(member) if slot == 0 else target
            elif event == 1:
                source = target = self.window(member, self.gx, zi, self.c, (0, half))
            elif event == 2:
                source = target = self.window(member, self.gy, zi, self.c, (half, rows))
            else:
                source = target = self.ring(member, zi, self.c)
            self.sender.send(cond_here, source, target, index, device)

    def finish(self, part):
        for member in self.parts[part][1]:
            for slot in range(7):
                zi, cond = self.item(slot)
                self.land(cond, self.ring(member, zi, 1 - self.c), member[6] * GATHER_SEMS + 35 + slot)


def staged(order, stages, delays):
    ticks = []
    for t in range(len(order) + delays[-1]):

        def tick(t=t):
            for stage, delay in zip(stages, delays):
                if 0 <= t - delay < len(order):
                    stage(*order[t - delay])

        ticks.append(tick)
    return ticks


def add_into(target, terms):
    rows, columns = target.shape
    step = next(s for s in (512, 256, columns) if columns % s == 0)

    def body(i, carry):
        cut = pl.ds(pl.multiple_of(i * step, step), step)
        value = terms[0][:, cut].astype(F32)
        for term in terms[1:]:
            value = value + term[:, cut].astype(F32)
        target[:, cut] = value.astype(target.dtype)
        return carry

    lax.fori_loop(0, columns // step, body, 0)


def sequence_core(g):
    return jnp.where(g < 2, g, PLANE - 1 - g)


class Exchange:
    def __init__(self, sources, targets, outward, sender, base, local_sems, local_base):
        self.sources, self.targets, self.outward = sources, targets, outward
        self.sender, self.base = sender, base
        self.local_sems, self.local_base = local_sems, local_base
        self.started = False
        g, x, y, z, c = place()
        self.g, self.z, self.c = g, z, c
        self.neighbours = {2: g + 1 - 2 * x, 3: g + 2 - 4 * y, 5: 3 - g}

    def device(self, index, outward):
        g, z, c = self.g, self.z, self.c
        if outward:
            return (c if index == 0 else PLANE - 1 - c, z * 2 + g // 2)
        return (2 * c + index, z * 2 + sequence_core(g))

    def same(self, device):
        return jnp.logical_and(device[0] == self.g, device[1] == self.z * 2 + self.c)

    def local(self, i, index, slot):
        return pltpu.make_async_copy(
            self.sources[i].at[index],
            self.targets[i].at[slot],
            self.local_sems.at[self.local_base + i],
        )

    def step(self, link):
        slot = lax.rem(self.g, 2) if self.outward else self.g // 2
        first = not self.started and not self.sender.draining
        self.started = True
        for i in range(len(self.sources)):
            for index in range(2):
                device = self.device(index, self.outward)
                if first:
                    when(self.same(device), lambda: self.local(i, index, slot).start())
                copy = remote(
                    self.sources[i].at[index],
                    self.targets[i].at[slot],
                    self.sender.send_sems.at[self.base + i * 4 + 2 + index],
                    self.sender.recv_sems.at[self.base + i * 4 + slot],
                    device,
                )
                cond = device[0] == self.neighbours[link]
                if link == 2:
                    here = jnp.logical_and(device[0] == self.g, device[1] != self.z * 2 + self.c)
                    cond = jnp.logical_or(cond, here)
                when(cond, copy.wait_send if self.sender.draining else copy.start)

    def arrive(self):
        for i in range(len(self.sources)):
            for index in range(2):
                device = self.device(index, not self.outward)
                target = self.targets[i].at[index]
                when(self.same(device), lambda: self.local(i, index, index).wait())
                when(
                    jnp.logical_not(self.same(device)),
                    lambda: self.sender.land(
                        target, self.base + i * 4 + index, (self.g, self.z * 2 + 1 - self.c)
                    ),
                )


def hbm():
    return pl.BlockSpec(memory_space=pltpu.HBM)


def vmem():
    return pl.BlockSpec(memory_space=pltpu.VMEM)


def chain(*ticks):
    def act():
        for tick in ticks:
            tick()

    return act


def run_with(ticks, steps, body):
    def act(i, carry):
        body(i)
        for j, tick in enumerate(ticks[:steps]):
            pl.when(i == j)(tick)
        return carry

    lax.fori_loop(0, steps, act, 0)
    for tick in ticks[steps:]:
        tick()


def lane_half(shape, period, half):
    lanes = lax.broadcasted_iota(jnp.int32, shape, 1)
    return lax.rem(lanes, period) < half


def turn(values):
    first = lane_half(values.shape, HEAD_DIM, HEAD_DIM // 2)
    return jnp.where(
        first,
        -pltpu.roll(values, values.shape[1] - HEAD_DIM // 2, 1),
        pltpu.roll(values, HEAD_DIM // 2, 1),
    )


def dot_rows(left, right):
    return lax.dot_general(left, right, (((1,), (0,)), ((), ())), preferred_element_type=F32)


def dot_columns(left, right):
    return lax.dot_general(left, right, (((1,), (1,)), ((), ())), preferred_element_type=F32)


def attend_pair(
    query_ref, key_ref, value_ref, far_key_ref, far_value_ref, seg_ref, seg_near_ref, seg_far_ref, out_ref, norm_ref
):
    rows = query_ref.shape[0]
    first = lane_half((rows, 128), 128, HEAD_DIM)
    tile = 256
    for r in range(rows // tile):
        rs = pl.ds(r * tile, tile)
        query = query_ref[rs, :]
        low_half = first[:tile]
        seg = seg_ref[rs, 0:1]
        near, far = seg == seg_near_ref[...], seg == seg_far_ref[...]
        outs, norms = [], []
        for h in range(2):
            keep = low_half if h == 0 else jnp.logical_not(low_half)
            one = jnp.where(keep, query, jnp.zeros_like(query))
            near_scores = jnp.where(near, dot_columns(one, key_ref[...]), neg_large)
            far_scores = jnp.where(far, dot_columns(one, far_key_ref[...]), neg_large)
            top = jnp.maximum(
                jnp.max(near_scores, axis=1, keepdims=True), jnp.max(far_scores, axis=1, keepdims=True)
            )
            near_expon, far_expon = jnp.exp(near_scores - top), jnp.exp(far_scores - top)
            total = jnp.sum(near_expon, axis=1, keepdims=True) + jnp.sum(
                far_expon, axis=1, keepdims=True
            )
            mixed = dot_rows(near_expon.astype(BF16), value_ref[...]) + dot_rows(
                far_expon.astype(BF16), far_value_ref[...]
            )
            outs.append(mixed / total)
            norms.append(jnp.broadcast_to(top + jnp.log(total), (tile, 128)))
        out_ref[rs, :] = jnp.where(low_half, outs[0], outs[1]).astype(BF16)
        flipped = jnp.transpose(jnp.where(low_half, norms[0], norms[1]))
        norm_ref[0:1, rs] = flipped[0:1]
        norm_ref[1:2, rs] = flipped[HEAD_DIM : HEAD_DIM + 1]


def stretch(packed, vectors, sizes):
    shards = packed.shape[0] // 32
    for row, lane, size, target in vectors:
        pick_rows = lax.broadcasted_iota(jnp.int32, (shards, shards * 32), 0) * 32 + row
        pick = lax.broadcasted_iota(jnp.int32, (shards, shards * 32), 1) == pick_rows
        part = dot_rows(pick.astype(F32).astype(BF16), packed).astype(BF16)
        step = 1024

        def body(i, carry):
            at = pl.multiple_of(i * step, step)
            column = (lax.broadcasted_iota(jnp.int32, (1, step), 1) + i * step).astype(F32)
            shard = jnp.floor((column + 0.5) * (1.0 / size))
            lane_of = (column - shard * size + lane).astype(jnp.int32)
            spread = lax.broadcasted_iota(jnp.int32, (128, step), 0) == lane_of
            value = dot_rows(part, spread.astype(F32).astype(BF16))
            keep = lax.broadcasted_iota(jnp.int32, (shards, step), 0) == shard.astype(jnp.int32)
            target[:, pl.ds(at, step)] = jnp.sum(jnp.where(keep, value, 0.0), axis=0, keepdims=True)
            return carry

        lax.fori_loop(0, shards * size // step, body, 0)


def flat(value):
    return value.reshape(-1, value.shape[-1])


def row_mean(value):
    return jnp.mean(value, axis=1, keepdims=True)


def forward_kernel(*refs):
    (project_shard, embed_shard, output_shard, up_shard, down_shard), refs = refs[:5], refs[5:]
    (tokens, out_cot, embed_cot), packed, refs = refs[:3], refs[3:11], refs[11:]
    (segments, frequency), refs = refs[:2], refs[2:]
    (
        project_out, token_out, qkv_out, far_out, context_out, norm, hidden_out, act_out, up_grad_out,
        down_grad_out, result_out, embed_cot_out, branch_grad_out, context_grad_out, first_grad_out,
        sums, seg_out, layer_back, embed_back, cosine_out, sine_out,
    ), refs = refs[:21], refs[21:]
    fulls, refs = refs[:6], refs[6:]
    (
        token_in, cot_in, embed_cot_in, far_seg, seg_column, vectors, qkv, far, context, normed, rstd,
        hidden_low, act, slope, result_low, embedded, sum_grad, down_grad, branch_grad, context_grad,
        cosine, sine, small_wide, small_shard,
        send_sems, recv_sems, local_sems,
    ) = refs
    shards = (project_shard, embed_shard, small_shard, output_shard, up_shard, down_shard)
    project_w, embed_w, small_w, output_w, up_w, down_w = fulls
    g, x, y, z, c = place()
    partner = (g, z * 2 + 1 - c)
    rows, width = context.shape
    sender = Sender(send_sems, recv_sems)
    spare = sum(len(p[1]) for p in FORWARD_PARTS) * GATHER_SEMS
    flushed = []

    def flush(source, target, index):
        copy = pltpu.make_async_copy(source, target, local_sems.at[40 + index])
        copy.start()
        flushed.append((source, target, index))

    small_wide[...] = jnp.zeros_like(small_wide)
    for (row, lane), vector in zip(PACKED_AT, packed):
        small_wide[row : row + 1, lane : lane + vector.shape[1]] = vector[...].astype(F32)
    small_shard[...] = small_wide[...].astype(BF16)
    entry_barrier()
    parts = []
    for line, members in FORWARD_PARTS:
        rows_of = []
        for array, first_row, last_row, first_column, last_column in members:
            height, breadth = shards[array].shape
            top, left = first_row * height // 4, first_column * breadth // 4
            rows_of.append(
                (
                    shards[array],
                    fulls[array],
                    top,
                    last_row * height // 4 - top,
                    left,
                    last_column * breadth // 4 - left,
                    sum(len(p[1]) for p in parts) + len(rows_of),
                )
            )
        parts.append((line, rows_of))
    plan = Gather(parts, sender, local_sems)
    exchanges = {
        20: Exchange([tokens], [token_in], True, sender, spare + 2, local_sems, 20),
        21: Exchange(
            [out_cot, embed_cot], [cot_in, embed_cot_in], True, sender, spare + 6, local_sems, 21
        ),
        22: Exchange(
            [result_low, embedded], [layer_back, embed_back], False, sender, spare + 14, local_sems, 23
        ),
    }

    def perform(steps):
        def act():
            for step in steps:
                part, event, slot, link = step // 1000, step // 100 % 10, step // 10 % 10, step % 10
                if part == 23:
                    if event == 9:
                        sender.do(True, lambda: sender.land(far, spare + 1, partner))
                    else:
                        sender.send(True, qkv.at[:, width:], far, spare + 1, partner)
                elif part >= 20:
                    if event != 9:
                        exchanges[part].step(link)
                    elif not sender.draining:
                        exchanges[part].arrive()
                elif event == 9:
                    plan.finish(part)
                else:
                    plan.step(part, event, slot, link)

        return act

    ticks = [[perform(steps) for steps in phase] for phase in FORWARD_STEPS]
    sender.post(True, segments, far_seg, spare, partner)
    opening = FORWARD_STEPS[0][0]
    ready = next(i for i, step in enumerate(opening) if step < 20000 and step // 10 % 100 > 0)
    perform(opening[:ready])()
    row_at = lax.broadcasted_iota(jnp.int32, cosine.shape, 0) + c * rows
    angles = row_at.astype(F32) * frequency[...]
    cosine[...] = jnp.cos(angles)
    sine[...] = jnp.sin(angles)
    flush(cosine, cosine_out, 14)
    flush(sine, sine_out, 15)
    perform(opening[ready:])()
    sender.land(far_seg, spare, partner)
    micro = g // 2
    own_ids, far_ids = segments[micro].astype(F32), far_seg[micro].astype(F32)
    ids = jnp.where(sequence_core(g) == c, own_ids, far_ids)
    halves = (ids[:, :rows], ids[:, rows:])
    near_row = jnp.where(c == 0, halves[0], halves[1])
    far_row = jnp.where(c == 0, halves[1], halves[0])
    seg_out[0:1, :] = near_row
    seg_out[1:2, :] = far_row
    seg_column[...] = jnp.transpose(jnp.broadcast_to(near_row, (128, rows)))
    flush(project_w, project_out, 0)
    flush(token_in, token_out, 1)
    vector = lambda i, size: vectors.at[i : i + 1, 0:size]
    stretch(
        flat(small_w[...]),
        (
            (0, 0, 96, vector(0, 3 * width)),
            (1, 0, 128, vector(1, 4 * width)),
            (2, 0, 32, vector(2, width)),
            (2, 32, 32, vector(3, width)),
            (2, 64, 32, vector(4, width)),
            (2, 96, 32, vector(5, width)),
            (3, 0, 32, vector(6, width)),
            (3, 32, 32, vector(7, width)),
        ),
        None,
    )
    tile = 512
    wide = qkv.shape[1] // tile

    def project_tile(i):
        t = lax.rem(i + 2, wide)
        cut = pl.ds(pl.multiple_of(t * tile, tile), tile)
        value = dot_rows(flat(token_in[...]), flat(project_w[:, :, :, :, cut]))
        value = value + vectors[0:1, cut]

        @pl.when(t < 4)
        def _():
            factor = jnp.where(t < 2, HEAD_DIM ** (-0.5), 1.0)
            for j in range(tile // 128):
                part = value[:, j * 128 : (j + 1) * 128]
                part = (part * cosine[...] + turn(part) * sine[...]) * factor
                qkv[:, pl.ds(pl.multiple_of(t * tile + j * 128, 128), 128)] = part.astype(BF16)

        @pl.when(t >= 4)
        def _():
            qkv[:, cut] = value.astype(BF16)

    ticks[1][0]()
    run_with(ticks[2], wide, project_tile)
    flush(qkv, qkv_out, 2)
    flush(far, far_out, 3)

    def attend_one(i):
        at = pl.multiple_of(i * 128, 128)
        cut = lambda ref, base: ref.at[:, pl.ds(base + at, 128)]
        attend_pair(
            cut(qkv, 0), cut(qkv, width), cut(qkv, 2 * width), cut(far, 0), cut(far, width),
            seg_column, seg_out.at[0:1], seg_out.at[1:2], cut(context, 0), norm.at[i],
        )

    run_with(ticks[3], width // 128, attend_one)
    flush(context, context_out, 4)
    half = rows // 2
    output_weight, bias_o = lambda: flat(output_w[...]), vectors[2:3, 0:width]

    def hidden_of(cut):
        return normed[cut, :] * vectors[3:4, 0:width] + vectors[4:5, 0:width]

    def branch_tile(i):
        cut = pl.ds(pl.multiple_of(i * half, half), half)
        resid = dot_rows(context[cut, :], output_weight()) + vectors[2:3, 0:width]
        resid = resid + token_in[i].astype(F32)
        center = resid - row_mean(resid)
        scale = lax.rsqrt(row_mean(center * center) + eps_norm)
        normed[cut, :] = center * scale
        rstd[0, cut, :] = jnp.broadcast_to(scale, (half, 128))
        hidden_low[cut, :] = hidden_of(cut).astype(BF16)

    run_with(ticks[4], 2, branch_tile)
    flush(hidden_low, hidden_out, 5)

    def up_tile(j):
        cut = pl.ds(pl.multiple_of(j * tile, tile), tile)
        value = dot_rows(hidden_low[...], flat(up_w[:, :, :, :, cut])) + vectors[1:2, cut]
        below = 0.5 + 0.5 * lax.erf(value * 0.7071067811865476)
        density = jnp.exp(-0.5 * value * value) * 0.3989422804014327
        act[:, cut] = (value * below).astype(BF16)
        slope[:, cut] = (below + value * density).astype(BF16)

    ff = act.shape[1]
    run_with(ticks[5], ff // tile, up_tile)
    flush(act, act_out, 6)
    flush(embed_cot_in, embed_cot_out, 7)
    sums[...] = jnp.zeros_like(sums)

    def add_sum(row, value):
        sums[row : row + 1, 0:width] += jnp.sum(value, axis=0, keepdims=True)

    def norm_back(grads, row_normed, scale, gain):
        scaled = grads * gain
        return scale * (
            scaled - row_mean(scaled) - row_normed * row_mean(scaled * row_normed)
        )

    def down_tile(i):
        cut = pl.ds(pl.multiple_of(i * half, half), half)
        gain, shift = vectors[6:7, 0:width], vectors[7:8, 0:width]
        resid = dot_rows(act[cut, :], flat(down_w[...])) + vectors[5:6, 0:width]
        resid = resid + hidden_of(cut)
        center = resid - row_mean(resid)
        scale = lax.rsqrt(row_mean(center * center) + eps_norm)
        row_normed = center * scale
        low = (row_normed * gain + shift).astype(BF16)
        result_low[i] = low
        embed_full = flat(embed_w[...])
        embedded[i] = dot_rows(low, embed_full).astype(BF16)
        grads = cot_in[i].astype(F32) + dot_columns(embed_cot_in[i], embed_full)
        add_sum(6, grads * row_normed)
        add_sum(7, grads)
        total = norm_back(grads, row_normed, scale, gain)
        sum_grad[cut, :] = total
        low = total.astype(BF16)
        down_grad[cut, :] = low
        add_sum(5, low.astype(F32))

    run_with(ticks[6], 2, down_tile)
    flush(result_low, result_out, 8)
    flush(down_grad, down_grad_out, 9)

    def up_grad_tile(j):
        cut = pl.ds(pl.multiple_of(j * tile, tile), tile)
        part = flat(down_w[j // 2, pl.ds(lax.rem(j, 2) * 2, 2)])
        value = (dot_columns(down_grad[...], part) * slope[:, cut].astype(F32)).astype(BF16)
        slope[:, cut] = value
        sums[1:2, cut] = jnp.sum(value.astype(F32), axis=0, keepdims=True)

    run_with(ticks[7], ff // tile, up_grad_tile)
    flush(slope, up_grad_out, 10)

    def first_tile(i):
        cut = pl.ds(pl.multiple_of(i * half, half), half)
        grads = sum_grad[cut, :] + dot_columns(slope[cut, :], flat(up_w[...]))
        row_normed = normed[cut, :]
        add_sum(3, grads * row_normed)
        add_sum(4, grads)
        total = norm_back(grads, row_normed, rstd[0, cut, 0:1], vectors[3:4, 0:width])
        sum_grad[cut, :] = total
        low = total.astype(BF16)
        branch_grad[cut, :] = low
        add_sum(2, low.astype(F32))
        context_grad[cut, :] = dot_columns(low, output_weight()).astype(BF16)

    run_with(ticks[8], 2, first_tile)
    flush(sum_grad, first_grad_out, 11)
    flush(branch_grad, branch_grad_out, 12)
    flush(context_grad, context_grad_out, 13)
    sender.drain([tick for phase in ticks for tick in phase])
    for source, target, index in flushed:
        pltpu.make_async_copy(source, target, local_sems.at[40 + index]).wait()


def forward(shards, sources, packed, segments, frequency, ff):
    piece, width = sources[0].shape[1:]
    lanes = sources[2].shape[2]
    rows = 2 * piece
    semaphores = sum(len(p[1]) for p in FORWARD_PARTS) * GATHER_SEMS + 32
    small = (32, lanes)
    heights = [s.shape for s in shards[:2]] + [small] + [s.shape for s in shards[2:]]
    fulls = [(PLANE, LINE, 2) + s for s in heights]
    shape = jax.ShapeDtypeStruct
    outs = [
        shape(fulls[0], BF16),
        shape((2, piece, width), BF16),
        shape((rows, 3 * width), BF16),
        shape((rows, 2 * width), BF16),
        shape((rows, width), BF16),
        shape((width // 128, 8, rows), F32),
        shape((rows, width), BF16),
        shape((rows, ff), BF16),
        shape((rows, ff), BF16),
        shape((rows, width), BF16),
        shape((2, piece, width), BF16),
        shape((2, piece, lanes), BF16),
        shape((rows, width), BF16),
        shape((rows, width), BF16),
        shape((rows, width), F32),
        shape((8, ff), F32),
        shape((8, rows), F32),
        shape((2, piece, width), BF16),
        shape((2, piece, lanes), BF16),
        shape((rows, 128), F32),
        shape((rows, 128), F32),
    ]
    spaces = [hbm()] * len(outs)
    for i in (5, 15, 16):
        spaces[i] = vmem()
    scratch = [pltpu.VMEM(f, BF16) for f in fulls] + [
        pltpu.VMEM((2, piece, width), BF16),
        pltpu.VMEM((2, piece, width), BF16),
        pltpu.VMEM((2, piece, lanes), BF16),
        pltpu.VMEM(segments.shape, jnp.int32),
        pltpu.VMEM((rows, 128), F32),
        pltpu.VMEM((8, ff), F32),
        pltpu.VMEM((rows, 3 * width), BF16),
        pltpu.VMEM((rows, 2 * width), BF16),
        pltpu.VMEM((rows, width), BF16),
        pltpu.VMEM((rows, width), F32),
        pltpu.VMEM((1, rows, 128), F32),
        pltpu.VMEM((rows, width), BF16),
        pltpu.VMEM((rows, ff), BF16),
        pltpu.VMEM((rows, ff), BF16),
        pltpu.VMEM((2, piece, width), BF16),
        pltpu.VMEM((2, piece, lanes), BF16),
        pltpu.VMEM((rows, width), F32),
        pltpu.VMEM((rows, width), BF16),
        pltpu.VMEM((rows, width), BF16),
        pltpu.VMEM((rows, width), BF16),
        pltpu.VMEM((rows, 128), F32),
        pltpu.VMEM((rows, 128), F32),
        pltpu.VMEM(small, F32),
        pltpu.VMEM(small, BF16),
        pltpu.SemaphoreType.DMA((semaphores,)),
        pltpu.SemaphoreType.DMA((semaphores,)),
        pltpu.SemaphoreType.DMA((60,)),
    ]
    return pl.pallas_call(
        forward_kernel,
        out_shape=outs,
        in_specs=[hbm()] * 8 + [vmem()] * 10,
        out_specs=spaces,
        scratch_shapes=scratch,
        compiler_params=pltpu.CompilerParams(
            collective_id=1, has_side_effects=True, vmem_limit_bytes=67043328
        ),
        name="forward",
    )(*shards, *sources, *packed, segments, frequency)


def attend_back_pair(
    query, key, value, far_key, far_value, grad, norm, seg_row, seg_near, seg_far, tables, summed
):
    rows = query.shape[0]
    tile = 256
    cosine, sine, shift = tables
    low_half = lane_half((rows, 128), 128, HEAD_DIM)
    query_low = lane_half((tile, 128), 128, HEAD_DIM)
    for total in summed:
        total[...] = jnp.zeros_like(total)

    def body(r, carry):
        rs = pl.ds(pl.multiple_of(r * tile, tile), tile)
        query_rows, grad_rows = query[rs, :], grad[rs, :]
        sides = ((key[...], value[...], seg_near), (far_key[...], far_value[...], seg_far))
        query_grads = []
        key_grads, value_grads = [[], []], [[], []]
        for h in range(2):
            keep = query_low if h == 0 else jnp.logical_not(query_low)
            one = jnp.where(keep, query_rows, jnp.zeros_like(query_rows))
            one_grad = jnp.where(keep, grad_rows, jnp.zeros_like(grad_rows))
            top = norm[h : h + 1, rs]
            kept = []
            delta = jnp.zeros((1, tile), F32)
            for keys, values, seg_key in sides:
                same = seg_key[:, 0:1] == seg_row[:, rs]
                scores = jnp.where(same, dot_columns(keys, one), neg_large)
                probs = jnp.exp(scores - top)
                product = probs * dot_columns(values, one_grad)
                delta = delta + jnp.sum(product, axis=0, keepdims=True)
                kept.append((probs, product))
            total = None
            for i, (keys, values, seg_key) in enumerate(sides):
                probs, product = kept[i]
                score_grad = (product - probs * delta).astype(BF16)
                key_grads[i].append(dot_rows(score_grad, query_rows))
                value_grads[i].append(dot_rows(probs.astype(BF16), grad_rows))
                part = contract_rows(score_grad, keys)
                total = part if total is None else total + part
            query_grads.append(total)
        for i in range(2):
            summed[i][...] += jnp.where(low_half, key_grads[i][0], key_grads[i][1])
            summed[2 + i][...] += jnp.where(low_half, value_grads[i][0], value_grads[i][1])
        joined = jnp.where(query_low, query_grads[0], query_grads[1]) * HEAD_DIM ** (-0.5)
        query[rs, :] = (joined * cosine[rs, :] - turn(joined) * sine[rs, :]).astype(BF16)
        return carry

    lax.fori_loop(0, rows // tile, body, 0)
    near, far = summed[0][...], summed[1][...]
    far_cosine = cosine[...] * shift[0:1, :] - sine[...] * shift[1:2, :]
    far_sine = sine[...] * shift[0:1, :] + cosine[...] * shift[1:2, :]
    key[...] = (near * cosine[...] - turn(near) * sine[...]).astype(BF16)
    value[...] = summed[2][...].astype(BF16)
    far_key[...] = (far * far_cosine - turn(far) * far_sine).astype(BF16)
    far_value[...] = summed[3][...].astype(BF16)


class Reduce:
    def __init__(self, arrays, sender):
        self.arrays, self.sender = arrays, sender
        g, x, y, z, c = place()
        self.g, self.z, self.c = g, z, c
        self.gx, self.gy, self.gd = g + 1 - 2 * x, g + 2 - 4 * y, 3 - g
        self.to_x, self.to_y = (self.gx, z * 2 + c), (self.gy, z * 2 + c)
        self.to_core = (g, z * 2 + 1 - c)
        lower = z < 2
        even = lax.rem(z, 2) == 0
        third = jnp.where(even, z + 1, z - 1)
        self.order = (jnp.where(lower, 3, 0), jnp.where(lower, 2, 1), third, z)
        self.rising = (lower, lower, even)

    def index(self, a, kind, i=0):
        return a * REDUCE_SEMS + kind + i

    def start(self, a, p):
        array, sender = self.arrays[a], self.sender

        def copy(b, i):
            other = self.arrays[b]
            return sender.copy(
                other.send.at[i % 2],
                other.held.at[self.order[i]],
                self.index(b, CORE, i),
                self.to_core,
            )

        if sender.draining:
            if p == 1 and a not in (1, 2):
                copy(a, 2).wait_send()
                copy(a, 3).wait_send()
            return
        before = (a, 0) if p == 1 else {2: (1, 2), 3: (2, 2)}.get(a)
        if before is not None:
            copy(before[0], before[1]).wait_send()
            copy(before[0], before[1] + 1).wait_send()
        zs = self.order[2 * p : 2 * p + 2]
        array.product(1 - self.c, zs, (array.send.at[0], array.send.at[1]), False)
        copy(a, 2 * p).start()
        copy(a, 2 * p + 1).start()

    def meet(self, a, p):
        array, sender = self.arrays[a], self.sender
        held, half_in, low = array.held, array.half, array.low
        rows, columns = held.shape[2:]
        cut = rows // 2
        zs = self.order[2 * p : 2 * p + 2]

        def work():
            for i in range(2):
                sender.land(held.at[zs[i]], self.index(a, CORE, 2 * p + i), self.to_x)
            array.product(self.c, zs, (held.at[zs[0]], held.at[zs[1]]), True)

        sender.do(True, work)
        for i in range(2):
            block = held.at[zs[i], self.gd]
            sender.send(
                True, block.at[0:cut, low:columns], half_in.at[zs[i], 0:cut],
                self.index(a, UPPER, 2 * p + i), self.to_y,
            )
            sender.send(
                True, block.at[cut:rows, low:columns], half_in.at[zs[i], cut:rows],
                self.index(a, LOWER, 2 * p + i), self.to_x,
            )

    def turn(self, a, i, upper):
        array, sender = self.arrays[a], self.sender
        held, half_in, whole_in, low = array.held, array.half, array.whole, array.low
        rows, columns = held.shape[2:]
        zi, cut = self.order[i], rows // 2
        first, last = (0, cut) if upper else (cut, rows)
        block = held.at[zi, self.gx if upper else self.gy, :, low:columns]

        def work():
            arrived = half_in.at[zi, first:last]
            sender.land(arrived, self.index(a, UPPER if upper else LOWER, i), self.to_x)
            add_into(block.at[first:last], [block.at[first:last], arrived])

        sender.do(True, work)
        sender.send(
            True, block, whole_in.at[zi, 0 if upper else 1],
            self.index(a, ROW if upper else COLUMN, i), self.to_x if upper else self.to_y,
        )

    def pass_on(self, i, source, lines, recv_kind, send_kind, a):
        z, zi = self.z, self.order[i]
        up = self.rising[i]
        slot = jnp.where(jnp.logical_and(jnp.logical_not(up), zi == z - 1), LINE, zi)
        copy = remote(
            source,
            lines.at[slot],
            self.sender.send_sems.at[self.index(a, send_kind, i)],
            self.sender.recv_sems.at[self.index(a, recv_kind) + slot],
            (self.g, jnp.where(up, z + 1, z - 1) * 2 + self.c),
        )
        if self.sender.draining:
            copy.wait_send()
        else:
            copy.start()

    def inner(self, i):
        return jnp.logical_or(
            jnp.logical_and(self.rising[i], self.z > 0),
            jnp.logical_and(jnp.logical_not(self.rising[i]), self.z < LINE - 1),
        )

    def along(self, a, i):
        array, sender = self.arrays[a], self.sender
        whole_in, lines, low = array.whole, array.line, array.low
        columns, zi, z = array.held.shape[3], self.order[i], self.z
        mine = array.held.at[zi, self.g, :, low:columns]
        terms = [mine, whole_in.at[zi, 0], whole_in.at[zi, 1]]
        arrived = self.index(a, ARRIVED)

        def work():
            sender.land(whole_in.at[zi, 0], self.index(a, ROW, i), self.to_x)
            sender.land(whole_in.at[zi, 1], self.index(a, COLUMN, i), self.to_x)
            if i < 3:
                inner = self.inner(i)

                def join():
                    sender.land(lines.at[zi], arrived + zi, self.to_x)
                    add_into(mine, terms + [lines.at[zi]])

                pl.when(inner)(join)
                pl.when(jnp.logical_not(inner))(lambda: add_into(mine, terms))
            else:
                self.close(lines, arrived, terms, array.out.at[:, low:columns])

        sender.do(True, work)
        if i < 3:
            self.pass_on(i, mine, lines, ARRIVED, HOP, a)

    def close(self, lines, arrived, terms, target):
        z, sender = self.z, self.sender
        rise, fall = lines.at[z], lines.at[LINE]
        pl.when(z > 0)(lambda: sender.land(rise, arrived + z, self.to_x))
        pl.when(z < LINE - 1)(lambda: sender.land(fall, arrived + LINE, self.to_x))
        pl.when(z == 0)(lambda: add_into(target, terms + [fall]))
        pl.when(z == LINE - 1)(lambda: add_into(target, terms + [rise]))
        pl.when(jnp.logical_and(z > 0, z < LINE - 1))(
            lambda: add_into(target, terms + [rise, fall])
        )

    def along_first(self, a, i):
        array, sender = self.arrays[a], self.sender
        low, rings, zi, z = array.low, array.rings, self.order[i], self.z
        mine = array.held.at[zi, :, :, 0:low]
        arrived = self.index(a, RING_ARRIVED)

        def add(slots):
            for j in range(PLANE):
                block = array.held.at[zi, j, :, 0:low]
                add_into(block, [block] + [rings.at[slot, j] for slot in slots])

        def work():
            if i < 3:

                def join():
                    sender.land(rings.at[zi], arrived + zi, self.to_x)
                    add([zi])

                pl.when(self.inner(i))(join)
                return
            pl.when(z > 0)(lambda: sender.land(rings.at[z], arrived + z, self.to_x))
            pl.when(z < LINE - 1)(lambda: sender.land(rings.at[LINE], arrived + LINE, self.to_x))
            pl.when(z == 0)(lambda: add([LINE]))
            pl.when(z == LINE - 1)(lambda: add([z]))
            pl.when(jnp.logical_and(z > 0, z < LINE - 1))(lambda: add([z, LINE]))

        sender.do(True, work)
        if i < 3:
            self.pass_on(i, mine, rings, RING_ARRIVED, RING_HOP, a)
            return
        block, half_in = array.held.at[z, self.gd, :, 0:low], array.own_half
        rows = half_in.shape[0]
        cut = rows // 2
        sender.send(
            True, block.at[0:cut], half_in.at[0:cut], self.index(a, OWN_UPPER), self.to_y
        )
        sender.send(
            True, block.at[cut:rows], half_in.at[cut:rows], self.index(a, OWN_LOWER), self.to_x
        )

    def turn_own(self, a, upper):
        array, sender = self.arrays[a], self.sender
        low, half_in = array.low, array.own_half
        rows = half_in.shape[0]
        first, last = (0, rows // 2) if upper else (rows // 2, rows)
        block = array.held.at[self.z, self.gx if upper else self.gy, :, 0:low]

        def work():
            arrived = half_in.at[first:last]
            sender.land(arrived, self.index(a, OWN_UPPER if upper else OWN_LOWER), self.to_x)
            add_into(block.at[first:last], [block.at[first:last], arrived])

        sender.do(True, work)
        sender.send(
            True, block, array.own_whole.at[0 if upper else 1],
            self.index(a, OWN_ROW if upper else OWN_COLUMN),
            self.to_x if upper else self.to_y,
        )

    def close_own(self, a):
        array, sender = self.arrays[a], self.sender
        low, whole_in = array.low, array.own_whole

        def work():
            sender.land(whole_in.at[0], self.index(a, OWN_ROW), self.to_x)
            sender.land(whole_in.at[1], self.index(a, OWN_COLUMN), self.to_x)
            mine = array.held.at[self.z, self.g, :, 0:low]
            add_into(array.out.at[:, 0:low], [mine, whole_in.at[0], whole_in.at[1]])

        sender.do(True, work)

    def step(self, code):
        kind, a, i = code // 100, code // 10 % 10, code % 10
        if kind == 0:
            self.start(a, i)
        elif kind == 1:
            self.meet(a, i)
        elif kind in (2, 3):
            self.turn(a, i, kind == 2)
        elif kind == 4:
            self.along(a, i)
        elif kind == 5:
            self.along_first(a, i)
        elif kind in (6, 7):
            self.turn_own(a, kind == 6)
        else:
            self.close_own(a)


def gather_up(vectors, target):
    shards = PLANE * LINE * 2
    total = None
    for row in sorted({v[0] for v in vectors}):
        share = jnp.zeros((shards, 128), F32)
        for at, lane, size, source in vectors:
            if at != row:
                continue
            step = 1024

            def body(i, carry):
                cut = pl.ds(pl.multiple_of(i * step, step), step)
                column = (lax.broadcasted_iota(jnp.int32, (1, step), 1) + i * step).astype(F32)
                shard = jnp.floor((column + 0.5) * (1.0 / size))
                lane_of = (column - shard * size + lane).astype(jnp.int32)
                spread = lax.broadcasted_iota(jnp.int32, (128, step), 0) == lane_of
                keep = lax.broadcasted_iota(jnp.int32, (shards, step), 0) == shard.astype(jnp.int32)
                value = jnp.where(keep, source[:, cut], 0.0).astype(BF16)
                return carry + dot_columns(value, spread.astype(F32).astype(BF16))

            share = lax.fori_loop(0, shards * size // step, body, share)
        pick_rows = lax.broadcasted_iota(jnp.int32, (shards, shards * 32), 0) * 32 + row
        pick = lax.broadcasted_iota(jnp.int32, (shards, shards * 32), 1) == pick_rows
        part = contract_rows(pick.astype(F32).astype(BF16), share.astype(BF16))
        total = part if total is None else total + part
    target[...] = total.astype(BF16).reshape(target.shape)


def backward_kernel(*refs):
    (
        act_hbm, down_grad_hbm, hidden_hbm, up_grad_hbm, context_hbm, branch_grad_hbm, result_hbm,
        embed_cot_hbm, token_hbm, qkv_hbm, far_hbm, context_grad_hbm, first_grad_hbm, weight_hbm,
        norm, segs, sums, cosine, sine, frequency,
    ), refs = refs[:20], refs[20:]
    outs, token_in, refs = refs[:5], refs[5], refs[6:]
    (send_d, send_u, send_s), refs = refs[:3], refs[3:]
    helds, halves, wholes, lines = [refs[i * 5 : (i + 1) * 5] for i in range(4)]
    (
        rings, own_half, own_whole,
        act, down_grad, up_grad, branch_grad, embed_cot, raw, turned_a, turned_b, qkv, far,
        far_back, context_grad, seg_near, seg_far, vectors, shares, token_out, shift,
        send_sems, recv_sems, local_sems,
    ) = refs[20:]
    g, x, y, z, c = place()
    partner = (g, z * 2 + 1 - c)
    rows, width = branch_grad.shape
    ff = act.shape[1]
    sender = Sender(send_sems, recv_sems)
    spare = 5 * REDUCE_SEMS

    def load(source, target, index):
        copy = lambda: pltpu.make_async_copy(source, target, local_sems.at[index])
        copy().start()
        return lambda: copy().wait()

    wait_act = load(act_hbm, act, 0)
    wait_down = load(down_grad_hbm, down_grad, 1)
    wait_raw = load(hidden_hbm, raw, 2)
    wait_up = load(up_grad_hbm, up_grad, 3)
    wait_branch = load(branch_grad_hbm, branch_grad, 4)
    wait_embed = load(embed_cot_hbm, embed_cot, 5)
    wait_qkv = load(qkv_hbm, qkv, 6)
    wait_far = load(far_hbm, far, 7)
    wait_grad = load(context_grad_hbm, context_grad, 8)
    entry_barrier()

    def turn_over(target):
        for j in range(width // 128):
            block = jnp.transpose(flat(raw[:, :, j * 128 : (j + 1) * 128]))
            target[j // 2, (j % 2) * 2 : (j % 2) * 2 + 2] = block.reshape(2, 2, 32, rows)

    def product_of(turned, right):
        columns = right.shape[1]
        step = min(columns, 512)

        def act_on(parity, zs, targets, added):
            left = jnp.concatenate([flat(turned[:, zi, parity]) for zi in zs], axis=0)

            def body(i, carry):
                cut = pl.ds(pl.multiple_of(i * step, step), step)
                value = dot_rows(left, right[:, cut]).reshape(2, PLANE, 32, step)
                for j, target in enumerate(targets):
                    part = value[j]
                    if added:
                        part = part + target[:, :, cut].astype(F32)
                    target[:, :, cut] = part.astype(BF16)
                return carry

            lax.fori_loop(0, columns // step, body, 0)

        return act_on

    def down_product(parity, zs, targets, added):
        def body(j, carry):
            pieces = []
            for zi in zs:
                at = ((j * LINE + zi) * 2 + parity) * 128
                pieces.append(act[:, pl.ds(pl.multiple_of(at, 128), 128)])
            value = contract_rows(jnp.concatenate(pieces, axis=1), down_grad[...])
            for i, target in enumerate(targets):
                part = value[i * 128 : (i + 1) * 128]
                if added:
                    part = part + target[j].astype(F32)
                target[j] = part.astype(BF16)
            return carry

        lax.fori_loop(0, PLANE, body, 0)

    def share_product(parity, zs, targets, added):
        for zi, target in zip(zs, targets):
            value = shares[:, zi, parity]
            if added:
                value = (value.astype(F32) + target[...].astype(F32)).astype(BF16)
            target[...] = value

    shared = lambda columns: send_u.at[:, :, :, 0:columns]
    sends = (send_d, send_u, shared(width), shared(3 * width), send_s)
    products = [
        down_product,
        product_of(turned_a, up_grad),
        product_of(turned_b, branch_grad),
        product_of(turned_a, qkv),
        share_product,
    ]
    arrays = [
        SimpleNamespace(product=p, send=s, held=h, half=i, whole=w, line=l, out=o, low=0)
        for p, s, h, i, w, l, o in zip(products, sends, helds, halves, wholes, lines, outs)
    ]
    arrays[3].low, arrays[3].rings = rings.shape[3], rings
    arrays[3].own_half, arrays[3].own_whole = own_half, own_whole
    plan = Reduce(arrays, sender)
    token_back = Exchange([raw], [token_in], False, sender, spare + 2, local_sems, 18)
    parts, tile = 3 * width // 512, 512

    def fetch(t, begin):
        for r in range(2):
            at = ((t % 4) * 2 + r) * tile
            copy = pltpu.make_async_copy(
                weight_hbm.at[r * rows : (r + 1) * rows, t * tile : (t + 1) * tile],
                act.at[:, at : at + tile],
                local_sems.at[10 + (t % 4) * 2 + r],
            )
            copy.start() if begin else copy.wait()

    def fetched(t):
        fetch(t, False)
        for r in range(2):
            at = ((t % 4) * 2 + r) * tile
            half = token_out[:, r * tile : (r + 1) * tile]
            token_out[:, r * tile : (r + 1) * tile] = half + dot_columns(
                qkv[:, t * tile : (t + 1) * tile], act[:, at : at + tile]
            )
        if t + 4 < parts:
            fetch(t + 4, True)

    def turn_hidden():
        wait_raw()
        turn_over(turned_a)
        load(context_hbm, raw, 2)

    def turn_context():
        wait_raw()
        turn_over(turned_b)
        load(result_hbm, raw, 2)

    def embed_share():
        wait_raw()
        wait_embed()
        value = contract_rows(flat(raw[...]), embed_cot[...]).astype(BF16)
        shares[:, :, :, 0:32, :] = value.reshape(PLANE, LINE, 2, 32, 128)
        load(token_hbm, raw, 2)

    def before_attention():
        turned_by = jnp.broadcast_to(frequency[...] * float(rows), shift.shape)
        row = lax.broadcasted_iota(jnp.int32, shift.shape, 0)
        side = jnp.where(c == 0, 1.0, -1.0)
        shift[...] = jnp.where(row == 0, jnp.cos(turned_by), jnp.sin(turned_by) * side)
        wait_qkv()
        wait_far()
        wait_grad()
        seg_near[...] = jnp.transpose(jnp.broadcast_to(segs[0:1, :], (128, rows)))
        seg_far[...] = jnp.transpose(jnp.broadcast_to(segs[1:2, :], (128, rows)))

    def turn_tokens():
        wait_raw()
        turn_over(turned_a)
        for t in range(4):
            fetch(t, True)

    def finish_tile(i):
        cut = pl.ds(pl.multiple_of(i * tile, tile), tile)

        @pl.when(i >= 2)
        def _():
            other = pl.ds(pl.multiple_of(jnp.maximum(i - 2, 0) * tile, tile), tile)
            qkv[:, cut] = (qkv[:, cut].astype(F32) + far_back[:, other].astype(F32)).astype(BF16)

        vectors[0:1, cut] = jnp.sum(qkv[:, cut].astype(F32), axis=0, keepdims=True)

    def other_shares():
        source = lambda i, size: (vectors if i == 0 else sums).at[i : i + 1, 0:size]
        gather_up(
            (
                (0, 0, 96, source(0, 3 * width)),
                (1, 0, 128, source(1, ff)),
                (2, 0, 32, source(2, width)),
                (2, 32, 32, source(3, width)),
                (2, 64, 32, source(4, width)),
                (2, 96, 32, source(5, width)),
                (3, 0, 32, source(6, width)),
                (3, 32, 32, source(7, width)),
            ),
            shares.at[:, :, :, 32:64, :],
        )

    def round_tokens():
        for i in range(2):
            raw[i] = token_out[i * (rows // 2) : (i + 1) * (rows // 2), :].astype(BF16)

    def attend_one(i):
        at = pl.multiple_of(i * 128, 128)
        cut = lambda ref, base: ref.at[:, pl.ds(base + at, 128)]
        attend_back_pair(
            cut(qkv, 0), cut(qkv, width), cut(qkv, 2 * width), cut(far, 0), cut(far, width),
            cut(context_grad, 0), norm.at[i], segs.at[0:1], seg_near, seg_far,
            (cosine, sine, shift), [token_out.at[:, j * 128 : (j + 1) * 128] for j in range(4)],
        )

    first_copy = pltpu.make_async_copy(first_grad_hbm, token_out, local_sems.at[9])
    others = {
        900: lambda: (wait_act(), wait_down()),
        901: lambda: (turn_hidden(), wait_up()),
        902: lambda: (turn_context(), wait_branch()),
        903: embed_share,
        904: turn_tokens,
        905: lambda: lax.fori_loop(0, parts, lambda i, carry: (finish_tile(i), carry)[1], 0),
        906: other_shares,
        907: round_tokens,
        908: lambda: None,
        909: lambda: sender.land(far_back, spare, partner),
        910: token_back.arrive,
        930: first_copy.wait,
    }
    for t in range(parts):
        others[920 + t] = lambda t=t: fetched(t)

    def perform(steps):
        def act_on():
            for step in steps:
                if step == 911:
                    sender.do(True, first_copy.start)
                    sender.send(True, far, far_back, spare, partner)
                elif step == 912:
                    for link in (5, 2, 3):
                        token_back.step(link)
                elif step >= 900:
                    if not sender.draining:
                        others[step]()
                else:
                    plan.step(step)

        return act_on

    first, middle, last = BACKWARD_STEPS
    ticks = [perform(steps) for steps in (first,) + middle + (last,)]
    ticks[0]()
    before_attention()
    run_with(ticks[1:-1], width // 128, attend_one)
    ticks[-1]()
    sender.drain(ticks)


def backward(operands, small_operands, shapes, rows, width, ff, lanes):
    shape = jax.ShapeDtypeStruct
    semaphores = 5 * REDUCE_SEMS + 16
    ring = (shapes[3][0], shapes[3][1] // 2)
    buffers = [pltpu.VMEM((2, PLANE) + shapes[i], BF16) for i in (0, 1, 4)]
    apart = shapes[:3] + [(ring[0], shapes[3][1] - ring[1])] + shapes[4:]
    buffers += [pltpu.VMEM((LINE, PLANE) + s, BF16) for s in shapes]
    for lead in ((LINE,), (LINE, 2), (LINE + 1,)):
        buffers += [pltpu.VMEM(lead + s, BF16) for s in apart]
    turned = pltpu.VMEM((PLANE, LINE, 2, 32, rows), BF16)
    piece = rows // 2
    scratch = buffers + [
        pltpu.VMEM((LINE + 1, PLANE) + ring, BF16),
        pltpu.VMEM(ring, BF16),
        pltpu.VMEM((2,) + ring, BF16),
        pltpu.VMEM((rows, ff), BF16),
        pltpu.VMEM((rows, width), BF16),
        pltpu.VMEM((rows, ff), BF16),
        pltpu.VMEM((rows, width), BF16),
        pltpu.VMEM((rows, lanes), BF16),
        pltpu.VMEM((2, piece, width), BF16),
        turned,
        turned,
        pltpu.VMEM((rows, 3 * width), BF16),
        pltpu.VMEM((rows, 2 * width), BF16),
        pltpu.VMEM((rows, 2 * width), BF16),
        pltpu.VMEM((rows, width), BF16),
        pltpu.VMEM((rows, 128), F32),
        pltpu.VMEM((rows, 128), F32),
        pltpu.VMEM((1, 3 * width), F32),
        pltpu.VMEM((PLANE, LINE, 2, 64, 128), BF16),
        pltpu.VMEM((rows, width), F32),
        pltpu.VMEM((8, 128), F32),
        pltpu.SemaphoreType.DMA((semaphores,)),
        pltpu.SemaphoreType.DMA((semaphores,)),
        pltpu.SemaphoreType.DMA((20,)),
    ]
    results = pl.pallas_call(
        backward_kernel,
        out_shape=[shape(s, F32) for s in shapes] + [shape((2, piece, width), BF16)],
        in_specs=[hbm()] * len(operands) + [vmem()] * len(small_operands),
        out_specs=[vmem()] * 6,
        scratch_shapes=scratch,
        compiler_params=pltpu.CompilerParams(
            collective_id=2, has_side_effects=True, vmem_limit_bytes=67043328
        ),
        name="backward",
    )(*operands, *small_operands)
    return (results[:5], results[5])


def deliver_kernel(count, vectors, *refs):
    sources, small, token, refs = refs[:count], refs[count], refs[count + 1], refs[count + 2 :]
    targets, small_out, token_out, refs = (
        refs[:count], refs[count : count + 1 + len(vectors)], refs[count + 1 + len(vectors)],
        refs[count + 2 + len(vectors) :],
    )
    held, sems = refs[:count], refs[count]
    inward = [
        pltpu.make_async_copy(s, h, sems.at[i]) for i, (s, h) in enumerate(zip(sources, held))
    ]
    outward = [
        pltpu.make_async_copy(h, t, sems.at[count + i])
        for i, (h, t) in enumerate(zip(held, targets))
    ]
    for copy in inward:
        copy.start()
    small_out[0][...] = small[: small_out[0].shape[0], :]
    top = small_out[0].shape[0]
    for target, (row, lane, size) in zip(small_out[1:], vectors):
        target[...] = small[top + row : top + row + 1, lane : lane + size]
    token_out[...] = token[...].astype(F32)
    for arrived, leave in zip(inward, outward):
        arrived.wait()
        leave.start()
    for copy in outward:
        copy.wait()


def deliver(arrays, small, token, embed_rows, vectors):
    shape = jax.ShapeDtypeStruct
    count = len(arrays)
    outs = [shape(a.shape, a.dtype) for a in arrays]
    outs += [shape((embed_rows, small.shape[1]), F32)]
    outs += [shape((1, size), F32) for row, lane, size in vectors]
    outs += [shape(token.shape, F32)]
    results = pl.pallas_call(
        functools.partial(deliver_kernel, count, vectors),
        out_shape=outs,
        in_specs=[hbm()] * count + [vmem()] * 2,
        out_specs=[hbm()] * count + [vmem()] * (2 + len(vectors)),
        scratch_shapes=[pltpu.VMEM(a.shape, a.dtype) for a in arrays]
        + [pltpu.SemaphoreType.DMA((2 * count,))],
        compiler_params=pltpu.CompilerParams(vmem_limit_bytes=67043328),
        name="deliver",
    )(*arrays, small, token)
    middle = [r.reshape(-1) for r in results[count + 1 : -1]]
    return (results[:count], results[count], middle, results[-1])


def plane_device(
    tokens,
    segment_ids,
    project_weight,
    project_bias,
    output_weight,
    output_bias,
    first_gain,
    first_shift,
    up_weight,
    up_bias,
    down_weight,
    down_bias,
    second_gain,
    second_shift,
    embed_weight,
    out_cotangent,
    embed_cotangent,
):
    width = HEADS * HEAD_DIM
    piece = tokens.shape[2]
    rows = 2 * piece
    group = lax.axis_index("group")
    core = lax.rem(lax.axis_index("wide"), 2)
    lanes = embed_weight.shape[1]
    embed_rows = embed_weight.shape[0]
    lane_at = lax.rem(jnp.arange(2 * HEAD_DIM), HEAD_DIM // 2).astype(F32)
    frequency = (10000.0 ** (-lane_at * (2.0 / HEAD_DIM)))[None, :]
    packed = [
        vector[None, :]
        for vector in (
            project_bias, up_bias, output_bias, first_gain, first_shift, down_bias, second_gain, second_shift,
        )
    ]
    (
        project_full, token_rows, qkv, far_kv, context_low, norms, hidden_low, act_low, up_grad,
        down_grad, result_low, embed_cot, branch_grad, context_grad, first_grad, sums, ids,
        layer_out, embed_out, cosine, sine,
    ) = forward(
        [project_weight, embed_weight, output_weight, up_weight, down_weight],
        [tokens[:, 0], out_cotangent[:, 0], embed_cotangent[:, 0]],
        packed,
        segment_ids,
        frequency,
        up_weight.shape[1],
    )
    shapes = [
        down_weight.shape,
        up_weight.shape,
        output_weight.shape,
        project_weight.shape,
        (embed_rows + 32, lanes),
    ]
    outs, token_low = backward(
        (
            act_low, down_grad, hidden_low.reshape(2, piece, width), up_grad,
            context_low.reshape(2, piece, width), branch_grad, result_low,
            embed_cot.reshape(rows, lanes), token_rows, qkv, far_kv, context_grad, first_grad,
            project_full.reshape(width, 3 * width),
        ),
        (norms, ids, sums, cosine, sine, frequency),
        shapes,
        rows,
        width,
        up_weight.shape[1],
        lanes,
    )
    vectors = (
        (0, 0, 96), (2, 0, 32), (2, 32, 32), (2, 64, 32), (1, 0, 128), (2, 96, 32), (3, 0, 32), (3, 32, 32),
    )
    arrays, embed_grad, parts, token_grad = deliver(
        (layer_out, embed_out) + tuple(outs[:4]), outs[4], token_low, embed_rows, vectors
    )
    return (
        arrays[0][:, None],
        arrays[1][:, None],
        token_grad[:, None],
        arrays[5],
        parts[0],
        arrays[4],
        parts[1],
        parts[2],
        parts[3],
        arrays[3],
        parts[4],
        arrays[2],
        parts[5],
        parts[6],
        parts[7],
        embed_grad,
    )


def choose_device(mesh):
    if mesh.shape["group"] == PLANE and mesh.shape["wide"] == 2 * LINE:
        return plane_device
    return general_device


def solution(mesh):
    in_specs = (
        P(None, "wide", "group", None),
        P(None, "wide", None),
        P(("group", "wide"), None),
        P(("group", "wide")),
        P(("group", "wide"), None),
        P(("group", "wide")),
        P(("group", "wide")),
        P(("group", "wide")),
        P(("group", "wide"), None),
        P(("group", "wide")),
        P(("group", "wide"), None),
        P(("group", "wide")),
        P(("group", "wide")),
        P(("group", "wide")),
        P(("group", "wide"), None),
        P(None, "wide", "group", None),
        P(None, "wide", "group", None),
    )
    out_specs = (
        P(None, "wide", "group", None),
        P(None, "wide", "group", None),
        P(None, "wide", "group", None),
        P(("group", "wide"), None),
        P(("group", "wide")),
        P(("group", "wide"), None),
        P(("group", "wide")),
        P(("group", "wide")),
        P(("group", "wide")),
        P(("group", "wide"), None),
        P(("group", "wide")),
        P(("group", "wide"), None),
        P(("group", "wide")),
        P(("group", "wide")),
        P(("group", "wide")),
        P(("group", "wide"), None),
    )
    return jax.shard_map(
        choose_device(mesh), mesh=mesh, in_specs=in_specs, out_specs=out_specs, check_vma=False
    )
```

```python
import functools
from types import SimpleNamespace

import jax
import jax.numpy as jnp
from jax import lax
from jax.experimental import pallas as pl
from jax.experimental.pallas import tpu as pltpu
from jax.sharding import PartitionSpec as P

HEADS = 16
HEAD_DIM = 64


eps_norm = 1e-05
neg_large = -1e30


def rotary_tables(positions):
    half_dim = HEAD_DIM // 2
    frequency = 10000.0 ** (-jnp.arange(half_dim, dtype=jnp.float32) * (2.0 / HEAD_DIM))
    angles = positions[:, None] * frequency[None, :]
    angles = jnp.concatenate([angles, angles], axis=1)
    return (jnp.cos(angles), jnp.sin(angles))


def rotate(values, cosine_table, sine_table):
    half_dim = HEAD_DIM // 2
    swapped = jnp.concatenate([-values[..., half_dim:], values[..., :half_dim]], axis=-1)
    return values * cosine_table[:, None, :] + swapped * sine_table[:, None, :]


def unrotate(grads, cosine_table, sine_table):
    half_dim = HEAD_DIM // 2
    scaled = grads * sine_table[:, None, :]
    swapped = jnp.concatenate([scaled[..., half_dim:], -scaled[..., :half_dim]], axis=-1)
    return grads * cosine_table[:, None, :] + swapped


def norm_forward(resid, gain, shift):
    center = resid - jnp.mean(resid, axis=-1, keepdims=True)
    spread = jnp.mean(center * center, axis=-1, keepdims=True)
    rstd_rows = lax.rsqrt(spread + eps_norm)
    normed = center * rstd_rows
    return (normed * gain + shift, normed, rstd_rows)


def norm_backward(grads, normed, rstd_rows, gain):
    scaled = grads * gain
    resid_grad = rstd_rows * (
        scaled
        - jnp.mean(scaled, axis=-1, keepdims=True)
        - normed * jnp.mean(scaled * normed, axis=-1, keepdims=True)
    )
    return (resid_grad, jnp.sum(grads * normed, axis=0), jnp.sum(grads, axis=0))


def contract_rows(left, right):
    return lax.dot_general(
        left, right, (((0,), (0,)), ((), ())), preferred_element_type=jnp.float32
    )


def times_transpose(left, right):
    return lax.dot_general(
        left, right, (((1,), (1,)), ((), ())), preferred_element_type=jnp.float32
    )


def gelu_slope(value):
    normal_cdf = 0.5 * (1.0 + lax.erf(value * 0.7071067811865476))
    density = jnp.exp(-0.5 * value * value) * 0.3989422804014327
    return normal_cdf + value * density


def key_blocks(kv_rows, seg_all):
    seq_len = kv_rows.shape[0]
    block_rows = min(512, seq_len)
    count = seq_len // block_rows
    return (
        kv_rows.reshape(count, block_rows, 2, HEADS, HEAD_DIM),
        seg_all.reshape(count, block_rows),
    )


def block_scores(queries, key_block, same):
    scores = jnp.einsum("qhd,khd->hqk", queries, key_block, preferred_element_type=jnp.float32)
    scores = scores * HEAD_DIM ** (-0.5)
    return jnp.where(same[None], scores, neg_large)


def attention_forward(queries, blocks, seg_blocks, seg_local):
    length = queries.shape[0]

    def norm_step(carry, pieces):
        kv_block, seg_block = pieces
        same = seg_local[:, None] == seg_block[None, :]

        def norm_update(running):
            run_max, run_sum = running
            scores = block_scores(queries, kv_block[:, 0], same)
            new_max = jnp.maximum(run_max, jnp.max(scores, axis=-1))
            new_sum = run_sum * jnp.exp(run_max - new_max) + jnp.sum(
                jnp.exp(scores - new_max[..., None]), axis=-1
            )
            return (new_max, new_sum)

        def norm_unchanged(running):
            return running

        return (lax.cond(jnp.any(same), norm_update, norm_unchanged, carry), None)

    start = (
        jnp.full((HEADS, length), neg_large, jnp.float32),
        jnp.zeros((HEADS, length), jnp.float32),
    )
    (run_max, run_sum), unused = lax.scan(norm_step, start, (blocks, seg_blocks))
    log_norm = run_max + jnp.log(run_sum)

    def value_step(total, pieces):
        kv_block, seg_block = pieces
        same = seg_local[:, None] == seg_block[None, :]

        def value_update(running):
            scores = block_scores(queries, kv_block[:, 0], same)
            weights = jnp.exp(scores - log_norm[..., None]).astype(jnp.bfloat16)
            return running + jnp.einsum(
                "hqk,khd->qhd", weights, kv_block[:, 1], preferred_element_type=jnp.float32
            )

        def value_unchanged(running):
            return running

        return (lax.cond(jnp.any(same), value_update, value_unchanged, total), None)

    context, unused = lax.scan(
        value_step, jnp.zeros(queries.shape, jnp.float32), (blocks, seg_blocks)
    )
    return (context, log_norm)


def attention_backward(queries, blocks, seg_blocks, seg_local, log_norm, context_grad, delta):

    def grad_step(query_grad, pieces):
        kv_block, seg_block = pieces
        same = seg_local[:, None] == seg_block[None, :]

        def work(running):
            scores = block_scores(queries, kv_block[:, 0], same)
            probs = jnp.exp(scores - log_norm[..., None])
            prob_grad = jnp.einsum(
                "qhd,khd->hqk", context_grad, kv_block[:, 1], preferred_element_type=jnp.float32
            )
            score_grad = (probs * (prob_grad - delta[..., None])).astype(jnp.bfloat16)
            running = running + jnp.einsum(
                "hqk,khd->qhd", score_grad, kv_block[:, 0], preferred_element_type=jnp.float32
            ) * HEAD_DIM ** (-0.5)
            prob_low = probs.astype(jnp.bfloat16)
            key_grad = jnp.einsum(
                "hqk,qhd->khd", score_grad, queries, preferred_element_type=jnp.float32
            ) * HEAD_DIM ** (-0.5)
            value_grad = jnp.einsum(
                "hqk,qhd->khd", prob_low, context_grad, preferred_element_type=jnp.float32
            )
            return (running, jnp.stack([key_grad, value_grad], axis=1))

        def skipped(running):
            return (running, jnp.zeros(kv_block.shape, jnp.float32))

        return lax.cond(jnp.any(same), work, skipped, query_grad)

    query_grad, kv_grad = lax.scan(
        grad_step, jnp.zeros(queries.shape, jnp.float32), (blocks, seg_blocks)
    )
    return (query_grad, kv_grad.reshape(-1, 2 * HEADS * HEAD_DIM))


def general_device(
    tokens,
    segment_ids,
    project_weight,
    project_bias,
    output_weight,
    output_bias,
    first_gain,
    first_shift,
    up_weight,
    up_bias,
    down_weight,
    down_bias,
    second_gain,
    second_shift,
    embed_weight,
    out_cotangent,
    embed_cotangent,
):
    shards = (
        project_weight,
        project_bias,
        output_weight,
        output_bias,
        first_gain,
        first_shift,
        up_weight,
        up_bias,
        down_weight,
        down_bias,
        second_gain,
        second_shift,
        embed_weight,
    )
    length = tokens.shape[2]
    width = HEADS * HEAD_DIM
    head_shape = (length, HEADS, HEAD_DIM)
    place = lax.axis_index("group")
    positions = (place * length + jnp.arange(length)).astype(jnp.float32)
    cosine_table, sine_table = rotary_tables(positions)
    grad_total = None
    results = []
    embeddings = []
    input_grads = []
    for micro_index in range(tokens.shape[0]):
        params = (
            lax.all_gather(shards[0], ("group", "wide"), axis=0, tiled=True),
            lax.all_gather(shards[1], ("group", "wide"), axis=0, tiled=True),
            lax.all_gather(shards[2], ("group", "wide"), axis=0, tiled=True),
            lax.all_gather(shards[3], ("group", "wide"), axis=0, tiled=True),
            lax.all_gather(shards[4], ("group", "wide"), axis=0, tiled=True),
            lax.all_gather(shards[5], ("group", "wide"), axis=0, tiled=True),
            lax.all_gather(shards[6], ("group", "wide"), axis=0, tiled=True),
            lax.all_gather(shards[7], ("group", "wide"), axis=0, tiled=True),
            lax.all_gather(shards[8], ("group", "wide"), axis=0, tiled=True),
            lax.all_gather(shards[9], ("group", "wide"), axis=0, tiled=True),
            lax.all_gather(shards[10], ("group", "wide"), axis=0, tiled=True),
            lax.all_gather(shards[11], ("group", "wide"), axis=0, tiled=True),
            lax.all_gather(shards[12], ("group", "wide"), axis=0, tiled=True),
        )
        seg_all = segment_ids[micro_index, 0]
        seg_local = lax.dynamic_slice_in_dim(seg_all, place * length, length)
        token_low = tokens[micro_index, 0]
        token_wide = token_low.astype(jnp.float32)
        projected = jnp.dot(token_low, params[0], preferred_element_type=jnp.float32) + params[
            1
        ].astype(jnp.float32)
        queries = rotate(projected[:, :width].reshape(head_shape), cosine_table, sine_table).astype(
            jnp.bfloat16
        )
        key_rows = rotate(
            projected[:, width : 2 * width].reshape(head_shape), cosine_table, sine_table
        ).astype(jnp.bfloat16)
        value_rows = projected[:, 2 * width :].astype(jnp.bfloat16)
        local_kv = jnp.concatenate([key_rows.reshape(length, width), value_rows], axis=1)
        kv_all = lax.all_gather(local_kv, "group", axis=0, tiled=True)
        blocks, seg_blocks = key_blocks(kv_all, seg_all)
        context, log_norm = attention_forward(queries, blocks, seg_blocks, seg_local)
        context_low = context.reshape(length, width).astype(jnp.bfloat16)
        branch = jnp.dot(context_low, params[2], preferred_element_type=jnp.float32) + params[
            3
        ].astype(jnp.float32)
        first_gain_wide = params[4].astype(jnp.float32)
        hidden, first_normed, first_rstd = norm_forward(
            token_wide + branch, first_gain_wide, params[5].astype(jnp.float32)
        )
        hidden_low = hidden.astype(jnp.bfloat16)
        up_value = jnp.dot(hidden_low, params[6], preferred_element_type=jnp.float32) + params[
            7
        ].astype(jnp.float32)
        act_low = jax.nn.gelu(up_value, approximate=False).astype(jnp.bfloat16)
        down_value = jnp.dot(act_low, params[8], preferred_element_type=jnp.float32) + params[
            9
        ].astype(jnp.float32)
        second_gain_wide = params[10].astype(jnp.float32)
        result, second_normed, second_rstd = norm_forward(
            hidden + down_value, second_gain_wide, params[11].astype(jnp.float32)
        )
        result_low = result.astype(jnp.bfloat16)
        embedded = jnp.dot(result_low, params[12], preferred_element_type=jnp.float32)
        results.append(result_low)
        embeddings.append(embedded.astype(jnp.bfloat16))
        params = (
            lax.all_gather(shards[0], ("group", "wide"), axis=0, tiled=True),
            lax.all_gather(shards[1], ("group", "wide"), axis=0, tiled=True),
            lax.all_gather(shards[2], ("group", "wide"), axis=0, tiled=True),
            lax.all_gather(shards[3], ("group", "wide"), axis=0, tiled=True),
            lax.all_gather(shards[4], ("group", "wide"), axis=0, tiled=True),
            lax.all_gather(shards[5], ("group", "wide"), axis=0, tiled=True),
            lax.all_gather(shards[6], ("group", "wide"), axis=0, tiled=True),
            lax.all_gather(shards[7], ("group", "wide"), axis=0, tiled=True),
            lax.all_gather(shards[8], ("group", "wide"), axis=0, tiled=True),
            lax.all_gather(shards[9], ("group", "wide"), axis=0, tiled=True),
            lax.all_gather(shards[10], ("group", "wide"), axis=0, tiled=True),
            lax.all_gather(shards[11], ("group", "wide"), axis=0, tiled=True),
            lax.all_gather(shards[12], ("group", "wide"), axis=0, tiled=True),
        )
        embed_cot = embed_cotangent[micro_index, 0]
        result_grad = out_cotangent[micro_index, 0].astype(jnp.float32) + times_transpose(
            embed_cot, params[12]
        )
        embed_weight_grad = contract_rows(result_low, embed_cot)
        sum_grad, second_gain_grad, second_shift_grad = norm_backward(
            result_grad, second_normed, second_rstd, second_gain_wide
        )
        down_grad = sum_grad.astype(jnp.bfloat16)
        down_bias_grad = jnp.sum(down_grad.astype(jnp.float32), axis=0)
        down_weight_grad = contract_rows(act_low, down_grad)
        up_grad = (times_transpose(down_grad, params[8]) * gelu_slope(up_value)).astype(
            jnp.bfloat16
        )
        up_bias_grad = jnp.sum(up_grad.astype(jnp.float32), axis=0)
        up_weight_grad = contract_rows(hidden_low, up_grad)
        hidden_grad = sum_grad + times_transpose(up_grad, params[6])
        first_grad, first_gain_grad, first_shift_grad = norm_backward(
            hidden_grad, first_normed, first_rstd, first_gain_wide
        )
        branch_grad = first_grad.astype(jnp.bfloat16)
        output_bias_grad = jnp.sum(branch_grad.astype(jnp.float32), axis=0)
        output_weight_grad = contract_rows(context_low, branch_grad)
        context_grad = (
            times_transpose(branch_grad, params[2]).astype(jnp.bfloat16).reshape(head_shape)
        )
        delta = jnp.transpose(jnp.sum(context_grad.astype(jnp.float32) * context, axis=-1))
        kv_again = lax.all_gather(local_kv, "group", axis=0, tiled=True)
        blocks, seg_blocks = key_blocks(kv_again, seg_all)
        query_grad, kv_partial = attention_backward(
            queries, blocks, seg_blocks, seg_local, log_norm, context_grad, delta
        )
        kv_grad = lax.psum_scatter(
            kv_partial.astype(jnp.bfloat16), "group", scatter_dimension=0, tiled=True
        ).astype(jnp.float32)
        key_part = kv_grad[:, :width].reshape(head_shape)
        value_part = kv_grad[:, width:]
        query_back = unrotate(query_grad, cosine_table, sine_table).reshape(length, width)
        key_back = unrotate(key_part, cosine_table, sine_table).reshape(length, width)
        projected_grad = jnp.concatenate([query_back, key_back, value_part], axis=1).astype(
            jnp.bfloat16
        )
        project_bias_grad = jnp.sum(projected_grad.astype(jnp.float32), axis=0)
        project_weight_grad = contract_rows(token_low, projected_grad)
        input_grads.append(first_grad + times_transpose(projected_grad, params[0]))
        local_grads = (
            project_weight_grad,
            project_bias_grad,
            output_weight_grad,
            output_bias_grad,
            first_gain_grad,
            first_shift_grad,
            up_weight_grad,
            up_bias_grad,
            down_weight_grad,
            down_bias_grad,
            second_gain_grad,
            second_shift_grad,
            embed_weight_grad,
        )
        summed = (
            lax.psum_scatter(local_grads[0], ("group", "wide"), scatter_dimension=0, tiled=True),
            lax.psum_scatter(local_grads[1], ("group", "wide"), scatter_dimension=0, tiled=True),
            lax.psum_scatter(local_grads[2], ("group", "wide"), scatter_dimension=0, tiled=True),
            lax.psum_scatter(local_grads[3], ("group", "wide"), scatter_dimension=0, tiled=True),
            lax.psum_scatter(local_grads[4], ("group", "wide"), scatter_dimension=0, tiled=True),
            lax.psum_scatter(local_grads[5], ("group", "wide"), scatter_dimension=0, tiled=True),
            lax.psum_scatter(local_grads[6], ("group", "wide"), scatter_dimension=0, tiled=True),
            lax.psum_scatter(local_grads[7], ("group", "wide"), scatter_dimension=0, tiled=True),
            lax.psum_scatter(local_grads[8], ("group", "wide"), scatter_dimension=0, tiled=True),
            lax.psum_scatter(local_grads[9], ("group", "wide"), scatter_dimension=0, tiled=True),
            lax.psum_scatter(local_grads[10], ("group", "wide"), scatter_dimension=0, tiled=True),
            lax.psum_scatter(local_grads[11], ("group", "wide"), scatter_dimension=0, tiled=True),
            lax.psum_scatter(local_grads[12], ("group", "wide"), scatter_dimension=0, tiled=True),
        )
        grad_total = (
            summed
            if grad_total is None
            else tuple((total + part for total, part in zip(grad_total, summed)))
        )
    layer_out = jnp.stack(results)[:, None]
    embed_out = jnp.stack(embeddings)[:, None]
    token_grad = jnp.stack(input_grads)[:, None]
    return (
        layer_out,
        embed_out,
        token_grad,
        grad_total[0],
        grad_total[1],
        grad_total[2],
        grad_total[3],
        grad_total[4],
        grad_total[5],
        grad_total[6],
        grad_total[7],
        grad_total[8],
        grad_total[9],
        grad_total[10],
        grad_total[11],
        grad_total[12],
    )


MESH = pl.DeviceIdType.MESH
F32 = jnp.float32
BF16 = jnp.bfloat16
PLANE = 4
LINE = 4
GATHER_SEMS = 42
REDUCE_SEMS = 42
CORE, UPPER, LOWER, ROW, COLUMN, ARRIVED, HOP = 0, 4, 8, 12, 16, 20, 25
OWN_UPPER, OWN_LOWER, OWN_ROW, OWN_COLUMN, RING_ARRIVED, RING_HOP = 29, 30, 31, 32, 33, 38
PACKED_AT = ((0, 0), (1, 0), (2, 0), (2, 32), (2, 64), (2, 96), (3, 0), (3, 32))
FORWARD_PARTS = ((True, ((0, 0, 4, 0, 2, ), (1, 0, 4, 0, 4, ), (2, 0, 4, 0, 4, ), ), ), (False, ((0, 0, 4, 2, 4, ), ), ), (True, ((3, 0, 4, 0, 4, ), ), ), (True, ((4, 0, 4, 0, 4, ), ), ), (False, ((5, 0, 2, 0, 4, ), ), ), (True, ((5, 2, 4, 0, 4, ), ), ), )
FORWARD_STEPS = (((1003, 1, 1002, 20005, 2001, 0, 3, 2, 2000, 3001, 41, 1202, 10, 12, 4002, 42, 1103, 2041, 23, 2010, 2003, 3000, 2012, 20003, 1401, 3003, 2023, 51, 3041, 20, 2043, 1404, 2020, 20002, 52, 33, 1400, 53, 43, 113, 2013, 2033, 2052, 2032, 32, 3012, 1410, 1441, 4003, 222, 62, 202, 2042, 3010, 153, 2212, 143, 3002, 103, 2222, 4103, 63, 22, 133, 242, 252, 1424, 1451, 2051, 2002, 232, 3051, 2113, 4202, 1420, 262, 2232, 2133, 1414, 13, 2143, 3113, 163, 123, 1444, 5001, 3103, 3020, 1454, 212, 5002, 3023, 3053, 354, 2022, 2242, 2314, 334, 2053, 4401, 21005, 2334, 324, 344, 3052, 3013, 1464, 1434, 5000, 314, 304, 4400, 2103, 3202, 364, 900, 1900, 2062, 20900, 2153, ), ), ((), ), ((3033, 2202, 2252, ), (), (2123, ), (23004, 3063, 3032, 2063, 3043, ), (3042, ), (3153, 2344, 5010, 5041, 23900, ), ), ((3252, 5043, 5053, 5052, 4441, 3062, 3022, 2304, ), (5013, 5022, 3212, 5023, 4410, ), (3133, 2163, 3304, 3242, 3232, 3222, ), (3143, ), (5051, 3163, 2354, 5020, 3123, 2262, 2324, 21003, 5012, 5042, 3354, ), (3262, 5153, 4404, ), (3334, 3314, 5242, 5063, 4451, 5032, 5033, 2364, ), (4414, 3324, 2900, 3344, 21002, 5062, 4420, 5003, 3364, ), ), ((), (5143, 5113, 3900, 4454, 5232, 5222, 5212, ), ), ((4424, 5133, 5123, 5252, ), (), (4464, ), (5202, 4434, 5103, 5334, 5344, 5262, 5163, ), (4444, 5314, 5324, ), (5304, 5364, 5354, ), (), (4900, 5900, 21900, ), ), ((), (22003, 22005, ), ), ((), (), (), (), (22002, ), (), (), (), ), ((), (22900, ), ), )
BACKWARD_STEPS = ((900, 901, 0, 10, 1, 100, 902, 11, 110, ), ((300, 310, 210, ), (111, 101, 311, ), (410, ), (211, 20, 200, 213, 201, ), (312, 302, 301, ), (21, ), (411, ), (202, ), ), (911, 400, 120, 903, 212, 121, 401, 904, 303, 909, 905, 313, 30, 203, 402, 220, 31, 222, 930, 920, 130, 321, 530, 223, 320, 131, 906, 231, 322, 40, 323, 921, 922, 420, 140, 531, 332, 221, 330, 331, 232, 41, 340, 532, 240, 923, 230, 924, 925, 412, 141, 907, 912, 341, 242, 342, 421, 243, 430, 533, 241, 431, 333, 233, 440, 422, 413, 910, 730, 432, 630, 403, 441, 423, 908, 343, 442, 433, 830, 443, ), )


def place():
    group = lax.axis_index("group")
    wide = lax.axis_index("wide")
    return (group, lax.rem(group, 2), group // 2, wide // 2, lax.rem(wide, 2))


def when(cond, act):
    if cond is True:
        act()
    else:
        pl.when(cond)(act)


def both(left, right):
    return right if left is True else jnp.logical_and(left, right)


def remote(src, dst, send_sem, recv_sem, device):
    return pltpu.make_async_remote_copy(
        src_ref=src,
        dst_ref=dst,
        send_sem=send_sem,
        recv_sem=recv_sem,
        device_id=device,
        device_id_type=MESH,
    )


def entry_barrier():
    g, x, y, z, c = place()
    devices = []
    for step in range(1, 8):
        other = lax.rem(g * 2 + c + step, 8)
        devices.append((other // 2, z * 2 + lax.rem(other, 2)))
    devices.append((g, lax.rem(z + 1, LINE) * 2 + c))
    devices.append((g, lax.rem(z + LINE - 1, LINE) * 2 + c))
    barrier = pltpu.get_barrier_semaphore()
    for device in devices:
        pl.semaphore_signal(barrier, inc=1, device_id=device, device_id_type=MESH)
    pl.semaphore_wait(barrier, len(devices))


class Sender:
    def __init__(self, send_sems, recv_sems):
        self.send_sems, self.recv_sems = send_sems, recv_sems
        self.pending, self.draining = [], False

    def copy(self, src, dst, index, device):
        return remote(src, dst, self.send_sems.at[index], self.recv_sems.at[index], device)

    def send(self, cond, src, dst, index, device):
        copy = self.copy(src, dst, index, device)
        when(cond, copy.wait_send if self.draining else copy.start)

    def post(self, cond, src, dst, index, device):
        self.send(cond, src, dst, index, device)
        self.pending.append((cond, src, dst, index, device))

    def land(self, ref, index, device):
        self.copy(ref, ref, index, device).wait_recv()

    def do(self, cond, act):
        if not self.draining:
            when(cond, act)

    def drain(self, ticks):
        self.draining = True
        for tick in ticks:
            tick()
        for call in self.pending:
            self.send(*call)


def near_items(z, distance):
    if distance == 0:
        return [(0, z, True)]
    return [
        (distance, jnp.maximum(z - distance, 0), z >= distance),
        (3 + distance, jnp.minimum(z + distance, LINE - 1), z + distance < LINE),
    ]


class Gather:
    def __init__(self, parts, sender, local_sems):
        self.parts, self.sender, self.local_sems = parts, sender, local_sems
        self.seen = set()
        g, x, y, z, c = place()
        self.g, self.z, self.c = g, z, c
        self.gx, self.gy, self.gd = g + 1 - 2 * x, g + 2 - 4 * y, 3 - g
        self.devices = (
            (g, jnp.minimum(z + 1, LINE - 1) * 2 + c),
            (g, jnp.maximum(z - 1, 0) * 2 + c),
            (self.gx, z * 2 + c),
            (self.gy, z * 2 + c),
            (g, z * 2 + 1 - c),
        )
        for part in parts:
            for member in part[1]:
                self.own(member).start()

    def window(self, member, g, zi, c, rows=None):
        shard, full, top, count, left, columns, index = member
        first, last = (0, count) if rows is None else rows
        return full.at[g, zi, c, top + first : top + last, left : left + columns]

    def shard(self, member):
        shard, full, top, count, left, columns, index = member
        return shard.at[top : top + count, left : left + columns]

    def own(self, member):
        return pltpu.make_async_copy(
            self.shard(member),
            self.window(member, self.g, self.z, self.c),
            self.local_sems.at[member[6]],
        )

    def ring(self, member, zi, c):
        shard, full, top, count, left, columns, index = member
        return full.at[:, zi, c, top : top + count, left : left + columns]

    def item(self, slot):
        z = self.z
        if slot == 0:
            return z, True
        if slot < 4:
            return jnp.maximum(z - slot, 0), z >= slot
        return jnp.minimum(z + slot - 3, LINE - 1), z + slot - 3 < LINE

    def land(self, cond, ref, index):
        self.sender.do(cond, lambda: self.sender.land(ref, index, self.devices[4]))

    def arrivals(self, part, event, slot):
        zi, cond = self.item(slot)
        line = self.parts[part][0]
        for member in self.parts[part][1]:
            base, half, rows = member[6] * GATHER_SEMS, member[3] // 2, member[3]
            diagonal = lambda: (
                self.land(cond, self.window(member, self.gd, zi, self.c, (0, half)), base + 21 + slot),
                self.land(cond, self.window(member, self.gd, zi, self.c, (half, rows)), base + 28 + slot),
            )
            if event == 0 and slot > 0:
                self.land(cond, self.window(member, self.g, zi, self.c), base + slot)
            elif event == 1:
                self.land(cond, self.window(member, self.gx, zi, self.c), base + 7 + slot)
            elif event == 2:
                self.land(cond, self.window(member, self.gy, zi, self.c), base + 14 + slot)
            elif event == 3 or (event == 4 and slot == 0):
                diagonal()
                if slot == 0:
                    self.sender.do(True, lambda: self.own(member).wait())
            elif event == 4:
                self.land(cond, self.ring(member, zi, self.c), base + slot)

    def step(self, part, event, slot, link):
        if (part, event, slot) not in self.seen:
            self.seen.add((part, event, slot))
            self.arrivals(part, event, slot)
        zi, cond = self.item(slot)
        z, device = self.z, self.devices[link]
        for member in self.parts[part][1]:
            base, half, rows = member[6] * GATHER_SEMS, member[3] // 2, member[3]
            if link == 0:
                cond_here, index = both(cond, z < LINE - 1), base + slot + 1
            elif link == 1:
                cond_here, index = both(cond, z > 0), base + (4 if slot == 0 else slot + 1)
            else:
                cond_here = cond
                index = base + slot + ({2: 7, 3: 14} if event == 0 else {3: 21, 2: 28, 4: 35})[link]
            if event == 0:
                target = self.window(member, self.g, zi, self.c)
                source = self.shard(member) if slot == 0 else target
            elif event == 1:
                source = target = self.window(member, self.gx, zi, self.c, (0, half))
            elif event == 2:
                source = target = self.window(member, self.gy, zi, self.c, (half, rows))
            else:
                source = target = self.ring(member, zi, self.c)
            self.sender.send(cond_here, source, target, index, device)

    def finish(self, part):
        for member in self.parts[part][1]:
            for slot in range(7):
                zi, cond = self.item(slot)
                self.land(cond, self.ring(member, zi, 1 - self.c), member[6] * GATHER_SEMS + 35 + slot)


def staged(order, stages, delays):
    ticks = []
    for t in range(len(order) + delays[-1]):

        def tick(t=t):
            for stage, delay in zip(stages, delays):
                if 0 <= t - delay < len(order):
                    stage(*order[t - delay])

        ticks.append(tick)
    return ticks


def add_into(target, terms):
    rows, columns = target.shape
    step = next(s for s in (512, 256, columns) if columns % s == 0)

    def body(i, carry):
        cut = pl.ds(pl.multiple_of(i * step, step), step)
        value = terms[0][:, cut].astype(F32)
        for term in terms[1:]:
            value = value + term[:, cut].astype(F32)
        target[:, cut] = value.astype(target.dtype)
        return carry

    lax.fori_loop(0, columns // step, body, 0)


def sequence_core(g):
    return jnp.where(g < 2, g, PLANE - 1 - g)


class Exchange:
    def __init__(self, sources, targets, outward, sender, base, local_sems, local_base):
        self.sources, self.targets, self.outward = sources, targets, outward
        self.sender, self.base = sender, base
        self.local_sems, self.local_base = local_sems, local_base
        self.started = False
        g, x, y, z, c = place()
        self.g, self.z, self.c = g, z, c
        self.neighbours = {2: g + 1 - 2 * x, 3: g + 2 - 4 * y, 5: 3 - g}

    def device(self, index, outward):
        g, z, c = self.g, self.z, self.c
        if outward:
            return (c if index == 0 else PLANE - 1 - c, z * 2 + g // 2)
        return (2 * c + index, z * 2 + sequence_core(g))

    def same(self, device):
        return jnp.logical_and(device[0] == self.g, device[1] == self.z * 2 + self.c)

    def local(self, i, index, slot):
        return pltpu.make_async_copy(
            self.sources[i].at[index],
            self.targets[i].at[slot],
            self.local_sems.at[self.local_base + i],
        )

    def step(self, link):
        slot = lax.rem(self.g, 2) if self.outward else self.g // 2
        first = not self.started and not self.sender.draining
        self.started = True
        for i in range(len(self.sources)):
            for index in range(2):
                device = self.device(index, self.outward)
                if first:
                    when(self.same(device), lambda: self.local(i, index, slot).start())
                copy = remote(
                    self.sources[i].at[index],
                    self.targets[i].at[slot],
                    self.sender.send_sems.at[self.base + i * 4 + 2 + index],
                    self.sender.recv_sems.at[self.base + i * 4 + slot],
                    device,
                )
                cond = device[0] == self.neighbours[link]
                if link == 2:
                    here = jnp.logical_and(device[0] == self.g, device[1] != self.z * 2 + self.c)
                    cond = jnp.logical_or(cond, here)
                when(cond, copy.wait_send if self.sender.draining else copy.start)

    def arrive(self):
        for i in range(len(self.sources)):
            for index in range(2):
                device = self.device(index, not self.outward)
                target = self.targets[i].at[index]
                when(self.same(device), lambda: self.local(i, index, index).wait())
                when(
                    jnp.logical_not(self.same(device)),
                    lambda: self.sender.land(
                        target, self.base + i * 4 + index, (self.g, self.z * 2 + 1 - self.c)
                    ),
                )


def hbm():
    return pl.BlockSpec(memory_space=pltpu.HBM)


def vmem():
    return pl.BlockSpec(memory_space=pltpu.VMEM)


def chain(*ticks):
    def act():
        for tick in ticks:
            tick()

    return act


def run_with(ticks, steps, body):
    def act(i, carry):
        body(i)
        for j, tick in enumerate(ticks[:steps]):
            pl.when(i == j)(tick)
        return carry

    lax.fori_loop(0, steps, act, 0)
    for tick in ticks[steps:]:
        tick()


def lane_half(shape, period, half):
    lanes = lax.broadcasted_iota(jnp.int32, shape, 1)
    return lax.rem(lanes, period) < half


def turn(values):
    first = lane_half(values.shape, HEAD_DIM, HEAD_DIM // 2)
    return jnp.where(
        first,
        -pltpu.roll(values, values.shape[1] - HEAD_DIM // 2, 1),
        pltpu.roll(values, HEAD_DIM // 2, 1),
    )


def dot_rows(left, right):
    return lax.dot_general(left, right, (((1,), (0,)), ((), ())), preferred_element_type=F32)


def dot_columns(left, right):
    return lax.dot_general(left, right, (((1,), (1,)), ((), ())), preferred_element_type=F32)


def attend_pair(
    query_ref, key_ref, value_ref, far_key_ref, far_value_ref, seg_ref, seg_near_ref, seg_far_ref, out_ref, norm_ref
):
    rows = query_ref.shape[0]
    first = lane_half((rows, 128), 128, HEAD_DIM)
    tile = 256
    for r in range(rows // tile):
        rs = pl.ds(r * tile, tile)
        query = query_ref[rs, :]
        low_half = first[:tile]
        seg = seg_ref[rs, 0:1]
        near, far = seg == seg_near_ref[...], seg == seg_far_ref[...]
        outs, norms = [], []
        for h in range(2):
            keep = low_half if h == 0 else jnp.logical_not(low_half)
            one = jnp.where(keep, query, jnp.zeros_like(query))
            near_scores = jnp.where(near, dot_columns(one, key_ref[...]), neg_large)
            far_scores = jnp.where(far, dot_columns(one, far_key_ref[...]), neg_large)
            top = jnp.maximum(
                jnp.max(near_scores, axis=1, keepdims=True), jnp.max(far_scores, axis=1, keepdims=True)
            )
            near_expon, far_expon = jnp.exp(near_scores - top), jnp.exp(far_scores - top)
            total = jnp.sum(near_expon, axis=1, keepdims=True) + jnp.sum(
                far_expon, axis=1, keepdims=True
            )
            mixed = dot_rows(near_expon.astype(BF16), value_ref[...]) + dot_rows(
                far_expon.astype(BF16), far_value_ref[...]
            )
            outs.append(mixed / total)
            norms.append(jnp.broadcast_to(top + jnp.log(total), (tile, 128)))
        out_ref[rs, :] = jnp.where(low_half, outs[0], outs[1]).astype(BF16)
        flipped = jnp.transpose(jnp.where(low_half, norms[0], norms[1]))
        norm_ref[0:1, rs] = flipped[0:1]
        norm_ref[1:2, rs] = flipped[HEAD_DIM : HEAD_DIM + 1]


def stretch(packed, vectors, sizes):
    shards = packed.shape[0] // 32
    for row, lane, size, target in vectors:
        pick_rows = lax.broadcasted_iota(jnp.int32, (shards, shards * 32), 0) * 32 + row
        pick = lax.broadcasted_iota(jnp.int32, (shards, shards * 32), 1) == pick_rows
        part = dot_rows(pick.astype(F32).astype(BF16), packed).astype(BF16)
        step = 1024

        def body(i, carry):
            at = pl.multiple_of(i * step, step)
            column = (lax.broadcasted_iota(jnp.int32, (1, step), 1) + i * step).astype(F32)
            shard = jnp.floor((column + 0.5) * (1.0 / size))
            lane_of = (column - shard * size + lane).astype(jnp.int32)
            spread = lax.broadcasted_iota(jnp.int32, (128, step), 0) == lane_of
            value = dot_rows(part, spread.astype(F32).astype(BF16))
            keep = lax.broadcasted_iota(jnp.int32, (shards, step), 0) == shard.astype(jnp.int32)
            target[:, pl.ds(at, step)] = jnp.sum(jnp.where(keep, value, 0.0), axis=0, keepdims=True)
            return carry

        lax.fori_loop(0, shards * size // step, body, 0)


def flat(value):
    return value.reshape(-1, value.shape[-1])


def row_mean(value):
    return jnp.mean(value, axis=1, keepdims=True)


def forward_kernel(*refs):
    (project_shard, embed_shard, output_shard, up_shard, down_shard), refs = refs[:5], refs[5:]
    (tokens, out_cot, embed_cot), packed, refs = refs[:3], refs[3:11], refs[11:]
    (segments, frequency), refs = refs[:2], refs[2:]
    (
        project_out, token_out, qkv_out, far_out, context_out, norm, hidden_out, act_out, up_grad_out,
        down_grad_out, result_out, embed_cot_out, branch_grad_out, context_grad_out, first_grad_out,
        sums, seg_out, layer_back, embed_back, cosine_out, sine_out,
    ), refs = refs[:21], refs[21:]
    fulls, refs = refs[:6], refs[6:]
    (
        token_in, cot_in, embed_cot_in, far_seg, seg_column, vectors, qkv, far, context, normed, rstd,
        hidden_low, act, slope, result_low, embedded, sum_grad, down_grad, branch_grad, context_grad,
        cosine, sine, small_wide, small_shard, token_turned, context_turned, hidden_turned,
        send_sems, recv_sems, local_sems,
    ) = refs
    shards = (project_shard, embed_shard, small_shard, output_shard, up_shard, down_shard)
    project_w, embed_w, small_w, output_w, up_w, down_w = fulls
    g, x, y, z, c = place()
    partner = (g, z * 2 + 1 - c)
    rows, width = context.shape
    sender = Sender(send_sems, recv_sems)
    spare = sum(len(p[1]) for p in FORWARD_PARTS) * GATHER_SEMS
    flushed = []

    def flush(source, target, index):
        copy = pltpu.make_async_copy(source, target, local_sems.at[40 + index])
        copy.start()
        flushed.append((source, target, index))

    small_wide[...] = jnp.zeros_like(small_wide)
    for (row, lane), vector in zip(PACKED_AT, packed):
        small_wide[row : row + 1, lane : lane + vector.shape[1]] = vector[...].astype(F32)
    small_shard[...] = small_wide[...].astype(BF16)
    entry_barrier()
    parts = []
    for line, members in FORWARD_PARTS:
        rows_of = []
        for array, first_row, last_row, first_column, last_column in members:
            height, breadth = shards[array].shape
            top, left = first_row * height // 4, first_column * breadth // 4
            rows_of.append(
                (
                    shards[array],
                    fulls[array],
                    top,
                    last_row * height // 4 - top,
                    left,
                    last_column * breadth // 4 - left,
                    sum(len(p[1]) for p in parts) + len(rows_of),
                )
            )
        parts.append((line, rows_of))
    plan = Gather(parts, sender, local_sems)
    exchanges = {
        20: Exchange([tokens], [token_in], True, sender, spare + 2, local_sems, 20),
        21: Exchange(
            [out_cot, embed_cot], [cot_in, embed_cot_in], True, sender, spare + 6, local_sems, 21
        ),
        22: Exchange(
            [result_low, embedded], [layer_back, embed_back], False, sender, spare + 14, local_sems, 23
        ),
    }

    def perform(steps):
        def act():
            for step in steps:
                part, event, slot, link = step // 1000, step // 100 % 10, step // 10 % 10, step % 10
                if part == 23:
                    if event == 9:
                        sender.do(True, lambda: sender.land(far, spare + 1, partner))
                    else:
                        sender.send(True, qkv.at[:, width:], far, spare + 1, partner)
                elif part >= 20:
                    if event != 9:
                        exchanges[part].step(link)
                    elif not sender.draining:
                        exchanges[part].arrive()
                elif event == 9:
                    plan.finish(part)
                else:
                    plan.step(part, event, slot, link)

        return act

    ticks = [[perform(steps) for steps in phase] for phase in FORWARD_STEPS]
    sender.post(True, segments, far_seg, spare, partner)
    opening = FORWARD_STEPS[0][0]
    ready = next(i for i, step in enumerate(opening) if step < 20000 and step // 10 % 100 > 0)
    perform(opening[:ready])()
    row_at = lax.broadcasted_iota(jnp.int32, cosine.shape, 0) + c * rows
    angles = row_at.astype(F32) * frequency[...]
    cosine[...] = jnp.cos(angles)
    sine[...] = jnp.sin(angles)
    flush(cosine, cosine_out, 14)
    flush(sine, sine_out, 15)
    perform(opening[ready:])()
    sender.land(far_seg, spare, partner)
    micro = g // 2
    own_ids, far_ids = segments[micro].astype(F32), far_seg[micro].astype(F32)
    ids = jnp.where(sequence_core(g) == c, own_ids, far_ids)
    halves = (ids[:, :rows], ids[:, rows:])
    near_row = jnp.where(c == 0, halves[0], halves[1])
    far_row = jnp.where(c == 0, halves[1], halves[0])
    seg_out[0:1, :] = near_row
    seg_out[1:2, :] = far_row
    seg_column[...] = jnp.transpose(jnp.broadcast_to(near_row, (128, rows)))
    flush(project_w, project_out, 0)
    vector = lambda i, size: vectors.at[i : i + 1, 0:size]
    stretch(
        flat(small_w[...]),
        (
            (0, 0, 96, vector(0, 3 * width)),
            (1, 0, 128, vector(1, 4 * width)),
            (2, 0, 32, vector(2, width)),
            (2, 32, 32, vector(3, width)),
            (2, 64, 32, vector(4, width)),
            (2, 96, 32, vector(5, width)),
            (3, 0, 32, vector(6, width)),
            (3, 32, 32, vector(7, width)),
        ),
        None,
    )
    tile = 512
    wide = qkv.shape[1] // tile

    def project_tile(i):
        t = lax.rem(i + 2, wide)
        cut = pl.ds(pl.multiple_of(t * tile, tile), tile)
        value = dot_rows(flat(token_in[...]), flat(project_w[:, :, :, :, cut]))
        value = value + vectors[0:1, cut]

        @pl.when(t < 4)
        def _():
            factor = jnp.where(t < 2, HEAD_DIM ** (-0.5), 1.0)
            for j in range(tile // 128):
                part = value[:, j * 128 : (j + 1) * 128]
                part = (part * cosine[...] + turn(part) * sine[...]) * factor
                qkv[:, pl.ds(pl.multiple_of(t * tile + j * 128, 128), 128)] = part.astype(BF16)

        @pl.when(t >= 4)
        def _():
            qkv[:, cut] = value.astype(BF16)

    ticks[1][0]()
    run_with(ticks[2], wide, project_tile)
    flush(qkv, qkv_out, 2)
    flush(far, far_out, 3)

    def attend_one(i):
        at = pl.multiple_of(i * 128, 128)
        cut = lambda ref, base: ref.at[:, pl.ds(base + at, 128)]
        attend_pair(
            cut(qkv, 0), cut(qkv, width), cut(qkv, 2 * width), cut(far, 0), cut(far, width),
            seg_column, seg_out.at[0:1], seg_out.at[1:2], cut(context, 0), norm.at[i],
        )
        block, first = i // 2, lax.rem(i, 2) * 2
        tokens_here = flat(token_in[:, :, pl.ds(at, 128)])
        for source, target in ((tokens_here, token_turned), (context[:, pl.ds(at, 128)], context_turned)):
            target[block, pl.ds(first, 2)] = jnp.transpose(source).reshape(2, 2, 32, rows)

    run_with(ticks[3], width // 128, attend_one)
    flush(context_turned, context_out, 4)
    flush(token_turned, token_out, 1)
    half = rows // 2
    output_weight, bias_o = lambda: flat(output_w[...]), vectors[2:3, 0:width]

    def hidden_of(cut):
        return normed[cut, :] * vectors[3:4, 0:width] + vectors[4:5, 0:width]

    def branch_tile(i):
        cut = pl.ds(pl.multiple_of(i * half, half), half)
        resid = dot_rows(context[cut, :], output_weight()) + vectors[2:3, 0:width]
        resid = resid + token_in[i].astype(F32)
        center = resid - row_mean(resid)
        scale = lax.rsqrt(row_mean(center * center) + eps_norm)
        normed[cut, :] = center * scale
        rstd[0, cut, :] = jnp.broadcast_to(scale, (half, 128))
        low = hidden_of(cut).astype(BF16)
        hidden_low[cut, :] = low
        for j in range(width // 128):
            turned = jnp.transpose(low[:, j * 128 : (j + 1) * 128]).reshape(2, 2, 32, half)
            hidden_turned[j // 2, (j % 2) * 2 : (j % 2) * 2 + 2, :, :, cut] = turned

    run_with(ticks[4], 2, branch_tile)
    flush(hidden_turned, hidden_out, 5)

    def up_tile(j):
        cut = pl.ds(pl.multiple_of(j * tile, tile), tile)
        value = dot_rows(hidden_low[...], flat(up_w[:, :, :, :, cut])) + vectors[1:2, cut]
        below = 0.5 + 0.5 * lax.erf(value * 0.7071067811865476)
        density = jnp.exp(-0.5 * value * value) * 0.3989422804014327
        act[:, cut] = (value * below).astype(BF16)
        slope[:, cut] = (below + value * density).astype(BF16)

    ff = act.shape[1]
    run_with(ticks[5], ff // tile, up_tile)
    flush(act, act_out, 6)
    flush(embed_cot_in, embed_cot_out, 7)
    sums[...] = jnp.zeros_like(sums)

    def add_sum(row, value):
        sums[row : row + 1, 0:width] += jnp.sum(value, axis=0, keepdims=True)

    def norm_back(grads, row_normed, scale, gain):
        scaled = grads * gain
        return scale * (
            scaled - row_mean(scaled) - row_normed * row_mean(scaled * row_normed)
        )

    def down_tile(i):
        cut = pl.ds(pl.multiple_of(i * half, half), half)
        gain, shift = vectors[6:7, 0:width], vectors[7:8, 0:width]
        resid = dot_rows(act[cut, :], flat(down_w[...])) + vectors[5:6, 0:width]
        resid = resid + hidden_of(cut)
        center = resid - row_mean(resid)
        scale = lax.rsqrt(row_mean(center * center) + eps_norm)
        row_normed = center * scale
        low = (row_normed * gain + shift).astype(BF16)
        result_low[i] = low
        embed_full = flat(embed_w[...])
        embedded[i] = dot_rows(low, embed_full).astype(BF16)
        grads = cot_in[i].astype(F32) + dot_columns(embed_cot_in[i], embed_full)
        add_sum(6, grads * row_normed)
        add_sum(7, grads)
        total = norm_back(grads, row_normed, scale, gain)
        sum_grad[cut, :] = total
        low = total.astype(BF16)
        down_grad[cut, :] = low
        add_sum(5, low.astype(F32))

    run_with(ticks[6], 2, down_tile)
    flush(result_low, result_out, 8)
    flush(down_grad, down_grad_out, 9)

    def up_grad_tile(j):
        cut = pl.ds(pl.multiple_of(j * tile, tile), tile)
        part = flat(down_w[j // 2, pl.ds(lax.rem(j, 2) * 2, 2)])
        value = (dot_columns(down_grad[...], part) * slope[:, cut].astype(F32)).astype(BF16)
        slope[:, cut] = value
        sums[1:2, cut] = jnp.sum(value.astype(F32), axis=0, keepdims=True)

    run_with(ticks[7], ff // tile, up_grad_tile)
    flush(slope, up_grad_out, 10)

    def first_tile(i):
        cut = pl.ds(pl.multiple_of(i * half, half), half)
        grads = sum_grad[cut, :] + dot_columns(slope[cut, :], flat(up_w[...]))
        row_normed = normed[cut, :]
        add_sum(3, grads * row_normed)
        add_sum(4, grads)
        total = norm_back(grads, row_normed, rstd[0, cut, 0:1], vectors[3:4, 0:width])
        sum_grad[cut, :] = total
        low = total.astype(BF16)
        branch_grad[cut, :] = low
        add_sum(2, low.astype(F32))
        context_grad[cut, :] = dot_columns(low, output_weight()).astype(BF16)

    run_with(ticks[8], 2, first_tile)
    flush(sum_grad, first_grad_out, 11)
    flush(branch_grad, branch_grad_out, 12)
    flush(context_grad, context_grad_out, 13)
    sender.drain([tick for phase in ticks for tick in phase])
    for source, target, index in flushed:
        pltpu.make_async_copy(source, target, local_sems.at[40 + index]).wait()


def forward(shards, sources, packed, segments, frequency, ff):
    piece, width = sources[0].shape[1:]
    lanes = sources[2].shape[2]
    rows = 2 * piece
    semaphores = sum(len(p[1]) for p in FORWARD_PARTS) * GATHER_SEMS + 32
    small = (32, lanes)
    turned = (PLANE, LINE, 2, 32, rows)
    heights = [s.shape for s in shards[:2]] + [small] + [s.shape for s in shards[2:]]
    fulls = [(PLANE, LINE, 2) + s for s in heights]
    shape = jax.ShapeDtypeStruct
    outs = [
        shape(fulls[0], BF16),
        shape(turned, BF16),
        shape((rows, 3 * width), BF16),
        shape((rows, 2 * width), BF16),
        shape(turned, BF16),
        shape((width // 128, 8, rows), F32),
        shape(turned, BF16),
        shape((rows, ff), BF16),
        shape((rows, ff), BF16),
        shape((rows, width), BF16),
        shape((2, piece, width), BF16),
        shape((2, piece, lanes), BF16),
        shape((rows, width), BF16),
        shape((rows, width), BF16),
        shape((rows, width), F32),
        shape((8, ff), F32),
        shape((8, rows), F32),
        shape((2, piece, width), BF16),
        shape((2, piece, lanes), BF16),
        shape((rows, 128), F32),
        shape((rows, 128), F32),
    ]
    spaces = [hbm()] * len(outs)
    for i in (5, 15, 16):
        spaces[i] = vmem()
    scratch = [pltpu.VMEM(f, BF16) for f in fulls] + [
        pltpu.VMEM((2, piece, width), BF16),
        pltpu.VMEM((2, piece, width), BF16),
        pltpu.VMEM((2, piece, lanes), BF16),
        pltpu.VMEM(segments.shape, jnp.int32),
        pltpu.VMEM((rows, 128), F32),
        pltpu.VMEM((8, ff), F32),
        pltpu.VMEM((rows, 3 * width), BF16),
        pltpu.VMEM((rows, 2 * width), BF16),
        pltpu.VMEM((rows, width), BF16),
        pltpu.VMEM((rows, width), F32),
        pltpu.VMEM((1, rows, 128), F32),
        pltpu.VMEM((rows, width), BF16),
        pltpu.VMEM((rows, ff), BF16),
        pltpu.VMEM((rows, ff), BF16),
        pltpu.VMEM((2, piece, width), BF16),
        pltpu.VMEM((2, piece, lanes), BF16),
        pltpu.VMEM((rows, width), F32),
        pltpu.VMEM((rows, width), BF16),
        pltpu.VMEM((rows, width), BF16),
        pltpu.VMEM((rows, width), BF16),
        pltpu.VMEM((rows, 128), F32),
        pltpu.VMEM((rows, 128), F32),
        pltpu.VMEM(small, F32),
        pltpu.VMEM(small, BF16),
        pltpu.VMEM(turned, BF16),
        pltpu.VMEM(turned, BF16),
        pltpu.VMEM(turned, BF16),
        pltpu.SemaphoreType.DMA((semaphores,)),
        pltpu.SemaphoreType.DMA((semaphores,)),
        pltpu.SemaphoreType.DMA((60,)),
    ]
    return pl.pallas_call(
        forward_kernel,
        out_shape=outs,
        in_specs=[hbm()] * 8 + [vmem()] * 10,
        out_specs=spaces,
        scratch_shapes=scratch,
        compiler_params=pltpu.CompilerParams(
            collective_id=1, has_side_effects=True, vmem_limit_bytes=67043328
        ),
        name="forward",
    )(*shards, *sources, *packed, segments, frequency)


def attend_back_pair(
    query, key, value, far_key, far_value, grad, norm, seg_row, seg_near, seg_far, tables, summed
):
    rows = query.shape[0]
    tile = 256
    cosine, sine, shift = tables
    low_half = lane_half((rows, 128), 128, HEAD_DIM)
    query_low = lane_half((tile, 128), 128, HEAD_DIM)
    for total in summed:
        total[...] = jnp.zeros_like(total)

    def body(r, carry):
        rs = pl.ds(pl.multiple_of(r * tile, tile), tile)
        query_rows, grad_rows = query[rs, :], grad[rs, :]
        sides = ((key[...], value[...], seg_near), (far_key[...], far_value[...], seg_far))
        query_grads = []
        key_grads, value_grads = [[], []], [[], []]
        for h in range(2):
            keep = query_low if h == 0 else jnp.logical_not(query_low)
            one = jnp.where(keep, query_rows, jnp.zeros_like(query_rows))
            one_grad = jnp.where(keep, grad_rows, jnp.zeros_like(grad_rows))
            top = norm[h : h + 1, rs]
            kept = []
            delta = jnp.zeros((1, tile), F32)
            for keys, values, seg_key in sides:
                same = seg_key[:, 0:1] == seg_row[:, rs]
                scores = jnp.where(same, dot_columns(keys, one), neg_large)
                probs = jnp.exp(scores - top)
                product = probs * dot_columns(values, one_grad)
                delta = delta + jnp.sum(product, axis=0, keepdims=True)
                kept.append((probs, product))
            total = None
            for i, (keys, values, seg_key) in enumerate(sides):
                probs, product = kept[i]
                score_grad = (product - probs * delta).astype(BF16)
                key_grads[i].append(dot_rows(score_grad, query_rows))
                value_grads[i].append(dot_rows(probs.astype(BF16), grad_rows))
                part = contract_rows(score_grad, keys)
                total = part if total is None else total + part
            query_grads.append(total)
        for i in range(2):
            summed[i][...] += jnp.where(low_half, key_grads[i][0], key_grads[i][1])
            summed[2 + i][...] += jnp.where(low_half, value_grads[i][0], value_grads[i][1])
        joined = jnp.where(query_low, query_grads[0], query_grads[1]) * HEAD_DIM ** (-0.5)
        query[rs, :] = (joined * cosine[rs, :] - turn(joined) * sine[rs, :]).astype(BF16)
        return carry

    lax.fori_loop(0, rows // tile, body, 0)
    near, far = summed[0][...], summed[1][...]
    far_cosine = cosine[...] * shift[0:1, :] - sine[...] * shift[1:2, :]
    far_sine = sine[...] * shift[0:1, :] + cosine[...] * shift[1:2, :]
    key[...] = (near * cosine[...] - turn(near) * sine[...]).astype(BF16)
    value[...] = summed[2][...].astype(BF16)
    far_key[...] = (far * far_cosine - turn(far) * far_sine).astype(BF16)
    far_value[...] = summed[3][...].astype(BF16)


class Reduce:
    def __init__(self, arrays, sender):
        self.arrays, self.sender = arrays, sender
        g, x, y, z, c = place()
        self.g, self.z, self.c = g, z, c
        self.gx, self.gy, self.gd = g + 1 - 2 * x, g + 2 - 4 * y, 3 - g
        self.to_x, self.to_y = (self.gx, z * 2 + c), (self.gy, z * 2 + c)
        self.to_core = (g, z * 2 + 1 - c)
        lower = z < 2
        even = lax.rem(z, 2) == 0
        third = jnp.where(even, z + 1, z - 1)
        self.order = (jnp.where(lower, 3, 0), jnp.where(lower, 2, 1), third, z)
        self.rising = (lower, lower, even)

    def index(self, a, kind, i=0):
        return a * REDUCE_SEMS + kind + i

    def start(self, a, p):
        array, sender = self.arrays[a], self.sender

        def copy(b, i):
            other = self.arrays[b]
            return sender.copy(
                other.send.at[i % 2],
                other.held.at[self.order[i]],
                self.index(b, CORE, i),
                self.to_core,
            )

        if sender.draining:
            if p == 1 and a not in (1, 2):
                copy(a, 2).wait_send()
                copy(a, 3).wait_send()
            return
        before = (a, 0) if p == 1 else {2: (1, 2), 3: (2, 2)}.get(a)
        if before is not None:
            copy(before[0], before[1]).wait_send()
            copy(before[0], before[1] + 1).wait_send()
        zs = self.order[2 * p : 2 * p + 2]
        array.product(1 - self.c, zs, (array.send.at[0], array.send.at[1]), False)
        copy(a, 2 * p).start()
        copy(a, 2 * p + 1).start()

    def meet(self, a, p):
        array, sender = self.arrays[a], self.sender
        held, half_in, low = array.held, array.half, array.low
        rows, columns = held.shape[2:]
        cut = rows // 2
        zs = self.order[2 * p : 2 * p + 2]

        def work():
            for i in range(2):
                sender.land(held.at[zs[i]], self.index(a, CORE, 2 * p + i), self.to_x)
            array.product(self.c, zs, (held.at[zs[0]], held.at[zs[1]]), True)

        sender.do(True, work)
        for i in range(2):
            block = held.at[zs[i], self.gd]
            sender.send(
                True, block.at[0:cut, low:columns], half_in.at[zs[i], 0:cut],
                self.index(a, UPPER, 2 * p + i), self.to_y,
            )
            sender.send(
                True, block.at[cut:rows, low:columns], half_in.at[zs[i], cut:rows],
                self.index(a, LOWER, 2 * p + i), self.to_x,
            )

    def turn(self, a, i, upper):
        array, sender = self.arrays[a], self.sender
        held, half_in, whole_in, low = array.held, array.half, array.whole, array.low
        rows, columns = held.shape[2:]
        zi, cut = self.order[i], rows // 2
        first, last = (0, cut) if upper else (cut, rows)
        block = held.at[zi, self.gx if upper else self.gy, :, low:columns]

        def work():
            arrived = half_in.at[zi, first:last]
            sender.land(arrived, self.index(a, UPPER if upper else LOWER, i), self.to_x)
            add_into(block.at[first:last], [block.at[first:last], arrived])

        sender.do(True, work)
        sender.send(
            True, block, whole_in.at[zi, 0 if upper else 1],
            self.index(a, ROW if upper else COLUMN, i), self.to_x if upper else self.to_y,
        )

    def pass_on(self, i, source, lines, recv_kind, send_kind, a):
        z, zi = self.z, self.order[i]
        up = self.rising[i]
        slot = jnp.where(jnp.logical_and(jnp.logical_not(up), zi == z - 1), LINE, zi)
        copy = remote(
            source,
            lines.at[slot],
            self.sender.send_sems.at[self.index(a, send_kind, i)],
            self.sender.recv_sems.at[self.index(a, recv_kind) + slot],
            (self.g, jnp.where(up, z + 1, z - 1) * 2 + self.c),
        )
        if self.sender.draining:
            copy.wait_send()
        else:
            copy.start()

    def inner(self, i):
        return jnp.logical_or(
            jnp.logical_and(self.rising[i], self.z > 0),
            jnp.logical_and(jnp.logical_not(self.rising[i]), self.z < LINE - 1),
        )

    def along(self, a, i):
        array, sender = self.arrays[a], self.sender
        whole_in, lines, low = array.whole, array.line, array.low
        columns, zi, z = array.held.shape[3], self.order[i], self.z
        mine = array.held.at[zi, self.g, :, low:columns]
        terms = [mine, whole_in.at[zi, 0], whole_in.at[zi, 1]]
        arrived = self.index(a, ARRIVED)

        def work():
            sender.land(whole_in.at[zi, 0], self.index(a, ROW, i), self.to_x)
            sender.land(whole_in.at[zi, 1], self.index(a, COLUMN, i), self.to_x)
            if i < 3:
                inner = self.inner(i)

                def join():
                    sender.land(lines.at[zi], arrived + zi, self.to_x)
                    add_into(mine, terms + [lines.at[zi]])

                pl.when(inner)(join)
                pl.when(jnp.logical_not(inner))(lambda: add_into(mine, terms))
            else:
                self.close(lines, arrived, terms, array.out.at[:, low:columns])

        sender.do(True, work)
        if i < 3:
            self.pass_on(i, mine, lines, ARRIVED, HOP, a)

    def close(self, lines, arrived, terms, target):
        z, sender = self.z, self.sender
        rise, fall = lines.at[z], lines.at[LINE]
        pl.when(z > 0)(lambda: sender.land(rise, arrived + z, self.to_x))
        pl.when(z < LINE - 1)(lambda: sender.land(fall, arrived + LINE, self.to_x))
        pl.when(z == 0)(lambda: add_into(target, terms + [fall]))
        pl.when(z == LINE - 1)(lambda: add_into(target, terms + [rise]))
        pl.when(jnp.logical_and(z > 0, z < LINE - 1))(
            lambda: add_into(target, terms + [rise, fall])
        )

    def along_first(self, a, i):
        array, sender = self.arrays[a], self.sender
        low, rings, zi, z = array.low, array.rings, self.order[i], self.z
        mine = array.held.at[zi, :, :, 0:low]
        arrived = self.index(a, RING_ARRIVED)

        def add(slots):
            for j in range(PLANE):
                block = array.held.at[zi, j, :, 0:low]
                add_into(block, [block] + [rings.at[slot, j] for slot in slots])

        def work():
            if i < 3:

                def join():
                    sender.land(rings.at[zi], arrived + zi, self.to_x)
                    add([zi])

                pl.when(self.inner(i))(join)
                return
            pl.when(z > 0)(lambda: sender.land(rings.at[z], arrived + z, self.to_x))
            pl.when(z < LINE - 1)(lambda: sender.land(rings.at[LINE], arrived + LINE, self.to_x))
            pl.when(z == 0)(lambda: add([LINE]))
            pl.when(z == LINE - 1)(lambda: add([z]))
            pl.when(jnp.logical_and(z > 0, z < LINE - 1))(lambda: add([z, LINE]))

        sender.do(True, work)
        if i < 3:
            self.pass_on(i, mine, rings, RING_ARRIVED, RING_HOP, a)
            return
        block, half_in = array.held.at[z, self.gd, :, 0:low], array.own_half
        rows = half_in.shape[0]
        cut = rows // 2
        sender.send(
            True, block.at[0:cut], half_in.at[0:cut], self.index(a, OWN_UPPER), self.to_y
        )
        sender.send(
            True, block.at[cut:rows], half_in.at[cut:rows], self.index(a, OWN_LOWER), self.to_x
        )

    def turn_own(self, a, upper):
        array, sender = self.arrays[a], self.sender
        low, half_in = array.low, array.own_half
        rows = half_in.shape[0]
        first, last = (0, rows // 2) if upper else (rows // 2, rows)
        block = array.held.at[self.z, self.gx if upper else self.gy, :, 0:low]

        def work():
            arrived = half_in.at[first:last]
            sender.land(arrived, self.index(a, OWN_UPPER if upper else OWN_LOWER), self.to_x)
            add_into(block.at[first:last], [block.at[first:last], arrived])

        sender.do(True, work)
        sender.send(
            True, block, array.own_whole.at[0 if upper else 1],
            self.index(a, OWN_ROW if upper else OWN_COLUMN),
            self.to_x if upper else self.to_y,
        )

    def close_own(self, a):
        array, sender = self.arrays[a], self.sender
        low, whole_in = array.low, array.own_whole

        def work():
            sender.land(whole_in.at[0], self.index(a, OWN_ROW), self.to_x)
            sender.land(whole_in.at[1], self.index(a, OWN_COLUMN), self.to_x)
            mine = array.held.at[self.z, self.g, :, 0:low]
            add_into(array.out.at[:, 0:low], [mine, whole_in.at[0], whole_in.at[1]])

        sender.do(True, work)

    def step(self, code):
        kind, a, i = code // 100, code // 10 % 10, code % 10
        if kind == 0:
            self.start(a, i)
        elif kind == 1:
            self.meet(a, i)
        elif kind in (2, 3):
            self.turn(a, i, kind == 2)
        elif kind == 4:
            self.along(a, i)
        elif kind == 5:
            self.along_first(a, i)
        elif kind in (6, 7):
            self.turn_own(a, kind == 6)
        else:
            self.close_own(a)


def gather_up(vectors, target):
    shards = PLANE * LINE * 2
    total = None
    for row in sorted({v[0] for v in vectors}):
        share = jnp.zeros((shards, 128), F32)
        for at, lane, size, source in vectors:
            if at != row:
                continue
            step = 1024

            def body(i, carry):
                cut = pl.ds(pl.multiple_of(i * step, step), step)
                column = (lax.broadcasted_iota(jnp.int32, (1, step), 1) + i * step).astype(F32)
                shard = jnp.floor((column + 0.5) * (1.0 / size))
                lane_of = (column - shard * size + lane).astype(jnp.int32)
                spread = lax.broadcasted_iota(jnp.int32, (128, step), 0) == lane_of
                keep = lax.broadcasted_iota(jnp.int32, (shards, step), 0) == shard.astype(jnp.int32)
                value = jnp.where(keep, source[:, cut], 0.0).astype(BF16)
                return carry + dot_columns(value, spread.astype(F32).astype(BF16))

            share = lax.fori_loop(0, shards * size // step, body, share)
        pick_rows = lax.broadcasted_iota(jnp.int32, (shards, shards * 32), 0) * 32 + row
        pick = lax.broadcasted_iota(jnp.int32, (shards, shards * 32), 1) == pick_rows
        part = contract_rows(pick.astype(F32).astype(BF16), share.astype(BF16))
        total = part if total is None else total + part
    target[...] = total.astype(BF16).reshape(target.shape)


def backward_kernel(*refs):
    (
        act_hbm, down_grad_hbm, hidden_hbm, up_grad_hbm, context_hbm, branch_grad_hbm, result_hbm,
        embed_cot_hbm, token_hbm, qkv_hbm, far_hbm, context_grad_hbm, first_grad_hbm, weight_hbm,
        norm, segs, sums, cosine, sine, frequency,
    ), refs = refs[:20], refs[20:]
    outs, token_in, refs = refs[:5], refs[5], refs[6:]
    (send_d, send_u, send_s), refs = refs[:3], refs[3:]
    helds, halves, wholes, lines = [refs[i * 5 : (i + 1) * 5] for i in range(4)]
    (
        rings, own_half, own_whole,
        act, down_grad, up_grad, branch_grad, embed_cot, raw, turned_a, turned_b, qkv, far,
        far_back, context_grad, seg_near, seg_far, vectors, shares, token_out, shift,
        send_sems, recv_sems, local_sems,
    ) = refs[20:]
    g, x, y, z, c = place()
    partner = (g, z * 2 + 1 - c)
    rows, width = branch_grad.shape
    ff = act.shape[1]
    sender = Sender(send_sems, recv_sems)
    spare = 5 * REDUCE_SEMS

    def load(source, target, index):
        copy = lambda: pltpu.make_async_copy(source, target, local_sems.at[index])
        copy().start()
        return lambda: copy().wait()

    wait_act = load(act_hbm, act, 0)
    wait_down = load(down_grad_hbm, down_grad, 1)
    wait_raw = load(result_hbm, raw, 2)
    wait_hidden = load(hidden_hbm, turned_a, 19)
    wait_context = load(context_hbm, turned_b, 20)
    wait_up = load(up_grad_hbm, up_grad, 3)
    wait_branch = load(branch_grad_hbm, branch_grad, 4)
    wait_embed = load(embed_cot_hbm, embed_cot, 5)
    wait_qkv = load(qkv_hbm, qkv, 6)
    wait_far = load(far_hbm, far, 7)
    wait_grad = load(context_grad_hbm, context_grad, 8)
    entry_barrier()

    def product_of(turned, right):
        columns = right.shape[1]
        step = min(columns, 512)

        def act_on(parity, zs, targets, added):
            left = jnp.concatenate([flat(turned[:, zi, parity]) for zi in zs], axis=0)

            def body(i, carry):
                cut = pl.ds(pl.multiple_of(i * step, step), step)
                value = dot_rows(left, right[:, cut]).reshape(2, PLANE, 32, step)
                for j, target in enumerate(targets):
                    part = value[j]
                    if added:
                        part = part + target[:, :, cut].astype(F32)
                    target[:, :, cut] = part.astype(BF16)
                return carry

            lax.fori_loop(0, columns // step, body, 0)

        return act_on

    def down_product(parity, zs, targets, added):
        def body(j, carry):
            pieces = []
            for zi in zs:
                at = ((j * LINE + zi) * 2 + parity) * 128
                pieces.append(act[:, pl.ds(pl.multiple_of(at, 128), 128)])
            value = contract_rows(jnp.concatenate(pieces, axis=1), down_grad[...])
            for i, target in enumerate(targets):
                part = value[i * 128 : (i + 1) * 128]
                if added:
                    part = part + target[j].astype(F32)
                target[j] = part.astype(BF16)
            return carry

        lax.fori_loop(0, PLANE, body, 0)

    def share_product(parity, zs, targets, added):
        for zi, target in zip(zs, targets):
            value = shares[:, zi, parity]
            if added:
                value = (value.astype(F32) + target[...].astype(F32)).astype(BF16)
            target[...] = value

    shared = lambda columns: send_u.at[:, :, :, 0:columns]
    sends = (send_d, send_u, shared(width), shared(3 * width), send_s)
    products = [
        down_product,
        product_of(turned_a, up_grad),
        product_of(turned_b, branch_grad),
        product_of(turned_a, qkv),
        share_product,
    ]
    arrays = [
        SimpleNamespace(product=p, send=s, held=h, half=i, whole=w, line=l, out=o, low=0)
        for p, s, h, i, w, l, o in zip(products, sends, helds, halves, wholes, lines, outs)
    ]
    arrays[3].low, arrays[3].rings = rings.shape[3], rings
    arrays[3].own_half, arrays[3].own_whole = own_half, own_whole
    plan = Reduce(arrays, sender)
    token_back = Exchange([raw], [token_in], False, sender, spare + 2, local_sems, 18)
    parts, tile = 3 * width // 512, 512

    def fetch(t, begin):
        for r in range(2):
            at = ((t % 4) * 2 + r) * tile
            copy = pltpu.make_async_copy(
                weight_hbm.at[r * rows : (r + 1) * rows, t * tile : (t + 1) * tile],
                act.at[:, at : at + tile],
                local_sems.at[10 + (t % 4) * 2 + r],
            )
            copy.start() if begin else copy.wait()

    def fetched(t):
        fetch(t, False)
        for r in range(2):
            at = ((t % 4) * 2 + r) * tile
            half = token_out[:, r * tile : (r + 1) * tile]
            token_out[:, r * tile : (r + 1) * tile] = half + dot_columns(
                qkv[:, t * tile : (t + 1) * tile], act[:, at : at + tile]
            )
        if t + 4 < parts:
            fetch(t + 4, True)

    def embed_share():
        wait_raw()
        wait_embed()
        value = contract_rows(flat(raw[...]), embed_cot[...]).astype(BF16)
        shares[:, :, :, 0:32, :] = value.reshape(PLANE, LINE, 2, 32, 128)

    def before_attention():
        turned_by = jnp.broadcast_to(frequency[...] * float(rows), shift.shape)
        row = lax.broadcasted_iota(jnp.int32, shift.shape, 0)
        side = jnp.where(c == 0, 1.0, -1.0)
        shift[...] = jnp.where(row == 0, jnp.cos(turned_by), jnp.sin(turned_by) * side)
        wait_qkv()
        wait_far()
        wait_grad()
        seg_near[...] = jnp.transpose(jnp.broadcast_to(segs[0:1, :], (128, rows)))
        seg_far[...] = jnp.transpose(jnp.broadcast_to(segs[1:2, :], (128, rows)))

    def turn_tokens():
        load(token_hbm, turned_a, 19)()
        for t in range(4):
            fetch(t, True)

    def finish_tile(i):
        cut = pl.ds(pl.multiple_of(i * tile, tile), tile)

        @pl.when(i >= 2)
        def _():
            other = pl.ds(pl.multiple_of(jnp.maximum(i - 2, 0) * tile, tile), tile)
            qkv[:, cut] = (qkv[:, cut].astype(F32) + far_back[:, other].astype(F32)).astype(BF16)

        vectors[0:1, cut] = jnp.sum(qkv[:, cut].astype(F32), axis=0, keepdims=True)

    def other_shares():
        source = lambda i, size: (vectors if i == 0 else sums).at[i : i + 1, 0:size]
        gather_up(
            (
                (0, 0, 96, source(0, 3 * width)),
                (1, 0, 128, source(1, ff)),
                (2, 0, 32, source(2, width)),
                (2, 32, 32, source(3, width)),
                (2, 64, 32, source(4, width)),
                (2, 96, 32, source(5, width)),
                (3, 0, 32, source(6, width)),
                (3, 32, 32, source(7, width)),
            ),
            shares.at[:, :, :, 32:64, :],
        )

    def round_tokens():
        for i in range(2):
            raw[i] = token_out[i * (rows // 2) : (i + 1) * (rows // 2), :].astype(BF16)

    def attend_one(i):
        at = pl.multiple_of(i * 128, 128)
        cut = lambda ref, base: ref.at[:, pl.ds(base + at, 128)]
        attend_back_pair(
            cut(qkv, 0), cut(qkv, width), cut(qkv, 2 * width), cut(far, 0), cut(far, width),
            cut(context_grad, 0), norm.at[i], segs.at[0:1], seg_near, seg_far,
            (cosine, sine, shift), [token_out.at[:, j * 128 : (j + 1) * 128] for j in range(4)],
        )

    first_copy = pltpu.make_async_copy(first_grad_hbm, token_out, local_sems.at[9])
    others = {
        900: lambda: (wait_act(), wait_down()),
        901: lambda: (wait_hidden(), wait_up()),
        902: lambda: (wait_context(), wait_branch()),
        903: embed_share,
        904: turn_tokens,
        905: lambda: lax.fori_loop(0, parts, lambda i, carry: (finish_tile(i), carry)[1], 0),
        906: other_shares,
        907: round_tokens,
        908: lambda: None,
        909: lambda: sender.land(far_back, spare, partner),
        910: token_back.arrive,
        930: first_copy.wait,
    }
    for t in range(parts):
        others[920 + t] = lambda t=t: fetched(t)

    def perform(steps):
        def act_on():
            for step in steps:
                if step == 911:
                    sender.do(True, first_copy.start)
                    sender.send(True, far, far_back, spare, partner)
                elif step == 912:
                    for link in (5, 2, 3):
                        token_back.step(link)
                elif step >= 900:
                    if not sender.draining:
                        others[step]()
                else:
                    plan.step(step)

        return act_on

    first, middle, last = BACKWARD_STEPS
    ticks = [perform(steps) for steps in (first,) + middle + (last,)]
    ticks[0]()
    before_attention()
    run_with(ticks[1:-1], width // 128, attend_one)
    ticks[-1]()
    sender.drain(ticks)


def backward(operands, small_operands, shapes, rows, width, ff, lanes):
    shape = jax.ShapeDtypeStruct
    semaphores = 5 * REDUCE_SEMS + 16
    ring = (shapes[3][0], shapes[3][1] // 2)
    buffers = [pltpu.VMEM((2, PLANE) + shapes[i], BF16) for i in (0, 1, 4)]
    apart = shapes[:3] + [(ring[0], shapes[3][1] - ring[1])] + shapes[4:]
    buffers += [pltpu.VMEM((LINE, PLANE) + s, BF16) for s in shapes]
    for lead in ((LINE,), (LINE, 2), (LINE + 1,)):
        buffers += [pltpu.VMEM(lead + s, BF16) for s in apart]
    turned = pltpu.VMEM((PLANE, LINE, 2, 32, rows), BF16)
    piece = rows // 2
    scratch = buffers + [
        pltpu.VMEM((LINE + 1, PLANE) + ring, BF16),
        pltpu.VMEM(ring, BF16),
        pltpu.VMEM((2,) + ring, BF16),
        pltpu.VMEM((rows, ff), BF16),
        pltpu.VMEM((rows, width), BF16),
        pltpu.VMEM((rows, ff), BF16),
        pltpu.VMEM((rows, width), BF16),
        pltpu.VMEM((rows, lanes), BF16),
        pltpu.VMEM((2, piece, width), BF16),
        turned,
        turned,
        pltpu.VMEM((rows, 3 * width), BF16),
        pltpu.VMEM((rows, 2 * width), BF16),
        pltpu.VMEM((rows, 2 * width), BF16),
        pltpu.VMEM((rows, width), BF16),
        pltpu.VMEM((rows, 128), F32),
        pltpu.VMEM((rows, 128), F32),
        pltpu.VMEM((1, 3 * width), F32),
        pltpu.VMEM((PLANE, LINE, 2, 64, 128), BF16),
        pltpu.VMEM((rows, width), F32),
        pltpu.VMEM((8, 128), F32),
        pltpu.SemaphoreType.DMA((semaphores,)),
        pltpu.SemaphoreType.DMA((semaphores,)),
        pltpu.SemaphoreType.DMA((24,)),
    ]
    results = pl.pallas_call(
        backward_kernel,
        out_shape=[shape(s, F32) for s in shapes] + [shape((2, piece, width), BF16)],
        in_specs=[hbm()] * len(operands) + [vmem()] * len(small_operands),
        out_specs=[vmem()] * 6,
        scratch_shapes=scratch,
        compiler_params=pltpu.CompilerParams(
            collective_id=2, has_side_effects=True, vmem_limit_bytes=67043328
        ),
        name="backward",
    )(*operands, *small_operands)
    return (results[:5], results[5])


def deliver_kernel(count, vectors, *refs):
    sources, small, token, refs = refs[:count], refs[count], refs[count + 1], refs[count + 2 :]
    targets, small_out, token_out, refs = (
        refs[:count], refs[count : count + 1 + len(vectors)], refs[count + 1 + len(vectors)],
        refs[count + 2 + len(vectors) :],
    )
    held, wide, sems = refs[:count], refs[count], refs[count + 1]
    inward = [
        pltpu.make_async_copy(s, h, sems.at[i]) for i, (s, h) in enumerate(zip(sources, held))
    ]
    outward = [
        pltpu.make_async_copy(h, t, sems.at[count + i])
        for i, (h, t) in enumerate(zip(held, targets))
    ]
    for copy in inward:
        copy.start()
    wide[...] = token[...].astype(F32)
    token_copy = pltpu.make_async_copy(wide, token_out, sems.at[2 * count])
    token_copy.start()
    for arrived, leave in zip(inward, outward):
        arrived.wait()
        leave.start()
    small_out[0][...] = small[: small_out[0].shape[0], :]
    top = small_out[0].shape[0]
    for target, (row, lane, size) in zip(small_out[1:], vectors):
        target[...] = small[top + row : top + row + 1, lane : lane + size]
    for copy in outward:
        copy.wait()
    token_copy.wait()


def deliver(arrays, small, token, embed_rows, vectors):
    shape = jax.ShapeDtypeStruct
    count = len(arrays)
    outs = [shape(a.shape, a.dtype) for a in arrays]
    outs += [shape((embed_rows, small.shape[1]), F32)]
    outs += [shape((1, size), F32) for row, lane, size in vectors]
    outs += [shape(token.shape, F32)]
    results = pl.pallas_call(
        functools.partial(deliver_kernel, count, vectors),
        out_shape=outs,
        in_specs=[hbm()] * count + [vmem()] * 2,
        out_specs=[hbm()] * count + [vmem()] * (1 + len(vectors)) + [hbm()],
        scratch_shapes=[pltpu.VMEM(a.shape, a.dtype) for a in arrays]
        + [pltpu.VMEM(token.shape, F32), pltpu.SemaphoreType.DMA((2 * count + 1,))],
        compiler_params=pltpu.CompilerParams(vmem_limit_bytes=67043328),
        name="deliver",
    )(*arrays, small, token)
    middle = [r.reshape(-1) for r in results[count + 1 : -1]]
    return (results[:count], results[count], middle, results[-1])


def plane_device(
    tokens,
    segment_ids,
    project_weight,
    project_bias,
    output_weight,
    output_bias,
    first_gain,
    first_shift,
    up_weight,
    up_bias,
    down_weight,
    down_bias,
    second_gain,
    second_shift,
    embed_weight,
    out_cotangent,
    embed_cotangent,
):
    width = HEADS * HEAD_DIM
    piece = tokens.shape[2]
    rows = 2 * piece
    group = lax.axis_index("group")
    core = lax.rem(lax.axis_index("wide"), 2)
    lanes = embed_weight.shape[1]
    embed_rows = embed_weight.shape[0]
    lane_at = lax.rem(jnp.arange(2 * HEAD_DIM), HEAD_DIM // 2).astype(F32)
    frequency = (10000.0 ** (-lane_at * (2.0 / HEAD_DIM)))[None, :]
    packed = [
        vector[None, :]
        for vector in (
            project_bias, up_bias, output_bias, first_gain, first_shift, down_bias, second_gain, second_shift,
        )
    ]
    (
        project_full, token_rows, qkv, far_kv, context_low, norms, hidden_low, act_low, up_grad,
        down_grad, result_low, embed_cot, branch_grad, context_grad, first_grad, sums, ids,
        layer_out, embed_out, cosine, sine,
    ) = forward(
        [project_weight, embed_weight, output_weight, up_weight, down_weight],
        [tokens[:, 0], out_cotangent[:, 0], embed_cotangent[:, 0]],
        packed,
        segment_ids,
        frequency,
        up_weight.shape[1],
    )
    shapes = [
        down_weight.shape,
        up_weight.shape,
        output_weight.shape,
        project_weight.shape,
        (embed_rows + 32, lanes),
    ]
    outs, token_low = backward(
        (
            act_low, down_grad, hidden_low, up_grad, context_low, branch_grad, result_low,
            embed_cot.reshape(rows, lanes), token_rows, qkv, far_kv, context_grad, first_grad,
            project_full.reshape(width, 3 * width),
        ),
        (norms, ids, sums, cosine, sine, frequency),
        shapes,
        rows,
        width,
        up_weight.shape[1],
        lanes,
    )
    vectors = (
        (0, 0, 96), (2, 0, 32), (2, 32, 32), (2, 64, 32), (1, 0, 128), (2, 96, 32), (3, 0, 32), (3, 32, 32),
    )
    arrays, embed_grad, parts, token_grad = deliver(
        (layer_out, embed_out) + tuple(outs[:4]), outs[4], token_low, embed_rows, vectors
    )
    return (
        arrays[0][:, None],
        arrays[1][:, None],
        token_grad[:, None],
        arrays[5],
        parts[0],
        arrays[4],
        parts[1],
        parts[2],
        parts[3],
        arrays[3],
        parts[4],
        arrays[2],
        parts[5],
        parts[6],
        parts[7],
        embed_grad,
    )


def choose_device(mesh):
    if mesh.shape["group"] == PLANE and mesh.shape["wide"] == 2 * LINE:
        return plane_device
    return general_device


def solution(mesh):
    in_specs = (
        P(None, "wide", "group", None),
        P(None, "wide", None),
        P(("group", "wide"), None),
        P(("group", "wide")),
        P(("group", "wide"), None),
        P(("group", "wide")),
        P(("group", "wide")),
        P(("group", "wide")),
        P(("group", "wide"), None),
        P(("group", "wide")),
        P(("group", "wide"), None),
        P(("group", "wide")),
        P(("group", "wide")),
        P(("group", "wide")),
        P(("group", "wide"), None),
        P(None, "wide", "group", None),
        P(None, "wide", "group", None),
    )
    out_specs = (
        P(None, "wide", "group", None),
        P(None, "wide", "group", None),
        P(None, "wide", "group", None),
        P(("group", "wide"), None),
        P(("group", "wide")),
        P(("group", "wide"), None),
        P(("group", "wide")),
        P(("group", "wide")),
        P(("group", "wide")),
        P(("group", "wide"), None),
        P(("group", "wide")),
        P(("group", "wide"), None),
        P(("group", "wide")),
        P(("group", "wide")),
        P(("group", "wide")),
        P(("group", "wide"), None),
    )
    return jax.shard_map(
        choose_device(mesh), mesh=mesh, in_specs=in_specs, out_specs=out_specs, check_vma=False
    )
```
